32 devices in a mesh: clip: 2 (over y), pos: 16 (over z, x, core).
Axes of the slice: x: 2, y: 2, z: 4, core: 2. Of those that a mesh axis runs over, the one named last changes fastest.
Arguments:
- tokens: bfloat16 [128, 256, 768], P('clip', 'pos'), may hold values from -6 to 6
- clip_lengths: int32 [2, 4], P('clip'), may hold values from 1 to 32, 64 in all within a row
- timesteps: int32 [2, 4], P('clip'), may hold values from 0 to 999
- embed_first: bfloat16 [256, 768], replicated, may hold values from -0.375 to 0.375
- embed_second: bfloat16 [768, 768], replicated, may hold values from -0.21875 to 0.21875
- adaln_weight: bfloat16 [768, 6912], replicated, may hold values from -0.4375 to 0.4375
- spatial_in: bfloat16 [768, 2304], replicated, may hold values from -0.21875 to 0.21875
- spatial_out: bfloat16 [768, 768], replicated, may hold values from -0.875 to 0.875
- temporal_in: bfloat16 [768, 2304], replicated, may hold values from -0.21875 to 0.21875
- temporal_out: bfloat16 [768, 768], replicated, may hold values from -0.4375 to 0.4375
- hidden_up: bfloat16 [768, 3072], replicated, may hold values from -0.21875 to 0.21875
- hidden_down: bfloat16 [3072, 768], replicated, may hold values from -0.109375 to 0.109375
- grad_output: bfloat16 [128, 256, 768], P('clip', 'pos'), may hold values from -6 to 6
Outputs:
- block_out: bfloat16 [128, 256, 768], P('clip', 'pos')
- grad_tokens: bfloat16 [128, 256, 768], P('clip', 'pos')
- grad_embed_first: float32 [256, 768], P('pos')
- grad_embed_second: float32 [768, 768], P('pos')
- grad_adaln_weight: float32 [768, 6912], P('pos')
- grad_spatial_in: float32 [768, 2304], P('pos')
- grad_spatial_out: float32 [768, 768], P('pos')
- grad_temporal_in: float32 [768, 2304], P('pos')
- grad_temporal_out: float32 [768, 768], P('pos')
- grad_hidden_up: float32 [768, 3072], P('pos')
- grad_hidden_down: float32 [3072, 768], P('pos')
The draws below stay inside these ranges and needn't reach their ends.
Inputs may be any that keep to these rules, and one draw needn't show every extreme that they name: `clip_lengths`: row r lists in order the frame counts of the 4 clips that fill frames r * 64 to (r + 1) * 64 - 1; every row sums to 64 and its longest clip has 32 frames. `timesteps`: one diffusion timestep index per clip, in the order of clip_lengths.
All inputs are finite; a program needn't handle non-finite values.
Results may differ from the reference program's by a relative error of at most 0.02.
Values may be sent and summed in bfloat16 or wider, within the bound.
A program may use at most 448 MiB of HBM per device.

```python
import math
import jax
import jax.numpy as jnp
import numpy as np
from jax import lax

D = 768
HEADS = 12
HEAD_DIM = 64
FF = 3072
PATCHES = 256
FREQ = 256
FR_DEV = 64
CLIPS_DEV = 4
FRAMES = 128
N_CLIP = 2


def touch_ends(result, key, least, largest):
    longest = result.shape.index(max(result.shape))
    spots = []
    for shift in (0, 1):
        where = [jax.random.randint(jax.random.fold_in(key, axis), (), 0, length) for axis, length in enumerate(result.shape)]
        where[longest] = (where[longest] + shift) % result.shape[longest]
        spots.append(tuple(where))
    return result.at[spots[0]].set(least).at[spots[1]].set(largest)


def shard_levels(stream_key, shape, cuts, low, high):
    loudness = 1.0
    for position, parts in cuts:
        draws = jax.random.uniform(jax.random.fold_in(jax.random.fold_in(stream_key, 6), position), (parts,), jnp.float32, low / len(cuts), high / len(cuts))
        loudness = loudness * jnp.repeat(jnp.exp(draws), shape[position] // parts).reshape((-1,) + (1,) * (len(shape) - 1 - position))
    return loudness


def profile(number_of, total, most, slope):
    loads = [(1 << 20) // math.isqrt(standing ** slope) + 1 for standing in range(2, number_of + 1)]
    surplus, holding = total - most - (number_of - 1), [1] * (number_of - 1)
    while surplus > 0:
        movable = [i for i in range(number_of - 1) if holding[i] < most]
        whole, remaining = sum([loads[i] for i in movable]), surplus
        for i in movable:
            extra = min(most - holding[i], max(1, remaining * loads[i] // whole), surplus)
            holding[i] = holding[i] + extra
            surplus = surplus - extra
    return np.array([most] + holding)


def ragged_sizes(rng, number_of, total, bound, skew):
    if number_of == 2:
        one = jax.random.randint(rng, (), max(1, total - bound), min(bound, total - 1) + 1)
        return jnp.stack([one, total - one])
    sizes = jnp.asarray(profile(number_of, total, bound, skew), jnp.int32)
    couples = (number_of - 1) // 2
    donor, taker = sizes[1:1 + 2 * couples:2], sizes[2:2 + 2 * couples:2]
    margin = jnp.minimum(donor - 1, bound - taker)
    shifted = jax.random.randint(jax.random.fold_in(rng, 1), (couples,), 0, 1 << 20) % (margin + 1)
    sizes = sizes.at[1:1 + 2 * couples:2].set(donor - shifted).at[2:2 + 2 * couples:2].set(taker + shifted)
    return sizes[jax.random.permutation(jax.random.fold_in(rng, 2), number_of)]


def gaussian(stream_key, shape, scale, limit, cuts=(), held_as=jnp.bfloat16):
    array = jax.random.normal(stream_key, shape, jnp.float32) * scale
    if len(cuts) > 0:
        array = shard_levels(stream_key, shape, cuts, -0.22, 0.18) * array
    return jnp.clip(array, min=-limit, max=limit).astype(held_as)


def setup_inputs(seed: int = 0) -> dict:
    keys = jax.random.split(jax.random.key(seed), 14)
    return {
        "tokens": gaussian(keys[0], (FRAMES, PATCHES, D), 1.0, 6.0, ((0, 2), (1, 16))),
        "clip_lengths": jax.vmap(lambda own: ragged_sizes(own, CLIPS_DEV, FR_DEV, FR_DEV // 2, 2))(jax.random.split(keys[1], N_CLIP)).reshape((N_CLIP, CLIPS_DEV)).astype(jnp.int32),
        "timesteps": touch_ends(jax.random.randint(keys[2], (N_CLIP, CLIPS_DEV), 0, 1000), jax.random.fold_in(keys[2], 1), 0, 999).astype(jnp.int32),
        "embed_first": gaussian(keys[3], (FREQ, D), FREQ ** -0.5, 0.375),
        "embed_second": gaussian(keys[4], (D, D), D ** -0.5, 0.21875),
        "adaln_weight": gaussian(keys[5], (D, 9 * D), (D // 4) ** -0.5, 0.4375),
        "spatial_in": gaussian(keys[6], (D, 3 * D), D ** -0.5, 0.21875),
        "spatial_out": gaussian(keys[7], (D, D), (D // 16) ** -0.5, 0.875),
        "temporal_in": gaussian(keys[8], (D, 3 * D), D ** -0.5, 0.21875),
        "temporal_out": gaussian(keys[9], (D, D), (D // 4) ** -0.5, 0.4375),
        "hidden_up": gaussian(keys[10], (D, FF), D ** -0.5, 0.21875),
        "hidden_down": gaussian(keys[11], (FF, D), FF ** -0.5, 0.109375),
        "grad_output": gaussian(keys[12], (FRAMES, PATCHES, D), 1.0, 6.0, ((0, 2), (1, 16))),
    }


@jax.custom_vjp
def low(v):
    return lax.optimization_barrier(v.astype(jnp.bfloat16)).astype(jnp.float32)

@jax.custom_vjp
def low_back(v):
    return v

def low_keep(v):
    return (low(v), None)

def low_pass(kept, grad):
    return (grad,)

def back_keep(v):
    return (v, None)

def back_low(kept, grad):
    return (low(grad),)
low.defvjp(low_keep, low_pass)
low_back.defvjp(back_keep, back_low)
epsilon = 1e-06
highest = lax.Precision.HIGHEST
masked_score = -1000000000.0

def matmul(left, right):
    return jnp.dot(left, right, precision=highest, preferred_element_type=jnp.float32)

def frequency(step_ids):
    half_width = FREQ // 2
    rate_table = jnp.exp(-math.log(10000.0) * jnp.arange(half_width, dtype=jnp.float32) / half_width)
    angles = step_ids.astype(jnp.float32)[:, None] * rate_table[None, :]
    return jnp.concatenate([jnp.cos(angles), jnp.sin(angles)], axis=1)

def modulation(step_ids, first_w, second_w, adaln_w):
    hidden_cond = jax.nn.silu(matmul(frequency(step_ids), first_w))
    cond_vec = matmul(hidden_cond, second_w)
    return matmul(jax.nn.silu(cond_vec), adaln_w)

def clip_onehot(lengths, frames):
    clip_ends = jnp.cumsum(lengths)
    frame_ids = jnp.arange(frames, dtype=jnp.int32)
    clip_ids = lax.optimization_barrier(jnp.sum((frame_ids[:, None] >= clip_ends[None, :]).astype(jnp.int32), axis=1))
    onehot = (clip_ids[:, None] == jnp.arange(lengths.shape[0], dtype=jnp.int32)[None, :]).astype(jnp.float32)
    return (onehot, clip_ids)

def norm_mod(values, shift_vec, scale_vec):
    centre = values - lax.optimization_barrier(jnp.mean(values, axis=-1, keepdims=True))
    spread = lax.optimization_barrier(jnp.mean(centre * centre, axis=-1, keepdims=True))
    return centre * lax.rsqrt(spread + epsilon) * (1.0 + scale_vec) + shift_vec

def gelu_tanh(values):
    return jax.nn.gelu(values, approximate=True)

def split_qkv(normed, weight):
    frames, places = (normed.shape[0], normed.shape[1])
    joined = low(low_back(matmul(normed.reshape(frames * places, D), weight)))
    joined = joined.reshape(frames, places, 3, HEADS, HEAD_DIM)
    return (joined[:, :, 0], joined[:, :, 1], joined[:, :, 2])

def spatial_attend(normed, w_in, w_out):
    frames, places = (normed.shape[0], normed.shape[1])
    factor = 1.0 / math.sqrt(HEAD_DIM)
    queries, key_heads, value_heads = split_qkv(normed, w_in)
    scores = low_back(jnp.einsum('fqhd,fkhd->fhqk', queries, key_heads, precision=highest, preferred_element_type=jnp.float32) * factor)
    attention = jax.nn.softmax(scores, axis=-1)
    mixed_heads = jnp.einsum('fhqk,fkhd->fqhd', low(attention), value_heads, precision=highest, preferred_element_type=jnp.float32)
    mixed_heads = low(low_back(mixed_heads)).reshape(frames * places, D)
    return low_back(matmul(mixed_heads, w_out)).reshape(frames, places, D)

def temporal_attend(normed, clip_ids, w_in, w_out):
    frames, places = (normed.shape[0], normed.shape[1])
    factor = 1.0 / math.sqrt(HEAD_DIM)
    queries, key_heads, value_heads = split_qkv(normed, w_in)
    scores = low_back(jnp.einsum('fphd,gphd->phfg', queries, key_heads, precision=highest, preferred_element_type=jnp.float32) * factor)
    same_clip = (clip_ids[:, None] == clip_ids[None, :])[None, None]
    scores = jnp.where(same_clip, scores, masked_score)
    attention = jax.nn.softmax(scores, axis=-1)
    mixed_heads = jnp.einsum('phfg,gphd->fphd', low(attention), value_heads, precision=highest, preferred_element_type=jnp.float32)
    mixed_heads = low(low_back(mixed_heads)).reshape(frames * places, D)
    return low_back(matmul(mixed_heads, w_out)).reshape(frames, places, D)

def feed_forward(normed, w_up, w_down):
    frames, places = (normed.shape[0], normed.shape[1])
    upward = low_back(matmul(normed.reshape(frames * places, D), w_up))
    activated = low(gelu_tanh(upward))
    return low_back(matmul(activated, w_down)).reshape(frames, places, D)

def group_block(tokens, lengths, step_ids, weights):
    embed_first, embed_second, adaln_weight, spatial_in, spatial_out, temporal_in, temporal_out, hidden_up, hidden_down = weights
    modulated = modulation(step_ids, embed_first, embed_second, adaln_weight)
    onehot, clip_ids = clip_onehot(lengths, FR_DEV)
    per_frame = jnp.einsum('fc,cm->fm', onehot, modulated, precision=highest, preferred_element_type=jnp.float32)
    pieces = [per_frame[:, None, slot_index * D:(slot_index + 1) * D] for slot_index in range(9)]
    h_one = low(norm_mod(tokens, pieces[0], pieces[1]))
    x_one = tokens + pieces[2] * spatial_attend(h_one, spatial_in, spatial_out)
    h_two = low(norm_mod(x_one, pieces[3], pieces[4]))
    x_two = x_one + pieces[5] * temporal_attend(h_two, clip_ids, temporal_in, temporal_out)
    h_three = low(norm_mod(x_two, pieces[6], pieces[7]))
    return x_two + pieces[8] * feed_forward(h_three, hidden_up, hidden_down)

def reference(tokens, clip_lengths, timesteps, embed_first, embed_second, adaln_weight, spatial_in, spatial_out, temporal_in, temporal_out, hidden_up, hidden_down, grad_output):
    weights = tuple((weight.astype(jnp.float32) for weight in (embed_first, embed_second, adaln_weight, spatial_in, spatial_out, temporal_in, temporal_out, hidden_up, hidden_down)))
    start = tokens.astype(jnp.float32).reshape(N_CLIP, FR_DEV, PATCHES, D)

    def whole_block(token_groups, weight_list):

        def one_group(group_items):
            return jax.checkpoint(group_block)(group_items[0], group_items[1], group_items[2], weight_list)
        return lax.map(one_group, (token_groups, clip_lengths, timesteps))
    block_out, pull_back = jax.vjp(whole_block, start, weights)
    cotangent = grad_output.astype(jnp.float32).reshape(N_CLIP, FR_DEV, PATCHES, D)
    grad_start, grad_weights = pull_back(cotangent)
    return (block_out.reshape(FRAMES, PATCHES, D).astype(jnp.bfloat16), grad_start.reshape(FRAMES, PATCHES, D).astype(jnp.bfloat16), grad_weights[0], grad_weights[1], grad_weights[2], grad_weights[3], grad_weights[4], grad_weights[5], grad_weights[6], grad_weights[7], grad_weights[8])
```

```python
from functools import partial
import math

import jax
import jax.numpy as jnp
from jax import lax
from jax.experimental import pallas as pl
from jax.experimental.pallas import tpu as pltpu
from jax.sharding import PartitionSpec as P

HEADS = 12
HEAD_DIM = 64
FREQ = 256

epsilon = 1e-06
highest = lax.Precision.HIGHEST
masked_score = -1000000000.0
f32 = jnp.float32
bf16 = jnp.bfloat16


def frequency(step_ids):
    half_width = FREQ // 2
    rate_table = jnp.exp(
        -math.log(10000.0) * jnp.arange(half_width, dtype=jnp.float32) / half_width
    )
    angles = step_ids.astype(jnp.float32)[:, None] * rate_table[None, :]
    return jnp.concatenate([jnp.cos(angles), jnp.sin(angles)], axis=1)


def dot_high(left, right):
    return jnp.dot(left, right, precision=highest, preferred_element_type=f32)


def silu_grad(values):
    gate = jax.nn.sigmoid(values)
    return gate * (1.0 + values * (1.0 - gate))


def clip_onehot(lengths, frames):
    clip_ends = jnp.cumsum(lengths)
    frame_ids = jnp.arange(frames, dtype=jnp.int32)
    clip_ids = jnp.sum((frame_ids[:, None] >= clip_ends[None, :]).astype(jnp.int32), axis=1)
    onehot = (clip_ids[:, None] == jnp.arange(lengths.shape[0], dtype=jnp.int32)[None, :]).astype(
        jnp.float32
    )
    return (onehot, clip_ids)


def weight_grad(left, right):
    return jnp.einsum("rd,rk->dk", left, right, preferred_element_type=f32).astype(bf16)


def bdot(left, right):
    return lax.dot_general(left, right, (((1,), (0,)), ((), ())), preferred_element_type=f32)


def bdot_nt(left, right):
    return lax.dot_general(left, right, (((1,), (1,)), ((), ())), preferred_element_type=f32)


def bdot_tn(left, right):
    return lax.dot_general(left, right, (((0,), (0,)), ((), ())), preferred_element_type=f32)


def norm_rows(values):
    width = values.shape[-1]
    centre = values - jnp.sum(values, axis=-1, keepdims=True) * (1.0 / width)
    spread = jnp.sum(centre * centre, axis=-1, keepdims=True) * (1.0 / width)
    inverse = lax.rsqrt(spread + epsilon)
    return centre * inverse, inverse


def norm_rows_back(normed, inverse, scale_vec, grad):
    width = grad.shape[-1]
    inner = grad * (1.0 + scale_vec)
    mean_one = jnp.sum(inner, axis=-1, keepdims=True) * (1.0 / width)
    mean_two = jnp.sum(inner * normed, axis=-1, keepdims=True) * (1.0 / width)
    return inverse * (inner - mean_one - normed * mean_two)


def pair_masks(scale):
    lanes = lax.broadcasted_iota(jnp.int32, (1, 2 * HEAD_DIM), 1)
    low_half = jnp.where(lanes < HEAD_DIM, scale, 0.0).astype(bf16)
    high_half = jnp.where(lanes < HEAD_DIM, 0.0, scale).astype(bf16)
    return low_half, high_half


ROWS = 32


def load_rows(ref, step):
    places, width = ref.shape[2:]
    count = max(1, ROWS // places)
    part = ref[pl.ds(step * count, count), 0].astype(f32)
    return part.reshape(count * places, width)


def store_rows(ref, step, values):
    places, width = ref.shape[2:]
    count = max(1, ROWS // places)
    ref[pl.ds(step * count, count), 0] = values.reshape(count, places, width).astype(bf16)


def space_forward(x_ref, mod_ref, w_ref, h_ref, qkv_ref, o_ref, lse_ref):
    patches, width = h_ref.shape[1:]
    places = x_ref.shape[2]
    pair = 2 * HEAD_DIM
    shift, scale = mod_ref[0, 0:1, :], mod_ref[0, 1:2, :]

    def norm_step(step, _):
        normed, _inverse = norm_rows(load_rows(x_ref, step))
        h_ref[0, pl.ds(step * ROWS, ROWS), :] = (normed * (1.0 + scale) + shift).astype(bf16)
        return 0

    lax.fori_loop(0, patches // ROWS, norm_step, 0)
    for part in range(3):
        cols = slice(part * width, (part + 1) * width)
        qkv_ref[0, :, cols] = bdot(h_ref[0], w_ref[:, cols]).astype(bf16)
    masks = pair_masks(1.0 / math.sqrt(HEAD_DIM))
    lane_ids = lax.broadcasted_iota(jnp.int32, (1, pair), 1)
    lse_ref[0] = jnp.zeros((patches, pair), f32)

    def head_pair(index, _):
        at = pl.multiple_of(index * pair, pair)
        q = qkv_ref[0, :, pl.ds(at, pair)]
        k = qkv_ref[0, :, pl.ds(pl.multiple_of(width + at, pair), pair)]
        v = qkv_ref[0, :, pl.ds(pl.multiple_of(2 * width + at, pair), pair)]
        outs = []
        lse = lse_ref[0]
        for half in range(2):
            scores = bdot_nt(q * masks[half], k)
            top = jnp.max(scores, axis=-1, keepdims=True)
            exps = jnp.exp(scores - top)
            total = jnp.sum(exps, axis=-1, keepdims=True)
            probs = (exps * (1.0 / total)).astype(bf16)
            outs.append(bdot(probs, v))
            lse = jnp.where(lane_ids == 2 * index + half, top + jnp.log(total), lse)
        lse_ref[0] = lse
        both = jnp.where(lane_ids < HEAD_DIM, outs[0], outs[1])
        o_ref[:, 0, :, pl.ds(at, pair)] = both.reshape(patches // places, places, pair).astype(bf16)
        return 0

    lax.fori_loop(0, HEADS // 2, head_pair, 0)


def space_backward(
    go_ref, qkv_ref, lse_ref, x_ref, mod_ref, w_ref, dqkv_ref, dv_ref, sum_ref, e_ref
):
    patches = qkv_ref.shape[1]
    width = x_ref.shape[3]
    places = x_ref.shape[2]
    pair = 2 * HEAD_DIM
    scale = mod_ref[0, 1:2, :]
    factor = 1.0 / math.sqrt(HEAD_DIM)
    masks_q = pair_masks(factor)
    masks = pair_masks(1.0)
    lane_ids = lax.broadcasted_iota(jnp.int32, (1, pair), 1)

    def head_pair(index, _):
        at = pl.multiple_of(index * pair, pair)
        k_at = pl.multiple_of(width + at, pair)
        v_at = pl.multiple_of(2 * width + at, pair)
        q = qkv_ref[0, :, pl.ds(at, pair)]
        k = qkv_ref[0, :, pl.ds(k_at, pair)]
        v = qkv_ref[0, :, pl.ds(v_at, pair)]
        go = go_ref[:, 0, :, pl.ds(at, pair)].astype(f32).reshape(patches, pair).astype(bf16)
        lse_all = lse_ref[0]
        gq, gk, gv = None, None, None
        for half in range(2):
            lse = jnp.sum(
                jnp.where(lane_ids == 2 * index + half, lse_all, 0.0), axis=-1, keepdims=True
            )
            q_half = q * masks_q[half]
            go_half = go * masks[half]
            probs = jnp.exp(bdot_nt(q_half, k) - lse)
            grad_p = bdot_nt(go_half, v)
            inner = jnp.sum(grad_p * probs, axis=-1, keepdims=True)
            grad_s = (probs * (grad_p - inner)).astype(bf16)
            part_q = bdot(grad_s, k * masks_q[half])
            part_k = bdot_tn(grad_s, q_half)
            part_v = bdot_tn(probs.astype(bf16), go_half)
            gq = part_q if gq is None else gq + part_q
            gk = part_k if gk is None else gk + part_k
            gv = part_v if gv is None else gv + part_v
        dqkv_ref[0, :, pl.ds(at, pair)] = gq.astype(bf16)
        dqkv_ref[0, :, pl.ds(k_at, pair)] = gk.astype(bf16)
        dqkv_ref[0, :, pl.ds(v_at, pair)] = gv.astype(bf16)
        return 0

    lax.fori_loop(0, HEADS // 2, head_pair, 0)
    e_ref[...] = bdot_nt(dqkv_ref[0], w_ref[...])

    def norm_step(step, sums):
        grad = e_ref[pl.ds(step * ROWS, ROWS), :]
        normed, inverse = norm_rows(load_rows(x_ref, step))
        store_rows(dv_ref, step, norm_rows_back(normed, inverse, scale, grad))
        folded = grad.reshape(ROWS // 8, 8, width).sum(axis=0)
        folded_n = (grad * normed).reshape(ROWS // 8, 8, width).sum(axis=0)
        return sums[0] + folded, sums[1] + folded_n

    zero = jnp.zeros((8, width), f32)
    shift_sum, scale_sum = lax.fori_loop(0, patches // ROWS, norm_step, (zero, zero))
    sum_ref[0, 0:1, :] = jnp.sum(shift_sum, axis=0, keepdims=True)
    sum_ref[0, 1:2, :] = jnp.sum(scale_sum, axis=0, keepdims=True)


GELU_C = math.sqrt(2.0 / math.pi)


def middle(
    o1_ref, x_ref, g_ref, mod_ref, clip_ref, wso_ref, wti_ref, wto_ref, wup_ref, wdn_ref,
    out_ref, act_ref, dz_ref, h3_ref, du_ref, o2_ref, dy2_ref, h2_ref, dqkv_ref, dy1_ref, do1_ref,
    dx1_ref, sum_ref,
    qkv_ref, p_ref, y1_ref, y2_ref, n2_ref, n3_ref, r2_ref, r3_ref, xa_ref, gp_ref, e_ref,
):
    count, frames, width = x_ref.shape
    rows = count * frames
    pair = 2 * HEAD_DIM
    hidden = act_ref.shape[1]
    factor = 1.0 / math.sqrt(HEAD_DIM)
    per = frames // ROWS
    steps = rows // ROWS

    @pl.when(pl.program_id(0) == 0)
    def _():
        sum_ref[...] = jnp.zeros_like(sum_ref)

    def at_rows(step):
        return step // per, pl.ds(lax.rem(step, per) * ROWS, ROWS), pl.ds(step * ROWS, ROWS)

    def mod(index, part):
        return mod_ref[index, part, :]

    y1_ref[...] = bdot(o1_ref[...].reshape(rows, width), wso_ref[...])

    def step_one(step, _):
        place, part, flat = at_rows(step)
        x_one = x_ref[place, part, :].astype(f32) + mod(2, part) * y1_ref[flat, :]
        xa_ref[flat, :] = x_one
        normed, inverse = norm_rows(x_one)
        n2_ref[flat, :] = normed
        r2_ref[flat, :] = jnp.broadcast_to(inverse, (ROWS, pair))
        h2_ref[flat, :] = (normed * (1.0 + mod(4, part)) + mod(3, part)).astype(bf16)
        return 0

    lax.fori_loop(0, steps, step_one, 0)
    for third in range(3):
        cols = slice(third * width, (third + 1) * width)
        qkv_ref[:, cols] = bdot(h2_ref[...], wti_ref[:, cols]).astype(bf16)

    masks = pair_masks(1.0)
    masks_q = pair_masks(factor)
    lane_ids = lax.broadcasted_iota(jnp.int32, (1, pair), 1)
    is_low = lane_ids < HEAD_DIM
    allowed = clip_ref[...] > 0.5

    def halves(values, reduce, neutral):
        low_part = reduce(jnp.where(is_low, values, neutral), axis=-1, keepdims=True)
        high_part = reduce(jnp.where(is_low, neutral, values), axis=-1, keepdims=True)
        return jnp.where(is_low, low_part, high_part)

    def stacked(values, pair_of_masks):
        return jnp.concatenate([values * pair_of_masks[0], values * pair_of_masks[1]], axis=0)

    def pair_at(index):
        at = pl.multiple_of(index * pair, pair)
        return (
            pl.ds(at, pair),
            pl.ds(pl.multiple_of(width + at, pair), pair),
            pl.ds(pl.multiple_of(2 * width + at, pair), pair),
        )

    def time_pair(index, _):
        q_at, k_at, v_at = pair_at(index)
        for place in range(count):
            part = slice(place * frames, (place + 1) * frames)
            q = qkv_ref[part, q_at]
            keys = stacked(qkv_ref[part, k_at], masks_q)
            values = stacked(qkv_ref[part, v_at], masks)
            scores = jnp.where(allowed, bdot_nt(q, keys), masked_score)
            exps = jnp.exp(scores - halves(scores, jnp.max, -jnp.inf))
            probs = exps / halves(exps, jnp.sum, 0.0)
            p_ref[index, part, :] = probs
            o2_ref[part, q_at] = bdot(probs.astype(bf16), values).astype(bf16)
        return 0

    lax.fori_loop(0, HEADS // 2, time_pair, 0)

    y2_ref[...] = bdot(o2_ref[...], wto_ref[...])

    def step_two(step, _):
        place, part, flat = at_rows(step)
        x_two = xa_ref[flat, :] + mod(5, part) * y2_ref[flat, :]
        xa_ref[flat, :] = x_two
        normed, inverse = norm_rows(x_two)
        n3_ref[flat, :] = normed
        r3_ref[flat, :] = jnp.broadcast_to(inverse, (ROWS, pair))
        h3_ref[flat, :] = (normed * (1.0 + mod(7, part)) + mod(6, part)).astype(bf16)
        dz_ref[flat, :] = (mod(8, part) * g_ref[place, part, :].astype(f32)).astype(bf16)
        return 0

    lax.fori_loop(0, steps, step_two, 0)

    tile = 256

    def up_tile(index, _):
        cols = pl.ds(pl.multiple_of(index * tile, tile), tile)
        u = bdot(h3_ref[...], wup_ref[:, cols])
        square = u * u
        tanh = jnp.tanh(GELU_C * (u * (1.0 + 0.044715 * square)))
        half = 0.5 * (1.0 + tanh)
        act_ref[:, cols] = (u * half).astype(bf16)
        slope = half + (0.5 * GELU_C) * u * (1.0 - tanh * tanh) * (1.0 + (3.0 * 0.044715) * square)
        du = bdot_nt(dz_ref[...], wdn_ref[cols, :]) * slope
        du_ref[:, cols] = du.astype(bf16)
        return 0

    lax.fori_loop(0, hidden // tile, up_tile, 0)
    e_ref[...] = bdot(act_ref[...], wdn_ref[...])

    def step_three(step, _):
        place, part, flat = at_rows(step)
        z = e_ref[flat, :]
        grad = g_ref[place, part, :].astype(f32)
        out_ref[place, part, :] = (xa_ref[flat, :] + mod(8, part) * z).astype(bf16)
        sum_ref[6, part, :] += grad * z
        return 0

    lax.fori_loop(0, steps, step_three, 0)
    e_ref[...] = bdot_nt(du_ref[...], wup_ref[...])

    def step_four(step, _):
        place, part, flat = at_rows(step)
        grad = e_ref[flat, :]
        normed = n3_ref[flat, :]
        sum_ref[4, part, :] += grad
        sum_ref[5, part, :] += grad * normed
        back = norm_rows_back(normed, r3_ref[flat, 0:1], mod(7, part), grad)
        grad_two = g_ref[place, part, :].astype(f32) + back
        xa_ref[flat, :] = grad_two
        sum_ref[3, part, :] += grad_two * y2_ref[flat, :]
        dy2_ref[flat, :] = (mod(5, part) * grad_two).astype(bf16)
        return 0

    lax.fori_loop(0, steps, step_four, 0)
    y2_ref[...] = bdot_nt(dy2_ref[...], wto_ref[...])

    def time_pair_back(index, _):
        q_at, k_at, v_at = pair_at(index)
        for place in range(count):
            part = slice(place * frames, (place + 1) * frames)
            go = y2_ref[part, q_at].astype(bf16)
            q = qkv_ref[part, q_at] * factor
            keys = stacked(qkv_ref[part, k_at], masks_q)
            values = stacked(qkv_ref[part, v_at], masks)
            probs = p_ref[index, part, :]
            grad_p = bdot_nt(go, values)
            inner = halves(grad_p * probs, jnp.sum, 0.0)
            grad_s = (probs * (grad_p - inner)).astype(bf16)
            dqkv_ref[part, q_at] = bdot(grad_s, keys).astype(bf16)
            grad_k = bdot_tn(grad_s, q)
            grad_v = bdot_tn(probs.astype(bf16), go)
            dqkv_ref[part, k_at] = jnp.where(is_low, grad_k[:frames], grad_k[frames:]).astype(bf16)
            dqkv_ref[part, v_at] = jnp.where(is_low, grad_v[:frames], grad_v[frames:]).astype(bf16)
        return 0

    lax.fori_loop(0, HEADS // 2, time_pair_back, 0)
    e_ref[...] = bdot_nt(dqkv_ref[...], wti_ref[...])

    def step_five(step, _):
        place, part, flat = at_rows(step)
        grad = e_ref[flat, :]
        normed = n2_ref[flat, :]
        sum_ref[1, part, :] += grad
        sum_ref[2, part, :] += grad * normed
        grad_one = xa_ref[flat, :] + norm_rows_back(normed, r2_ref[flat, 0:1], mod(4, part), grad)
        dx1_ref[place, part, :] = grad_one
        sum_ref[0, part, :] += grad_one * y1_ref[flat, :]
        dy1_ref[flat, :] = (mod(2, part) * grad_one).astype(bf16)
        return 0

    lax.fori_loop(0, steps, step_five, 0)
    do1_ref[...] = bdot_nt(dy1_ref[...], wso_ref[...]).astype(bf16).reshape(count, frames, width)


VMEM_LIMIT = 62 * 1024 * 1024


def resident(shape):
    return pl.BlockSpec(shape, lambda i: (0,) * len(shape), pipeline_mode=pl.Buffered(1))


def call_space_forward(x, mods, weight):
    n_pos, own, places, width = x.shape
    patches = n_pos * places
    pair = 2 * HEAD_DIM
    spread = pl.BlockSpec((n_pos, 1, places, width), lambda i: (0, i, 0, 0))

    def by_frame(*shape):
        return pl.BlockSpec((1,) + shape, lambda i: (i, 0, 0))

    rows = own * patches
    return pl.pallas_call(
        space_forward,
        grid=(own,),
        in_specs=[spread, by_frame(2, width), resident(weight.shape)],
        out_specs=[
            by_frame(patches, width),
            by_frame(patches, 3 * width),
            spread,
            by_frame(patches, pair),
        ],
        out_shape=[
            jax.ShapeDtypeStruct((own, patches, width), bf16),
            jax.ShapeDtypeStruct((own, patches, 3 * width), bf16),
            jax.ShapeDtypeStruct(x.shape, bf16),
            jax.ShapeDtypeStruct((own, patches, pair), f32),
        ],
        compiler_params=pltpu.CompilerParams(vmem_limit_bytes=VMEM_LIMIT),
        cost_estimate=pl.CostEstimate(
            flops=2 * rows * width * 3 * width + 4 * rows * patches * width,
            bytes_accessed=rows * width * 12 + weight.size * 2,
            transcendentals=rows * patches * HEADS,
        ),
        name="space_forward",
    )(x, mods, weight)


def call_space_backward(go, qkv, lse, x, mods, weight):
    n_pos, own, places, width = x.shape
    patches = n_pos * places
    pair = 2 * HEAD_DIM
    spread = pl.BlockSpec((n_pos, 1, places, width), lambda i: (0, i, 0, 0))

    def by_frame(*shape):
        return pl.BlockSpec((1,) + shape, lambda i: (i, 0, 0))

    rows = own * patches
    return pl.pallas_call(
        space_backward,
        grid=(own,),
        in_specs=[
            spread,
            by_frame(patches, 3 * width),
            by_frame(patches, pair),
            spread,
            by_frame(2, width),
            resident(weight.shape),
        ],
        out_specs=[by_frame(patches, 3 * width), spread, by_frame(2, width)],
        out_shape=[
            jax.ShapeDtypeStruct((own, patches, 3 * width), bf16),
            jax.ShapeDtypeStruct(x.shape, bf16),
            jax.ShapeDtypeStruct((own, 2, width), f32),
        ],
        scratch_shapes=[pltpu.VMEM((patches, width), f32)],
        compiler_params=pltpu.CompilerParams(vmem_limit_bytes=VMEM_LIMIT),
        cost_estimate=pl.CostEstimate(
            flops=2 * rows * width * 3 * width + 10 * rows * patches * width,
            bytes_accessed=rows * width * 16 + weight.size * 2,
            transcendentals=rows * patches * HEADS,
        ),
        name="space_backward",
    )(go, qkv, lse, x, mods, weight)


def call_middle(o_one, x, grad, mods, same_clip, wso, wti, wto, wup, wdn):
    places, frames, width = x.shape
    count = max(1, min(places, 256 // frames))
    rows = count * frames
    hidden = wup.shape[1]
    pair = 2 * HEAD_DIM
    total = places * frames
    chunk = pl.BlockSpec((count, frames, width), lambda i: (i, 0, 0))

    def flat(cols):
        return pl.BlockSpec((rows, cols), lambda i: (i, 0))

    def flat_shape(cols):
        return jax.ShapeDtypeStruct((total, cols), bf16)

    def scratch(cols, dtype=f32):
        return pltpu.VMEM((rows, cols), dtype)

    lanes = jnp.concatenate([same_clip, same_clip], axis=1)
    flops = 2 * total * (2 * (wso.size + wti.size + wto.size + wup.size + wdn.size))
    return pl.pallas_call(
        middle,
        grid=(places // count,),
        in_specs=[chunk, chunk, chunk, resident(mods.shape), resident(lanes.shape)]
        + [resident(w.shape) for w in (wso, wti, wto, wup, wdn)],
        out_specs=[
            chunk,
            flat(hidden),
            flat(width),
            flat(width),
            flat(hidden),
            flat(width),
            flat(width),
            flat(width),
            flat(3 * width),
            flat(width),
            chunk,
            chunk,
            pl.BlockSpec((7, frames, width), lambda i: (0, 0, 0)),
        ],
        out_shape=[
            jax.ShapeDtypeStruct(x.shape, bf16),
            flat_shape(hidden),
            flat_shape(width),
            flat_shape(width),
            flat_shape(hidden),
            flat_shape(width),
            flat_shape(width),
            flat_shape(width),
            flat_shape(3 * width),
            flat_shape(width),
            jax.ShapeDtypeStruct(x.shape, bf16),
            jax.ShapeDtypeStruct(x.shape, f32),
            jax.ShapeDtypeStruct((7, frames, width), f32),
        ],
        scratch_shapes=[
            scratch(3 * width, bf16),
            pltpu.VMEM((HEADS // 2, rows, pair), f32),
            scratch(width),
            scratch(width),
            scratch(width),
            scratch(width),
            scratch(pair),
            scratch(pair),
            scratch(width),
            pltpu.VMEM((8, pair), f32),
            scratch(width),
        ],
        compiler_params=pltpu.CompilerParams(vmem_limit_bytes=VMEM_LIMIT),
        cost_estimate=pl.CostEstimate(
            flops=flops, bytes_accessed=total * 40000, transcendentals=total * hidden
        ),
        name="middle",
    )(o_one, x, grad, mods, lanes, wso, wti, wto, wup, wdn)


def on_device(
    tokens,
    clip_lengths,
    timesteps,
    embed_first,
    embed_second,
    adaln_weight,
    spatial_in,
    spatial_out,
    temporal_in,
    temporal_out,
    hidden_up,
    hidden_down,
    grad_output,
    n_pos=16,
    n_clip=2,
):
    frames, places, width = tokens.shape
    rows = frames * places
    own = frames // n_pos
    patches = places * n_pos
    me = lax.axis_index("pos")
    clip_at = lax.axis_index("clip")
    clips = clip_lengths.shape[1]

    def exchange(values):
        sent = values.reshape(frames, places, width)
        got = lax.all_to_all(sent, "pos", split_axis=0, concat_axis=0, tiled=True)
        return got.reshape(n_pos, own, places, width)

    x_space = exchange(tokens)

    all_steps = lax.all_gather(timesteps[0], "clip", axis=0, tiled=True)
    freq = frequency(all_steps)
    first_w, second_w, adaln_w = (
        embed_first.astype(f32),
        embed_second.astype(f32),
        adaln_weight.astype(f32),
    )
    pre_cond = dot_high(freq, first_w)
    hidden_cond = jax.nn.silu(pre_cond)
    cond = dot_high(hidden_cond, second_w)
    cond_act = jax.nn.silu(cond)
    own_act = lax.dynamic_slice_in_dim(cond_act, clip_at * clips, clips, 0)
    modulated = dot_high(own_act, adaln_w)
    onehot, clip_ids = clip_onehot(clip_lengths[0], frames)
    per_frame = dot_high(onehot, modulated)
    own_frames = lax.dynamic_slice_in_dim(per_frame, me * own, own, 0)

    own_mods = own_frames[:, : 2 * width].reshape(own, 2, width)
    h_one, qkv_one, o_one_space, lse_one = call_space_forward(x_space, own_mods, spatial_in)
    o_one = exchange(o_one_space).reshape(frames, places, width)

    def turn(values):
        return values.transpose(1, 0, 2)

    o_one = turn(o_one)
    mods = per_frame.reshape(frames, 9, width).transpose(1, 0, 2)
    same_clip = jnp.dot(onehot, onehot.T)
    (block_turned, act, grad_z, h_three, grad_u, o_two, grad_y_two, h_two, grad_qkv_two, grad_y_one, grad_o_one,
     grad_one, sums) = call_middle(
        o_one, turn(tokens), turn(grad_output), mods, same_clip, spatial_out, temporal_in, temporal_out,
        hidden_up, hidden_down,
    )
    block_out = turn(block_turned)
    grad_o_space = exchange(turn(grad_o_one))
    grad_qkv_one, back_one, sums_one = call_space_backward(
        grad_o_space, qkv_one, lse_one, x_space, own_mods, spatial_in
    )
    back_places = exchange(back_one).reshape(frames, places, width)
    grad_tokens = (turn(grad_one) + back_places.astype(f32)).astype(bf16)
    g_hidden_down = weight_grad(act, grad_z)
    g_hidden_up = weight_grad(h_three, grad_u)
    g_temporal_out = weight_grad(o_two, grad_y_two)
    g_temporal_in = weight_grad(h_two, grad_qkv_two)
    g_spatial_out = weight_grad(o_one.reshape(rows, width), grad_y_one)
    patches = n_pos * places
    g_spatial_in = weight_grad(
        h_one.reshape(own * patches, width), grad_qkv_one.reshape(own * patches, 3 * width)
    )
    shift_own, scale_own = sums_one[:, 0], sums_one[:, 1]

    own_hot = lax.dynamic_slice_in_dim(onehot, me * own, own, 0)
    dmod_own = dot_high(own_hot.T, jnp.concatenate([shift_own, scale_own], axis=1))
    dmod_rest = dot_high(onehot.T, sums.transpose(1, 0, 2).reshape(frames, 7 * width))
    dmod = lax.psum(jnp.concatenate([dmod_own, dmod_rest], axis=1), "pos")
    dmod_all = lax.all_gather(dmod, "clip", axis=0, tiled=True)

    def own_columns(values):
        block = values.shape[1] // n_pos
        return lax.dynamic_slice_in_dim(values, me * block, block, 1)

    g_adaln = dot_high(own_columns(cond_act).T, dmod_all)
    grad_cond = dot_high(dmod_all, adaln_w.T) * silu_grad(cond)
    g_second = dot_high(own_columns(hidden_cond).T, grad_cond)
    grad_pre = dot_high(grad_cond, second_w.T) * silu_grad(pre_cond)
    g_first = dot_high(own_columns(freq).T, grad_pre)

    quarter = g_hidden_down.shape[0] // width
    down = g_hidden_down.reshape(n_pos, quarter, width // n_pos, width)
    down = [down[:, j].reshape(width, width) for j in range(quarter)]

    def reduce(parts):
        joined = jnp.concatenate(parts, axis=1)
        scattered = lax.psum_scatter(joined, "pos", scatter_dimension=0, tiled=True)
        return lax.psum(scattered, "clip").astype(f32)

    mlp = reduce([g_hidden_up] + down)
    rest = reduce([g_temporal_in, g_temporal_out, g_spatial_out, g_spatial_in])
    wide = 3 * width
    up_cols = g_hidden_up.shape[1]
    return (
        block_out,
        grad_tokens,
        g_first,
        g_second,
        g_adaln,
        rest[:, wide + 2 * width :],
        rest[:, wide + width : wide + 2 * width],
        rest[:, :wide],
        rest[:, wide : wide + width],
        mlp[:, :up_cols],
        jnp.concatenate(
            [mlp[:, up_cols + j * width : up_cols + (j + 1) * width] for j in range(quarter)], axis=0
        ),
    )


def solution(mesh):
    in_specs = (
        P("clip", "pos", None),
        P("clip", None),
        P("clip", None),
        P(),
        P(),
        P(),
        P(),
        P(),
        P(),
        P(),
        P(),
        P(),
        P("clip", "pos", None),
    )
    out_specs = (P("clip", "pos", None),) * 2 + (P("pos", None),) * 9
    body = partial(on_device, n_pos=mesh.shape["pos"], n_clip=mesh.shape["clip"])
    return jax.shard_map(body, mesh=mesh, in_specs=in_specs, out_specs=out_specs, check_vma=False)
```

```python
from functools import partial
import math

import jax
import jax.numpy as jnp
from jax import lax
from jax.experimental import pallas as pl
from jax.experimental.pallas import tpu as pltpu
from jax.sharding import PartitionSpec as P

HEADS = 12
HEAD_DIM = 64
FREQ = 256

epsilon = 1e-06
highest = lax.Precision.HIGHEST
masked_score = -1000000000.0
f32 = jnp.float32
bf16 = jnp.bfloat16


def frequency(step_ids):
    half_width = FREQ // 2
    rate_table = jnp.exp(
        -math.log(10000.0) * jnp.arange(half_width, dtype=jnp.float32) / half_width
    )
    angles = step_ids.astype(jnp.float32)[:, None] * rate_table[None, :]
    return jnp.concatenate([jnp.cos(angles), jnp.sin(angles)], axis=1)


def dot_high(left, right):
    return jnp.dot(left, right, precision=highest, preferred_element_type=f32)


def silu_grad(values):
    gate = jax.nn.sigmoid(values)
    return gate * (1.0 + values * (1.0 - gate))


def clip_onehot(lengths, frames):
    clip_ends = jnp.cumsum(lengths)
    frame_ids = jnp.arange(frames, dtype=jnp.int32)
    clip_ids = jnp.sum((frame_ids[:, None] >= clip_ends[None, :]).astype(jnp.int32), axis=1)
    onehot = (clip_ids[:, None] == jnp.arange(lengths.shape[0], dtype=jnp.int32)[None, :]).astype(
        jnp.float32
    )
    return (onehot, clip_ids)


def weight_grad(left, right):
    return jnp.einsum("rd,rk->dk", left, right, preferred_element_type=f32).astype(bf16)


def bdot(left, right):
    return lax.dot_general(left, right, (((1,), (0,)), ((), ())), preferred_element_type=f32)


def bdot_nt(left, right):
    return lax.dot_general(left, right, (((1,), (1,)), ((), ())), preferred_element_type=f32)


def bdot_tn(left, right):
    return lax.dot_general(left, right, (((0,), (0,)), ((), ())), preferred_element_type=f32)


def norm_rows(values):
    width = values.shape[-1]
    centre = values - jnp.sum(values, axis=-1, keepdims=True) * (1.0 / width)
    spread = jnp.sum(centre * centre, axis=-1, keepdims=True) * (1.0 / width)
    inverse = lax.rsqrt(spread + epsilon)
    return centre * inverse, inverse


def norm_rows_back(normed, inverse, scale_vec, grad):
    width = grad.shape[-1]
    inner = grad * (1.0 + scale_vec)
    mean_one = jnp.sum(inner, axis=-1, keepdims=True) * (1.0 / width)
    mean_two = jnp.sum(inner * normed, axis=-1, keepdims=True) * (1.0 / width)
    return inverse * (inner - mean_one - normed * mean_two)


def pair_masks(scale):
    lanes = lax.broadcasted_iota(jnp.int32, (1, 2 * HEAD_DIM), 1)
    low_half = jnp.where(lanes < HEAD_DIM, scale, 0.0).astype(bf16)
    high_half = jnp.where(lanes < HEAD_DIM, 0.0, scale).astype(bf16)
    return low_half, high_half


ROWS = 32


def load_rows(ref, step):
    places, width = ref.shape[2:]
    count = max(1, ROWS // places)
    part = ref[pl.ds(step * count, count), 0].astype(f32)
    return part.reshape(count * places, width)


def store_rows(ref, step, values):
    places, width = ref.shape[2:]
    count = max(1, ROWS // places)
    ref[pl.ds(step * count, count), 0] = values.reshape(count, places, width).astype(bf16)


def space_forward(x_ref, mod_ref, w_ref, h_ref, qkv_ref, o_ref, lse_ref):
    patches, width = h_ref.shape[1:]
    places = x_ref.shape[2]
    pair = 2 * HEAD_DIM
    shift, scale = mod_ref[0, 0:1, :], mod_ref[0, 1:2, :]

    def norm_step(step, _):
        normed, _inverse = norm_rows(load_rows(x_ref, step))
        h_ref[0, pl.ds(step * ROWS, ROWS), :] = (normed * (1.0 + scale) + shift).astype(bf16)
        return 0

    lax.fori_loop(0, patches // ROWS, norm_step, 0)
    for part in range(3):
        cols = slice(part * width, (part + 1) * width)
        qkv_ref[0, :, cols] = bdot(h_ref[0], w_ref[:, cols]).astype(bf16)
    masks = pair_masks(1.0 / math.sqrt(HEAD_DIM))
    lane_ids = lax.broadcasted_iota(jnp.int32, (1, pair), 1)
    lse_ref[0] = jnp.zeros((patches, pair), f32)

    def head_pair(index, _):
        at = pl.multiple_of(index * pair, pair)
        q = qkv_ref[0, :, pl.ds(at, pair)]
        k = qkv_ref[0, :, pl.ds(pl.multiple_of(width + at, pair), pair)]
        v = qkv_ref[0, :, pl.ds(pl.multiple_of(2 * width + at, pair), pair)]
        outs = []
        lse = lse_ref[0]
        for half in range(2):
            scores = bdot_nt(q * masks[half], k)
            top = jnp.max(scores, axis=-1, keepdims=True)
            exps = jnp.exp(scores - top)
            total = jnp.sum(exps, axis=-1, keepdims=True)
            probs = (exps * (1.0 / total)).astype(bf16)
            outs.append(bdot(probs, v))
            lse = jnp.where(lane_ids == 2 * index + half, top + jnp.log(total), lse)
        lse_ref[0] = lse
        both = jnp.where(lane_ids < HEAD_DIM, outs[0], outs[1])
        o_ref[:, 0, :, pl.ds(at, pair)] = both.reshape(patches // places, places, pair).astype(bf16)
        return 0

    lax.fori_loop(0, HEADS // 2, head_pair, 0)


def space_backward(
    go_ref, qkv_ref, lse_ref, x_ref, mod_ref, w_ref, dqkv_ref, dv_ref, sum_ref, e_ref
):
    patches = qkv_ref.shape[1]
    width = x_ref.shape[3]
    places = x_ref.shape[2]
    pair = 2 * HEAD_DIM
    scale = mod_ref[0, 1:2, :]
    factor = 1.0 / math.sqrt(HEAD_DIM)
    masks_q = pair_masks(factor)
    masks = pair_masks(1.0)
    lane_ids = lax.broadcasted_iota(jnp.int32, (1, pair), 1)

    def head_pair(index, _):
        at = pl.multiple_of(index * pair, pair)
        k_at = pl.multiple_of(width + at, pair)
        v_at = pl.multiple_of(2 * width + at, pair)
        q = qkv_ref[0, :, pl.ds(at, pair)]
        k = qkv_ref[0, :, pl.ds(k_at, pair)]
        v = qkv_ref[0, :, pl.ds(v_at, pair)]
        go = go_ref[:, 0, :, pl.ds(at, pair)].astype(f32).reshape(patches, pair).astype(bf16)
        lse_all = lse_ref[0]
        gq, gk, gv = None, None, None
        for half in range(2):
            lse = jnp.sum(
                jnp.where(lane_ids == 2 * index + half, lse_all, 0.0), axis=-1, keepdims=True
            )
            q_half = q * masks_q[half]
            go_half = go * masks[half]
            probs = jnp.exp(bdot_nt(q_half, k) - lse)
            grad_p = bdot_nt(go_half, v)
            inner = jnp.sum(grad_p * probs, axis=-1, keepdims=True)
            grad_s = (probs * (grad_p - inner)).astype(bf16)
            part_q = bdot(grad_s, k * masks_q[half])
            part_k = bdot_tn(grad_s, q_half)
            part_v = bdot_tn(probs.astype(bf16), go_half)
            gq = part_q if gq is None else gq + part_q
            gk = part_k if gk is None else gk + part_k
            gv = part_v if gv is None else gv + part_v
        dqkv_ref[0, :, pl.ds(at, pair)] = gq.astype(bf16)
        dqkv_ref[0, :, pl.ds(k_at, pair)] = gk.astype(bf16)
        dqkv_ref[0, :, pl.ds(v_at, pair)] = gv.astype(bf16)
        return 0

    lax.fori_loop(0, HEADS // 2, head_pair, 0)
    e_ref[...] = bdot_nt(dqkv_ref[0], w_ref[...])

    def norm_step(step, sums):
        grad = e_ref[pl.ds(step * ROWS, ROWS), :]
        normed, inverse = norm_rows(load_rows(x_ref, step))
        store_rows(dv_ref, step, norm_rows_back(normed, inverse, scale, grad))
        folded = grad.reshape(ROWS // 8, 8, width).sum(axis=0)
        folded_n = (grad * normed).reshape(ROWS // 8, 8, width).sum(axis=0)
        return sums[0] + folded, sums[1] + folded_n

    zero = jnp.zeros((8, width), f32)
    shift_sum, scale_sum = lax.fori_loop(0, patches // ROWS, norm_step, (zero, zero))
    sum_ref[0, 0:1, :] = jnp.sum(shift_sum, axis=0, keepdims=True)
    sum_ref[0, 1:2, :] = jnp.sum(scale_sum, axis=0, keepdims=True)


GELU_C = math.sqrt(2.0 / math.pi)


def middle(
    o1_ref, x_ref, g_ref, mod_ref, clip_ref, wso_ref, wti_ref, wto_ref, wup_ref, wdn_ref,
    out_ref, act_ref, dz_ref, h3_ref, du_ref, o2_ref, dy2_ref, h2_ref, dqkv_ref, dy1_ref, do1_ref,
    dx1_ref, sum_ref,
    qkv_ref, p_ref, y1_ref, y2_ref, n2_ref, n3_ref, r2_ref, r3_ref, xa_ref, gp_ref, e_ref,
):
    count, frames, width = x_ref.shape
    rows = count * frames
    pair = 2 * HEAD_DIM
    hidden = act_ref.shape[1]
    factor = 1.0 / math.sqrt(HEAD_DIM)
    per = frames // ROWS
    steps = rows // ROWS

    @pl.when(pl.program_id(0) == 0)
    def _():
        sum_ref[...] = jnp.zeros_like(sum_ref)

    def at_rows(step):
        return step // per, pl.ds(lax.rem(step, per) * ROWS, ROWS), pl.ds(step * ROWS, ROWS)

    def mod(index, part):
        return mod_ref[index, part, :]

    y1_ref[...] = bdot(o1_ref[...].reshape(rows, width), wso_ref[...])

    def step_one(step, _):
        place, part, flat = at_rows(step)
        x_one = x_ref[place, part, :].astype(f32) + mod(2, part) * y1_ref[flat, :]
        xa_ref[flat, :] = x_one
        normed, inverse = norm_rows(x_one)
        n2_ref[flat, :] = normed
        r2_ref[flat, :] = jnp.broadcast_to(inverse, (ROWS, pair))
        h2_ref[flat, :] = (normed * (1.0 + mod(4, part)) + mod(3, part)).astype(bf16)
        return 0

    lax.fori_loop(0, steps, step_one, 0)
    for third in range(3):
        cols = slice(third * width, (third + 1) * width)
        qkv_ref[:, cols] = bdot(h2_ref[...], wti_ref[:, cols]).astype(bf16)

    masks = pair_masks(1.0)
    masks_q = pair_masks(factor)
    lane_ids = lax.broadcasted_iota(jnp.int32, (1, pair), 1)
    is_low = lane_ids < HEAD_DIM
    allowed = clip_ref[...] > 0.5

    def halves(values, reduce, neutral):
        low_part = reduce(jnp.where(is_low, values, neutral), axis=-1, keepdims=True)
        high_part = reduce(jnp.where(is_low, neutral, values), axis=-1, keepdims=True)
        return jnp.where(is_low, low_part, high_part)

    def stacked(values, pair_of_masks):
        return jnp.concatenate([values * pair_of_masks[0], values * pair_of_masks[1]], axis=0)

    def pair_at(index):
        at = pl.multiple_of(index * pair, pair)
        return (
            pl.ds(at, pair),
            pl.ds(pl.multiple_of(width + at, pair), pair),
            pl.ds(pl.multiple_of(2 * width + at, pair), pair),
        )

    def time_pair(index, _):
        q_at, k_at, v_at = pair_at(index)
        for place in range(count):
            part = slice(place * frames, (place + 1) * frames)
            q = qkv_ref[part, q_at]
            keys = stacked(qkv_ref[part, k_at], masks_q)
            values = stacked(qkv_ref[part, v_at], masks)
            scores = jnp.where(allowed, bdot_nt(q, keys), masked_score)
            exps = jnp.exp(scores - halves(scores, jnp.max, -jnp.inf))
            probs = exps / halves(exps, jnp.sum, 0.0)
            p_ref[index, part, :] = probs
            o2_ref[part, q_at] = bdot(probs.astype(bf16), values).astype(bf16)
        return 0

    lax.fori_loop(0, HEADS // 2, time_pair, 0)

    y2_ref[...] = bdot(o2_ref[...], wto_ref[...])

    def step_two(step, _):
        place, part, flat = at_rows(step)
        x_two = xa_ref[flat, :] + mod(5, part) * y2_ref[flat, :]
        xa_ref[flat, :] = x_two
        normed, inverse = norm_rows(x_two)
        n3_ref[flat, :] = normed
        r3_ref[flat, :] = jnp.broadcast_to(inverse, (ROWS, pair))
        h3_ref[flat, :] = (normed * (1.0 + mod(7, part)) + mod(6, part)).astype(bf16)
        dz_ref[flat, :] = (mod(8, part) * g_ref[place, part, :].astype(f32)).astype(bf16)
        return 0

    lax.fori_loop(0, steps, step_two, 0)

    tile = 256

    def up_tile(index, _):
        cols = pl.ds(pl.multiple_of(index * tile, tile), tile)
        u = bdot(h3_ref[...], wup_ref[:, cols])
        square = u * u
        tanh = jnp.tanh(GELU_C * (u * (1.0 + 0.044715 * square)))
        half = 0.5 * (1.0 + tanh)
        act_ref[:, cols] = (u * half).astype(bf16)
        slope = half + (0.5 * GELU_C) * u * (1.0 - tanh * tanh) * (1.0 + (3.0 * 0.044715) * square)
        du = bdot_nt(dz_ref[...], wdn_ref[cols, :]) * slope
        du_ref[:, cols] = du.astype(bf16)
        return 0

    lax.fori_loop(0, hidden // tile, up_tile, 0)
    e_ref[...] = bdot(act_ref[...], wdn_ref[...])

    def step_three(step, _):
        place, part, flat = at_rows(step)
        z = e_ref[flat, :]
        grad = g_ref[place, part, :].astype(f32)
        out_ref[place, part, :] = (xa_ref[flat, :] + mod(8, part) * z).astype(bf16)
        sum_ref[6, part, :] += grad * z
        return 0

    lax.fori_loop(0, steps, step_three, 0)
    e_ref[...] = bdot_nt(du_ref[...], wup_ref[...])

    def step_four(step, _):
        place, part, flat = at_rows(step)
        grad = e_ref[flat, :]
        normed = n3_ref[flat, :]
        sum_ref[4, part, :] += grad
        sum_ref[5, part, :] += grad * normed
        back = norm_rows_back(normed, r3_ref[flat, 0:1], mod(7, part), grad)
        grad_two = g_ref[place, part, :].astype(f32) + back
        xa_ref[flat, :] = grad_two
        sum_ref[3, part, :] += grad_two * y2_ref[flat, :]
        dy2_ref[flat, :] = (mod(5, part) * grad_two).astype(bf16)
        return 0

    lax.fori_loop(0, steps, step_four, 0)
    y2_ref[...] = bdot_nt(dy2_ref[...], wto_ref[...])

    def time_pair_back(index, _):
        q_at, k_at, v_at = pair_at(index)
        for place in range(count):
            part = slice(place * frames, (place + 1) * frames)
            go = y2_ref[part, q_at].astype(bf16)
            q = qkv_ref[part, q_at] * factor
            keys = stacked(qkv_ref[part, k_at], masks_q)
            values = stacked(qkv_ref[part, v_at], masks)
            probs = p_ref[index, part, :]
            grad_p = bdot_nt(go, values)
            inner = halves(grad_p * probs, jnp.sum, 0.0)
            grad_s = (probs * (grad_p - inner)).astype(bf16)
            dqkv_ref[part, q_at] = bdot(grad_s, keys).astype(bf16)
            grad_k = bdot_tn(grad_s, q)
            grad_v = bdot_tn(probs.astype(bf16), go)
            dqkv_ref[part, k_at] = jnp.where(is_low, grad_k[:frames], grad_k[frames:]).astype(bf16)
            dqkv_ref[part, v_at] = jnp.where(is_low, grad_v[:frames], grad_v[frames:]).astype(bf16)
        return 0

    lax.fori_loop(0, HEADS // 2, time_pair_back, 0)
    e_ref[...] = bdot_nt(dqkv_ref[...], wti_ref[...])

    def step_five(step, _):
        place, part, flat = at_rows(step)
        grad = e_ref[flat, :]
        normed = n2_ref[flat, :]
        sum_ref[1, part, :] += grad
        sum_ref[2, part, :] += grad * normed
        grad_one = xa_ref[flat, :] + norm_rows_back(normed, r2_ref[flat, 0:1], mod(4, part), grad)
        dx1_ref[place, part, :] = grad_one
        sum_ref[0, part, :] += grad_one * y1_ref[flat, :]
        dy1_ref[flat, :] = (mod(2, part) * grad_one).astype(bf16)
        return 0

    lax.fori_loop(0, steps, step_five, 0)
    do1_ref[...] = bdot_nt(dy1_ref[...], wso_ref[...]).astype(bf16).reshape(count, frames, width)


VMEM_LIMIT = 62 * 1024 * 1024


def resident(shape):
    return pl.BlockSpec(shape, lambda i: (0,) * len(shape), pipeline_mode=pl.Buffered(1))


def call_space_forward(x, mods, weight):
    n_pos, own, places, width = x.shape
    patches = n_pos * places
    pair = 2 * HEAD_DIM
    spread = pl.BlockSpec((n_pos, 1, places, width), lambda i: (0, i, 0, 0))

    def by_frame(*shape):
        return pl.BlockSpec((1,) + shape, lambda i: (i, 0, 0))

    rows = own * patches
    return pl.pallas_call(
        space_forward,
        grid=(own,),
        in_specs=[spread, by_frame(2, width), resident(weight.shape)],
        out_specs=[
            by_frame(patches, width),
            by_frame(patches, 3 * width),
            spread,
            by_frame(patches, pair),
        ],
        out_shape=[
            jax.ShapeDtypeStruct((own, patches, width), bf16),
            jax.ShapeDtypeStruct((own, patches, 3 * width), bf16),
            jax.ShapeDtypeStruct(x.shape, bf16),
            jax.ShapeDtypeStruct((own, patches, pair), f32),
        ],
        compiler_params=pltpu.CompilerParams(vmem_limit_bytes=VMEM_LIMIT),
        cost_estimate=pl.CostEstimate(
            flops=2 * rows * width * 3 * width + 4 * rows * patches * width,
            bytes_accessed=rows * width * 12 + weight.size * 2,
            transcendentals=rows * patches * HEADS,
        ),
        name="space_forward",
    )(x, mods, weight)


def call_space_backward(go, qkv, lse, x, mods, weight):
    n_pos, own, places, width = x.shape
    patches = n_pos * places
    pair = 2 * HEAD_DIM
    spread = pl.BlockSpec((n_pos, 1, places, width), lambda i: (0, i, 0, 0))

    def by_frame(*shape):
        return pl.BlockSpec((1,) + shape, lambda i: (i, 0, 0))

    rows = own * patches
    return pl.pallas_call(
        space_backward,
        grid=(own,),
        in_specs=[
            spread,
            by_frame(patches, 3 * width),
            by_frame(patches, pair),
            spread,
            by_frame(2, width),
            resident(weight.shape),
        ],
        out_specs=[by_frame(patches, 3 * width), spread, by_frame(2, width)],
        out_shape=[
            jax.ShapeDtypeStruct((own, patches, 3 * width), bf16),
            jax.ShapeDtypeStruct(x.shape, bf16),
            jax.ShapeDtypeStruct((own, 2, width), f32),
        ],
        scratch_shapes=[pltpu.VMEM((patches, width), f32)],
        compiler_params=pltpu.CompilerParams(vmem_limit_bytes=VMEM_LIMIT),
        cost_estimate=pl.CostEstimate(
            flops=2 * rows * width * 3 * width + 10 * rows * patches * width,
            bytes_accessed=rows * width * 16 + weight.size * 2,
            transcendentals=rows * patches * HEADS,
        ),
        name="space_backward",
    )(go, qkv, lse, x, mods, weight)


def call_middle(o_one, x, grad, mods, same_clip, wso, wti, wto, wup, wdn):
    places, frames, width = x.shape
    count = max(1, min(places, 256 // frames))
    rows = count * frames
    hidden = wup.shape[1]
    pair = 2 * HEAD_DIM
    total = places * frames
    chunk = pl.BlockSpec((count, frames, width), lambda i: (i, 0, 0))

    def flat(cols):
        return pl.BlockSpec((rows, cols), lambda i: (i, 0))

    def flat_shape(cols):
        return jax.ShapeDtypeStruct((total, cols), bf16)

    def scratch(cols, dtype=f32):
        return pltpu.VMEM((rows, cols), dtype)

    lanes = jnp.concatenate([same_clip, same_clip], axis=1)
    flops = 2 * total * (2 * (wso.size + wti.size + wto.size + wup.size + wdn.size))
    return pl.pallas_call(
        middle,
        grid=(places // count,),
        in_specs=[chunk, chunk, chunk, resident(mods.shape), resident(lanes.shape)]
        + [resident(w.shape) for w in (wso, wti, wto, wup, wdn)],
        out_specs=[
            chunk,
            flat(hidden),
            flat(width),
            flat(width),
            flat(hidden),
            flat(width),
            flat(width),
            flat(width),
            flat(3 * width),
            flat(width),
            chunk,
            chunk,
            pl.BlockSpec((7, frames, width), lambda i: (0, 0, 0)),
        ],
        out_shape=[
            jax.ShapeDtypeStruct(x.shape, bf16),
            flat_shape(hidden),
            flat_shape(width),
            flat_shape(width),
            flat_shape(hidden),
            flat_shape(width),
            flat_shape(width),
            flat_shape(width),
            flat_shape(3 * width),
            flat_shape(width),
            jax.ShapeDtypeStruct(x.shape, bf16),
            jax.ShapeDtypeStruct(x.shape, f32),
            jax.ShapeDtypeStruct((7, frames, width), f32),
        ],
        scratch_shapes=[
            scratch(3 * width, bf16),
            pltpu.VMEM((HEADS // 2, rows, pair), f32),
            scratch(width),
            scratch(width),
            scratch(width),
            scratch(width),
            scratch(pair),
            scratch(pair),
            scratch(width),
            pltpu.VMEM((8, pair), f32),
            scratch(width),
        ],
        compiler_params=pltpu.CompilerParams(vmem_limit_bytes=VMEM_LIMIT),
        cost_estimate=pl.CostEstimate(
            flops=flops, bytes_accessed=total * 40000, transcendentals=total * hidden
        ),
        name="middle",
    )(o_one, x, grad, mods, lanes, wso, wti, wto, wup, wdn)


def swap(values, axis, size, bit):
    return lax.ppermute(values, axis, [(i, i ^ bit) for i in range(size)])


def bits_of(size):
    return [1 << i for i in range(size.bit_length() - 1)]


def by_distance(values, axis, size):
    for bit in bits_of(size):
        values = jnp.concatenate([values, swap(values, axis, size, bit)], axis=0)
    return values


def butterfly(values, axis, size):
    for bit in bits_of(size):
        values = values + swap(values, axis, size, bit)
    return values


def halve(values, index, axis):
    def pick(at):
        return lax.dynamic_index_in_dim(values, at, axis, keepdims=False)

    return pick(index), pick(1 - index)


def reduce_rows(grad, n_pos, n_clip, clip_first):
    rows, cols = grad.shape
    block = rows // n_pos
    me, clip_at = lax.axis_index("pos"), lax.axis_index("clip")
    values = grad.reshape(n_pos, block, cols)

    def add(keep, got):
        return (keep.astype(f32) + got.astype(f32)).astype(bf16)

    def pos_step(values, bit):
        left = values.shape[0] // 2
        split = values.reshape(left, 2, *values.shape[1:])
        keep, send = halve(split, lax.rem(me // bit, 2), 1)
        return add(keep, swap(send, "pos", n_pos, bit))

    bits = bits_of(n_pos)
    values = pos_step(values, bits[0])
    if clip_first:
        for bit in reversed(bits_of(n_clip)):
            split = values.reshape(*values.shape[:2], 2, values.shape[2] // 2)
            keep, send = halve(split, lax.rem(clip_at // bit, 2), 2)
            values = add(keep, swap(send, "clip", n_clip, bit))
    for bit in bits[1:]:
        values = pos_step(values, bit)
    values = values[0]
    for bit in bits_of(n_clip):
        got = swap(values, "clip", n_clip, bit)
        if clip_first:
            upper = lax.rem(clip_at // bit, 2) == 1
            values = jnp.concatenate(
                [jnp.where(upper, got, values), jnp.where(upper, values, got)], axis=1
            )
        elif 2 * bit == n_clip:
            return values.astype(f32) + got.astype(f32)
        else:
            values = add(values, got)
    return values.astype(f32)


def on_device(
    tokens,
    clip_lengths,
    timesteps,
    embed_first,
    embed_second,
    adaln_weight,
    spatial_in,
    spatial_out,
    temporal_in,
    temporal_out,
    hidden_up,
    hidden_down,
    grad_output,
    n_pos=16,
    n_clip=2,
):
    frames, places, width = tokens.shape
    rows = frames * places
    own = frames // n_pos
    patches = places * n_pos
    me = lax.axis_index("pos")
    clips = clip_lengths.shape[1]

    def exchange(values):
        sent = values.reshape(frames, places, width)
        got = lax.all_to_all(sent, "pos", split_axis=0, concat_axis=0, tiled=True)
        return got.reshape(n_pos, own, places, width)

    x_space = exchange(tokens)

    all_steps = by_distance(timesteps[0], "clip", n_clip)
    freq = frequency(all_steps)
    first_w, second_w, adaln_w = (
        embed_first.astype(f32),
        embed_second.astype(f32),
        adaln_weight.astype(f32),
    )
    pre_cond = dot_high(freq, first_w)
    hidden_cond = jax.nn.silu(pre_cond)
    cond = dot_high(hidden_cond, second_w)
    cond_act = jax.nn.silu(cond)
    modulated = dot_high(cond_act[:clips], adaln_w)
    onehot, clip_ids = clip_onehot(clip_lengths[0], frames)
    per_frame = dot_high(onehot, modulated)
    own_frames = lax.dynamic_slice_in_dim(per_frame, me * own, own, 0)

    own_mods = own_frames[:, : 2 * width].reshape(own, 2, width)
    h_one, qkv_one, o_one_space, lse_one = call_space_forward(x_space, own_mods, spatial_in)
    o_one = exchange(o_one_space).reshape(frames, places, width)

    def turn(values):
        return values.transpose(1, 0, 2)

    o_one = turn(o_one)
    mods = per_frame.reshape(frames, 9, width).transpose(1, 0, 2)
    same_clip = jnp.dot(onehot, onehot.T)
    (block_turned, act, grad_z, h_three, grad_u, o_two, grad_y_two, h_two, grad_qkv_two, grad_y_one, grad_o_one,
     grad_one, sums) = call_middle(
        o_one, turn(tokens), turn(grad_output), mods, same_clip, spatial_out, temporal_in, temporal_out,
        hidden_up, hidden_down,
    )
    block_out = turn(block_turned)
    grad_o_space = exchange(turn(grad_o_one))
    grad_qkv_one, back_one, sums_one = call_space_backward(
        grad_o_space, qkv_one, lse_one, x_space, own_mods, spatial_in
    )
    back_places = exchange(back_one).reshape(frames, places, width)
    grad_tokens = (turn(grad_one) + back_places.astype(f32)).astype(bf16)

    def own_columns(values):
        block = values.shape[1] // n_pos
        return lax.dynamic_slice_in_dim(values, me * block, block, 1)

    def total(values):
        return by_distance(butterfly(values, "pos", n_pos), "clip", n_clip)

    own_act = own_columns(cond_act).T
    first_cols = 2 * width
    dmod_rest = total(dot_high(onehot.T, sums.transpose(1, 0, 2).reshape(frames, 7 * width)))
    g_adaln_rest = dot_high(own_act, dmod_rest)
    back_rest = dot_high(dmod_rest, adaln_w[:, first_cols:].T)
    own_hot = lax.dynamic_slice_in_dim(onehot, me * own, own, 0)
    dmod_first = total(dot_high(own_hot.T, sums_one.reshape(own, first_cols)))
    g_adaln_first = dot_high(own_act, dmod_first)
    back_first = dot_high(dmod_first, adaln_w[:, :first_cols].T)
    g_adaln = jnp.concatenate([g_adaln_first, g_adaln_rest], axis=1)
    grad_cond = (back_first + back_rest) * silu_grad(cond)
    g_second = dot_high(own_columns(hidden_cond).T, grad_cond)
    grad_pre = dot_high(grad_cond, second_w.T) * silu_grad(pre_cond)
    g_first = dot_high(own_columns(freq).T, grad_pre)

    early = partial(reduce_rows, n_pos=n_pos, n_clip=n_clip, clip_first=False)
    late = partial(reduce_rows, n_pos=n_pos, n_clip=n_clip, clip_first=True)
    g_hidden_up = early(weight_grad(h_three, grad_u))
    g_hidden_down = late(weight_grad(act, grad_z))
    g_temporal_in = early(weight_grad(h_two, grad_qkv_two))
    outs = late(
        jnp.concatenate(
            [
                weight_grad(o_two, grad_y_two),
                weight_grad(o_one.reshape(rows, width), grad_y_one),
            ],
            axis=1,
        )
    )
    h_flat = h_one.reshape(own * patches, width)
    grad_flat = grad_qkv_one.reshape(own * patches, 3 * width)
    half = grad_flat.shape[1] // 2
    g_spatial_in = jnp.concatenate(
        [
            early(weight_grad(h_flat, grad_flat[:, :half])),
            late(weight_grad(h_flat, grad_flat[:, half:])),
        ],
        axis=1,
    )
    return (
        block_out,
        grad_tokens,
        g_first,
        g_second,
        g_adaln,
        g_spatial_in,
        outs[:, width:],
        g_temporal_in,
        outs[:, :width],
        g_hidden_up,
        g_hidden_down,
    )


def solution(mesh):
    in_specs = (
        P("clip", "pos", None),
        P("clip", None),
        P("clip", None),
        P(),
        P(),
        P(),
        P(),
        P(),
        P(),
        P(),
        P(),
        P(),
        P("clip", "pos", None),
    )
    out_specs = (P("clip", "pos", None),) * 2 + (P("pos", None),) * 9
    body = partial(on_device, n_pos=mesh.shape["pos"], n_clip=mesh.shape["clip"])
    return jax.shard_map(body, mesh=mesh, in_specs=in_specs, out_specs=out_specs, check_vma=False)
```

```python
from functools import partial
import math

import jax
import jax.numpy as jnp
from jax import lax
from jax.experimental import pallas as pl
from jax.experimental.pallas import tpu as pltpu
from jax.sharding import PartitionSpec as P

HEADS = 12
HEAD_DIM = 64
FREQ = 256

epsilon = 1e-06
highest = lax.Precision.HIGHEST
masked_score = -1000000000.0
f32 = jnp.float32
bf16 = jnp.bfloat16


def frequency(step_ids):
    half_width = FREQ // 2
    rate_table = jnp.exp(
        -math.log(10000.0) * jnp.arange(half_width, dtype=jnp.float32) / half_width
    )
    angles = step_ids.astype(jnp.float32)[:, None] * rate_table[None, :]
    return jnp.concatenate([jnp.cos(angles), jnp.sin(angles)], axis=1)


def dot_high(left, right):
    return jnp.dot(left, right, precision=highest, preferred_element_type=f32)


def silu_grad(values):
    gate = jax.nn.sigmoid(values)
    return gate * (1.0 + values * (1.0 - gate))


def clip_onehot(lengths, frames):
    clip_ends = jnp.cumsum(lengths)
    frame_ids = jnp.arange(frames, dtype=jnp.int32)
    clip_ids = jnp.sum((frame_ids[:, None] >= clip_ends[None, :]).astype(jnp.int32), axis=1)
    onehot = (clip_ids[:, None] == jnp.arange(lengths.shape[0], dtype=jnp.int32)[None, :]).astype(
        jnp.float32
    )
    return (onehot, clip_ids)


def weight_grad(left, right):
    return jnp.einsum("rd,rk->dk", left, right, preferred_element_type=f32).astype(bf16)


def bdot(left, right):
    return lax.dot_general(left, right, (((1,), (0,)), ((), ())), preferred_element_type=f32)


def bdot_nt(left, right):
    return lax.dot_general(left, right, (((1,), (1,)), ((), ())), preferred_element_type=f32)


def bdot_tn(left, right):
    return lax.dot_general(left, right, (((0,), (0,)), ((), ())), preferred_element_type=f32)


def norm_rows(values):
    width = values.shape[-1]
    centre = values - jnp.sum(values, axis=-1, keepdims=True) * (1.0 / width)
    spread = jnp.sum(centre * centre, axis=-1, keepdims=True) * (1.0 / width)
    inverse = lax.rsqrt(spread + epsilon)
    return centre * inverse, inverse


def norm_rows_back(normed, inverse, scale_vec, grad):
    width = grad.shape[-1]
    inner = grad * (1.0 + scale_vec)
    mean_one = jnp.sum(inner, axis=-1, keepdims=True) * (1.0 / width)
    mean_two = jnp.sum(inner * normed, axis=-1, keepdims=True) * (1.0 / width)
    return inverse * (inner - mean_one - normed * mean_two)


def pair_masks(scale):
    lanes = lax.broadcasted_iota(jnp.int32, (1, 2 * HEAD_DIM), 1)
    low_half = jnp.where(lanes < HEAD_DIM, scale, 0.0).astype(bf16)
    high_half = jnp.where(lanes < HEAD_DIM, 0.0, scale).astype(bf16)
    return low_half, high_half


ROWS = 32


def load_rows(ref, step):
    places, width = ref.shape[2:]
    count = max(1, ROWS // places)
    part = ref[pl.ds(step * count, count), 0].astype(f32)
    return part.reshape(count * places, width)


class Spread:

    def __init__(self, n_pos, step, steps, hold, out, send_sem, recv_sem, own_sem):
        self.n_pos, self.step, self.steps = n_pos, step, steps
        self.hold, self.out = hold, out
        self.send_sem, self.recv_sem, self.own_sem = send_sem, recv_sem, own_sem
        self.me = lax.axis_index("pos")

    def greet(self):
        barrier = pltpu.get_barrier_semaphore()

        def signal(shift, _):
            target = lax.rem(self.me + shift, self.n_pos)
            pl.semaphore_signal(
                barrier, inc=1, device_id={"pos": target}, device_id_type=pl.DeviceIdType.MESH
            )
            return 0

        lax.fori_loop(1, self.n_pos, signal, 0)
        pl.semaphore_wait(barrier, self.n_pos - 1)

    def copy(self, step, shift, source):
        target = lax.rem(self.me + shift, self.n_pos)
        return pltpu.make_async_remote_copy(
            self.hold.at[step, target],
            self.out.at[source * self.steps + step],
            self.send_sem.at[step, shift],
            self.recv_sem.at[step, shift],
            device_id={"pos": target},
            device_id_type=pl.DeviceIdType.MESH,
        )

    def stay(self, step):
        return pltpu.make_async_copy(
            self.hold.at[step, self.me],
            self.out.at[self.me * self.steps + step],
            self.own_sem.at[step],
        )

    def send(self):
        def one(shift, _):
            self.copy(self.step, shift, self.me).start()
            return 0

        lax.fori_loop(1, self.n_pos, one, 0)
        self.stay(self.step).start()

    def finish(self):
        def one_step(step, _):
            def one(shift, _):
                self.copy(step, shift, self.me).wait_send()
                source = lax.rem(self.me + self.n_pos - shift, self.n_pos)
                self.copy(step, shift, source).wait_recv()
                return 0

            lax.fori_loop(1, self.n_pos, one, 0)
            self.stay(step).wait()
            return 0

        lax.fori_loop(0, self.steps, one_step, 0)


def spread_scratch(own, n_pos, places, width):
    return [
        pltpu.VMEM((own, n_pos, places, width), bf16),
        pltpu.SemaphoreType.DMA((own, n_pos)),
        pltpu.SemaphoreType.DMA((own, n_pos)),
        pltpu.SemaphoreType.DMA((own,)),
    ]


def space_forward(
    x_ref, mod_ref, w_ref, h_ref, qkv_ref, o_ref, lse_ref, hold, send_sem, recv_sem, own_sem
):
    own, n_pos = hold.shape[:2]
    frame = pl.program_id(0)
    spread = Spread(n_pos, frame, own, hold, o_ref, send_sem, recv_sem, own_sem)
    pl.when(frame == 0)(spread.greet)
    patches, width = h_ref.shape[1:]
    places = x_ref.shape[2]
    pair = 2 * HEAD_DIM
    shift, scale = mod_ref[0, 0:1, :], mod_ref[0, 1:2, :]

    def norm_step(step, _):
        normed, _inverse = norm_rows(load_rows(x_ref, step))
        h_ref[0, pl.ds(step * ROWS, ROWS), :] = (normed * (1.0 + scale) + shift).astype(bf16)
        return 0

    lax.fori_loop(0, patches // ROWS, norm_step, 0)
    for part in range(3):
        cols = slice(part * width, (part + 1) * width)
        qkv_ref[0, :, cols] = bdot(h_ref[0], w_ref[:, cols]).astype(bf16)
    masks = pair_masks(1.0 / math.sqrt(HEAD_DIM))
    lane_ids = lax.broadcasted_iota(jnp.int32, (1, pair), 1)
    lse_ref[0] = jnp.zeros((patches, pair), f32)

    def head_pair(index, _):
        at = pl.multiple_of(index * pair, pair)
        q = qkv_ref[0, :, pl.ds(at, pair)]
        k = qkv_ref[0, :, pl.ds(pl.multiple_of(width + at, pair), pair)]
        v = qkv_ref[0, :, pl.ds(pl.multiple_of(2 * width + at, pair), pair)]
        outs = []
        lse = lse_ref[0]
        for half in range(2):
            scores = bdot_nt(q * masks[half], k)
            top = jnp.max(scores, axis=-1, keepdims=True)
            exps = jnp.exp(scores - top)
            total = jnp.sum(exps, axis=-1, keepdims=True)
            probs = (exps * (1.0 / total)).astype(bf16)
            outs.append(bdot(probs, v))
            lse = jnp.where(lane_ids == 2 * index + half, top + jnp.log(total), lse)
        lse_ref[0] = lse
        both = jnp.where(lane_ids < HEAD_DIM, outs[0], outs[1])
        hold[frame, :, :, pl.ds(at, pair)] = both.reshape(n_pos, places, pair).astype(bf16)
        return 0

    lax.fori_loop(0, HEADS // 2, head_pair, 0)
    spread.send()
    pl.when(frame == own - 1)(spread.finish)


def space_backward(
    go_ref, qkv_ref, lse_ref, x_ref, mod_ref, w_ref, dqkv_ref, dv_ref, sum_ref, e_ref,
    hold, send_sem, recv_sem, own_sem,
):
    own, n_pos = hold.shape[:2]
    frame = pl.program_id(0)
    spread = Spread(n_pos, frame, own, hold, dv_ref, send_sem, recv_sem, own_sem)
    pl.when(frame == 0)(spread.greet)
    patches = qkv_ref.shape[1]
    width = x_ref.shape[3]
    places = x_ref.shape[2]
    pair = 2 * HEAD_DIM
    scale = mod_ref[0, 1:2, :]
    factor = 1.0 / math.sqrt(HEAD_DIM)
    masks_q = pair_masks(factor)
    masks = pair_masks(1.0)
    lane_ids = lax.broadcasted_iota(jnp.int32, (1, pair), 1)

    def head_pair(index, _):
        at = pl.multiple_of(index * pair, pair)
        k_at = pl.multiple_of(width + at, pair)
        v_at = pl.multiple_of(2 * width + at, pair)
        q = qkv_ref[0, :, pl.ds(at, pair)]
        k = qkv_ref[0, :, pl.ds(k_at, pair)]
        v = qkv_ref[0, :, pl.ds(v_at, pair)]
        go = go_ref[:, 0, :, pl.ds(at, pair)].astype(f32).reshape(patches, pair).astype(bf16)
        lse_all = lse_ref[0]
        gq, gk, gv = None, None, None
        for half in range(2):
            lse = jnp.sum(
                jnp.where(lane_ids == 2 * index + half, lse_all, 0.0), axis=-1, keepdims=True
            )
            q_half = q * masks_q[half]
            go_half = go * masks[half]
            probs = jnp.exp(bdot_nt(q_half, k) - lse)
            grad_p = bdot_nt(go_half, v)
            inner = jnp.sum(grad_p * probs, axis=-1, keepdims=True)
            grad_s = (probs * (grad_p - inner)).astype(bf16)
            part_q = bdot(grad_s, k * masks_q[half])
            part_k = bdot_tn(grad_s, q_half)
            part_v = bdot_tn(probs.astype(bf16), go_half)
            gq = part_q if gq is None else gq + part_q
            gk = part_k if gk is None else gk + part_k
            gv = part_v if gv is None else gv + part_v
        dqkv_ref[0, :, pl.ds(at, pair)] = gq.astype(bf16)
        dqkv_ref[0, :, pl.ds(k_at, pair)] = gk.astype(bf16)
        dqkv_ref[0, :, pl.ds(v_at, pair)] = gv.astype(bf16)
        return 0

    lax.fori_loop(0, HEADS // 2, head_pair, 0)
    e_ref[...] = bdot_nt(dqkv_ref[0], w_ref[...])

    def norm_step(step, sums):
        grad = e_ref[pl.ds(step * ROWS, ROWS), :]
        normed, inverse = norm_rows(load_rows(x_ref, step))
        back = norm_rows_back(normed, inverse, scale, grad)
        count = max(1, ROWS // places)
        back = back.reshape(count, places, width).astype(bf16)
        hold[frame, pl.ds(step * count, count)] = back
        folded = grad.reshape(ROWS // 8, 8, width).sum(axis=0)
        folded_n = (grad * normed).reshape(ROWS // 8, 8, width).sum(axis=0)
        return sums[0] + folded, sums[1] + folded_n

    zero = jnp.zeros((8, width), f32)
    shift_sum, scale_sum = lax.fori_loop(0, patches // ROWS, norm_step, (zero, zero))
    spread.send()
    sum_ref[0, 0:1, :] = jnp.sum(shift_sum, axis=0, keepdims=True)
    sum_ref[0, 1:2, :] = jnp.sum(scale_sum, axis=0, keepdims=True)
    pl.when(frame == own - 1)(spread.finish)


GELU_C = math.sqrt(2.0 / math.pi)


def middle(
    o1_ref, x_ref, g_ref, mod_ref, clip_ref, wso_ref, wti_ref, wto_ref, wup_ref, wdn_ref,
    out_ref, act_ref, dz_ref, h3_ref, du_ref, o2_ref, dy2_ref, h2_ref, dqkv_ref, dy1_ref, do1_ref,
    dx1_ref, sum_ref,
    qkv_ref, p_ref, y1_ref, y2_ref, n2_ref, n3_ref, r2_ref, r3_ref, xa_ref, gp_ref, e_ref,
):
    count, frames, width = x_ref.shape
    rows = count * frames
    pair = 2 * HEAD_DIM
    hidden = act_ref.shape[1]
    factor = 1.0 / math.sqrt(HEAD_DIM)
    per = frames // ROWS
    steps = rows // ROWS

    @pl.when(pl.program_id(0) == 0)
    def _():
        sum_ref[...] = jnp.zeros_like(sum_ref)

    def at_rows(step):
        return step // per, pl.ds(lax.rem(step, per) * ROWS, ROWS), pl.ds(step * ROWS, ROWS)

    def mod(index, part):
        return mod_ref[index, part, :]

    y1_ref[...] = bdot(o1_ref[...].reshape(rows, width), wso_ref[...])

    def step_one(step, _):
        place, part, flat = at_rows(step)
        x_one = x_ref[place, part, :].astype(f32) + mod(2, part) * y1_ref[flat, :]
        xa_ref[flat, :] = x_one
        normed, inverse = norm_rows(x_one)
        n2_ref[flat, :] = normed
        r2_ref[flat, :] = jnp.broadcast_to(inverse, (ROWS, pair))
        h2_ref[flat, :] = (normed * (1.0 + mod(4, part)) + mod(3, part)).astype(bf16)
        return 0

    lax.fori_loop(0, steps, step_one, 0)
    for third in range(3):
        cols = slice(third * width, (third + 1) * width)
        qkv_ref[:, cols] = bdot(h2_ref[...], wti_ref[:, cols]).astype(bf16)

    masks = pair_masks(1.0)
    masks_q = pair_masks(factor)
    lane_ids = lax.broadcasted_iota(jnp.int32, (1, pair), 1)
    is_low = lane_ids < HEAD_DIM
    allowed = clip_ref[...] > 0.5

    def halves(values, reduce, neutral):
        low_part = reduce(jnp.where(is_low, values, neutral), axis=-1, keepdims=True)
        high_part = reduce(jnp.where(is_low, neutral, values), axis=-1, keepdims=True)
        return jnp.where(is_low, low_part, high_part)

    def stacked(values, pair_of_masks):
        return jnp.concatenate([values * pair_of_masks[0], values * pair_of_masks[1]], axis=0)

    def pair_at(index):
        at = pl.multiple_of(index * pair, pair)
        return (
            pl.ds(at, pair),
            pl.ds(pl.multiple_of(width + at, pair), pair),
            pl.ds(pl.multiple_of(2 * width + at, pair), pair),
        )

    def time_pair(index, _):
        q_at, k_at, v_at = pair_at(index)
        for place in range(count):
            part = slice(place * frames, (place + 1) * frames)
            q = qkv_ref[part, q_at]
            keys = stacked(qkv_ref[part, k_at], masks_q)
            values = stacked(qkv_ref[part, v_at], masks)
            scores = jnp.where(allowed, bdot_nt(q, keys), masked_score)
            exps = jnp.exp(scores - halves(scores, jnp.max, -jnp.inf))
            probs = exps / halves(exps, jnp.sum, 0.0)
            p_ref[index, part, :] = probs
            o2_ref[part, q_at] = bdot(probs.astype(bf16), values).astype(bf16)
        return 0

    lax.fori_loop(0, HEADS // 2, time_pair, 0)

    y2_ref[...] = bdot(o2_ref[...], wto_ref[...])

    def step_two(step, _):
        place, part, flat = at_rows(step)
        x_two = xa_ref[flat, :] + mod(5, part) * y2_ref[flat, :]
        xa_ref[flat, :] = x_two
        normed, inverse = norm_rows(x_two)
        n3_ref[flat, :] = normed
        r3_ref[flat, :] = jnp.broadcast_to(inverse, (ROWS, pair))
        h3_ref[flat, :] = (normed * (1.0 + mod(7, part)) + mod(6, part)).astype(bf16)
        dz_ref[flat, :] = (mod(8, part) * g_ref[place, part, :].astype(f32)).astype(bf16)
        return 0

    lax.fori_loop(0, steps, step_two, 0)

    tile = 256

    def up_tile(index, _):
        cols = pl.ds(pl.multiple_of(index * tile, tile), tile)
        u = bdot(h3_ref[...], wup_ref[:, cols])
        square = u * u
        tanh = jnp.tanh(GELU_C * (u * (1.0 + 0.044715 * square)))
        half = 0.5 * (1.0 + tanh)
        act_ref[:, cols] = (u * half).astype(bf16)
        slope = half + (0.5 * GELU_C) * u * (1.0 - tanh * tanh) * (1.0 + (3.0 * 0.044715) * square)
        du = bdot_nt(dz_ref[...], wdn_ref[cols, :]) * slope
        du_ref[:, cols] = du.astype(bf16)
        return 0

    lax.fori_loop(0, hidden // tile, up_tile, 0)
    e_ref[...] = bdot(act_ref[...], wdn_ref[...])

    def step_three(step, _):
        place, part, flat = at_rows(step)
        z = e_ref[flat, :]
        grad = g_ref[place, part, :].astype(f32)
        out_ref[place, part, :] = (xa_ref[flat, :] + mod(8, part) * z).astype(bf16)
        sum_ref[6, part, :] += grad * z
        return 0

    lax.fori_loop(0, steps, step_three, 0)
    e_ref[...] = bdot_nt(du_ref[...], wup_ref[...])

    def step_four(step, _):
        place, part, flat = at_rows(step)
        grad = e_ref[flat, :]
        normed = n3_ref[flat, :]
        sum_ref[4, part, :] += grad
        sum_ref[5, part, :] += grad * normed
        back = norm_rows_back(normed, r3_ref[flat, 0:1], mod(7, part), grad)
        grad_two = g_ref[place, part, :].astype(f32) + back
        xa_ref[flat, :] = grad_two
        sum_ref[3, part, :] += grad_two * y2_ref[flat, :]
        dy2_ref[flat, :] = (mod(5, part) * grad_two).astype(bf16)
        return 0

    lax.fori_loop(0, steps, step_four, 0)
    y2_ref[...] = bdot_nt(dy2_ref[...], wto_ref[...])

    def time_pair_back(index, _):
        q_at, k_at, v_at = pair_at(index)
        for place in range(count):
            part = slice(place * frames, (place + 1) * frames)
            go = y2_ref[part, q_at].astype(bf16)
            q = qkv_ref[part, q_at] * factor
            keys = stacked(qkv_ref[part, k_at], masks_q)
            values = stacked(qkv_ref[part, v_at], masks)
            probs = p_ref[index, part, :]
            grad_p = bdot_nt(go, values)
            inner = halves(grad_p * probs, jnp.sum, 0.0)
            grad_s = (probs * (grad_p - inner)).astype(bf16)
            dqkv_ref[part, q_at] = bdot(grad_s, keys).astype(bf16)
            grad_k = bdot_tn(grad_s, q)
            grad_v = bdot_tn(probs.astype(bf16), go)
            dqkv_ref[part, k_at] = jnp.where(is_low, grad_k[:frames], grad_k[frames:]).astype(bf16)
            dqkv_ref[part, v_at] = jnp.where(is_low, grad_v[:frames], grad_v[frames:]).astype(bf16)
        return 0

    lax.fori_loop(0, HEADS // 2, time_pair_back, 0)
    e_ref[...] = bdot_nt(dqkv_ref[...], wti_ref[...])

    def step_five(step, _):
        place, part, flat = at_rows(step)
        grad = e_ref[flat, :]
        normed = n2_ref[flat, :]
        sum_ref[1, part, :] += grad
        sum_ref[2, part, :] += grad * normed
        grad_one = xa_ref[flat, :] + norm_rows_back(normed, r2_ref[flat, 0:1], mod(4, part), grad)
        dx1_ref[place, part, :] = grad_one
        sum_ref[0, part, :] += grad_one * y1_ref[flat, :]
        dy1_ref[flat, :] = (mod(2, part) * grad_one).astype(bf16)
        return 0

    lax.fori_loop(0, steps, step_five, 0)
    do1_ref[...] = bdot_nt(dy1_ref[...], wso_ref[...]).astype(bf16).reshape(count, frames, width)


VMEM_LIMIT = 62 * 1024 * 1024


def resident(shape):
    return pl.BlockSpec(shape, lambda i: (0,) * len(shape), pipeline_mode=pl.Buffered(1))


def call_space_forward(x, mods, weight):
    n_pos, own, places, width = x.shape
    patches = n_pos * places
    pair = 2 * HEAD_DIM
    spread = pl.BlockSpec((n_pos, 1, places, width), lambda i: (0, i, 0, 0))

    def by_frame(*shape):
        return pl.BlockSpec((1,) + shape, lambda i: (i, 0, 0))

    rows = own * patches
    return pl.pallas_call(
        space_forward,
        grid=(own,),
        in_specs=[spread, by_frame(2, width), resident(weight.shape)],
        out_specs=[
            by_frame(patches, width),
            by_frame(patches, 3 * width),
            pl.BlockSpec(memory_space=pl.ANY),
            by_frame(patches, pair),
        ],
        out_shape=[
            jax.ShapeDtypeStruct((own, patches, width), bf16),
            jax.ShapeDtypeStruct((own, patches, 3 * width), bf16),
            jax.ShapeDtypeStruct((n_pos * own, places, width), bf16),
            jax.ShapeDtypeStruct((own, patches, pair), f32),
        ],
        scratch_shapes=spread_scratch(own, n_pos, places, width),
        compiler_params=pltpu.CompilerParams(
            vmem_limit_bytes=VMEM_LIMIT, collective_id=0, has_side_effects=True
        ),
        cost_estimate=pl.CostEstimate(
            flops=2 * rows * width * 3 * width + 4 * rows * patches * width,
            bytes_accessed=rows * width * 12 + weight.size * 2,
            transcendentals=rows * patches * HEADS,
        ),
        name="space_forward",
    )(x, mods, weight)


def call_space_backward(go, qkv, lse, x, mods, weight):
    n_pos, own, places, width = x.shape
    patches = n_pos * places
    pair = 2 * HEAD_DIM
    spread = pl.BlockSpec((n_pos, 1, places, width), lambda i: (0, i, 0, 0))

    def by_frame(*shape):
        return pl.BlockSpec((1,) + shape, lambda i: (i, 0, 0))

    rows = own * patches
    return pl.pallas_call(
        space_backward,
        grid=(own,),
        in_specs=[
            spread,
            by_frame(patches, 3 * width),
            by_frame(patches, pair),
            spread,
            by_frame(2, width),
            resident(weight.shape),
        ],
        out_specs=[
            by_frame(patches, 3 * width),
            pl.BlockSpec(memory_space=pl.ANY),
            by_frame(2, width),
        ],
        out_shape=[
            jax.ShapeDtypeStruct((own, patches, 3 * width), bf16),
            jax.ShapeDtypeStruct((n_pos * own, places, width), bf16),
            jax.ShapeDtypeStruct((own, 2, width), f32),
        ],
        scratch_shapes=[pltpu.VMEM((patches, width), f32)]
        + spread_scratch(own, n_pos, places, width),
        compiler_params=pltpu.CompilerParams(
            vmem_limit_bytes=VMEM_LIMIT, collective_id=1, has_side_effects=True
        ),
        cost_estimate=pl.CostEstimate(
            flops=2 * rows * width * 3 * width + 10 * rows * patches * width,
            bytes_accessed=rows * width * 16 + weight.size * 2,
            transcendentals=rows * patches * HEADS,
        ),
        name="space_backward",
    )(go, qkv, lse, x, mods, weight)


def call_middle(o_one, x, grad, mods, same_clip, wso, wti, wto, wup, wdn):
    places, frames, width = x.shape
    count = max(1, min(places, 256 // frames))
    rows = count * frames
    hidden = wup.shape[1]
    pair = 2 * HEAD_DIM
    total = places * frames
    chunk = pl.BlockSpec((count, frames, width), lambda i: (i, 0, 0))

    def flat(cols):
        return pl.BlockSpec((rows, cols), lambda i: (i, 0))

    def flat_shape(cols):
        return jax.ShapeDtypeStruct((total, cols), bf16)

    def scratch(cols, dtype=f32):
        return pltpu.VMEM((rows, cols), dtype)

    lanes = jnp.concatenate([same_clip, same_clip], axis=1)
    flops = 2 * total * (2 * (wso.size + wti.size + wto.size + wup.size + wdn.size))
    return pl.pallas_call(
        middle,
        grid=(places // count,),
        in_specs=[chunk, chunk, chunk, resident(mods.shape), resident(lanes.shape)]
        + [resident(w.shape) for w in (wso, wti, wto, wup, wdn)],
        out_specs=[
            chunk,
            flat(hidden),
            flat(width),
            flat(width),
            flat(hidden),
            flat(width),
            flat(width),
            flat(width),
            flat(3 * width),
            flat(width),
            chunk,
            chunk,
            pl.BlockSpec((7, frames, width), lambda i: (0, 0, 0)),
        ],
        out_shape=[
            jax.ShapeDtypeStruct(x.shape, bf16),
            flat_shape(hidden),
            flat_shape(width),
            flat_shape(width),
            flat_shape(hidden),
            flat_shape(width),
            flat_shape(width),
            flat_shape(width),
            flat_shape(3 * width),
            flat_shape(width),
            jax.ShapeDtypeStruct(x.shape, bf16),
            jax.ShapeDtypeStruct(x.shape, f32),
            jax.ShapeDtypeStruct((7, frames, width), f32),
        ],
        scratch_shapes=[
            scratch(3 * width, bf16),
            pltpu.VMEM((HEADS // 2, rows, pair), f32),
            scratch(width),
            scratch(width),
            scratch(width),
            scratch(width),
            scratch(pair),
            scratch(pair),
            scratch(width),
            pltpu.VMEM((8, pair), f32),
            scratch(width),
        ],
        compiler_params=pltpu.CompilerParams(vmem_limit_bytes=VMEM_LIMIT),
        cost_estimate=pl.CostEstimate(
            flops=flops, bytes_accessed=total * 40000, transcendentals=total * hidden
        ),
        name="middle",
    )(o_one, x, grad, mods, lanes, wso, wti, wto, wup, wdn)


def swap(values, axis, size, bit):
    return lax.ppermute(values, axis, [(i, i ^ bit) for i in range(size)])


def bits_of(size):
    return [1 << i for i in range(size.bit_length() - 1)]


def by_distance(values, axis, size):
    for bit in bits_of(size):
        values = jnp.concatenate([values, swap(values, axis, size, bit)], axis=0)
    return values


def butterfly(values, axis, size):
    for bit in bits_of(size):
        values = values + swap(values, axis, size, bit)
    return values


def halve(values, index, axis):
    def pick(at):
        return lax.dynamic_index_in_dim(values, at, axis, keepdims=False)

    return pick(index), pick(1 - index)


def reduce_rows(grad, n_pos, n_clip, clip_first):
    rows, cols = grad.shape
    block = rows // n_pos
    me, clip_at = lax.axis_index("pos"), lax.axis_index("clip")
    values = grad.reshape(n_pos, block, cols)

    def add(keep, got):
        return (keep.astype(f32) + got.astype(f32)).astype(bf16)

    def pos_step(values, bit):
        left = values.shape[0] // 2
        split = values.reshape(left, 2, *values.shape[1:])
        keep, send = halve(split, lax.rem(me // bit, 2), 1)
        return add(keep, swap(send, "pos", n_pos, bit))

    bits = bits_of(n_pos)
    values = pos_step(values, bits[0])
    if clip_first:
        for bit in reversed(bits_of(n_clip)):
            split = values.reshape(*values.shape[:2], 2, values.shape[2] // 2)
            keep, send = halve(split, lax.rem(clip_at // bit, 2), 2)
            values = add(keep, swap(send, "clip", n_clip, bit))
    for bit in bits[1:]:
        values = pos_step(values, bit)
    values = values[0]
    for bit in bits_of(n_clip):
        got = swap(values, "clip", n_clip, bit)
        if clip_first:
            upper = lax.rem(clip_at // bit, 2) == 1
            values = jnp.concatenate(
                [jnp.where(upper, got, values), jnp.where(upper, values, got)], axis=1
            )
        elif 2 * bit == n_clip:
            return values.astype(f32) + got.astype(f32)
        else:
            values = add(values, got)
    return values.astype(f32)


def on_device(
    tokens,
    clip_lengths,
    timesteps,
    embed_first,
    embed_second,
    adaln_weight,
    spatial_in,
    spatial_out,
    temporal_in,
    temporal_out,
    hidden_up,
    hidden_down,
    grad_output,
    n_pos=16,
    n_clip=2,
):
    frames, places, width = tokens.shape
    rows = frames * places
    own = frames // n_pos
    patches = places * n_pos
    me = lax.axis_index("pos")
    clips = clip_lengths.shape[1]

    def exchange(values):
        sent = values.reshape(frames, places, width)
        got = lax.all_to_all(sent, "pos", split_axis=0, concat_axis=0, tiled=True)
        return got.reshape(n_pos, own, places, width)

    x_space = exchange(tokens)

    all_steps = by_distance(timesteps[0], "clip", n_clip)
    freq = frequency(all_steps)
    first_w, second_w, adaln_w = (
        embed_first.astype(f32),
        embed_second.astype(f32),
        adaln_weight.astype(f32),
    )
    pre_cond = dot_high(freq, first_w)
    hidden_cond = jax.nn.silu(pre_cond)
    cond = dot_high(hidden_cond, second_w)
    cond_act = jax.nn.silu(cond)
    modulated = dot_high(cond_act[:clips], adaln_w)
    onehot, clip_ids = clip_onehot(clip_lengths[0], frames)
    per_frame = dot_high(onehot, modulated)
    own_frames = lax.dynamic_slice_in_dim(per_frame, me * own, own, 0)

    own_mods = own_frames[:, : 2 * width].reshape(own, 2, width)
    h_one, qkv_one, o_one, lse_one = call_space_forward(x_space, own_mods, spatial_in)

    def turn(values):
        return values.transpose(1, 0, 2)

    o_one = turn(o_one)
    mods = per_frame.reshape(frames, 9, width).transpose(1, 0, 2)
    same_clip = jnp.dot(onehot, onehot.T)
    (block_turned, act, grad_z, h_three, grad_u, o_two, grad_y_two, h_two, grad_qkv_two, grad_y_one, grad_o_one,
     grad_one, sums) = call_middle(
        o_one, turn(tokens), turn(grad_output), mods, same_clip, spatial_out, temporal_in, temporal_out,
        hidden_up, hidden_down,
    )
    block_out = turn(block_turned)
    grad_o_space = exchange(turn(grad_o_one))
    grad_qkv_one, back_places, sums_one = call_space_backward(
        grad_o_space, qkv_one, lse_one, x_space, own_mods, spatial_in
    )
    grad_tokens = (turn(grad_one) + back_places.astype(f32)).astype(bf16)

    def own_columns(values):
        block = values.shape[1] // n_pos
        return lax.dynamic_slice_in_dim(values, me * block, block, 1)

    def total(values):
        return by_distance(butterfly(values, "pos", n_pos), "clip", n_clip)

    own_act = own_columns(cond_act).T
    first_cols = 2 * width
    dmod_rest = total(dot_high(onehot.T, sums.transpose(1, 0, 2).reshape(frames, 7 * width)))
    g_adaln_rest = dot_high(own_act, dmod_rest)
    back_rest = dot_high(dmod_rest, adaln_w[:, first_cols:].T)
    own_hot = lax.dynamic_slice_in_dim(onehot, me * own, own, 0)
    dmod_first = total(dot_high(own_hot.T, sums_one.reshape(own, first_cols)))
    g_adaln_first = dot_high(own_act, dmod_first)
    back_first = dot_high(dmod_first, adaln_w[:, :first_cols].T)
    g_adaln = jnp.concatenate([g_adaln_first, g_adaln_rest], axis=1)
    grad_cond = (back_first + back_rest) * silu_grad(cond)
    g_second = dot_high(own_columns(hidden_cond).T, grad_cond)
    grad_pre = dot_high(grad_cond, second_w.T) * silu_grad(pre_cond)
    g_first = dot_high(own_columns(freq).T, grad_pre)

    h_two, grad_qkv_two, o_two, grad_y_two, o_one, grad_y_one, grad_qkv_one = lax.optimization_barrier(
        (h_two, grad_qkv_two, o_two, grad_y_two, o_one, grad_y_one, grad_qkv_one)
    )
    early = partial(reduce_rows, n_pos=n_pos, n_clip=n_clip, clip_first=False)
    late = partial(reduce_rows, n_pos=n_pos, n_clip=n_clip, clip_first=True)
    g_hidden_up = early(weight_grad(h_three, grad_u))
    g_hidden_down = late(weight_grad(act, grad_z))
    g_temporal_in = early(weight_grad(h_two, grad_qkv_two))
    outs = late(
        jnp.concatenate(
            [
                weight_grad(o_two, grad_y_two),
                weight_grad(o_one.reshape(rows, width), grad_y_one),
            ],
            axis=1,
        )
    )
    h_flat = h_one.reshape(own * patches, width)
    grad_flat = grad_qkv_one.reshape(own * patches, 3 * width)
    half = grad_flat.shape[1] // 2
    g_spatial_in = jnp.concatenate(
        [
            early(weight_grad(h_flat, grad_flat[:, :half])),
            late(weight_grad(h_flat, grad_flat[:, half:])),
        ],
        axis=1,
    )
    return (
        block_out,
        grad_tokens,
        g_first,
        g_second,
        g_adaln,
        g_spatial_in,
        outs[:, width:],
        g_temporal_in,
        outs[:, :width],
        g_hidden_up,
        g_hidden_down,
    )


def solution(mesh):
    in_specs = (
        P("clip", "pos", None),
        P("clip", None),
        P("clip", None),
        P(),
        P(),
        P(),
        P(),
        P(),
        P(),
        P(),
        P(),
        P(),
        P("clip", "pos", None),
    )
    out_specs = (P("clip", "pos", None),) * 2 + (P("pos", None),) * 9
    body = partial(on_device, n_pos=mesh.shape["pos"], n_clip=mesh.shape["clip"])
    return jax.shard_map(body, mesh=mesh, in_specs=in_specs, out_specs=out_specs, check_vma=False)
```

```python
from functools import partial
import math

import jax
import jax.numpy as jnp
from jax import lax
from jax.experimental import pallas as pl
from jax.experimental.pallas import tpu as pltpu
from jax.sharding import PartitionSpec as P

HEADS = 12
HEAD_DIM = 64
FREQ = 256

epsilon = 1e-06
highest = lax.Precision.HIGHEST
masked_score = -1000000000.0
f32 = jnp.float32
bf16 = jnp.bfloat16


def frequency(step_ids):
    half_width = FREQ // 2
    rate_table = jnp.exp(
        -math.log(10000.0) * jnp.arange(half_width, dtype=jnp.float32) / half_width
    )
    angles = step_ids.astype(jnp.float32)[:, None] * rate_table[None, :]
    return jnp.concatenate([jnp.cos(angles), jnp.sin(angles)], axis=1)


def dot_high(left, right):
    return jnp.dot(left, right, precision=highest, preferred_element_type=f32)


def silu_grad(values):
    gate = jax.nn.sigmoid(values)
    return gate * (1.0 + values * (1.0 - gate))


def clip_onehot(lengths, frames):
    clip_ends = jnp.cumsum(lengths)
    frame_ids = jnp.arange(frames, dtype=jnp.int32)
    clip_ids = jnp.sum((frame_ids[:, None] >= clip_ends[None, :]).astype(jnp.int32), axis=1)
    onehot = (clip_ids[:, None] == jnp.arange(lengths.shape[0], dtype=jnp.int32)[None, :]).astype(
        jnp.float32
    )
    return (onehot, clip_ids)


def weight_grad(left, right):
    return jnp.einsum("rd,rk->dk", left, right, preferred_element_type=f32).astype(bf16)


def bdot(left, right):
    return lax.dot_general(left, right, (((1,), (0,)), ((), ())), preferred_element_type=f32)


def bdot_nt(left, right):
    return lax.dot_general(left, right, (((1,), (1,)), ((), ())), preferred_element_type=f32)


def bdot_tn(left, right):
    return lax.dot_general(left, right, (((0,), (0,)), ((), ())), preferred_element_type=f32)


def norm_rows(values):
    width = values.shape[-1]
    centre = values - jnp.sum(values, axis=-1, keepdims=True) * (1.0 / width)
    spread = jnp.sum(centre * centre, axis=-1, keepdims=True) * (1.0 / width)
    inverse = lax.rsqrt(spread + epsilon)
    return centre * inverse, inverse


def norm_rows_back(normed, inverse, scale_vec, grad):
    width = grad.shape[-1]
    inner = grad * (1.0 + scale_vec)
    mean_one = jnp.sum(inner, axis=-1, keepdims=True) * (1.0 / width)
    mean_two = jnp.sum(inner * normed, axis=-1, keepdims=True) * (1.0 / width)
    return inverse * (inner - mean_one - normed * mean_two)


def pair_masks(scale):
    lanes = lax.broadcasted_iota(jnp.int32, (1, 2 * HEAD_DIM), 1)
    low_half = jnp.where(lanes < HEAD_DIM, scale, 0.0).astype(bf16)
    high_half = jnp.where(lanes < HEAD_DIM, 0.0, scale).astype(bf16)
    return low_half, high_half


ROWS = 32


def load_rows(ref, step):
    places, width = ref.shape[2:]
    count = max(1, ROWS // places)
    part = ref[pl.ds(step * count, count), 0].astype(f32)
    return part.reshape(count * places, width)


class Spread:

    def __init__(self, n_pos, step, steps, hold, out, send_sem, recv_sem, own_sem):
        self.n_pos, self.step, self.steps = n_pos, step, steps
        self.hold, self.out = hold, out
        self.send_sem, self.recv_sem, self.own_sem = send_sem, recv_sem, own_sem
        self.me = lax.axis_index("pos")

    def greet(self):
        barrier = pltpu.get_barrier_semaphore()

        def signal(shift, _):
            target = lax.rem(self.me + shift, self.n_pos)
            pl.semaphore_signal(
                barrier, inc=1, device_id={"pos": target}, device_id_type=pl.DeviceIdType.MESH
            )
            return 0

        lax.fori_loop(1, self.n_pos, signal, 0)
        pl.semaphore_wait(barrier, self.n_pos - 1)

    def copy(self, step, shift, source):
        target = lax.rem(self.me + shift, self.n_pos)
        return pltpu.make_async_remote_copy(
            self.hold.at[step, target],
            self.out.at[source * self.steps + step],
            self.send_sem.at[step, shift],
            self.recv_sem.at[step, shift],
            device_id={"pos": target},
            device_id_type=pl.DeviceIdType.MESH,
        )

    def stay(self, step):
        return pltpu.make_async_copy(
            self.hold.at[step, self.me],
            self.out.at[self.me * self.steps + step],
            self.own_sem.at[step],
        )

    def send(self):
        def one(shift, _):
            self.copy(self.step, shift, self.me).start()
            return 0

        lax.fori_loop(1, self.n_pos, one, 0)
        self.stay(self.step).start()

    def finish(self):
        def one_step(step, _):
            def one(shift, _):
                self.copy(step, shift, self.me).wait_send()
                source = lax.rem(self.me + self.n_pos - shift, self.n_pos)
                self.copy(step, shift, source).wait_recv()
                return 0

            lax.fori_loop(1, self.n_pos, one, 0)
            self.stay(step).wait()
            return 0

        lax.fori_loop(0, self.steps, one_step, 0)


def spread_scratch(own, n_pos, places, width):
    return [
        pltpu.VMEM((own, n_pos, places, width), bf16),
        pltpu.SemaphoreType.DMA((own, n_pos)),
        pltpu.SemaphoreType.DMA((own, n_pos)),
        pltpu.SemaphoreType.DMA((own,)),
    ]


def space_forward(
    x_ref, mod_ref, w_ref, h_ref, qkv_ref, o_ref, lse_ref, hold, send_sem, recv_sem, own_sem
):
    own, n_pos = hold.shape[:2]
    frame = pl.program_id(0)
    spread = Spread(n_pos, frame, own, hold, o_ref, send_sem, recv_sem, own_sem)
    pl.when(frame == 0)(spread.greet)
    patches, width = h_ref.shape[1:]
    places = x_ref.shape[2]
    pair = 2 * HEAD_DIM
    shift, scale = mod_ref[0, 0:1, :], mod_ref[0, 1:2, :]

    def norm_step(step, _):
        normed, _inverse = norm_rows(load_rows(x_ref, step))
        h_ref[0, pl.ds(step * ROWS, ROWS), :] = (normed * (1.0 + scale) + shift).astype(bf16)
        return 0

    lax.fori_loop(0, patches // ROWS, norm_step, 0)
    for part in range(3):
        cols = slice(part * width, (part + 1) * width)
        qkv_ref[0, :, cols] = bdot(h_ref[0], w_ref[:, cols]).astype(bf16)
    masks = pair_masks(1.0 / math.sqrt(HEAD_DIM))
    lane_ids = lax.broadcasted_iota(jnp.int32, (1, pair), 1)
    lse_ref[0] = jnp.zeros((patches, pair), f32)

    def head_pair(index, _):
        at = pl.multiple_of(index * pair, pair)
        q = qkv_ref[0, :, pl.ds(at, pair)]
        k = qkv_ref[0, :, pl.ds(pl.multiple_of(width + at, pair), pair)]
        v = qkv_ref[0, :, pl.ds(pl.multiple_of(2 * width + at, pair), pair)]
        outs = []
        lse = lse_ref[0]
        for half in range(2):
            scores = bdot_nt(q * masks[half], k)
            top = jnp.max(scores, axis=-1, keepdims=True)
            exps = jnp.exp(scores - top)
            total = jnp.sum(exps, axis=-1, keepdims=True)
            probs = (exps * (1.0 / total)).astype(bf16)
            outs.append(bdot(probs, v))
            lse = jnp.where(lane_ids == 2 * index + half, top + jnp.log(total), lse)
        lse_ref[0] = lse
        both = jnp.where(lane_ids < HEAD_DIM, outs[0], outs[1])
        hold[frame, :, :, pl.ds(at, pair)] = both.reshape(n_pos, places, pair).astype(bf16)
        return 0

    lax.fori_loop(0, HEADS // 2, head_pair, 0)
    spread.send()
    pl.when(frame == own - 1)(spread.finish)


def space_backward(
    go_ref, qkv_ref, lse_ref, x_ref, mod_ref, w_ref, dqkv_ref, dv_ref, sum_ref, e_ref,
    hold, send_sem, recv_sem, own_sem,
):
    own, n_pos = hold.shape[:2]
    frame = pl.program_id(0)
    spread = Spread(n_pos, frame, own, hold, dv_ref, send_sem, recv_sem, own_sem)
    pl.when(frame == 0)(spread.greet)
    patches = qkv_ref.shape[1]
    width = x_ref.shape[3]
    places = x_ref.shape[2]
    pair = 2 * HEAD_DIM
    scale = mod_ref[0, 1:2, :]
    factor = 1.0 / math.sqrt(HEAD_DIM)
    masks_q = pair_masks(factor)
    masks = pair_masks(1.0)
    lane_ids = lax.broadcasted_iota(jnp.int32, (1, pair), 1)

    def head_pair(index, _):
        at = pl.multiple_of(index * pair, pair)
        k_at = pl.multiple_of(width + at, pair)
        v_at = pl.multiple_of(2 * width + at, pair)
        q = qkv_ref[0, :, pl.ds(at, pair)]
        k = qkv_ref[0, :, pl.ds(k_at, pair)]
        v = qkv_ref[0, :, pl.ds(v_at, pair)]
        go = go_ref[:, 0, :, pl.ds(at, pair)].astype(f32).reshape(patches, pair).astype(bf16)
        lse_all = lse_ref[0]
        gq, gk, gv = None, None, None
        for half in range(2):
            lse = jnp.sum(
                jnp.where(lane_ids == 2 * index + half, lse_all, 0.0), axis=-1, keepdims=True
            )
            q_half = q * masks_q[half]
            go_half = go * masks[half]
            probs = jnp.exp(bdot_nt(q_half, k) - lse)
            grad_p = bdot_nt(go_half, v)
            inner = jnp.sum(grad_p * probs, axis=-1, keepdims=True)
            grad_s = (probs * (grad_p - inner)).astype(bf16)
            part_q = bdot(grad_s, k * masks_q[half])
            part_k = bdot_tn(grad_s, q_half)
            part_v = bdot_tn(probs.astype(bf16), go_half)
            gq = part_q if gq is None else gq + part_q
            gk = part_k if gk is None else gk + part_k
            gv = part_v if gv is None else gv + part_v
        dqkv_ref[0, :, pl.ds(at, pair)] = gq.astype(bf16)
        dqkv_ref[0, :, pl.ds(k_at, pair)] = gk.astype(bf16)
        dqkv_ref[0, :, pl.ds(v_at, pair)] = gv.astype(bf16)
        return 0

    lax.fori_loop(0, HEADS // 2, head_pair, 0)
    e_ref[...] = bdot_nt(dqkv_ref[0], w_ref[...])

    def norm_step(step, sums):
        grad = e_ref[pl.ds(step * ROWS, ROWS), :]
        normed, inverse = norm_rows(load_rows(x_ref, step))
        back = norm_rows_back(normed, inverse, scale, grad)
        count = max(1, ROWS // places)
        back = back.reshape(count, places, width).astype(bf16)
        hold[frame, pl.ds(step * count, count)] = back
        folded = grad.reshape(ROWS // 8, 8, width).sum(axis=0)
        folded_n = (grad * normed).reshape(ROWS // 8, 8, width).sum(axis=0)
        return sums[0] + folded, sums[1] + folded_n

    zero = jnp.zeros((8, width), f32)
    shift_sum, scale_sum = lax.fori_loop(0, patches // ROWS, norm_step, (zero, zero))
    spread.send()
    sum_ref[0, 0:1, :] = jnp.sum(shift_sum, axis=0, keepdims=True)
    sum_ref[0, 1:2, :] = jnp.sum(scale_sum, axis=0, keepdims=True)
    pl.when(frame == own - 1)(spread.finish)


GELU_C = math.sqrt(2.0 / math.pi)


def middle(
    o1_ref, x_ref, g_ref, mod_ref, clip_ref, wso_ref, wti_ref, wto_ref, wup_ref, wdn_ref,
    out_ref, act_ref, dz_ref, h3_ref, du_ref, o2_ref, dy2_ref, h2_ref, dqkv_ref, dy1_ref, do1_ref,
    dx1_ref, sum_ref,
    qkv_ref, p_ref, y1_ref, y2_ref, n2_ref, n3_ref, r2_ref, r3_ref, xa_ref, gp_ref, e_ref,
):
    count, frames, width = x_ref.shape
    rows = count * frames
    pair = 2 * HEAD_DIM
    hidden = act_ref.shape[1]
    factor = 1.0 / math.sqrt(HEAD_DIM)
    per = frames // ROWS
    steps = rows // ROWS

    @pl.when(pl.program_id(0) == 0)
    def _():
        sum_ref[...] = jnp.zeros_like(sum_ref)

    def at_rows(step):
        return step // per, pl.ds(lax.rem(step, per) * ROWS, ROWS), pl.ds(step * ROWS, ROWS)

    def mod(index, part):
        return mod_ref[index, part, :]

    y1_ref[...] = bdot(o1_ref[...].reshape(rows, width), wso_ref[...])

    def step_one(step, _):
        place, part, flat = at_rows(step)
        x_one = x_ref[place, part, :].astype(f32) + mod(2, part) * y1_ref[flat, :]
        xa_ref[flat, :] = x_one
        normed, inverse = norm_rows(x_one)
        n2_ref[flat, :] = normed
        r2_ref[flat, :] = jnp.broadcast_to(inverse, (ROWS, pair))
        h2_ref[flat, :] = (normed * (1.0 + mod(4, part)) + mod(3, part)).astype(bf16)
        return 0

    lax.fori_loop(0, steps, step_one, 0)
    for third in range(3):
        cols = slice(third * width, (third + 1) * width)
        qkv_ref[:, cols] = bdot(h2_ref[...], wti_ref[:, cols]).astype(bf16)

    masks = pair_masks(1.0)
    masks_q = pair_masks(factor)
    lane_ids = lax.broadcasted_iota(jnp.int32, (1, pair), 1)
    is_low = lane_ids < HEAD_DIM
    allowed = clip_ref[...] > 0.5

    def halves(values, reduce, neutral):
        low_part = reduce(jnp.where(is_low, values, neutral), axis=-1, keepdims=True)
        high_part = reduce(jnp.where(is_low, neutral, values), axis=-1, keepdims=True)
        return jnp.where(is_low, low_part, high_part)

    def stacked(values, pair_of_masks):
        return jnp.concatenate([values * pair_of_masks[0], values * pair_of_masks[1]], axis=0)

    def pair_at(index):
        at = pl.multiple_of(index * pair, pair)
        return (
            pl.ds(at, pair),
            pl.ds(pl.multiple_of(width + at, pair), pair),
            pl.ds(pl.multiple_of(2 * width + at, pair), pair),
        )

    def time_pair(index, _):
        q_at, k_at, v_at = pair_at(index)
        for place in range(count):
            part = slice(place * frames, (place + 1) * frames)
            q = qkv_ref[part, q_at]
            keys = stacked(qkv_ref[part, k_at], masks_q)
            values = stacked(qkv_ref[part, v_at], masks)
            scores = jnp.where(allowed, bdot_nt(q, keys), masked_score)
            exps = jnp.exp(scores - halves(scores, jnp.max, -jnp.inf))
            probs = exps / halves(exps, jnp.sum, 0.0)
            p_ref[index, part, :] = probs
            o2_ref[part, q_at] = bdot(probs.astype(bf16), values).astype(bf16)
        return 0

    lax.fori_loop(0, HEADS // 2, time_pair, 0)

    y2_ref[...] = bdot(o2_ref[...], wto_ref[...])

    def step_two(step, _):
        place, part, flat = at_rows(step)
        x_two = xa_ref[flat, :] + mod(5, part) * y2_ref[flat, :]
        xa_ref[flat, :] = x_two
        normed, inverse = norm_rows(x_two)
        n3_ref[flat, :] = normed
        r3_ref[flat, :] = jnp.broadcast_to(inverse, (ROWS, pair))
        h3_ref[flat, :] = (normed * (1.0 + mod(7, part)) + mod(6, part)).astype(bf16)
        dz_ref[flat, :] = (mod(8, part) * g_ref[place, part, :].astype(f32)).astype(bf16)
        return 0

    lax.fori_loop(0, steps, step_two, 0)

    tile = 256

    def up_tile(index, _):
        cols = pl.ds(pl.multiple_of(index * tile, tile), tile)
        u = bdot(h3_ref[...], wup_ref[:, cols])
        square = u * u
        tanh = jnp.tanh(GELU_C * (u * (1.0 + 0.044715 * square)))
        half = 0.5 * (1.0 + tanh)
        act_ref[:, cols] = (u * half).astype(bf16)
        slope = half + (0.5 * GELU_C) * u * (1.0 - tanh * tanh) * (1.0 + (3.0 * 0.044715) * square)
        du = bdot_nt(dz_ref[...], wdn_ref[cols, :]) * slope
        du_ref[:, cols] = du.astype(bf16)
        return 0

    lax.fori_loop(0, hidden // tile, up_tile, 0)
    e_ref[...] = bdot(act_ref[...], wdn_ref[...])

    def step_three(step, _):
        place, part, flat = at_rows(step)
        z = e_ref[flat, :]
        grad = g_ref[place, part, :].astype(f32)
        out_ref[place, part, :] = (xa_ref[flat, :] + mod(8, part) * z).astype(bf16)
        sum_ref[6, part, :] += grad * z
        return 0

    lax.fori_loop(0, steps, step_three, 0)
    e_ref[...] = bdot_nt(du_ref[...], wup_ref[...])

    def step_four(step, _):
        place, part, flat = at_rows(step)
        grad = e_ref[flat, :]
        normed = n3_ref[flat, :]
        sum_ref[4, part, :] += grad
        sum_ref[5, part, :] += grad * normed
        back = norm_rows_back(normed, r3_ref[flat, 0:1], mod(7, part), grad)
        grad_two = g_ref[place, part, :].astype(f32) + back
        xa_ref[flat, :] = grad_two
        sum_ref[3, part, :] += grad_two * y2_ref[flat, :]
        dy2_ref[flat, :] = (mod(5, part) * grad_two).astype(bf16)
        return 0

    lax.fori_loop(0, steps, step_four, 0)
    y2_ref[...] = bdot_nt(dy2_ref[...], wto_ref[...])

    def time_pair_back(index, _):
        q_at, k_at, v_at = pair_at(index)
        for place in range(count):
            part = slice(place * frames, (place + 1) * frames)
            go = y2_ref[part, q_at].astype(bf16)
            q = qkv_ref[part, q_at] * factor
            keys = stacked(qkv_ref[part, k_at], masks_q)
            values = stacked(qkv_ref[part, v_at], masks)
            probs = p_ref[index, part, :]
            grad_p = bdot_nt(go, values)
            inner = halves(grad_p * probs, jnp.sum, 0.0)
            grad_s = (probs * (grad_p - inner)).astype(bf16)
            dqkv_ref[part, q_at] = bdot(grad_s, keys).astype(bf16)
            grad_k = bdot_tn(grad_s, q)
            grad_v = bdot_tn(probs.astype(bf16), go)
            dqkv_ref[part, k_at] = jnp.where(is_low, grad_k[:frames], grad_k[frames:]).astype(bf16)
            dqkv_ref[part, v_at] = jnp.where(is_low, grad_v[:frames], grad_v[frames:]).astype(bf16)
        return 0

    lax.fori_loop(0, HEADS // 2, time_pair_back, 0)
    e_ref[...] = bdot_nt(dqkv_ref[...], wti_ref[...])

    def step_five(step, _):
        place, part, flat = at_rows(step)
        grad = e_ref[flat, :]
        normed = n2_ref[flat, :]
        sum_ref[1, part, :] += grad
        sum_ref[2, part, :] += grad * normed
        grad_one = xa_ref[flat, :] + norm_rows_back(normed, r2_ref[flat, 0:1], mod(4, part), grad)
        dx1_ref[place, part, :] = grad_one
        sum_ref[0, part, :] += grad_one * y1_ref[flat, :]
        dy1_ref[flat, :] = (mod(2, part) * grad_one).astype(bf16)
        return 0

    lax.fori_loop(0, steps, step_five, 0)
    do1_ref[...] = bdot_nt(dy1_ref[...], wso_ref[...]).astype(bf16).reshape(count, frames, width)


VMEM_LIMIT = 62 * 1024 * 1024


def resident(shape):
    return pl.BlockSpec(shape, lambda i: (0,) * len(shape), pipeline_mode=pl.Buffered(1))


def call_space_forward(x, mods, weight):
    n_pos, own, places, width = x.shape
    patches = n_pos * places
    pair = 2 * HEAD_DIM
    spread = pl.BlockSpec((n_pos, 1, places, width), lambda i: (0, i, 0, 0))

    def by_frame(*shape):
        return pl.BlockSpec((1,) + shape, lambda i: (i, 0, 0))

    rows = own * patches
    return pl.pallas_call(
        space_forward,
        grid=(own,),
        in_specs=[spread, by_frame(2, width), resident(weight.shape)],
        out_specs=[
            by_frame(patches, width),
            by_frame(patches, 3 * width),
            pl.BlockSpec(memory_space=pl.ANY),
            by_frame(patches, pair),
        ],
        out_shape=[
            jax.ShapeDtypeStruct((own, patches, width), bf16),
            jax.ShapeDtypeStruct((own, patches, 3 * width), bf16),
            jax.ShapeDtypeStruct((n_pos * own, places, width), bf16),
            jax.ShapeDtypeStruct((own, patches, pair), f32),
        ],
        scratch_shapes=spread_scratch(own, n_pos, places, width),
        compiler_params=pltpu.CompilerParams(
            vmem_limit_bytes=VMEM_LIMIT, collective_id=0, has_side_effects=True
        ),
        cost_estimate=pl.CostEstimate(
            flops=2 * rows * width * 3 * width + 4 * rows * patches * width,
            bytes_accessed=rows * width * 12 + weight.size * 2,
            transcendentals=rows * patches * HEADS,
        ),
        name="space_forward",
    )(x, mods, weight)


def call_space_backward(go, qkv, lse, x, mods, weight):
    n_pos, own, places, width = x.shape
    patches = n_pos * places
    pair = 2 * HEAD_DIM
    spread = pl.BlockSpec((n_pos, 1, places, width), lambda i: (0, i, 0, 0))

    def by_frame(*shape):
        return pl.BlockSpec((1,) + shape, lambda i: (i, 0, 0))

    rows = own * patches
    return pl.pallas_call(
        space_backward,
        grid=(own,),
        in_specs=[
            spread,
            by_frame(patches, 3 * width),
            by_frame(patches, pair),
            spread,
            by_frame(2, width),
            resident(weight.shape),
        ],
        out_specs=[
            by_frame(patches, 3 * width),
            pl.BlockSpec(memory_space=pl.ANY),
            by_frame(2, width),
        ],
        out_shape=[
            jax.ShapeDtypeStruct((own, patches, 3 * width), bf16),
            jax.ShapeDtypeStruct((n_pos * own, places, width), bf16),
            jax.ShapeDtypeStruct((own, 2, width), f32),
        ],
        scratch_shapes=[pltpu.VMEM((patches, width), f32)]
        + spread_scratch(own, n_pos, places, width),
        compiler_params=pltpu.CompilerParams(
            vmem_limit_bytes=VMEM_LIMIT, collective_id=1, has_side_effects=True
        ),
        cost_estimate=pl.CostEstimate(
            flops=2 * rows * width * 3 * width + 10 * rows * patches * width,
            bytes_accessed=rows * width * 16 + weight.size * 2,
            transcendentals=rows * patches * HEADS,
        ),
        name="space_backward",
    )(go, qkv, lse, x, mods, weight)


def call_middle(o_one, x, grad, mods, same_clip, wso, wti, wto, wup, wdn):
    places, frames, width = x.shape
    count = max(1, min(places, 256 // frames))
    rows = count * frames
    hidden = wup.shape[1]
    pair = 2 * HEAD_DIM
    total = places * frames
    chunk = pl.BlockSpec((count, frames, width), lambda i: (i, 0, 0))

    def flat(cols):
        return pl.BlockSpec((rows, cols), lambda i: (i, 0))

    def flat_shape(cols):
        return jax.ShapeDtypeStruct((total, cols), bf16)

    def scratch(cols, dtype=f32):
        return pltpu.VMEM((rows, cols), dtype)

    lanes = jnp.concatenate([same_clip, same_clip], axis=1)
    flops = 2 * total * (2 * (wso.size + wti.size + wto.size + wup.size + wdn.size))
    return pl.pallas_call(
        middle,
        grid=(places // count,),
        in_specs=[chunk, chunk, chunk, resident(mods.shape), resident(lanes.shape)]
        + [resident(w.shape) for w in (wso, wti, wto, wup, wdn)],
        out_specs=[
            chunk,
            flat(hidden),
            flat(width),
            flat(width),
            flat(hidden),
            flat(width),
            flat(width),
            flat(width),
            flat(3 * width),
            flat(width),
            chunk,
            chunk,
            pl.BlockSpec((7, frames, width), lambda i: (0, 0, 0)),
        ],
        out_shape=[
            jax.ShapeDtypeStruct(x.shape, bf16),
            flat_shape(hidden),
            flat_shape(width),
            flat_shape(width),
            flat_shape(hidden),
            flat_shape(width),
            flat_shape(width),
            flat_shape(width),
            flat_shape(3 * width),
            flat_shape(width),
            jax.ShapeDtypeStruct(x.shape, bf16),
            jax.ShapeDtypeStruct(x.shape, f32),
            jax.ShapeDtypeStruct((7, frames, width), f32),
        ],
        scratch_shapes=[
            scratch(3 * width, bf16),
            pltpu.VMEM((HEADS // 2, rows, pair), f32),
            scratch(width),
            scratch(width),
            scratch(width),
            scratch(width),
            scratch(pair),
            scratch(pair),
            scratch(width),
            pltpu.VMEM((8, pair), f32),
            scratch(width),
        ],
        compiler_params=pltpu.CompilerParams(vmem_limit_bytes=VMEM_LIMIT),
        cost_estimate=pl.CostEstimate(
            flops=flops, bytes_accessed=total * 40000, transcendentals=total * hidden
        ),
        name="middle",
    )(o_one, x, grad, mods, lanes, wso, wti, wto, wup, wdn)


def swap(values, axis, size, bit):
    return lax.ppermute(values, axis, [(i, i ^ bit) for i in range(size)])


def bits_of(size):
    return [1 << i for i in range(size.bit_length() - 1)]


def by_distance(values, axis, size):
    for bit in bits_of(size):
        values = jnp.concatenate([values, swap(values, axis, size, bit)], axis=0)
    return values


def dot_exact(left, right):
    parts = []
    for _ in range(3):
        part = left.astype(bf16)
        parts.append(part)
        left = left - part.astype(f32)
    count = parts[0].shape[0]
    got = jnp.dot(jnp.concatenate(parts, axis=0), right, preferred_element_type=f32)
    return got[:count] + (got[count : 2 * count] + got[2 * count :])


def flow_stages(n_pos, n_clip, clip_first):
    pos = [("pos", bit, "halve") for bit in bits_of(n_pos)]
    clip = bits_of(n_clip)
    if not clip_first:
        return pos + [("clip", bit, "sum") for bit in clip]
    first = [("clip", clip[0], "columns")]
    last = [("clip", clip[0], "gather")]
    return pos[:1] + first + pos[1:] + [("clip", bit, "sum") for bit in clip[1:]] + last


def flow_shapes(stages, n_pos, block, cols):
    lead = n_pos.bit_length() - 1
    shapes = []
    for _, _, what in stages:
        if what == "halve":
            lead -= 1
        elif what == "columns":
            cols //= 2
        shapes.append((2,) * lead + (block, cols))
    return shapes


class Flow:
    def __init__(self, number, stages, grad, out, keep, gots, sems, place):
        self.number, self.stages = number, stages
        self.grad, self.out, self.keep, self.gots = grad, out, keep, gots
        self.send_sem, self.recv_sem, self.keep_sem = sems
        self.place = place

    def side(self, stage):
        axis, bit, _ = self.stages[stage]
        return lax.rem(self.place[axis] // bit, 2)

    def columns(self, side, width):
        return pl.ds(pl.multiple_of(side * width, width), width)

    def part(self, ref, stage, side):
        what = self.stages[stage][2]
        lead = len(ref.shape) - 2
        if what == "halve":
            return (slice(None),) * (lead - 1) + (side,)
        if what == "columns":
            half = ref.shape[-1] // 2
            return (slice(None),) * (lead + 1) + (self.columns(side, half),)
        return None

    def held(self, stage):
        if stage == 0:
            return self.grad
        return self.keep if stage == 1 else self.gots[stage - 1]

    def copy(self, stage):
        axis, bit, _ = self.stages[stage]
        side = self.side(stage)
        source = self.held(stage)
        at = self.part(source, stage, 1 - side)
        return pltpu.make_async_remote_copy(
            source if at is None else source.at[at],
            self.gots[stage],
            self.send_sem.at[self.number, stage],
            self.recv_sem.at[self.number, stage],
            device_id={axis: self.place[axis] + bit * (1 - 2 * side)},
            device_id_type=pl.DeviceIdType.MESH,
        )

    def own(self):
        at = self.part(self.grad, 0, self.side(0))
        return pltpu.make_async_copy(self.grad.at[at], self.keep, self.keep_sem.at[self.number])

    def start(self):
        self.copy(0).start()
        self.own().start()

    def take(self, stage):
        self.copy(stage).wait_recv()
        if stage == 0:
            self.own().wait()
        what = self.stages[stage][2]
        got = self.gots[stage]
        side = self.side(stage)
        last = stage == len(self.stages) - 1
        lead = len(got.shape) - 2
        if what == "gather":
            half = got.shape[-1]
            self.out[:, self.columns(side, half)] = self.held(stage)[...].astype(f32)
            self.out[:, self.columns(1 - side, half)] = got[...].astype(f32)
            return
        if last:
            self.out[...] = self.held(stage)[...].astype(f32) + got[...].astype(f32)
            return
        target = self.keep if stage == 0 else got

        def one(index, _):
            at = tuple(lax.rem(index // (1 << i), 2) for i in range(lead))
            if stage == 0:
                mine = self.keep[at]
            elif what == "halve":
                mine = self.held(stage)[at + (side,)]
            elif what == "columns":
                mine = self.held(stage)[at + (slice(None), self.columns(side, got.shape[-1]))]
            else:
                mine = self.held(stage)[at]
            target[at] = mine + got[at]
            return 0

        lax.fori_loop(0, 1 << lead, one, 0)
        self.copy(stage + 1).start()

    def finish(self):
        for stage in range(len(self.stages)):
            self.copy(stage).wait_send()


class Butterfly:
    def __init__(self, n_pos, n_clip, values, out, got, acc, sems, place):
        self.pos_bits, self.clip_bits = bits_of(n_pos), bits_of(n_clip)
        self.values, self.out, self.got, self.acc = values, out, got, acc
        self.send_sem, self.recv_sem = sems
        self.place = place
        self.count = len(self.pos_bits) + len(self.clip_bits)

    def copy(self, stage):
        if stage < len(self.pos_bits):
            axis, bit = "pos", self.pos_bits[stage]
            source = self.values if stage == 0 else self.acc.at[stage - 1]
            target = self.got.at[stage]
        else:
            axis, bit = "clip", self.clip_bits[stage - len(self.pos_bits)]
            source, target = self.out.at[pl.ds(0, bit)], self.out.at[pl.ds(bit, bit)]
        side = lax.rem(self.place[axis] // bit, 2)
        return pltpu.make_async_remote_copy(
            source,
            target,
            self.send_sem.at[stage],
            self.recv_sem.at[stage],
            device_id={axis: self.place[axis] + bit * (1 - 2 * side)},
            device_id_type=pl.DeviceIdType.MESH,
        )

    def start(self):
        self.copy(0).start()

    def take(self, stage):
        self.copy(stage).wait_recv()
        last = len(self.pos_bits) - 1
        if stage <= last:
            mine = self.values[...] if stage == 0 else self.acc[stage - 1]
            if stage < last:
                self.acc[stage] = mine + self.got[stage]
            else:
                self.out[0] = mine + self.got[stage]
        if stage + 1 < self.count:
            self.copy(stage + 1).start()

    def finish(self):
        for stage in range(self.count):
            self.copy(stage).wait_send()


def combine(n_pos, n_clip, kinds, *refs):
    count = len(kinds)
    grads, small = refs[:count], refs[count]
    outs, small_out = refs[count + 1 : 2 * count + 1], refs[2 * count + 1]
    rest = list(refs[2 * count + 2 :])
    place = {"pos": lax.axis_index("pos"), "clip": lax.axis_index("clip")}
    partners = [("pos", bit) for bit in bits_of(n_pos)] + [("clip", bit) for bit in bits_of(n_clip)]
    barrier = pltpu.get_barrier_semaphore()
    for axis, bit in partners:
        side = lax.rem(place[axis] // bit, 2)
        pl.semaphore_signal(
            barrier,
            inc=1,
            device_id={axis: place[axis] + bit * (1 - 2 * side)},
            device_id_type=pl.DeviceIdType.MESH,
        )
    pl.semaphore_wait(barrier, len(partners))

    sems = rest[:3]
    small_sems = rest[3:5]
    got, acc = rest[5:7]
    rest = rest[7:]
    flows = []
    for number, clip_first in enumerate(kinds):
        stages = flow_stages(n_pos, n_clip, clip_first)
        keep, gots = rest[0], rest[1 : 1 + len(stages)]
        rest = rest[1 + len(stages) :]
        flows.append(Flow(number, stages, grads[number], outs[number], keep, gots, sems, place))
    tree = Butterfly(n_pos, n_clip, small, small_out, got, acc, small_sems, place)
    tree.start()
    for flow in flows:
        flow.start()
    for stage in range(max(tree.count, max(len(flow.stages) for flow in flows))):
        if stage < tree.count:
            tree.take(stage)
        for flow in flows:
            if stage < len(flow.stages):
                flow.take(stage)
    tree.finish()
    for flow in flows:
        flow.finish()


def call_combine(grads, kinds, small, n_pos, n_clip):
    lead = n_pos.bit_length() - 1
    most = lead + len(bits_of(n_clip)) + 1
    views, out_shape, buffers = [], [], []
    for grad, clip_first in zip(grads, kinds):
        rows, cols = grad.shape
        block = rows // n_pos
        views.append(grad.reshape((2,) * lead + (block, cols)))
        out_shape.append(jax.ShapeDtypeStruct((block, cols), f32))
        stages = flow_stages(n_pos, n_clip, clip_first)
        shapes = flow_shapes(stages, n_pos, block, cols)
        buffers += [pltpu.VMEM(shape, bf16) for shape in [shapes[0]] + shapes]
    clips, wide = small.shape
    out_shape.append(jax.ShapeDtypeStruct((n_clip, clips, wide), f32))
    dma = pltpu.SemaphoreType.DMA
    whole = pl.BlockSpec(memory_space=pltpu.VMEM)
    sizes = sum(grad.size for grad in grads)
    return pl.pallas_call(
        partial(combine, n_pos, n_clip, kinds),
        in_specs=[pl.BlockSpec(memory_space=pl.ANY)] * len(grads) + [whole],
        out_specs=[whole] * len(out_shape),
        out_shape=out_shape,
        scratch_shapes=[
            dma((len(grads), most)),
            dma((len(grads), most)),
            dma((len(grads),)),
            dma((most,)),
            dma((most,)),
            pltpu.VMEM((lead, clips, wide), f32),
            pltpu.VMEM((lead, clips, wide), f32),
        ]
        + buffers,
        compiler_params=pltpu.CompilerParams(
            vmem_limit_bytes=VMEM_LIMIT, collective_id=2, has_side_effects=True
        ),
        cost_estimate=pl.CostEstimate(flops=sizes, bytes_accessed=sizes * 4, transcendentals=0),
        name="combine",
    )(*views, small)


def on_device(
    tokens,
    clip_lengths,
    timesteps,
    embed_first,
    embed_second,
    adaln_weight,
    spatial_in,
    spatial_out,
    temporal_in,
    temporal_out,
    hidden_up,
    hidden_down,
    grad_output,
    n_pos=16,
    n_clip=2,
):
    frames, places, width = tokens.shape
    rows = frames * places
    own = frames // n_pos
    patches = places * n_pos
    me = lax.axis_index("pos")
    clips = clip_lengths.shape[1]

    def exchange(values):
        sent = values.reshape(frames, places, width)
        got = lax.all_to_all(sent, "pos", split_axis=0, concat_axis=0, tiled=True)
        return got.reshape(n_pos, own, places, width)

    x_space = exchange(tokens)

    all_steps = by_distance(timesteps[0], "clip", n_clip)
    freq = frequency(all_steps)
    pre_cond = dot_exact(freq, embed_first)
    hidden_cond = jax.nn.silu(pre_cond)
    cond = dot_exact(hidden_cond, embed_second)
    cond_act = jax.nn.silu(cond)
    modulated = dot_exact(cond_act[:clips], adaln_weight)
    onehot, clip_ids = clip_onehot(clip_lengths[0], frames)
    per_frame = dot_high(onehot, modulated)
    own_frames = lax.dynamic_slice_in_dim(per_frame, me * own, own, 0)

    own_mods = own_frames[:, : 2 * width].reshape(own, 2, width)
    h_one, qkv_one, o_one, lse_one = call_space_forward(x_space, own_mods, spatial_in)

    def turn(values):
        return values.transpose(1, 0, 2)

    o_one = turn(o_one)
    mods = per_frame.reshape(frames, 9, width).transpose(1, 0, 2)
    same_clip = jnp.dot(onehot, onehot.T)
    (block_turned, act, grad_z, h_three, grad_u, o_two, grad_y_two, h_two, grad_qkv_two, grad_y_one, grad_o_one,
     grad_one, sums) = call_middle(
        o_one, turn(tokens), turn(grad_output), mods, same_clip, spatial_out, temporal_in, temporal_out,
        hidden_up, hidden_down,
    )
    block_out = turn(block_turned)
    grad_o_space = exchange(turn(grad_o_one))
    grad_qkv_one, back_places, sums_one = call_space_backward(
        grad_o_space, qkv_one, lse_one, x_space, own_mods, spatial_in
    )
    grad_tokens = (turn(grad_one) + back_places.astype(f32)).astype(bf16)

    h_flat = h_one.reshape(own * patches, width)
    grad_flat = grad_qkv_one.reshape(own * patches, 3 * width)
    own_hot = lax.dynamic_slice_in_dim(onehot, me * own, own, 0)
    dmod_first = dot_high(own_hot.T, sums_one.reshape(own, 2 * width))
    dmod_rest = dot_high(onehot.T, sums.transpose(1, 0, 2).reshape(frames, 7 * width))
    grads = (
        weight_grad(h_three, grad_u),
        weight_grad(act, grad_z),
        weight_grad(h_two, grad_qkv_two),
        weight_grad(h_flat, grad_flat),
        weight_grad(o_two, grad_y_two),
        weight_grad(o_one.reshape(rows, width), grad_y_one),
    )
    kinds = (False, True, False, True, False, True)
    dmod_local = jnp.concatenate([dmod_first, dmod_rest], axis=1)
    (
        g_hidden_up, g_hidden_down, g_temporal_in, g_spatial_in, g_temporal_out, g_spatial_out, dmod
    ) = call_combine(grads, kinds, dmod_local, n_pos, n_clip)
    dmod = dmod.reshape(n_clip * clips, 9 * width)

    def own_columns(values):
        block = values.shape[1] // n_pos
        return lax.dynamic_slice_in_dim(values, me * block, block, 1)

    g_adaln = dot_high(own_columns(cond_act).T, dmod)
    grad_cond = dot_exact(dmod, adaln_weight.T) * silu_grad(cond)
    g_second = dot_high(own_columns(hidden_cond).T, grad_cond)
    grad_pre = dot_exact(grad_cond, embed_second.T) * silu_grad(pre_cond)
    g_first = dot_high(own_columns(freq).T, grad_pre)
    return (
        block_out,
        grad_tokens,
        g_first,
        g_second,
        g_adaln,
        g_spatial_in,
        g_spatial_out,
        g_temporal_in,
        g_temporal_out,
        g_hidden_up,
        g_hidden_down,
    )


def solution(mesh):
    in_specs = (
        P("clip", "pos", None),
        P("clip", None),
        P("clip", None),
        P(),
        P(),
        P(),
        P(),
        P(),
        P(),
        P(),
        P(),
        P(),
        P("clip", "pos", None),
    )
    out_specs = (P("clip", "pos", None),) * 2 + (P("pos", None),) * 9
    body = partial(on_device, n_pos=mesh.shape["pos"], n_clip=mesh.shape["clip"])
    return jax.shard_map(body, mesh=mesh, in_specs=in_specs, out_specs=out_specs, check_vma=False)
```

```python
from functools import partial
import math

import jax
import jax.numpy as jnp
from jax import lax
from jax.experimental import pallas as pl
from jax.experimental.pallas import tpu as pltpu
from jax.sharding import PartitionSpec as P

HEADS = 12
HEAD_DIM = 64
FREQ = 256

epsilon = 1e-06
highest = lax.Precision.HIGHEST
masked_score = -1000000000.0
f32 = jnp.float32
bf16 = jnp.bfloat16


def frequency(step_ids):
    half_width = FREQ // 2
    rate_table = jnp.exp(
        -math.log(10000.0) * jnp.arange(half_width, dtype=jnp.float32) / half_width
    )
    angles = step_ids.astype(jnp.float32)[:, None] * rate_table[None, :]
    return jnp.concatenate([jnp.cos(angles), jnp.sin(angles)], axis=1)


def dot_high(left, right):
    return jnp.dot(left, right, precision=highest, preferred_element_type=f32)


def silu_grad(values):
    gate = jax.nn.sigmoid(values)
    return gate * (1.0 + values * (1.0 - gate))


def clip_onehot(lengths, frames):
    clip_ends = jnp.cumsum(lengths)
    frame_ids = jnp.arange(frames, dtype=jnp.int32)
    clip_ids = jnp.sum((frame_ids[:, None] >= clip_ends[None, :]).astype(jnp.int32), axis=1)
    onehot = (clip_ids[:, None] == jnp.arange(lengths.shape[0], dtype=jnp.int32)[None, :]).astype(
        jnp.float32
    )
    return (onehot, clip_ids)


def weight_grad(left, right):
    return jnp.einsum("rd,rk->dk", left, right, preferred_element_type=f32).astype(bf16)


def bdot(left, right):
    return lax.dot_general(left, right, (((1,), (0,)), ((), ())), preferred_element_type=f32)


def bdot_nt(left, right):
    return lax.dot_general(left, right, (((1,), (1,)), ((), ())), preferred_element_type=f32)


def bdot_tn(left, right):
    return lax.dot_general(left, right, (((0,), (0,)), ((), ())), preferred_element_type=f32)


def norm_rows(values):
    width = values.shape[-1]
    centre = values - jnp.sum(values, axis=-1, keepdims=True) * (1.0 / width)
    spread = jnp.sum(centre * centre, axis=-1, keepdims=True) * (1.0 / width)
    inverse = lax.rsqrt(spread + epsilon)
    return centre * inverse, inverse


def norm_rows_back(normed, inverse, scale_vec, grad):
    width = grad.shape[-1]
    inner = grad * (1.0 + scale_vec)
    mean_one = jnp.sum(inner, axis=-1, keepdims=True) * (1.0 / width)
    mean_two = jnp.sum(inner * normed, axis=-1, keepdims=True) * (1.0 / width)
    return inverse * (inner - mean_one - normed * mean_two)


def pair_masks(scale):
    lanes = lax.broadcasted_iota(jnp.int32, (1, 2 * HEAD_DIM), 1)
    low_half = jnp.where(lanes < HEAD_DIM, scale, 0.0).astype(bf16)
    high_half = jnp.where(lanes < HEAD_DIM, 0.0, scale).astype(bf16)
    return low_half, high_half


ROWS = 32


def load_rows(ref, step):
    places, width = ref.shape[2:]
    count = max(1, ROWS // places)
    part = ref[pl.ds(step * count, count), 0].astype(f32)
    return part.reshape(count * places, width)


def swap(values, axis, size, bit):
    return lax.ppermute(values, axis, [(i, i ^ bit) for i in range(size)])


def bits_of(size):
    return [1 << i for i in range(size.bit_length() - 1)]


def by_distance(values, axis, size):
    for bit in bits_of(size):
        values = jnp.concatenate([values, swap(values, axis, size, bit)], axis=0)
    return values


def dot_exact(left, right):
    parts = []
    for _ in range(3):
        part = left.astype(bf16)
        parts.append(part)
        left = left - part.astype(f32)
    count = parts[0].shape[0]
    got = jnp.dot(jnp.concatenate(parts, axis=0), right, preferred_element_type=f32)
    return got[:count] + (got[count : 2 * count] + got[2 * count :])


def flow_stages(n_pos, n_clip, clip_first):
    pos = [("pos", bit, "halve") for bit in bits_of(n_pos)]
    clip = bits_of(n_clip)
    if not clip_first:
        return pos + [("clip", bit, "sum") for bit in clip]
    first = [("clip", clip[0], "columns")]
    last = [("clip", clip[0], "gather")]
    return pos[:1] + first + pos[1:] + [("clip", bit, "sum") for bit in clip[1:]] + last


def flow_shapes(stages, n_pos, block, cols):
    lead = n_pos.bit_length() - 1
    shapes = []
    for _, _, what in stages:
        if what == "halve":
            lead -= 1
        elif what == "columns":
            cols //= 2
        shapes.append((2,) * lead + (block, cols))
    return shapes


class Flow:
    def __init__(self, number, stages, grad, out, keep, gots, sems, place):
        self.number, self.stages = number, stages
        self.grad, self.out, self.keep, self.gots = grad, out, keep, gots
        self.send_sem, self.recv_sem, self.keep_sem = sems
        self.place = place

    def side(self, stage):
        axis, bit, _ = self.stages[stage]
        return lax.rem(self.place[axis] // bit, 2)

    def columns(self, side, width):
        return pl.ds(pl.multiple_of(side * width, width), width)

    def part(self, ref, stage, side):
        what = self.stages[stage][2]
        lead = len(ref.shape) - 2
        if what == "halve":
            return (slice(None),) * (lead - 1) + (side,)
        if what == "columns":
            half = ref.shape[-1] // 2
            return (slice(None),) * (lead + 1) + (self.columns(side, half),)
        return None

    def held(self, stage):
        if stage == 0:
            return self.grad
        return self.keep if stage == 1 else self.gots[stage - 1]

    def copy(self, stage):
        axis, bit, _ = self.stages[stage]
        side = self.side(stage)
        source = self.held(stage)
        at = self.part(source, stage, 1 - side)
        return pltpu.make_async_remote_copy(
            source if at is None else source.at[at],
            self.gots[stage],
            self.send_sem.at[self.number, stage],
            self.recv_sem.at[self.number, stage],
            device_id={axis: self.place[axis] + bit * (1 - 2 * side)},
            device_id_type=pl.DeviceIdType.MESH,
        )

    def own(self):
        at = self.part(self.grad, 0, self.side(0))
        return pltpu.make_async_copy(self.grad.at[at], self.keep, self.keep_sem.at[self.number])

    def start(self):
        self.copy(0).start()
        self.own().start()

    def take(self, stage):
        self.copy(stage).wait_recv()
        if stage == 0:
            self.own().wait()
        what = self.stages[stage][2]
        got = self.gots[stage]
        side = self.side(stage)
        last = stage == len(self.stages) - 1
        lead = len(got.shape) - 2
        if what == "gather":
            half = got.shape[-1]
            self.out[:, self.columns(side, half)] = self.held(stage)[...].astype(f32)
            self.out[:, self.columns(1 - side, half)] = got[...].astype(f32)
            return
        if last:
            self.out[...] = self.held(stage)[...].astype(f32) + got[...].astype(f32)
            return
        target = self.keep if stage == 0 else got

        def one(index, _):
            at = tuple(lax.rem(index // (1 << i), 2) for i in range(lead))
            if stage == 0:
                mine = self.keep[at]
            elif what == "halve":
                mine = self.held(stage)[at + (side,)]
            elif what == "columns":
                mine = self.held(stage)[at + (slice(None), self.columns(side, got.shape[-1]))]
            else:
                mine = self.held(stage)[at]
            target[at] = mine + got[at]
            return 0

        lax.fori_loop(0, 1 << lead, one, 0)
        self.copy(stage + 1).start()

    def finish(self):
        for stage in range(len(self.stages)):
            self.copy(stage).wait_send()


class Butterfly:
    def __init__(self, n_pos, n_clip, values, out, got, acc, sems, place):
        self.pos_bits, self.clip_bits = bits_of(n_pos), bits_of(n_clip)
        self.values, self.out, self.got, self.acc = values, out, got, acc
        self.send_sem, self.recv_sem = sems
        self.place = place
        self.count = len(self.pos_bits) + len(self.clip_bits)

    def copy(self, stage):
        if stage < len(self.pos_bits):
            axis, bit = "pos", self.pos_bits[stage]
            source = self.values if stage == 0 else self.acc.at[stage - 1]
            target = self.got.at[stage]
        else:
            axis, bit = "clip", self.clip_bits[stage - len(self.pos_bits)]
            source, target = self.out.at[pl.ds(0, bit)], self.out.at[pl.ds(bit, bit)]
        side = lax.rem(self.place[axis] // bit, 2)
        return pltpu.make_async_remote_copy(
            source,
            target,
            self.send_sem.at[stage],
            self.recv_sem.at[stage],
            device_id={axis: self.place[axis] + bit * (1 - 2 * side)},
            device_id_type=pl.DeviceIdType.MESH,
        )

    def start(self):
        self.copy(0).start()

    def take(self, stage):
        self.copy(stage).wait_recv()
        last = len(self.pos_bits) - 1
        if stage <= last:
            mine = self.values[...] if stage == 0 else self.acc[stage - 1]
            if stage < last:
                self.acc[stage] = mine + self.got[stage]
            else:
                self.out[0] = mine + self.got[stage]
        if stage + 1 < self.count:
            self.copy(stage + 1).start()

    def finish(self):
        for stage in range(self.count):
            self.copy(stage).wait_send()


def partner_list(n_pos, n_clip):
    return [("pos", bit) for bit in bits_of(n_pos)] + [("clip", bit) for bit in bits_of(n_clip)]


def here():
    return {"pos": lax.axis_index("pos"), "clip": lax.axis_index("clip")}


def signal_swap(barrier, place, axis, bit):
    side = lax.rem(place[axis] // bit, 2)
    pl.semaphore_signal(
        barrier,
        inc=1,
        device_id={axis: place[axis] + bit * (1 - 2 * side)},
        device_id_type=pl.DeviceIdType.MESH,
    )


def make_flows(n_pos, n_clip, kinds, grads, outs, scratch):
    sems, rest = scratch[:3], list(scratch[3:])
    flows = []
    for number, clip_first in enumerate(kinds):
        stages = flow_stages(n_pos, n_clip, clip_first)
        keep, gots = rest[0], rest[1 : 1 + len(stages)]
        rest = rest[1 + len(stages) :]
        flows.append(Flow(number, stages, grads[number], outs[number], keep, gots, sems, here()))
    return flows


def flow_plan(grads, kinds, n_pos, n_clip):
    lead = n_pos.bit_length() - 1
    most = lead + len(bits_of(n_clip)) + 1
    dma = pltpu.SemaphoreType.DMA
    scratch = [dma((len(grads), most)), dma((len(grads), most)), dma((len(grads),))]
    views, out_shape = [], []
    for grad, clip_first in zip(grads, kinds):
        rows, cols = grad.shape
        block = rows // n_pos
        views.append(grad.reshape((2,) * lead + (block, cols)))
        out_shape.append(jax.ShapeDtypeStruct((block, cols), f32))
        shapes = flow_shapes(flow_stages(n_pos, n_clip, clip_first), n_pos, block, cols)
        scratch += [pltpu.VMEM(shape, bf16) for shape in [shapes[0]] + shapes]
    return views, out_shape, scratch


class Spread:

    def __init__(self, n_pos, step, steps, hold, out, send_sem, recv_sem, own_sem):
        self.n_pos, self.step, self.steps = n_pos, step, steps
        self.hold, self.out = hold, out
        self.send_sem, self.recv_sem, self.own_sem = send_sem, recv_sem, own_sem
        self.me = lax.axis_index("pos")

    def greet(self, more=0):
        barrier = pltpu.get_barrier_semaphore()

        def signal(shift, _):
            target = lax.rem(self.me + shift, self.n_pos)
            pl.semaphore_signal(
                barrier, inc=1, device_id={"pos": target}, device_id_type=pl.DeviceIdType.MESH
            )
            return 0

        lax.fori_loop(1, self.n_pos, signal, 0)
        pl.semaphore_wait(barrier, self.n_pos - 1 + more)

    def copy(self, step, shift, source):
        target = lax.rem(self.me + shift, self.n_pos)
        return pltpu.make_async_remote_copy(
            self.hold.at[step, target],
            self.out.at[source * self.steps + step],
            self.send_sem.at[step, shift],
            self.recv_sem.at[step, shift],
            device_id={"pos": target},
            device_id_type=pl.DeviceIdType.MESH,
        )

    def stay(self, step):
        return pltpu.make_async_copy(
            self.hold.at[step, self.me],
            self.out.at[self.me * self.steps + step],
            self.own_sem.at[step],
        )

    def send(self):
        def one(shift, _):
            self.copy(self.step, shift, self.me).start()
            return 0

        lax.fori_loop(1, self.n_pos, one, 0)
        self.stay(self.step).start()

    def finish(self):
        def one_step(step, _):
            def one(shift, _):
                self.copy(step, shift, self.me).wait_send()
                source = lax.rem(self.me + self.n_pos - shift, self.n_pos)
                self.copy(step, shift, source).wait_recv()
                return 0

            lax.fori_loop(1, self.n_pos, one, 0)
            self.stay(step).wait()
            return 0

        lax.fori_loop(0, self.steps, one_step, 0)


def spread_scratch(own, n_pos, places, width):
    return [
        pltpu.VMEM((own, n_pos, places, width), bf16),
        pltpu.SemaphoreType.DMA((own, n_pos)),
        pltpu.SemaphoreType.DMA((own, n_pos)),
        pltpu.SemaphoreType.DMA((own,)),
    ]


def space_forward(
    x_ref, mod_ref, w_ref, h_ref, qkv_ref, o_ref, lse_ref, hold, send_sem, recv_sem, own_sem
):
    own, n_pos = hold.shape[:2]
    frame = pl.program_id(0)
    spread = Spread(n_pos, frame, own, hold, o_ref, send_sem, recv_sem, own_sem)
    pl.when(frame == 0)(spread.greet)
    patches, width = h_ref.shape[1:]
    places = x_ref.shape[2]
    pair = 2 * HEAD_DIM
    shift, scale = mod_ref[0, 0:1, :], mod_ref[0, 1:2, :]

    def norm_step(step, _):
        normed, _inverse = norm_rows(load_rows(x_ref, step))
        h_ref[0, pl.ds(step * ROWS, ROWS), :] = (normed * (1.0 + scale) + shift).astype(bf16)
        return 0

    lax.fori_loop(0, patches // ROWS, norm_step, 0)
    for part in range(3):
        cols = slice(part * width, (part + 1) * width)
        qkv_ref[0, :, cols] = bdot(h_ref[0], w_ref[:, cols]).astype(bf16)
    masks = pair_masks(1.0 / math.sqrt(HEAD_DIM))
    lane_ids = lax.broadcasted_iota(jnp.int32, (1, pair), 1)
    lse_ref[0] = jnp.zeros((patches, pair), f32)

    def head_pair(index, _):
        at = pl.multiple_of(index * pair, pair)
        q = qkv_ref[0, :, pl.ds(at, pair)]
        k = qkv_ref[0, :, pl.ds(pl.multiple_of(width + at, pair), pair)]
        v = qkv_ref[0, :, pl.ds(pl.multiple_of(2 * width + at, pair), pair)]
        outs = []
        lse = lse_ref[0]
        for half in range(2):
            scores = bdot_nt(q * masks[half], k)
            top = jnp.max(scores, axis=-1, keepdims=True)
            exps = jnp.exp(scores - top)
            total = jnp.sum(exps, axis=-1, keepdims=True)
            probs = (exps * (1.0 / total)).astype(bf16)
            outs.append(bdot(probs, v))
            lse = jnp.where(lane_ids == 2 * index + half, top + jnp.log(total), lse)
        lse_ref[0] = lse
        both = jnp.where(lane_ids < HEAD_DIM, outs[0], outs[1])
        hold[frame, :, :, pl.ds(at, pair)] = both.reshape(n_pos, places, pair).astype(bf16)
        return 0

    lax.fori_loop(0, HEADS // 2, head_pair, 0)
    spread.send()
    pl.when(frame == own - 1)(spread.finish)


def space_backward(n_clip, kinds, *refs):
    flow_count = len(kinds)
    go_ref, qkv_ref, lse_ref, x_ref, mod_ref, w_ref = refs[:6]
    grads, refs = refs[6 : 6 + flow_count], refs[6 + flow_count :]
    dqkv_ref, dv_ref, sum_ref = refs[:3]
    outs, refs = refs[3 : 3 + flow_count], refs[3 + flow_count :]
    e_ref, hold, send_sem, recv_sem, own_sem = refs[:5]
    own, n_pos = hold.shape[:2]
    frame = pl.program_id(0)
    spread = Spread(n_pos, frame, own, hold, dv_ref, send_sem, recv_sem, own_sem)
    flows = make_flows(n_pos, n_clip, kinds, grads, outs, refs[5:])
    stages = max(len(flow.stages) for flow in flows)
    order = [(i, stage) for stage in range(stages) for i in range(flow_count)]
    order = [(i, stage) for i, stage in order if stage < len(flows[i].stages)]
    cuts = [2, flow_count, flow_count + 2]

    @pl.when(frame == 0)
    def _():
        place = here()
        others = [("clip", bit) for bit in bits_of(n_clip)]
        barrier = pltpu.get_barrier_semaphore()
        for axis, bit in others:
            signal_swap(barrier, place, axis, bit)
        spread.greet(len(others))
        for flow in flows:
            flow.start()

    def advance(first, last):
        for i, stage in order[first:last]:
            flows[i].take(stage)

    patches = qkv_ref.shape[1]
    width = x_ref.shape[3]
    places = x_ref.shape[2]
    pair = 2 * HEAD_DIM
    scale = mod_ref[0, 1:2, :]
    factor = 1.0 / math.sqrt(HEAD_DIM)
    masks_q = pair_masks(factor)
    masks = pair_masks(1.0)
    lane_ids = lax.broadcasted_iota(jnp.int32, (1, pair), 1)

    def head_pair(index, _):
        at = pl.multiple_of(index * pair, pair)
        k_at = pl.multiple_of(width + at, pair)
        v_at = pl.multiple_of(2 * width + at, pair)
        q = qkv_ref[0, :, pl.ds(at, pair)]
        k = qkv_ref[0, :, pl.ds(k_at, pair)]
        v = qkv_ref[0, :, pl.ds(v_at, pair)]
        go = go_ref[:, 0, :, pl.ds(at, pair)].astype(f32).reshape(patches, pair).astype(bf16)
        lse_all = lse_ref[0]
        gq, gk, gv = None, None, None
        for half in range(2):
            lse = jnp.sum(
                jnp.where(lane_ids == 2 * index + half, lse_all, 0.0), axis=-1, keepdims=True
            )
            q_half = q * masks_q[half]
            go_half = go * masks[half]
            probs = jnp.exp(bdot_nt(q_half, k) - lse)
            grad_p = bdot_nt(go_half, v)
            inner = jnp.sum(grad_p * probs, axis=-1, keepdims=True)
            grad_s = (probs * (grad_p - inner)).astype(bf16)
            part_q = bdot(grad_s, k * masks_q[half])
            part_k = bdot_tn(grad_s, q_half)
            part_v = bdot_tn(probs.astype(bf16), go_half)
            gq = part_q if gq is None else gq + part_q
            gk = part_k if gk is None else gk + part_k
            gv = part_v if gv is None else gv + part_v
        dqkv_ref[0, :, pl.ds(at, pair)] = gq.astype(bf16)
        dqkv_ref[0, :, pl.ds(k_at, pair)] = gk.astype(bf16)
        dqkv_ref[0, :, pl.ds(v_at, pair)] = gv.astype(bf16)
        return 0

    lax.fori_loop(0, HEADS // 2, head_pair, 0)
    e_ref[...] = bdot_nt(dqkv_ref[0], w_ref[...])

    def norm_step(step, sums):
        grad = e_ref[pl.ds(step * ROWS, ROWS), :]
        normed, inverse = norm_rows(load_rows(x_ref, step))
        back = norm_rows_back(normed, inverse, scale, grad)
        count = max(1, ROWS // places)
        back = back.reshape(count, places, width).astype(bf16)
        hold[frame, pl.ds(step * count, count)] = back
        folded = grad.reshape(ROWS // 8, 8, width).sum(axis=0)
        folded_n = (grad * normed).reshape(ROWS // 8, 8, width).sum(axis=0)
        return sums[0] + folded, sums[1] + folded_n

    zero = jnp.zeros((8, width), f32)
    shift_sum, scale_sum = lax.fori_loop(0, patches // ROWS, norm_step, (zero, zero))
    spread.send()
    sum_ref[0, 0:1, :] = jnp.sum(shift_sum, axis=0, keepdims=True)
    sum_ref[0, 1:2, :] = jnp.sum(scale_sum, axis=0, keepdims=True)
    done = 0
    for index, cut in enumerate(cuts[: own - 1]):
        pl.when(frame == index)(partial(advance, done, cut))
        done = cut

    @pl.when(frame == own - 1)
    def _():
        advance(done, len(order))
        spread.finish()
        for flow in flows:
            flow.finish()


GELU_C = math.sqrt(2.0 / math.pi)


def middle(
    o1_ref, x_ref, g_ref, mod_ref, clip_ref, wso_ref, wti_ref, wto_ref, wup_ref, wdn_ref,
    out_ref, act_ref, dz_ref, h3_ref, du_ref, o2_ref, dy2_ref, h2_ref, dqkv_ref, dy1_ref, do1_ref,
    dx1_ref, sum_ref,
    qkv_ref, p_ref, y1_ref, y2_ref, n2_ref, n3_ref, r2_ref, r3_ref, xa_ref, gp_ref, e_ref,
):
    count, frames, width = x_ref.shape
    rows = count * frames
    pair = 2 * HEAD_DIM
    hidden = act_ref.shape[1]
    factor = 1.0 / math.sqrt(HEAD_DIM)
    per = frames // ROWS
    steps = rows // ROWS

    @pl.when(pl.program_id(0) == 0)
    def _():
        sum_ref[...] = jnp.zeros_like(sum_ref)

    def at_rows(step):
        return step // per, pl.ds(lax.rem(step, per) * ROWS, ROWS), pl.ds(step * ROWS, ROWS)

    def mod(index, part):
        return mod_ref[index, part, :]

    y1_ref[...] = bdot(o1_ref[...].reshape(rows, width), wso_ref[...])

    def step_one(step, _):
        place, part, flat = at_rows(step)
        x_one = x_ref[place, part, :].astype(f32) + mod(2, part) * y1_ref[flat, :]
        xa_ref[flat, :] = x_one
        normed, inverse = norm_rows(x_one)
        n2_ref[flat, :] = normed
        r2_ref[flat, :] = jnp.broadcast_to(inverse, (ROWS, pair))
        h2_ref[flat, :] = (normed * (1.0 + mod(4, part)) + mod(3, part)).astype(bf16)
        return 0

    lax.fori_loop(0, steps, step_one, 0)
    for third in range(3):
        cols = slice(third * width, (third + 1) * width)
        qkv_ref[:, cols] = bdot(h2_ref[...], wti_ref[:, cols]).astype(bf16)

    masks = pair_masks(1.0)
    masks_q = pair_masks(factor)
    lane_ids = lax.broadcasted_iota(jnp.int32, (1, pair), 1)
    is_low = lane_ids < HEAD_DIM
    allowed = clip_ref[...] > 0.5

    def halves(values, reduce, neutral):
        low_part = reduce(jnp.where(is_low, values, neutral), axis=-1, keepdims=True)
        high_part = reduce(jnp.where(is_low, neutral, values), axis=-1, keepdims=True)
        return jnp.where(is_low, low_part, high_part)

    def stacked(values, pair_of_masks):
        return jnp.concatenate([values * pair_of_masks[0], values * pair_of_masks[1]], axis=0)

    def pair_at(index):
        at = pl.multiple_of(index * pair, pair)
        return (
            pl.ds(at, pair),
            pl.ds(pl.multiple_of(width + at, pair), pair),
            pl.ds(pl.multiple_of(2 * width + at, pair), pair),
        )

    parts = [slice(place * frames, (place + 1) * frames) for place in range(count)]
    same_half = (
        lax.broadcasted_iota(jnp.int32, (pair, pair), 0) // HEAD_DIM
        == lax.broadcasted_iota(jnp.int32, (pair, pair), 1) // HEAD_DIM
    )
    ones = jnp.where(same_half, 1.0, 0.0).astype(bf16)

    def half_sums(values):
        high = values.astype(bf16)
        low = (values - high.astype(f32)).astype(bf16)
        return bdot(high, ones) + bdot(low, ones)

    def time_pair(index, _):
        jobs = [(2 * index + i, part) + pair_at(2 * index + i) for i in range(2) for part in parts]
        keys = [stacked(qkv_ref[part, k_at], masks_q) for _i, part, q_at, k_at, v_at in jobs]
        scores = [bdot_nt(qkv_ref[job[1], job[2]], key) for job, key in zip(jobs, keys)]
        scores = [jnp.where(allowed, score, masked_score) for score in scores]
        tops = [halves(score, jnp.max, -jnp.inf) for score in scores]
        exps = [jnp.exp(score - top) for score, top in zip(scores, tops)]
        sums = [half_sums(exp) for exp in exps]
        probs = [exp / total for exp, total in zip(exps, sums)]
        values = [stacked(qkv_ref[job[1], job[4]], masks) for job in jobs]
        outs = [bdot(prob.astype(bf16), value) for prob, value in zip(probs, values)]
        for (i, part, q_at, _k, _v), prob, out in zip(jobs, probs, outs):
            p_ref[i, part, :] = prob
            o2_ref[part, q_at] = out.astype(bf16)
        return 0

    lax.fori_loop(0, HEADS // 4, time_pair, 0)

    y2_ref[...] = bdot(o2_ref[...], wto_ref[...])

    def step_two(step, _):
        place, part, flat = at_rows(step)
        x_two = xa_ref[flat, :] + mod(5, part) * y2_ref[flat, :]
        xa_ref[flat, :] = x_two
        normed, inverse = norm_rows(x_two)
        n3_ref[flat, :] = normed
        r3_ref[flat, :] = jnp.broadcast_to(inverse, (ROWS, pair))
        h3_ref[flat, :] = (normed * (1.0 + mod(7, part)) + mod(6, part)).astype(bf16)
        dz_ref[flat, :] = (mod(8, part) * g_ref[place, part, :].astype(f32)).astype(bf16)
        return 0

    lax.fori_loop(0, steps, step_two, 0)

    tile = 256

    def up_tile(index, _):
        cols = pl.ds(pl.multiple_of(index * tile, tile), tile)
        u = bdot(h3_ref[...], wup_ref[:, cols])
        square = u * u
        tanh = jnp.tanh(GELU_C * (u * (1.0 + 0.044715 * square)))
        half = 0.5 * (1.0 + tanh)
        act_ref[:, cols] = (u * half).astype(bf16)
        slope = half + (0.5 * GELU_C) * u * (1.0 - tanh * tanh) * (1.0 + (3.0 * 0.044715) * square)
        du = bdot_nt(dz_ref[...], wdn_ref[cols, :]) * slope
        du_ref[:, cols] = du.astype(bf16)
        return 0

    lax.fori_loop(0, hidden // tile, up_tile, 0)
    e_ref[...] = bdot(act_ref[...], wdn_ref[...])

    def step_three(step, _):
        place, part, flat = at_rows(step)
        z = e_ref[flat, :]
        grad = g_ref[place, part, :].astype(f32)
        out_ref[place, part, :] = (xa_ref[flat, :] + mod(8, part) * z).astype(bf16)
        sum_ref[6, part, :] += grad * z
        return 0

    lax.fori_loop(0, steps, step_three, 0)
    e_ref[...] = bdot_nt(du_ref[...], wup_ref[...])

    def step_four(step, _):
        place, part, flat = at_rows(step)
        grad = e_ref[flat, :]
        normed = n3_ref[flat, :]
        sum_ref[4, part, :] += grad
        sum_ref[5, part, :] += grad * normed
        back = norm_rows_back(normed, r3_ref[flat, 0:1], mod(7, part), grad)
        grad_two = g_ref[place, part, :].astype(f32) + back
        xa_ref[flat, :] = grad_two
        sum_ref[3, part, :] += grad_two * y2_ref[flat, :]
        dy2_ref[flat, :] = (mod(5, part) * grad_two).astype(bf16)
        return 0

    lax.fori_loop(0, steps, step_four, 0)
    y2_ref[...] = bdot_nt(dy2_ref[...], wto_ref[...])

    def time_pair_back(index, _):
        q_at, k_at, v_at = pair_at(index)
        gos = [y2_ref[part, q_at].astype(bf16) for part in parts]
        values = [stacked(qkv_ref[part, v_at], masks) for part in parts]
        grads = [bdot_nt(go, value) for go, value in zip(gos, values)]
        probs = [p_ref[index, part, :] for part in parts]
        inner = [half_sums(grad * prob) for grad, prob in zip(grads, probs)]
        scores = [
            (prob * (grad - mean)).astype(bf16) for prob, grad, mean in zip(probs, grads, inner)
        ]
        keys = [stacked(qkv_ref[part, k_at], masks_q) for part in parts]
        qs = [qkv_ref[part, q_at] * factor for part in parts]
        grad_q = [bdot(score, key) for score, key in zip(scores, keys)]
        grad_k = [bdot_tn(score, q) for score, q in zip(scores, qs)]
        grad_v = [bdot_tn(prob.astype(bf16), go) for prob, go in zip(probs, gos)]
        for part, g_q, g_k, g_v in zip(parts, grad_q, grad_k, grad_v):
            dqkv_ref[part, q_at] = g_q.astype(bf16)
            dqkv_ref[part, k_at] = jnp.where(is_low, g_k[:frames], g_k[frames:]).astype(bf16)
            dqkv_ref[part, v_at] = jnp.where(is_low, g_v[:frames], g_v[frames:]).astype(bf16)
        return 0

    lax.fori_loop(0, HEADS // 2, time_pair_back, 0)
    e_ref[...] = bdot_nt(dqkv_ref[...], wti_ref[...])

    def step_five(step, _):
        place, part, flat = at_rows(step)
        grad = e_ref[flat, :]
        normed = n2_ref[flat, :]
        sum_ref[1, part, :] += grad
        sum_ref[2, part, :] += grad * normed
        grad_one = xa_ref[flat, :] + norm_rows_back(normed, r2_ref[flat, 0:1], mod(4, part), grad)
        dx1_ref[place, part, :] = grad_one
        sum_ref[0, part, :] += grad_one * y1_ref[flat, :]
        dy1_ref[flat, :] = (mod(2, part) * grad_one).astype(bf16)
        return 0

    lax.fori_loop(0, steps, step_five, 0)
    do1_ref[...] = bdot_nt(dy1_ref[...], wso_ref[...]).astype(bf16).reshape(count, frames, width)


VMEM_LIMIT = 62 * 1024 * 1024


def resident(shape):
    return pl.BlockSpec(shape, lambda i: (0,) * len(shape), pipeline_mode=pl.Buffered(1))


def call_space_forward(x, mods, weight):
    n_pos, own, places, width = x.shape
    patches = n_pos * places
    pair = 2 * HEAD_DIM
    spread = pl.BlockSpec((n_pos, 1, places, width), lambda i: (0, i, 0, 0))

    def by_frame(*shape):
        return pl.BlockSpec((1,) + shape, lambda i: (i, 0, 0))

    rows = own * patches
    return pl.pallas_call(
        space_forward,
        grid=(own,),
        in_specs=[spread, by_frame(2, width), resident(weight.shape)],
        out_specs=[
            by_frame(patches, width),
            by_frame(patches, 3 * width),
            pl.BlockSpec(memory_space=pl.ANY),
            by_frame(patches, pair),
        ],
        out_shape=[
            jax.ShapeDtypeStruct((own, patches, width), bf16),
            jax.ShapeDtypeStruct((own, patches, 3 * width), bf16),
            jax.ShapeDtypeStruct((n_pos * own, places, width), bf16),
            jax.ShapeDtypeStruct((own, patches, pair), f32),
        ],
        scratch_shapes=spread_scratch(own, n_pos, places, width),
        compiler_params=pltpu.CompilerParams(
            vmem_limit_bytes=VMEM_LIMIT, collective_id=0, has_side_effects=True
        ),
        cost_estimate=pl.CostEstimate(
            flops=2 * rows * width * 3 * width + 4 * rows * patches * width,
            bytes_accessed=rows * width * 12 + weight.size * 2,
            transcendentals=rows * patches * HEADS,
        ),
        name="space_forward",
    )(x, mods, weight)


def call_space_backward(go, qkv, lse, x, mods, weight, grads, kinds, n_clip):
    n_pos, own, places, width = x.shape
    patches = n_pos * places
    pair = 2 * HEAD_DIM
    spread = pl.BlockSpec((n_pos, 1, places, width), lambda i: (0, i, 0, 0))
    anywhere = pl.BlockSpec(memory_space=pl.ANY)

    def by_frame(*shape):
        return pl.BlockSpec((1,) + shape, lambda i: (i, 0, 0))

    rows = own * patches
    views, flow_outs, flow_scratch = flow_plan(grads, kinds, n_pos, n_clip)
    sizes = sum(grad.size for grad in grads)
    return pl.pallas_call(
        partial(space_backward, n_clip, kinds),
        grid=(own,),
        in_specs=[
            spread,
            by_frame(patches, 3 * width),
            by_frame(patches, pair),
            spread,
            by_frame(2, width),
            resident(weight.shape),
        ]
        + [anywhere] * len(grads),
        out_specs=[by_frame(patches, 3 * width), anywhere, by_frame(2, width)]
        + [resident(out.shape) for out in flow_outs],
        out_shape=[
            jax.ShapeDtypeStruct((own, patches, 3 * width), bf16),
            jax.ShapeDtypeStruct((n_pos * own, places, width), bf16),
            jax.ShapeDtypeStruct((own, 2, width), f32),
        ]
        + flow_outs,
        scratch_shapes=[pltpu.VMEM((patches, width), f32)]
        + spread_scratch(own, n_pos, places, width)
        + flow_scratch,
        compiler_params=pltpu.CompilerParams(
            vmem_limit_bytes=VMEM_LIMIT, collective_id=1, has_side_effects=True
        ),
        cost_estimate=pl.CostEstimate(
            flops=2 * rows * width * 3 * width + 10 * rows * patches * width,
            bytes_accessed=rows * width * 16 + weight.size * 2 + sizes * 4,
            transcendentals=rows * patches * HEADS,
        ),
        name="space_backward",
    )(go, qkv, lse, x, mods, weight, *views)


def call_middle(o_one, x, grad, mods, same_clip, wso, wti, wto, wup, wdn):
    places, frames, width = x.shape
    count = max(1, min(places, 256 // frames))
    rows = count * frames
    hidden = wup.shape[1]
    pair = 2 * HEAD_DIM
    total = places * frames
    chunk = pl.BlockSpec((count, frames, width), lambda i: (i, 0, 0))

    def flat(cols):
        return pl.BlockSpec((rows, cols), lambda i: (i, 0))

    def flat_shape(cols):
        return jax.ShapeDtypeStruct((total, cols), bf16)

    def scratch(cols, dtype=f32):
        return pltpu.VMEM((rows, cols), dtype)

    lanes = jnp.concatenate([same_clip, same_clip], axis=1)
    flops = 2 * total * (2 * (wso.size + wti.size + wto.size + wup.size + wdn.size))
    return pl.pallas_call(
        middle,
        grid=(places // count,),
        in_specs=[chunk, chunk, chunk, resident(mods.shape), resident(lanes.shape)]
        + [resident(w.shape) for w in (wso, wti, wto, wup, wdn)],
        out_specs=[
            chunk,
            flat(hidden),
            flat(width),
            flat(width),
            flat(hidden),
            flat(width),
            flat(width),
            flat(width),
            flat(3 * width),
            flat(width),
            chunk,
            chunk,
            pl.BlockSpec((7, frames, width), lambda i: (0, 0, 0)),
        ],
        out_shape=[
            jax.ShapeDtypeStruct(x.shape, bf16),
            flat_shape(hidden),
            flat_shape(width),
            flat_shape(width),
            flat_shape(hidden),
            flat_shape(width),
            flat_shape(width),
            flat_shape(width),
            flat_shape(3 * width),
            flat_shape(width),
            jax.ShapeDtypeStruct(x.shape, bf16),
            jax.ShapeDtypeStruct(x.shape, f32),
            jax.ShapeDtypeStruct((7, frames, width), f32),
        ],
        scratch_shapes=[
            scratch(3 * width, bf16),
            pltpu.VMEM((HEADS // 2, rows, pair), f32),
            scratch(width),
            scratch(width),
            scratch(width),
            scratch(width),
            scratch(pair),
            scratch(pair),
            scratch(width),
            pltpu.VMEM((8, pair), f32),
            scratch(width),
        ],
        compiler_params=pltpu.CompilerParams(vmem_limit_bytes=VMEM_LIMIT),
        cost_estimate=pl.CostEstimate(
            flops=flops, bytes_accessed=total * 40000, transcendentals=total * hidden
        ),
        name="middle",
    )(o_one, x, grad, mods, lanes, wso, wti, wto, wup, wdn)


def combine(n_pos, n_clip, kinds, *refs):
    count = len(kinds)
    grads, small = refs[:count], refs[count]
    outs, small_out = refs[count + 1 : 2 * count + 1], refs[2 * count + 1]
    small_sems, got, acc = refs[2 * count + 2 : 2 * count + 4], refs[2 * count + 4], refs[2 * count + 5]
    place = here()
    partners = partner_list(n_pos, n_clip)
    barrier = pltpu.get_barrier_semaphore()
    for axis, bit in partners:
        signal_swap(barrier, place, axis, bit)
    pl.semaphore_wait(barrier, len(partners))
    flows = make_flows(n_pos, n_clip, kinds, grads, outs, refs[2 * count + 6 :])
    tree = Butterfly(n_pos, n_clip, small, small_out, got, acc, small_sems, place)
    tree.start()
    for flow in flows:
        flow.start()
    for stage in range(max(tree.count, max(len(flow.stages) for flow in flows))):
        if stage < tree.count:
            tree.take(stage)
        for flow in flows:
            if stage < len(flow.stages):
                flow.take(stage)
    tree.finish()
    for flow in flows:
        flow.finish()


def call_combine(grads, kinds, small, n_pos, n_clip):
    lead = n_pos.bit_length() - 1
    most = lead + len(bits_of(n_clip))
    views, out_shape, scratch = flow_plan(grads, kinds, n_pos, n_clip)
    clips, wide = small.shape
    out_shape.append(jax.ShapeDtypeStruct((n_clip, clips, wide), f32))
    dma = pltpu.SemaphoreType.DMA
    whole = pl.BlockSpec(memory_space=pltpu.VMEM)
    sizes = sum(grad.size for grad in grads)
    return pl.pallas_call(
        partial(combine, n_pos, n_clip, kinds),
        in_specs=[pl.BlockSpec(memory_space=pl.ANY)] * len(grads) + [whole],
        out_specs=[whole] * len(out_shape),
        out_shape=out_shape,
        scratch_shapes=[
            dma((most,)),
            dma((most,)),
            pltpu.VMEM((lead, clips, wide), f32),
            pltpu.VMEM((lead, clips, wide), f32),
        ]
        + scratch,
        compiler_params=pltpu.CompilerParams(
            vmem_limit_bytes=VMEM_LIMIT, collective_id=2, has_side_effects=True
        ),
        cost_estimate=pl.CostEstimate(flops=sizes, bytes_accessed=sizes * 4, transcendentals=0),
        name="combine",
    )(*views, small)


def on_device(
    tokens,
    clip_lengths,
    timesteps,
    embed_first,
    embed_second,
    adaln_weight,
    spatial_in,
    spatial_out,
    temporal_in,
    temporal_out,
    hidden_up,
    hidden_down,
    grad_output,
    n_pos=16,
    n_clip=2,
):
    frames, places, width = tokens.shape
    rows = frames * places
    own = frames // n_pos
    patches = places * n_pos
    me = lax.axis_index("pos")
    clips = clip_lengths.shape[1]

    def exchange(values):
        sent = values.reshape(frames, places, width)
        got = lax.all_to_all(sent, "pos", split_axis=0, concat_axis=0, tiled=True)
        return got.reshape(n_pos, own, places, width)

    x_space = exchange(tokens)

    all_steps = by_distance(timesteps[0], "clip", n_clip)
    freq = frequency(all_steps)
    pre_cond = dot_exact(freq, embed_first)
    hidden_cond = jax.nn.silu(pre_cond)
    cond = dot_exact(hidden_cond, embed_second)
    cond_act = jax.nn.silu(cond)
    modulated = dot_exact(cond_act[:clips], adaln_weight)
    onehot, clip_ids = clip_onehot(clip_lengths[0], frames)
    per_frame = dot_high(onehot, modulated)
    own_frames = lax.dynamic_slice_in_dim(per_frame, me * own, own, 0)

    own_mods = own_frames[:, : 2 * width].reshape(own, 2, width)
    h_one, qkv_one, o_one, lse_one = call_space_forward(x_space, own_mods, spatial_in)

    def turn(values):
        return values.transpose(1, 0, 2)

    o_one = turn(o_one)
    mods = per_frame.reshape(frames, 9, width).transpose(1, 0, 2)
    same_clip = jnp.dot(onehot, onehot.T)
    (block_turned, act, grad_z, h_three, grad_u, o_two, grad_y_two, h_two, grad_qkv_two, grad_y_one, grad_o_one,
     grad_one, sums) = call_middle(
        o_one, turn(tokens), turn(grad_output), mods, same_clip, spatial_out, temporal_in, temporal_out,
        hidden_up, hidden_down,
    )
    block_out = turn(block_turned)
    grad_o_space = exchange(turn(grad_o_one))
    early = (
        weight_grad(h_three, grad_u),
        weight_grad(act, grad_z),
        weight_grad(h_two, grad_qkv_two),
        weight_grad(o_one.reshape(rows, width), grad_y_one),
        weight_grad(o_two, grad_y_two),
    )
    (
        grad_qkv_one, back_places, sums_one,
        g_hidden_up, g_hidden_down, g_temporal_in, g_spatial_out, g_temporal_out,
    ) = call_space_backward(
        grad_o_space, qkv_one, lse_one, x_space, own_mods, spatial_in,
        early, (False, True, False, True, True), n_clip,
    )
    grad_tokens = (turn(grad_one) + back_places.astype(f32)).astype(bf16)

    h_flat = h_one.reshape(own * patches, width)
    grad_flat = grad_qkv_one.reshape(own * patches, 3 * width)
    cut = grad_flat.shape[1] // 512 * 256
    own_hot = lax.dynamic_slice_in_dim(onehot, me * own, own, 0)
    dmod_first = dot_high(own_hot.T, sums_one.reshape(own, 2 * width))
    dmod_rest = dot_high(onehot.T, sums.transpose(1, 0, 2).reshape(frames, 7 * width))
    dmod_local = jnp.concatenate([dmod_first, dmod_rest], axis=1)
    late = (weight_grad(h_flat, grad_flat[:, :cut]), weight_grad(h_flat, grad_flat[:, cut:]))
    in_low, in_high, dmod = call_combine(late, (True, False), dmod_local, n_pos, n_clip)
    g_spatial_in = jnp.concatenate([in_low, in_high], axis=1)
    dmod = dmod.reshape(n_clip * clips, 9 * width)

    def own_columns(values):
        block = values.shape[1] // n_pos
        return lax.dynamic_slice_in_dim(values, me * block, block, 1)

    g_adaln = dot_high(own_columns(cond_act).T, dmod)
    grad_cond = dot_exact(dmod, adaln_weight.T) * silu_grad(cond)
    g_second = dot_high(own_columns(hidden_cond).T, grad_cond)
    grad_pre = dot_exact(grad_cond, embed_second.T) * silu_grad(pre_cond)
    g_first = dot_high(own_columns(freq).T, grad_pre)
    return (
        block_out,
        grad_tokens,
        g_first,
        g_second,
        g_adaln,
        g_spatial_in,
        g_spatial_out,
        g_temporal_in,
        g_temporal_out,
        g_hidden_up,
        g_hidden_down,
    )


def solution(mesh):
    in_specs = (
        P("clip", "pos", None),
        P("clip", None),
        P("clip", None),
        P(),
        P(),
        P(),
        P(),
        P(),
        P(),
        P(),
        P(),
        P(),
        P("clip", "pos", None),
    )
    out_specs = (P("clip", "pos", None),) * 2 + (P("pos", None),) * 9
    body = partial(on_device, n_pos=mesh.shape["pos"], n_clip=mesh.shape["clip"])
    return jax.shard_map(body, mesh=mesh, in_specs=in_specs, out_specs=out_specs, check_vma=False)
```

```python
from functools import partial
import math

import jax
import jax.numpy as jnp
from jax import lax
from jax.experimental import pallas as pl
from jax.experimental.pallas import tpu as pltpu
from jax.sharding import PartitionSpec as P

HEADS = 12
HEAD_DIM = 64
FREQ = 256

epsilon = 1e-06
highest = lax.Precision.HIGHEST
masked_score = -1000000000.0
f32 = jnp.float32
bf16 = jnp.bfloat16


def frequency(step_ids):
    half_width = FREQ // 2
    rate_table = jnp.exp(
        -math.log(10000.0) * jnp.arange(half_width, dtype=jnp.float32) / half_width
    )
    angles = step_ids.astype(jnp.float32)[:, None] * rate_table[None, :]
    return jnp.concatenate([jnp.cos(angles), jnp.sin(angles)], axis=1)


def dot_high(left, right):
    return jnp.dot(left, right, precision=highest, preferred_element_type=f32)


def silu_grad(values):
    gate = jax.nn.sigmoid(values)
    return gate * (1.0 + values * (1.0 - gate))


def clip_onehot(lengths, frames):
    clip_ends = jnp.cumsum(lengths)
    frame_ids = jnp.arange(frames, dtype=jnp.int32)
    clip_ids = jnp.sum((frame_ids[:, None] >= clip_ends[None, :]).astype(jnp.int32), axis=1)
    onehot = (clip_ids[:, None] == jnp.arange(lengths.shape[0], dtype=jnp.int32)[None, :]).astype(
        jnp.float32
    )
    return (onehot, clip_ids)


def weight_grad(left, right):
    return jnp.einsum("rd,rk->dk", left, right, preferred_element_type=f32).astype(bf16)


def bdot(left, right):
    return lax.dot_general(left, right, (((1,), (0,)), ((), ())), preferred_element_type=f32)


def bdot_nt(left, right):
    return lax.dot_general(left, right, (((1,), (1,)), ((), ())), preferred_element_type=f32)


def bdot_tn(left, right):
    return lax.dot_general(left, right, (((0,), (0,)), ((), ())), preferred_element_type=f32)


def norm_rows(values):
    width = values.shape[-1]
    centre = values - jnp.sum(values, axis=-1, keepdims=True) * (1.0 / width)
    spread = jnp.sum(centre * centre, axis=-1, keepdims=True) * (1.0 / width)
    inverse = lax.rsqrt(spread + epsilon)
    return centre * inverse, inverse


def norm_rows_back(normed, inverse, scale_vec, grad):
    width = grad.shape[-1]
    inner = grad * (1.0 + scale_vec)
    mean_one = jnp.sum(inner, axis=-1, keepdims=True) * (1.0 / width)
    mean_two = jnp.sum(inner * normed, axis=-1, keepdims=True) * (1.0 / width)
    return inverse * (inner - mean_one - normed * mean_two)


def pair_masks(scale):
    lanes = lax.broadcasted_iota(jnp.int32, (1, 2 * HEAD_DIM), 1)
    low_half = jnp.where(lanes < HEAD_DIM, scale, 0.0).astype(bf16)
    high_half = jnp.where(lanes < HEAD_DIM, 0.0, scale).astype(bf16)
    return low_half, high_half


ROWS = 32


def load_rows(ref, step):
    places, width = ref.shape[2:]
    count = max(1, ROWS // places)
    part = ref[pl.ds(step * count, count), 0].astype(f32)
    return part.reshape(count * places, width)


def swap(values, axis, size, bit):
    return lax.ppermute(values, axis, [(i, i ^ bit) for i in range(size)])


def bits_of(size):
    return [1 << i for i in range(size.bit_length() - 1)]


def by_distance(values, axis, size):
    for bit in bits_of(size):
        values = jnp.concatenate([values, swap(values, axis, size, bit)], axis=0)
    return values


def dot_exact(left, right):
    parts = []
    for _ in range(3):
        part = left.astype(bf16)
        parts.append(part)
        left = left - part.astype(f32)
    count = parts[0].shape[0]
    got = jnp.dot(jnp.concatenate(parts, axis=0), right, preferred_element_type=f32)
    return got[:count] + (got[count : 2 * count] + got[2 * count :])


def flow_stages(n_pos, n_clip, clip_first):
    pos = [("pos", bit, "halve") for bit in bits_of(n_pos)]
    clip = bits_of(n_clip)
    if not clip_first:
        return pos + [("clip", bit, "sum") for bit in clip]
    first = [("clip", clip[0], "columns")]
    last = [("clip", clip[0], "gather")]
    return pos[:1] + first + pos[1:] + [("clip", bit, "sum") for bit in clip[1:]] + last


def flow_shapes(stages, n_pos, block, cols):
    lead = n_pos.bit_length() - 1
    shapes = []
    for _, _, what in stages:
        if what == "halve":
            lead -= 1
        elif what == "columns":
            cols //= 2
        shapes.append((2,) * lead + (block, cols))
    return shapes


class Flow:
    def __init__(self, number, stages, grad, out, keep, gots, sems, place):
        self.number, self.stages = number, stages
        self.grad, self.out, self.keep, self.gots = grad, out, keep, gots
        self.send_sem, self.recv_sem, self.keep_sem = sems
        self.place = place

    def side(self, stage):
        axis, bit, _ = self.stages[stage]
        return lax.rem(self.place[axis] // bit, 2)

    def columns(self, side, width):
        return pl.ds(pl.multiple_of(side * width, width), width)

    def part(self, ref, stage, side):
        what = self.stages[stage][2]
        lead = len(ref.shape) - 2
        if what == "halve":
            return (slice(None),) * (lead - 1) + (side,)
        if what == "columns":
            half = ref.shape[-1] // 2
            return (slice(None),) * (lead + 1) + (self.columns(side, half),)
        return None

    def held(self, stage):
        if stage == 0:
            return self.grad
        return self.keep if stage == 1 else self.gots[stage - 1]

    def copy(self, stage):
        axis, bit, _ = self.stages[stage]
        side = self.side(stage)
        source = self.held(stage)
        at = self.part(source, stage, 1 - side)
        return pltpu.make_async_remote_copy(
            source if at is None else source.at[at],
            self.gots[stage],
            self.send_sem.at[self.number, stage],
            self.recv_sem.at[self.number, stage],
            device_id={axis: self.place[axis] + bit * (1 - 2 * side)},
            device_id_type=pl.DeviceIdType.MESH,
        )

    def own(self):
        at = self.part(self.grad, 0, self.side(0))
        return pltpu.make_async_copy(self.grad.at[at], self.keep, self.keep_sem.at[self.number])

    def start(self):
        self.copy(0).start()
        self.own().start()

    def take(self, stage):
        self.copy(stage).wait_recv()
        if stage == 0:
            self.own().wait()
        what = self.stages[stage][2]
        got = self.gots[stage]
        side = self.side(stage)
        last = stage == len(self.stages) - 1
        lead = len(got.shape) - 2
        if what == "gather":
            half = got.shape[-1]
            self.out[:, self.columns(side, half)] = self.held(stage)[...].astype(f32)
            self.out[:, self.columns(1 - side, half)] = got[...].astype(f32)
            return
        if last:
            self.out[...] = self.held(stage)[...].astype(f32) + got[...].astype(f32)
            return
        target = self.keep if stage == 0 else got

        def one(index, _):
            at = tuple(lax.rem(index // (1 << i), 2) for i in range(lead))
            if stage == 0:
                mine = self.keep[at]
            elif what == "halve":
                mine = self.held(stage)[at + (side,)]
            elif what == "columns":
                mine = self.held(stage)[at + (slice(None), self.columns(side, got.shape[-1]))]
            else:
                mine = self.held(stage)[at]
            target[at] = mine + got[at]
            return 0

        lax.fori_loop(0, 1 << lead, one, 0)
        self.copy(stage + 1).start()

    def finish(self):
        for stage in range(len(self.stages)):
            self.copy(stage).wait_send()


class Butterfly:
    def __init__(self, n_pos, n_clip, values, out, got, acc, sems, place):
        self.pos_bits, self.clip_bits = bits_of(n_pos), bits_of(n_clip)
        self.values, self.out, self.got, self.acc = values, out, got, acc
        self.send_sem, self.recv_sem = sems
        self.place = place
        self.count = len(self.pos_bits) + len(self.clip_bits)

    def copy(self, stage):
        if stage < len(self.pos_bits):
            axis, bit = "pos", self.pos_bits[stage]
            source = self.values if stage == 0 else self.acc.at[stage - 1]
            target = self.got.at[stage]
        else:
            axis, bit = "clip", self.clip_bits[stage - len(self.pos_bits)]
            source, target = self.out.at[pl.ds(0, bit)], self.out.at[pl.ds(bit, bit)]
        side = lax.rem(self.place[axis] // bit, 2)
        return pltpu.make_async_remote_copy(
            source,
            target,
            self.send_sem.at[stage],
            self.recv_sem.at[stage],
            device_id={axis: self.place[axis] + bit * (1 - 2 * side)},
            device_id_type=pl.DeviceIdType.MESH,
        )

    def start(self):
        self.copy(0).start()

    def take(self, stage):
        self.copy(stage).wait_recv()
        last = len(self.pos_bits) - 1
        if stage <= last:
            mine = self.values[...] if stage == 0 else self.acc[stage - 1]
            if stage < last:
                self.acc[stage] = mine + self.got[stage]
            else:
                self.out[0] = mine + self.got[stage]
        if stage + 1 < self.count:
            self.copy(stage + 1).start()

    def finish(self):
        for stage in range(self.count):
            self.copy(stage).wait_send()


def partner_list(n_pos, n_clip):
    return [("pos", bit) for bit in bits_of(n_pos)] + [("clip", bit) for bit in bits_of(n_clip)]


def here():
    return {"pos": lax.axis_index("pos"), "clip": lax.axis_index("clip")}


def signal_swap(barrier, place, axis, bit):
    side = lax.rem(place[axis] // bit, 2)
    pl.semaphore_signal(
        barrier,
        inc=1,
        device_id={axis: place[axis] + bit * (1 - 2 * side)},
        device_id_type=pl.DeviceIdType.MESH,
    )


def make_flows(n_pos, n_clip, kinds, grads, outs, scratch):
    sems, rest = scratch[:3], list(scratch[3:])
    flows = []
    for number, clip_first in enumerate(kinds):
        stages = flow_stages(n_pos, n_clip, clip_first)
        keep, gots = rest[0], rest[1 : 1 + len(stages)]
        rest = rest[1 + len(stages) :]
        flows.append(Flow(number, stages, grads[number], outs[number], keep, gots, sems, here()))
    return flows


def flow_plan(grads, kinds, n_pos, n_clip):
    lead = n_pos.bit_length() - 1
    most = lead + len(bits_of(n_clip)) + 1
    dma = pltpu.SemaphoreType.DMA
    scratch = [dma((len(grads), most)), dma((len(grads), most)), dma((len(grads),))]
    views, out_shape = [], []
    for grad, clip_first in zip(grads, kinds):
        rows, cols = grad.shape
        block = rows // n_pos
        if isinstance(grad, jax.ShapeDtypeStruct):
            views.append(pltpu.VMEM((2,) * lead + (block, cols), bf16))
        else:
            views.append(grad.reshape((2,) * lead + (block, cols)))
        out_shape.append(jax.ShapeDtypeStruct((block, cols), f32))
        shapes = flow_shapes(flow_stages(n_pos, n_clip, clip_first), n_pos, block, cols)
        scratch += [pltpu.VMEM(shape, bf16) for shape in [shapes[0]] + shapes]
    return views, out_shape, scratch


class Spread:

    def __init__(self, n_pos, step, steps, hold, out, send_sem, recv_sem, own_sem):
        self.n_pos, self.step, self.steps = n_pos, step, steps
        self.hold, self.out = hold, out
        self.send_sem, self.recv_sem, self.own_sem = send_sem, recv_sem, own_sem
        self.me = lax.axis_index("pos")

    def greet(self, more=0):
        barrier = pltpu.get_barrier_semaphore()

        def signal(shift, _):
            target = lax.rem(self.me + shift, self.n_pos)
            pl.semaphore_signal(
                barrier, inc=1, device_id={"pos": target}, device_id_type=pl.DeviceIdType.MESH
            )
            return 0

        lax.fori_loop(1, self.n_pos, signal, 0)
        pl.semaphore_wait(barrier, self.n_pos - 1 + more)

    def copy(self, step, shift, source):
        target = lax.rem(self.me + shift, self.n_pos)
        return pltpu.make_async_remote_copy(
            self.hold.at[step, target],
            self.out.at[source * self.steps + step],
            self.send_sem.at[step, shift],
            self.recv_sem.at[step, shift],
            device_id={"pos": target},
            device_id_type=pl.DeviceIdType.MESH,
        )

    def stay(self, step):
        return pltpu.make_async_copy(
            self.hold.at[step, self.me],
            self.out.at[self.me * self.steps + step],
            self.own_sem.at[step],
        )

    def send(self):
        def one(shift, _):
            self.copy(self.step, shift, self.me).start()
            return 0

        lax.fori_loop(1, self.n_pos, one, 0)
        self.stay(self.step).start()

    def finish(self):
        def one_step(step, _):
            def one(shift, _):
                self.copy(step, shift, self.me).wait_send()
                source = lax.rem(self.me + self.n_pos - shift, self.n_pos)
                self.copy(step, shift, source).wait_recv()
                return 0

            lax.fori_loop(1, self.n_pos, one, 0)
            self.stay(step).wait()
            return 0

        lax.fori_loop(0, self.steps, one_step, 0)


def spread_scratch(own, n_pos, places, width):
    return [
        pltpu.VMEM((own, n_pos, places, width), bf16),
        pltpu.SemaphoreType.DMA((own, n_pos)),
        pltpu.SemaphoreType.DMA((own, n_pos)),
        pltpu.SemaphoreType.DMA((own,)),
    ]


def space_forward(
    x_ref, mod_ref, w_ref, h_ref, qkv_ref, o_ref, lse_ref, hold, send_sem, recv_sem, own_sem
):
    own, n_pos = hold.shape[:2]
    frame = pl.program_id(0)
    spread = Spread(n_pos, frame, own, hold, o_ref, send_sem, recv_sem, own_sem)
    pl.when(frame == 0)(spread.greet)
    patches, width = h_ref.shape[1:]
    places = x_ref.shape[2]
    pair = 2 * HEAD_DIM
    shift, scale = mod_ref[0, 0:1, :], mod_ref[0, 1:2, :]

    def norm_step(step, _):
        normed, _inverse = norm_rows(load_rows(x_ref, step))
        h_ref[0, pl.ds(step * ROWS, ROWS), :] = (normed * (1.0 + scale) + shift).astype(bf16)
        return 0

    lax.fori_loop(0, patches // ROWS, norm_step, 0)
    for part in range(3):
        cols = slice(part * width, (part + 1) * width)
        qkv_ref[0, :, cols] = bdot(h_ref[0], w_ref[:, cols]).astype(bf16)
    masks = pair_masks(1.0 / math.sqrt(HEAD_DIM))
    lane_ids = lax.broadcasted_iota(jnp.int32, (1, pair), 1)
    lse_ref[0] = jnp.zeros((patches, pair), f32)

    def head_pair(index, _):
        at = pl.multiple_of(index * pair, pair)
        q = qkv_ref[0, :, pl.ds(at, pair)]
        k = qkv_ref[0, :, pl.ds(pl.multiple_of(width + at, pair), pair)]
        v = qkv_ref[0, :, pl.ds(pl.multiple_of(2 * width + at, pair), pair)]
        outs = []
        lse = lse_ref[0]
        for half in range(2):
            scores = bdot_nt(q * masks[half], k)
            top = jnp.max(scores, axis=-1, keepdims=True)
            exps = jnp.exp(scores - top)
            total = jnp.sum(exps, axis=-1, keepdims=True)
            probs = (exps * (1.0 / total)).astype(bf16)
            outs.append(bdot(probs, v))
            lse = jnp.where(lane_ids == 2 * index + half, top + jnp.log(total), lse)
        lse_ref[0] = lse
        both = jnp.where(lane_ids < HEAD_DIM, outs[0], outs[1])
        hold[frame, :, :, pl.ds(at, pair)] = both.reshape(n_pos, places, pair).astype(bf16)
        return 0

    lax.fori_loop(0, HEADS // 2, head_pair, 0)
    spread.send()
    pl.when(frame == own - 1)(spread.finish)


def space_backward(n_clip, kinds, early, *refs):
    go_ref, qkv_ref, lse_ref, x_ref, h_ref, mod_ref, w_ref, hot_ref, rest_ref = refs[:9]
    grads, refs = refs[9 : 9 + early], refs[9 + early :]
    dv_ref, dmod_ref = refs[:2]
    outs, refs = refs[2 : 2 + len(kinds)], refs[2 + len(kinds) :]
    e_ref, dqkv_ref, total_ref, small_ref, got_ref, acc_ref, every_ref = refs[:7]
    small_send, small_recv, hold, send_sem, recv_sem, own_sem = refs[7:13]
    late_grads, refs = refs[13 : 13 + len(kinds) - early], refs[13 + len(kinds) - early :]
    own, n_pos = hold.shape[:2]
    frame = pl.program_id(0)
    spread = Spread(n_pos, frame, own, hold, dv_ref, send_sem, recv_sem, own_sem)
    flows = make_flows(n_pos, n_clip, kinds, tuple(grads) + tuple(late_grads), outs, refs)
    late = flows[early:]
    tree = Butterfly(
        n_pos, n_clip, small_ref, every_ref, got_ref, acc_ref, (small_send, small_recv), here()
    )
    stages = max(len(flow.stages) for flow in flows)
    order = [(i, stage) for stage in range(stages) for i in range(early)]
    order = [(i, stage) for i, stage in order if stage < len(flows[i].stages)]
    cuts = [2, early, early + 2]

    @pl.when(frame == 0)
    def _():
        place = here()
        others = [("clip", bit) for bit in bits_of(n_clip)]
        barrier = pltpu.get_barrier_semaphore()
        for axis, bit in others:
            signal_swap(barrier, place, axis, bit)
        spread.greet(len(others))
        for flow in flows[:early]:
            flow.start()
        total_ref[...] = jnp.zeros_like(total_ref)
        small_ref[:, : 2 * x_ref.shape[3]] = jnp.zeros_like(small_ref[:, : 2 * x_ref.shape[3]])
        small_ref[:, 2 * x_ref.shape[3] :] = rest_ref[...]

    def advance(steps):
        for i, stage in steps:
            flows[i].take(stage)

    def start_late():
        block = late_grads[0].shape[-2]
        lead = len(late_grads[0].shape) - 2

        def one(index, _):
            at = tuple(lax.rem(index // (1 << i), 2) for i in reversed(range(lead)))
            rows = pl.ds(pl.multiple_of(index * block, 8), block)
            first = 0
            for grad in late_grads:
                cols = grad.shape[-1]
                grad[at] = total_ref[rows, first : first + cols].astype(bf16)
                first += cols
            return 0

        lax.fori_loop(0, n_pos, one, 0)
        for flow in late:
            flow.start()

    patches = qkv_ref.shape[1]
    width = x_ref.shape[3]
    places = x_ref.shape[2]
    pair = 2 * HEAD_DIM
    scale = mod_ref[0, 1:2, :]
    factor = 1.0 / math.sqrt(HEAD_DIM)
    masks_q = pair_masks(factor)
    masks = pair_masks(1.0)
    lane_ids = lax.broadcasted_iota(jnp.int32, (1, pair), 1)

    def head_pair(index, _):
        at = pl.multiple_of(index * pair, pair)
        k_at = pl.multiple_of(width + at, pair)
        v_at = pl.multiple_of(2 * width + at, pair)
        q = qkv_ref[0, :, pl.ds(at, pair)]
        k = qkv_ref[0, :, pl.ds(k_at, pair)]
        v = qkv_ref[0, :, pl.ds(v_at, pair)]
        go = go_ref[:, 0, :, pl.ds(at, pair)].astype(f32).reshape(patches, pair).astype(bf16)
        lse_all = lse_ref[0]
        gq, gk, gv = None, None, None
        for half in range(2):
            lse = jnp.sum(
                jnp.where(lane_ids == 2 * index + half, lse_all, 0.0), axis=-1, keepdims=True
            )
            q_half = q * masks_q[half]
            go_half = go * masks[half]
            probs = jnp.exp(bdot_nt(q_half, k) - lse)
            grad_p = bdot_nt(go_half, v)
            inner = jnp.sum(grad_p * probs, axis=-1, keepdims=True)
            grad_s = (probs * (grad_p - inner)).astype(bf16)
            part_q = bdot(grad_s, k * masks_q[half])
            part_k = bdot_tn(grad_s, q_half)
            part_v = bdot_tn(probs.astype(bf16), go_half)
            gq = part_q if gq is None else gq + part_q
            gk = part_k if gk is None else gk + part_k
            gv = part_v if gv is None else gv + part_v
        dqkv_ref[:, pl.ds(at, pair)] = gq.astype(bf16)
        dqkv_ref[:, pl.ds(k_at, pair)] = gk.astype(bf16)
        dqkv_ref[:, pl.ds(v_at, pair)] = gv.astype(bf16)
        return 0

    lax.fori_loop(0, HEADS // 2, head_pair, 0)
    e_ref[...] = bdot_nt(dqkv_ref[...], w_ref[...])

    def norm_step(step, sums):
        grad = e_ref[pl.ds(step * ROWS, ROWS), :]
        normed, inverse = norm_rows(load_rows(x_ref, step))
        back = norm_rows_back(normed, inverse, scale, grad)
        count = max(1, ROWS // places)
        back = back.reshape(count, places, width).astype(bf16)
        hold[frame, pl.ds(step * count, count)] = back
        folded = grad.reshape(ROWS // 8, 8, width).sum(axis=0)
        folded_n = (grad * normed).reshape(ROWS // 8, 8, width).sum(axis=0)
        return sums[0] + folded, sums[1] + folded_n

    zero = jnp.zeros((8, width), f32)
    shift_sum, scale_sum = lax.fori_loop(0, patches // ROWS, norm_step, (zero, zero))
    spread.send()
    hot = hot_ref[frame][:, 0:1]
    small_ref[:, :width] += hot * jnp.sum(shift_sum, axis=0, keepdims=True)
    small_ref[:, width : 2 * width] += hot * jnp.sum(scale_sum, axis=0, keepdims=True)
    for third in range(3):
        cols = slice(third * width, (third + 1) * width)
        total_ref[:, cols] += bdot_tn(h_ref[0], dqkv_ref[:, cols])
    done = 0
    for index, cut in enumerate(cuts[: own - 1]):
        pl.when(frame == index)(partial(advance, order[done:cut]))
        done = cut

    @pl.when(frame == own - 1)
    def _():
        tree.start()
        start_late()
        left = order[done:]
        for stage in range(stages + 1):
            advance([step for step in left if step[1] == stage])
            if stage < tree.count:
                tree.take(stage)
            for flow in late:
                if 0 <= stage - 1 < len(flow.stages):
                    flow.take(stage - 1)
        dmod_ref[...] = every_ref[...]
        spread.finish()
        tree.finish()
        for flow in flows:
            flow.finish()


GELU_C = math.sqrt(2.0 / math.pi)


def middle(
    o1_ref, x_ref, g_ref, mod_ref, clip_ref, wso_ref, wti_ref, wto_ref, wup_ref, wdn_ref,
    out_ref, act_ref, dz_ref, h3_ref, du_ref, o2_ref, dy2_ref, h2_ref, dqkv_ref, dy1_ref, do1_ref,
    dx1_ref, sum_ref,
    qkv_ref, p_ref, y1_ref, y2_ref, n2_ref, n3_ref, r2_ref, r3_ref, xa_ref, gp_ref, e_ref,
):
    count, frames, width = x_ref.shape
    rows = count * frames
    pair = 2 * HEAD_DIM
    hidden = act_ref.shape[1]
    factor = 1.0 / math.sqrt(HEAD_DIM)
    per = frames // ROWS
    steps = rows // ROWS

    @pl.when(pl.program_id(0) == 0)
    def _():
        sum_ref[...] = jnp.zeros_like(sum_ref)

    def at_rows(step):
        return step // per, pl.ds(lax.rem(step, per) * ROWS, ROWS), pl.ds(step * ROWS, ROWS)

    def mod(index, part):
        return mod_ref[index, part, :]

    y1_ref[...] = bdot(o1_ref[...].reshape(rows, width), wso_ref[...])

    def step_one(step, _):
        place, part, flat = at_rows(step)
        x_one = x_ref[place, part, :].astype(f32) + mod(2, part) * y1_ref[flat, :]
        xa_ref[flat, :] = x_one
        normed, inverse = norm_rows(x_one)
        n2_ref[flat, :] = normed
        r2_ref[flat, :] = jnp.broadcast_to(inverse, (ROWS, pair))
        h2_ref[flat, :] = (normed * (1.0 + mod(4, part)) + mod(3, part)).astype(bf16)
        return 0

    lax.fori_loop(0, steps, step_one, 0)
    for third in range(3):
        cols = slice(third * width, (third + 1) * width)
        qkv_ref[:, cols] = bdot(h2_ref[...], wti_ref[:, cols]).astype(bf16)

    masks = pair_masks(1.0)
    masks_q = pair_masks(factor)
    lane_ids = lax.broadcasted_iota(jnp.int32, (1, pair), 1)
    is_low = lane_ids < HEAD_DIM
    allowed = clip_ref[...] > 0.5

    def halves(values, reduce, neutral):
        low_part = reduce(jnp.where(is_low, values, neutral), axis=-1, keepdims=True)
        high_part = reduce(jnp.where(is_low, neutral, values), axis=-1, keepdims=True)
        return jnp.where(is_low, low_part, high_part)

    def stacked(values, pair_of_masks):
        return jnp.concatenate([values * pair_of_masks[0], values * pair_of_masks[1]], axis=0)

    def pair_at(index):
        at = pl.multiple_of(index * pair, pair)
        return (
            pl.ds(at, pair),
            pl.ds(pl.multiple_of(width + at, pair), pair),
            pl.ds(pl.multiple_of(2 * width + at, pair), pair),
        )

    parts = [slice(place * frames, (place + 1) * frames) for place in range(count)]
    same_half = (
        lax.broadcasted_iota(jnp.int32, (pair, pair), 0) // HEAD_DIM
        == lax.broadcasted_iota(jnp.int32, (pair, pair), 1) // HEAD_DIM
    )
    ones = jnp.where(same_half, 1.0, 0.0).astype(bf16)

    def half_sums(values):
        high = values.astype(bf16)
        low = (values - high.astype(f32)).astype(bf16)
        return bdot(high, ones) + bdot(low, ones)

    def time_pair(index, _):
        jobs = [(2 * index + i, part) + pair_at(2 * index + i) for i in range(2) for part in parts]
        keys = [stacked(qkv_ref[part, k_at], masks_q) for _i, part, q_at, k_at, v_at in jobs]
        scores = [bdot_nt(qkv_ref[job[1], job[2]], key) for job, key in zip(jobs, keys)]
        scores = [jnp.where(allowed, score, masked_score) for score in scores]
        tops = [halves(score, jnp.max, -jnp.inf) for score in scores]
        exps = [jnp.exp(score - top) for score, top in zip(scores, tops)]
        sums = [half_sums(exp) for exp in exps]
        probs = [exp / total for exp, total in zip(exps, sums)]
        values = [stacked(qkv_ref[job[1], job[4]], masks) for job in jobs]
        outs = [bdot(prob.astype(bf16), value) for prob, value in zip(probs, values)]
        for (i, part, q_at, _k, _v), prob, out in zip(jobs, probs, outs):
            p_ref[i, part, :] = prob
            o2_ref[part, q_at] = out.astype(bf16)
        return 0

    lax.fori_loop(0, HEADS // 4, time_pair, 0)

    y2_ref[...] = bdot(o2_ref[...], wto_ref[...])

    def step_two(step, _):
        place, part, flat = at_rows(step)
        x_two = xa_ref[flat, :] + mod(5, part) * y2_ref[flat, :]
        xa_ref[flat, :] = x_two
        normed, inverse = norm_rows(x_two)
        n3_ref[flat, :] = normed
        r3_ref[flat, :] = jnp.broadcast_to(inverse, (ROWS, pair))
        h3_ref[flat, :] = (normed * (1.0 + mod(7, part)) + mod(6, part)).astype(bf16)
        dz_ref[flat, :] = (mod(8, part) * g_ref[place, part, :].astype(f32)).astype(bf16)
        return 0

    lax.fori_loop(0, steps, step_two, 0)

    tile = 256

    def up_tile(index, _):
        cols = pl.ds(pl.multiple_of(index * tile, tile), tile)
        u = bdot(h3_ref[...], wup_ref[:, cols])
        square = u * u
        tanh = jnp.tanh(GELU_C * (u * (1.0 + 0.044715 * square)))
        half = 0.5 * (1.0 + tanh)
        act_ref[:, cols] = (u * half).astype(bf16)
        slope = half + (0.5 * GELU_C) * u * (1.0 - tanh * tanh) * (1.0 + (3.0 * 0.044715) * square)
        du = bdot_nt(dz_ref[...], wdn_ref[cols, :]) * slope
        du_ref[:, cols] = du.astype(bf16)
        return 0

    lax.fori_loop(0, hidden // tile, up_tile, 0)
    e_ref[...] = bdot(act_ref[...], wdn_ref[...])

    def step_three(step, _):
        place, part, flat = at_rows(step)
        z = e_ref[flat, :]
        grad = g_ref[place, part, :].astype(f32)
        out_ref[place, part, :] = (xa_ref[flat, :] + mod(8, part) * z).astype(bf16)
        sum_ref[6, part, :] += grad * z
        return 0

    lax.fori_loop(0, steps, step_three, 0)
    e_ref[...] = bdot_nt(du_ref[...], wup_ref[...])

    def step_four(step, _):
        place, part, flat = at_rows(step)
        grad = e_ref[flat, :]
        normed = n3_ref[flat, :]
        sum_ref[4, part, :] += grad
        sum_ref[5, part, :] += grad * normed
        back = norm_rows_back(normed, r3_ref[flat, 0:1], mod(7, part), grad)
        grad_two = g_ref[place, part, :].astype(f32) + back
        xa_ref[flat, :] = grad_two
        sum_ref[3, part, :] += grad_two * y2_ref[flat, :]
        dy2_ref[flat, :] = (mod(5, part) * grad_two).astype(bf16)
        return 0

    lax.fori_loop(0, steps, step_four, 0)
    y2_ref[...] = bdot_nt(dy2_ref[...], wto_ref[...])

    def time_pair_back(index, _):
        q_at, k_at, v_at = pair_at(index)
        gos = [y2_ref[part, q_at].astype(bf16) for part in parts]
        values = [stacked(qkv_ref[part, v_at], masks) for part in parts]
        grads = [bdot_nt(go, value) for go, value in zip(gos, values)]
        probs = [p_ref[index, part, :] for part in parts]
        inner = [half_sums(grad * prob) for grad, prob in zip(grads, probs)]
        scores = [
            (prob * (grad - mean)).astype(bf16) for prob, grad, mean in zip(probs, grads, inner)
        ]
        keys = [stacked(qkv_ref[part, k_at], masks_q) for part in parts]
        qs = [qkv_ref[part, q_at] * factor for part in parts]
        grad_q = [bdot(score, key) for score, key in zip(scores, keys)]
        grad_k = [bdot_tn(score, q) for score, q in zip(scores, qs)]
        grad_v = [bdot_tn(prob.astype(bf16), go) for prob, go in zip(probs, gos)]
        for part, g_q, g_k, g_v in zip(parts, grad_q, grad_k, grad_v):
            dqkv_ref[part, q_at] = g_q.astype(bf16)
            dqkv_ref[part, k_at] = jnp.where(is_low, g_k[:frames], g_k[frames:]).astype(bf16)
            dqkv_ref[part, v_at] = jnp.where(is_low, g_v[:frames], g_v[frames:]).astype(bf16)
        return 0

    lax.fori_loop(0, HEADS // 2, time_pair_back, 0)
    e_ref[...] = bdot_nt(dqkv_ref[...], wti_ref[...])

    def step_five(step, _):
        place, part, flat = at_rows(step)
        grad = e_ref[flat, :]
        normed = n2_ref[flat, :]
        sum_ref[1, part, :] += grad
        sum_ref[2, part, :] += grad * normed
        grad_one = xa_ref[flat, :] + norm_rows_back(normed, r2_ref[flat, 0:1], mod(4, part), grad)
        dx1_ref[place, part, :] = grad_one
        sum_ref[0, part, :] += grad_one * y1_ref[flat, :]
        dy1_ref[flat, :] = (mod(2, part) * grad_one).astype(bf16)
        return 0

    lax.fori_loop(0, steps, step_five, 0)
    do1_ref[...] = bdot_nt(dy1_ref[...], wso_ref[...]).astype(bf16).reshape(count, frames, width)


VMEM_LIMIT = 62 * 1024 * 1024


def resident(shape):
    return pl.BlockSpec(shape, lambda i: (0,) * len(shape), pipeline_mode=pl.Buffered(1))


def call_space_forward(x, mods, weight):
    n_pos, own, places, width = x.shape
    patches = n_pos * places
    pair = 2 * HEAD_DIM
    spread = pl.BlockSpec((n_pos, 1, places, width), lambda i: (0, i, 0, 0))

    def by_frame(*shape):
        return pl.BlockSpec((1,) + shape, lambda i: (i, 0, 0))

    rows = own * patches
    return pl.pallas_call(
        space_forward,
        grid=(own,),
        in_specs=[spread, by_frame(2, width), resident(weight.shape)],
        out_specs=[
            by_frame(patches, width),
            by_frame(patches, 3 * width),
            pl.BlockSpec(memory_space=pl.ANY),
            by_frame(patches, pair),
        ],
        out_shape=[
            jax.ShapeDtypeStruct((own, patches, width), bf16),
            jax.ShapeDtypeStruct((own, patches, 3 * width), bf16),
            jax.ShapeDtypeStruct((n_pos * own, places, width), bf16),
            jax.ShapeDtypeStruct((own, patches, pair), f32),
        ],
        scratch_shapes=spread_scratch(own, n_pos, places, width),
        compiler_params=pltpu.CompilerParams(
            vmem_limit_bytes=VMEM_LIMIT, collective_id=0, has_side_effects=True
        ),
        cost_estimate=pl.CostEstimate(
            flops=2 * rows * width * 3 * width + 4 * rows * patches * width,
            bytes_accessed=rows * width * 12 + weight.size * 2,
            transcendentals=rows * patches * HEADS,
        ),
        name="space_forward",
    )(x, mods, weight)


def call_space_backward(go, qkv, lse, x, h, mods, weight, hot, dmod_rest, grads, kinds, n_clip):
    n_pos, own, places, width = x.shape
    patches = n_pos * places
    pair = 2 * HEAD_DIM
    lead = n_pos.bit_length() - 1
    clips = dmod_rest.shape[0]
    spread = pl.BlockSpec((n_pos, 1, places, width), lambda i: (0, i, 0, 0))
    anywhere = pl.BlockSpec(memory_space=pl.ANY)

    def by_frame(*shape):
        return pl.BlockSpec((1,) + shape, lambda i: (i, 0, 0))

    rows = own * patches
    cut = 3 * width // 512 * 256
    late = [jax.ShapeDtypeStruct((width, cols), bf16) for cols in (cut, 3 * width - cut)]
    kinds = kinds + (True, False)
    views, flow_outs, flow_scratch = flow_plan(list(grads) + late, kinds, n_pos, n_clip)
    early = len(grads)
    sizes = sum(grad.size for grad in grads)
    dmod_shape = (n_clip, clips, 9 * width)
    swaps = lead + len(bits_of(n_clip))
    return pl.pallas_call(
        partial(space_backward, n_clip, kinds, early),
        grid=(own,),
        in_specs=[
            spread,
            by_frame(patches, 3 * width),
            by_frame(patches, pair),
            spread,
            by_frame(patches, width),
            by_frame(2, width),
            resident(weight.shape),
            resident(hot.shape),
            resident(dmod_rest.shape),
        ]
        + [anywhere] * early,
        out_specs=[anywhere, resident(dmod_shape)] + [resident(out.shape) for out in flow_outs],
        out_shape=[
            jax.ShapeDtypeStruct((n_pos * own, places, width), bf16),
            jax.ShapeDtypeStruct(dmod_shape, f32),
        ]
        + flow_outs,
        scratch_shapes=[
            pltpu.VMEM((patches, width), f32),
            pltpu.VMEM((patches, 3 * width), bf16),
            pltpu.VMEM((width, 3 * width), f32),
            pltpu.VMEM((clips, 9 * width), f32),
            pltpu.VMEM((lead, clips, 9 * width), f32),
            pltpu.VMEM((lead, clips, 9 * width), f32),
            pltpu.VMEM(dmod_shape, f32),
            pltpu.SemaphoreType.DMA((swaps,)),
            pltpu.SemaphoreType.DMA((swaps,)),
        ]
        + spread_scratch(own, n_pos, places, width)
        + views[early:]
        + flow_scratch,
        compiler_params=pltpu.CompilerParams(
            vmem_limit_bytes=VMEM_LIMIT, collective_id=1, has_side_effects=True
        ),
        cost_estimate=pl.CostEstimate(
            flops=4 * rows * width * 3 * width + 10 * rows * patches * width,
            bytes_accessed=rows * width * 16 + weight.size * 2 + sizes * 4,
            transcendentals=rows * patches * HEADS,
        ),
        name="space_backward",
    )(go, qkv, lse, x, h, mods, weight, hot, dmod_rest, *views[:early])


def call_middle(o_one, x, grad, mods, same_clip, wso, wti, wto, wup, wdn):
    places, frames, width = x.shape
    count = max(1, min(places, 256 // frames))
    rows = count * frames
    hidden = wup.shape[1]
    pair = 2 * HEAD_DIM
    total = places * frames
    chunk = pl.BlockSpec((count, frames, width), lambda i: (i, 0, 0))

    def flat(cols):
        return pl.BlockSpec((rows, cols), lambda i: (i, 0))

    def flat_shape(cols):
        return jax.ShapeDtypeStruct((total, cols), bf16)

    def scratch(cols, dtype=f32):
        return pltpu.VMEM((rows, cols), dtype)

    lanes = jnp.concatenate([same_clip, same_clip], axis=1)
    flops = 2 * total * (2 * (wso.size + wti.size + wto.size + wup.size + wdn.size))
    return pl.pallas_call(
        middle,
        grid=(places // count,),
        in_specs=[chunk, chunk, chunk, resident(mods.shape), resident(lanes.shape)]
        + [resident(w.shape) for w in (wso, wti, wto, wup, wdn)],
        out_specs=[
            chunk,
            flat(hidden),
            flat(width),
            flat(width),
            flat(hidden),
            flat(width),
            flat(width),
            flat(width),
            flat(3 * width),
            flat(width),
            chunk,
            chunk,
            pl.BlockSpec((7, frames, width), lambda i: (0, 0, 0)),
        ],
        out_shape=[
            jax.ShapeDtypeStruct(x.shape, bf16),
            flat_shape(hidden),
            flat_shape(width),
            flat_shape(width),
            flat_shape(hidden),
            flat_shape(width),
            flat_shape(width),
            flat_shape(width),
            flat_shape(3 * width),
            flat_shape(width),
            jax.ShapeDtypeStruct(x.shape, bf16),
            jax.ShapeDtypeStruct(x.shape, f32),
            jax.ShapeDtypeStruct((7, frames, width), f32),
        ],
        scratch_shapes=[
            scratch(3 * width, bf16),
            pltpu.VMEM((HEADS // 2, rows, pair), f32),
            scratch(width),
            scratch(width),
            scratch(width),
            scratch(width),
            scratch(pair),
            scratch(pair),
            scratch(width),
            pltpu.VMEM((8, pair), f32),
            scratch(width),
        ],
        compiler_params=pltpu.CompilerParams(vmem_limit_bytes=VMEM_LIMIT),
        cost_estimate=pl.CostEstimate(
            flops=flops, bytes_accessed=total * 40000, transcendentals=total * hidden
        ),
        name="middle",
    )(o_one, x, grad, mods, lanes, wso, wti, wto, wup, wdn)


def on_device(
    tokens,
    clip_lengths,
    timesteps,
    embed_first,
    embed_second,
    adaln_weight,
    spatial_in,
    spatial_out,
    temporal_in,
    temporal_out,
    hidden_up,
    hidden_down,
    grad_output,
    n_pos=16,
    n_clip=2,
):
    frames, places, width = tokens.shape
    rows = frames * places
    own = frames // n_pos
    patches = places * n_pos
    me = lax.axis_index("pos")
    clips = clip_lengths.shape[1]

    def exchange(values):
        sent = values.reshape(frames, places, width)
        got = lax.all_to_all(sent, "pos", split_axis=0, concat_axis=0, tiled=True)
        return got.reshape(n_pos, own, places, width)

    x_space = exchange(tokens)

    all_steps = by_distance(timesteps[0], "clip", n_clip)
    freq = frequency(all_steps)
    pre_cond = dot_exact(freq, embed_first)
    hidden_cond = jax.nn.silu(pre_cond)
    cond = dot_exact(hidden_cond, embed_second)
    cond_act = jax.nn.silu(cond)
    modulated = dot_exact(cond_act[:clips], adaln_weight)
    onehot, clip_ids = clip_onehot(clip_lengths[0], frames)
    per_frame = dot_high(onehot, modulated)
    own_frames = lax.dynamic_slice_in_dim(per_frame, me * own, own, 0)

    own_mods = own_frames[:, : 2 * width].reshape(own, 2, width)
    h_one, qkv_one, o_one, lse_one = call_space_forward(x_space, own_mods, spatial_in)

    def turn(values):
        return values.transpose(1, 0, 2)

    o_one = turn(o_one)
    mods = per_frame.reshape(frames, 9, width).transpose(1, 0, 2)
    same_clip = jnp.dot(onehot, onehot.T)
    (block_turned, act, grad_z, h_three, grad_u, o_two, grad_y_two, h_two, grad_qkv_two, grad_y_one, grad_o_one,
     grad_one, sums) = call_middle(
        o_one, turn(tokens), turn(grad_output), mods, same_clip, spatial_out, temporal_in, temporal_out,
        hidden_up, hidden_down,
    )
    block_out = turn(block_turned)
    grad_o_space = exchange(turn(grad_o_one))
    early = (
        weight_grad(h_three, grad_u),
        weight_grad(act, grad_z),
        weight_grad(h_two, grad_qkv_two),
        weight_grad(o_one.reshape(rows, width), grad_y_one),
        weight_grad(o_two, grad_y_two),
    )
    own_hot = lax.dynamic_slice_in_dim(onehot, me * own, own, 0)
    hot = jnp.broadcast_to(own_hot[:, :, None], (own, clips, 128))
    dmod_rest = dot_high(onehot.T, sums.transpose(1, 0, 2).reshape(frames, 7 * width))
    (
        back_places, dmod, g_hidden_up, g_hidden_down, g_temporal_in, g_spatial_out, g_temporal_out,
        in_low, in_high,
    ) = call_space_backward(
        grad_o_space, qkv_one, lse_one, x_space, h_one, own_mods, spatial_in, hot, dmod_rest,
        early, (False, True, True, True, True), n_clip,
    )
    grad_tokens = (turn(grad_one) + back_places.astype(f32)).astype(bf16)
    g_spatial_in = jnp.concatenate([in_low, in_high], axis=1)
    dmod = dmod.reshape(n_clip * clips, 9 * width)

    def own_columns(values):
        block = values.shape[1] // n_pos
        return lax.dynamic_slice_in_dim(values, me * block, block, 1)

    g_adaln = dot_high(own_columns(cond_act).T, dmod)
    grad_cond = dot_exact(dmod, adaln_weight.T) * silu_grad(cond)
    g_second = dot_high(own_columns(hidden_cond).T, grad_cond)
    grad_pre = dot_exact(grad_cond, embed_second.T) * silu_grad(pre_cond)
    g_first = dot_high(own_columns(freq).T, grad_pre)
    return (
        block_out,
        grad_tokens,
        g_first,
        g_second,
        g_adaln,
        g_spatial_in,
        g_spatial_out,
        g_temporal_in,
        g_temporal_out,
        g_hidden_up,
        g_hidden_down,
    )


def solution(mesh):
    in_specs = (
        P("clip", "pos", None),
        P("clip", None),
        P("clip", None),
        P(),
        P(),
        P(),
        P(),
        P(),
        P(),
        P(),
        P(),
        P(),
        P("clip", "pos", None),
    )
    out_specs = (P("clip", "pos", None),) * 2 + (P("pos", None),) * 9
    body = partial(on_device, n_pos=mesh.shape["pos"], n_clip=mesh.shape["clip"])
    return jax.shard_map(body, mesh=mesh, in_specs=in_specs, out_specs=out_specs, check_vma=False)
```

```python
from functools import partial
import math

import jax
import jax.numpy as jnp
from jax import lax
from jax.experimental import pallas as pl
from jax.experimental.pallas import tpu as pltpu
from jax.sharding import PartitionSpec as P

HEADS = 12
HEAD_DIM = 64
FREQ = 256

epsilon = 1e-06
highest = lax.Precision.HIGHEST
masked_score = -1000000000.0
f32 = jnp.float32
bf16 = jnp.bfloat16


def frequency(step_ids):
    half_width = FREQ // 2
    rate_table = jnp.exp(
        -math.log(10000.0) * jnp.arange(half_width, dtype=jnp.float32) / half_width
    )
    angles = step_ids.astype(jnp.float32)[:, None] * rate_table[None, :]
    return jnp.concatenate([jnp.cos(angles), jnp.sin(angles)], axis=1)


def dot_high(left, right):
    return jnp.dot(left, right, precision=highest, preferred_element_type=f32)


def silu_grad(values):
    gate = jax.nn.sigmoid(values)
    return gate * (1.0 + values * (1.0 - gate))


def clip_onehot(lengths, frames):
    clip_ends = jnp.cumsum(lengths)
    frame_ids = jnp.arange(frames, dtype=jnp.int32)
    clip_ids = jnp.sum((frame_ids[:, None] >= clip_ends[None, :]).astype(jnp.int32), axis=1)
    onehot = (clip_ids[:, None] == jnp.arange(lengths.shape[0], dtype=jnp.int32)[None, :]).astype(
        jnp.float32
    )
    return (onehot, clip_ids)


def weight_grad(left, right):
    return jnp.einsum("rd,rk->dk", left, right, preferred_element_type=f32).astype(bf16)


def bdot(left, right):
    return lax.dot_general(left, right, (((1,), (0,)), ((), ())), preferred_element_type=f32)


def bdot_nt(left, right):
    return lax.dot_general(left, right, (((1,), (1,)), ((), ())), preferred_element_type=f32)


def bdot_tn(left, right):
    return lax.dot_general(left, right, (((0,), (0,)), ((), ())), preferred_element_type=f32)


def norm_rows(values):
    width = values.shape[-1]
    centre = values - jnp.sum(values, axis=-1, keepdims=True) * (1.0 / width)
    spread = jnp.sum(centre * centre, axis=-1, keepdims=True) * (1.0 / width)
    inverse = lax.rsqrt(spread + epsilon)
    return centre * inverse, inverse


def norm_rows_back(normed, inverse, scale_vec, grad):
    width = grad.shape[-1]
    inner = grad * (1.0 + scale_vec)
    mean_one = jnp.sum(inner, axis=-1, keepdims=True) * (1.0 / width)
    mean_two = jnp.sum(inner * normed, axis=-1, keepdims=True) * (1.0 / width)
    return inverse * (inner - mean_one - normed * mean_two)


def pair_masks(scale):
    lanes = lax.broadcasted_iota(jnp.int32, (1, 2 * HEAD_DIM), 1)
    low_half = jnp.where(lanes < HEAD_DIM, scale, 0.0).astype(bf16)
    high_half = jnp.where(lanes < HEAD_DIM, 0.0, scale).astype(bf16)
    return low_half, high_half


ROWS = 32


def load_rows(ref, step):
    places, width = ref.shape[2:]
    count = max(1, ROWS // places)
    part = ref[pl.ds(step * count, count), 0].astype(f32)
    return part.reshape(count * places, width)


def swap(values, axis, size, bit):
    return lax.ppermute(values, axis, [(i, i ^ bit) for i in range(size)])


def bits_of(size):
    return [1 << i for i in range(size.bit_length() - 1)]


def by_distance(values, axis, size):
    for bit in bits_of(size):
        values = jnp.concatenate([values, swap(values, axis, size, bit)], axis=0)
    return values


def dot_exact(left, right):
    parts = []
    for _ in range(3):
        part = left.astype(bf16)
        parts.append(part)
        left = left - part.astype(f32)
    count = parts[0].shape[0]
    got = jnp.dot(jnp.concatenate(parts, axis=0), right, preferred_element_type=f32)
    return got[:count] + (got[count : 2 * count] + got[2 * count :])


def flow_stages(n_pos, n_clip, clip_first):
    pos = [("pos", bit, "halve") for bit in bits_of(n_pos)]
    clip = bits_of(n_clip)
    if not clip_first:
        return pos + [("clip", bit, "sum") for bit in clip]
    first = [("clip", clip[0], "columns")]
    last = [("clip", clip[0], "gather")]
    return pos[:1] + first + pos[1:] + [("clip", bit, "sum") for bit in clip[1:]] + last


def flow_shapes(stages, n_pos, block, cols):
    lead = n_pos.bit_length() - 1
    shapes = []
    for _, _, what in stages:
        if what == "halve":
            lead -= 1
        elif what == "columns":
            cols //= 2
        shapes.append((2,) * lead + (block, cols))
    return shapes


class Flow:
    def __init__(self, number, stages, grad, out, keep, gots, sems, place):
        self.number, self.stages = number, stages
        self.grad, self.out, self.keep, self.gots = grad, out, keep, gots
        self.send_sem, self.recv_sem, self.keep_sem = sems
        self.place = place

    def side(self, stage):
        axis, bit, _ = self.stages[stage]
        return lax.rem(self.place[axis] // bit, 2)

    def columns(self, side, width):
        return pl.ds(pl.multiple_of(side * width, width), width)

    def part(self, ref, stage, side):
        what = self.stages[stage][2]
        lead = len(ref.shape) - 2
        if what == "halve":
            return (slice(None),) * (lead - 1) + (side,)
        if what == "columns":
            half = ref.shape[-1] // 2
            return (slice(None),) * (lead + 1) + (self.columns(side, half),)
        return None

    def held(self, stage):
        if stage == 0:
            return self.grad
        return self.keep if stage == 1 else self.gots[stage - 1]

    def copy(self, stage):
        axis, bit, _ = self.stages[stage]
        side = self.side(stage)
        source = self.held(stage)
        at = self.part(source, stage, 1 - side)
        return pltpu.make_async_remote_copy(
            source if at is None else source.at[at],
            self.gots[stage],
            self.send_sem.at[self.number, stage],
            self.recv_sem.at[self.number, stage],
            device_id={axis: self.place[axis] + bit * (1 - 2 * side)},
            device_id_type=pl.DeviceIdType.MESH,
        )

    def own(self):
        at = self.part(self.grad, 0, self.side(0))
        return pltpu.make_async_copy(self.grad.at[at], self.keep, self.keep_sem.at[self.number])

    def start(self):
        self.copy(0).start()
        self.own().start()

    def take(self, stage):
        self.copy(stage).wait_recv()
        if stage == 0:
            self.own().wait()
        what = self.stages[stage][2]
        got = self.gots[stage]
        side = self.side(stage)
        last = stage == len(self.stages) - 1
        lead = len(got.shape) - 2
        if what == "gather":
            half = got.shape[-1]
            self.out[:, self.columns(side, half)] = self.held(stage)[...].astype(f32)
            self.out[:, self.columns(1 - side, half)] = got[...].astype(f32)
            return
        if last:
            self.out[...] = self.held(stage)[...].astype(f32) + got[...].astype(f32)
            return
        target = self.keep if stage == 0 else got

        def one(index, _):
            at = tuple(lax.rem(index // (1 << i), 2) for i in range(lead))
            if stage == 0:
                mine = self.keep[at]
            elif what == "halve":
                mine = self.held(stage)[at + (side,)]
            elif what == "columns":
                mine = self.held(stage)[at + (slice(None), self.columns(side, got.shape[-1]))]
            else:
                mine = self.held(stage)[at]
            target[at] = mine + got[at]
            return 0

        lax.fori_loop(0, 1 << lead, one, 0)
        self.copy(stage + 1).start()

    def finish(self):
        for stage in range(len(self.stages)):
            self.copy(stage).wait_send()


class Butterfly:
    def __init__(self, n_pos, n_clip, values, out, got, acc, sems, place):
        self.pos_bits, self.clip_bits = bits_of(n_pos), bits_of(n_clip)
        self.values, self.out, self.got, self.acc = values, out, got, acc
        self.send_sem, self.recv_sem = sems
        self.place = place
        self.count = len(self.pos_bits) + len(self.clip_bits)

    def copy(self, stage):
        if stage < len(self.pos_bits):
            axis, bit = "pos", self.pos_bits[stage]
            source = self.values if stage == 0 else self.acc.at[stage - 1]
            target = self.got.at[stage]
        else:
            axis, bit = "clip", self.clip_bits[stage - len(self.pos_bits)]
            source, target = self.out.at[pl.ds(0, bit)], self.out.at[pl.ds(bit, bit)]
        side = lax.rem(self.place[axis] // bit, 2)
        return pltpu.make_async_remote_copy(
            source,
            target,
            self.send_sem.at[stage],
            self.recv_sem.at[stage],
            device_id={axis: self.place[axis] + bit * (1 - 2 * side)},
            device_id_type=pl.DeviceIdType.MESH,
        )

    def start(self):
        self.copy(0).start()

    def take(self, stage):
        self.copy(stage).wait_recv()
        last = len(self.pos_bits) - 1
        if stage <= last:
            mine = self.values[...] if stage == 0 else self.acc[stage - 1]
            if stage < last:
                self.acc[stage] = mine + self.got[stage]
            else:
                self.out[0] = mine + self.got[stage]
        if stage + 1 < self.count:
            self.copy(stage + 1).start()

    def finish(self):
        for stage in range(self.count):
            self.copy(stage).wait_send()


def partner_list(n_pos, n_clip):
    return [("pos", bit) for bit in bits_of(n_pos)] + [("clip", bit) for bit in bits_of(n_clip)]


def here():
    return {"pos": lax.axis_index("pos"), "clip": lax.axis_index("clip")}


def signal_swap(barrier, place, axis, bit):
    side = lax.rem(place[axis] // bit, 2)
    pl.semaphore_signal(
        barrier,
        inc=1,
        device_id={axis: place[axis] + bit * (1 - 2 * side)},
        device_id_type=pl.DeviceIdType.MESH,
    )


def make_flows(n_pos, n_clip, kinds, grads, outs, scratch):
    sems, rest = scratch[:3], list(scratch[3:])
    flows = []
    for number, clip_first in enumerate(kinds):
        stages = flow_stages(n_pos, n_clip, clip_first)
        keep, gots = rest[0], rest[1 : 1 + len(stages)]
        rest = rest[1 + len(stages) :]
        flows.append(Flow(number, stages, grads[number], outs[number], keep, gots, sems, here()))
    return flows


def flow_plan(grads, kinds, n_pos, n_clip):
    lead = n_pos.bit_length() - 1
    most = lead + len(bits_of(n_clip)) + 1
    dma = pltpu.SemaphoreType.DMA
    scratch = [dma((len(grads), most)), dma((len(grads), most)), dma((len(grads),))]
    views, out_shape = [], []
    for grad, clip_first in zip(grads, kinds):
        rows, cols = grad.shape
        block = rows // n_pos
        if isinstance(grad, jax.ShapeDtypeStruct):
            views.append(pltpu.VMEM((2,) * lead + (block, cols), bf16))
        else:
            views.append(grad.reshape((2,) * lead + (block, cols)))
        out_shape.append(jax.ShapeDtypeStruct((block, cols), f32))
        shapes = flow_shapes(flow_stages(n_pos, n_clip, clip_first), n_pos, block, cols)
        scratch += [pltpu.VMEM(shape, bf16) for shape in [shapes[0]] + shapes]
    return views, out_shape, scratch


class Spread:

    def __init__(self, n_pos, step, steps, hold, out, send_sem, recv_sem, own_sem):
        self.n_pos, self.step, self.steps = n_pos, step, steps
        self.hold, self.out = hold, out
        self.send_sem, self.recv_sem, self.own_sem = send_sem, recv_sem, own_sem
        self.me = lax.axis_index("pos")

    def greet(self, more=0):
        barrier = pltpu.get_barrier_semaphore()

        def signal(shift, _):
            target = lax.rem(self.me + shift, self.n_pos)
            pl.semaphore_signal(
                barrier, inc=1, device_id={"pos": target}, device_id_type=pl.DeviceIdType.MESH
            )
            return 0

        lax.fori_loop(1, self.n_pos, signal, 0)
        pl.semaphore_wait(barrier, self.n_pos - 1 + more)

    def copy(self, step, shift, source):
        target = lax.rem(self.me + shift, self.n_pos)
        return pltpu.make_async_remote_copy(
            self.hold.at[step, target],
            self.out.at[source * self.steps + step],
            self.send_sem.at[step, shift],
            self.recv_sem.at[step, shift],
            device_id={"pos": target},
            device_id_type=pl.DeviceIdType.MESH,
        )

    def stay(self, step):
        return pltpu.make_async_copy(
            self.hold.at[step, self.me],
            self.out.at[self.me * self.steps + step],
            self.own_sem.at[step],
        )

    def send(self):
        def one(shift, _):
            self.copy(self.step, shift, self.me).start()
            return 0

        lax.fori_loop(1, self.n_pos, one, 0)
        self.stay(self.step).start()

    def finish(self):
        def one_step(step, _):
            def one(shift, _):
                self.copy(step, shift, self.me).wait_send()
                source = lax.rem(self.me + self.n_pos - shift, self.n_pos)
                self.copy(step, shift, source).wait_recv()
                return 0

            lax.fori_loop(1, self.n_pos, one, 0)
            self.stay(step).wait()
            return 0

        lax.fori_loop(0, self.steps, one_step, 0)


def spread_scratch(own, n_pos, places, width):
    return [
        pltpu.VMEM((own, n_pos, places, width), bf16),
        pltpu.SemaphoreType.DMA((own, n_pos)),
        pltpu.SemaphoreType.DMA((own, n_pos)),
        pltpu.SemaphoreType.DMA((own,)),
    ]


def space_forward(
    x_ref, mod_ref, w_ref, h_ref, qkv_ref, o_ref, lse_ref, hold, send_sem, recv_sem, own_sem
):
    own, n_pos = hold.shape[:2]
    frame = pl.program_id(0)
    spread = Spread(n_pos, frame, own, hold, o_ref, send_sem, recv_sem, own_sem)
    pl.when(frame == 0)(spread.greet)
    patches, width = h_ref.shape[1:]
    places = x_ref.shape[2]
    pair = 2 * HEAD_DIM
    shift, scale = mod_ref[0, 0:1, :], mod_ref[0, 1:2, :]

    def norm_step(step, _):
        normed, _inverse = norm_rows(load_rows(x_ref, step))
        h_ref[0, pl.ds(step * ROWS, ROWS), :] = (normed * (1.0 + scale) + shift).astype(bf16)
        return 0

    lax.fori_loop(0, patches // ROWS, norm_step, 0)
    for part in range(3):
        cols = slice(part * width, (part + 1) * width)
        qkv_ref[0, :, cols] = bdot(h_ref[0], w_ref[:, cols]).astype(bf16)
    masks = pair_masks(1.0 / math.sqrt(HEAD_DIM))
    is_low = lax.broadcasted_iota(jnp.int32, (1, pair), 1) < HEAD_DIM

    def head_pair(index, _):
        at = pl.multiple_of(index * pair, pair)
        q = qkv_ref[0, :, pl.ds(at, pair)]
        k = qkv_ref[0, :, pl.ds(pl.multiple_of(width + at, pair), pair)]
        v = qkv_ref[0, :, pl.ds(pl.multiple_of(2 * width + at, pair), pair)]
        one = jnp.ones_like(v)
        values = [jnp.where(is_low, v, one), jnp.where(is_low, one, v)]
        scores = [bdot_nt(q * mask, k) for mask in masks]
        tops = [jnp.max(score, axis=-1, keepdims=True) for score in scores]
        exps = [jnp.exp(score - top).astype(bf16) for score, top in zip(scores, tops)]
        outs = [bdot(exp, value) for exp, value in zip(exps, values)]
        total = pltpu.roll(jnp.where(is_low, outs[1], outs[0]), HEAD_DIM, 1)
        both = jnp.where(is_low, outs[0], outs[1]) / total
        lse_ref[0, index] = jnp.where(is_low, tops[0], tops[1]) + jnp.log(total)
        hold[frame, :, :, pl.ds(at, pair)] = both.reshape(n_pos, places, pair).astype(bf16)
        return 0

    lax.fori_loop(0, HEADS // 2, head_pair, 0)
    spread.send()
    pl.when(frame == own - 1)(spread.finish)


def space_backward(n_clip, kinds, early, *refs):
    go_ref, qkv_ref, lse_ref, x_ref, h_ref, mod_ref, w_ref, hot_ref, rest_ref = refs[:9]
    grads, refs = refs[9 : 9 + early], refs[9 + early :]
    dv_ref, dmod_ref = refs[:2]
    outs, refs = refs[2 : 2 + len(kinds)], refs[2 + len(kinds) :]
    e_ref, dqkv_ref, total_ref, small_ref, got_ref, acc_ref, every_ref = refs[:7]
    small_send, small_recv, hold, send_sem, recv_sem, own_sem = refs[7:13]
    late_grads, refs = refs[13 : 13 + len(kinds) - early], refs[13 + len(kinds) - early :]
    own, n_pos = hold.shape[:2]
    frame = pl.program_id(0)
    spread = Spread(n_pos, frame, own, hold, dv_ref, send_sem, recv_sem, own_sem)
    flows = make_flows(n_pos, n_clip, kinds, tuple(grads) + tuple(late_grads), outs, refs)
    late = flows[early:]
    tree = Butterfly(
        n_pos, n_clip, small_ref, every_ref, got_ref, acc_ref, (small_send, small_recv), here()
    )
    stages = max(len(flow.stages) for flow in flows)
    order = [(i, stage) for stage in range(stages) for i in range(early)]
    order = [(i, stage) for i, stage in order if stage < len(flows[i].stages)]
    cuts = [2, early, early + 2]

    @pl.when(frame == 0)
    def _():
        place = here()
        others = [("clip", bit) for bit in bits_of(n_clip)]
        barrier = pltpu.get_barrier_semaphore()
        for axis, bit in others:
            signal_swap(barrier, place, axis, bit)
        spread.greet(len(others))
        for flow in flows[:early]:
            flow.start()
        total_ref[...] = jnp.zeros_like(total_ref)
        small_ref[:, : 2 * x_ref.shape[3]] = jnp.zeros_like(small_ref[:, : 2 * x_ref.shape[3]])
        small_ref[:, 2 * x_ref.shape[3] :] = rest_ref[...]

    def advance(steps):
        for i, stage in steps:
            flows[i].take(stage)

    def start_late():
        block = late_grads[0].shape[-2]
        lead = len(late_grads[0].shape) - 2

        def one(index, _):
            at = tuple(lax.rem(index // (1 << i), 2) for i in reversed(range(lead)))
            rows = pl.ds(pl.multiple_of(index * block, 8), block)
            first = 0
            for grad in late_grads:
                cols = grad.shape[-1]
                grad[at] = total_ref[rows, first : first + cols].astype(bf16)
                first += cols
            return 0

        lax.fori_loop(0, n_pos, one, 0)
        for flow in late:
            flow.start()

    patches = qkv_ref.shape[1]
    width = x_ref.shape[3]
    places = x_ref.shape[2]
    pair = 2 * HEAD_DIM
    scale = mod_ref[0, 1:2, :]
    factor = 1.0 / math.sqrt(HEAD_DIM)
    masks_q = pair_masks(factor)
    masks = pair_masks(1.0)
    ones = jnp.ones((patches, pair), bf16)

    def key_sums(values):
        high = values.astype(bf16)
        low = (values - high.astype(f32)).astype(bf16)
        total = bdot(high, ones) + bdot(low, ones)
        return jnp.concatenate([total] * (patches // pair), axis=1)

    def head_pair(index, _):
        at = pl.multiple_of(index * pair, pair)
        k_at = pl.multiple_of(width + at, pair)
        v_at = pl.multiple_of(2 * width + at, pair)
        q = qkv_ref[0, :, pl.ds(at, pair)]
        k = qkv_ref[0, :, pl.ds(k_at, pair)]
        v = qkv_ref[0, :, pl.ds(v_at, pair)]
        go = go_ref[:, 0, :, pl.ds(at, pair)].astype(f32).reshape(patches, pair).astype(bf16)
        lse_pair = lse_ref[0, index]
        lses = [lse_pair[:, 0:1], lse_pair[:, HEAD_DIM : HEAD_DIM + 1]]
        q_halves = [q * mask for mask in masks_q]
        go_halves = [go * mask for mask in masks]
        probs = [jnp.exp(bdot_nt(half, k) - lse) for half, lse in zip(q_halves, lses)]
        grads = [bdot_nt(half, v) for half in go_halves]
        inner = [key_sums(grad * prob) for grad, prob in zip(grads, probs)]
        scores = [
            (prob * (grad - mean)).astype(bf16) for prob, grad, mean in zip(probs, grads, inner)
        ]
        gq = sum(bdot(score, k * mask) for score, mask in zip(scores, masks_q))
        gk = sum(bdot_tn(score, half) for score, half in zip(scores, q_halves))
        gv = sum(bdot_tn(prob.astype(bf16), half) for prob, half in zip(probs, go_halves))
        dqkv_ref[:, pl.ds(at, pair)] = gq.astype(bf16)
        dqkv_ref[:, pl.ds(k_at, pair)] = gk.astype(bf16)
        dqkv_ref[:, pl.ds(v_at, pair)] = gv.astype(bf16)
        return 0

    lax.fori_loop(0, HEADS // 2, head_pair, 0)
    e_ref[...] = bdot_nt(dqkv_ref[...], w_ref[...])

    def norm_step(step, sums):
        grad = e_ref[pl.ds(step * ROWS, ROWS), :]
        normed, inverse = norm_rows(load_rows(x_ref, step))
        back = norm_rows_back(normed, inverse, scale, grad)
        count = max(1, ROWS // places)
        back = back.reshape(count, places, width).astype(bf16)
        hold[frame, pl.ds(step * count, count)] = back
        folded = grad.reshape(ROWS // 8, 8, width).sum(axis=0)
        folded_n = (grad * normed).reshape(ROWS // 8, 8, width).sum(axis=0)
        return sums[0] + folded, sums[1] + folded_n

    zero = jnp.zeros((8, width), f32)
    shift_sum, scale_sum = lax.fori_loop(0, patches // ROWS, norm_step, (zero, zero))
    spread.send()
    hot = hot_ref[frame][:, 0:1]
    small_ref[:, :width] += hot * jnp.sum(shift_sum, axis=0, keepdims=True)
    small_ref[:, width : 2 * width] += hot * jnp.sum(scale_sum, axis=0, keepdims=True)
    for third in range(3):
        cols = slice(third * width, (third + 1) * width)
        total_ref[:, cols] += bdot_tn(h_ref[0], dqkv_ref[:, cols])
    done = 0
    for index, cut in enumerate(cuts[: own - 1]):
        pl.when(frame == index)(partial(advance, order[done:cut]))
        done = cut

    @pl.when(frame == own - 1)
    def _():
        tree.start()
        start_late()
        left = order[done:]
        for stage in range(stages + 1):
            advance([step for step in left if step[1] == stage])
            if stage < tree.count:
                tree.take(stage)
            for flow in late:
                if 0 <= stage - 1 < len(flow.stages):
                    flow.take(stage - 1)
        dmod_ref[...] = every_ref[...]
        spread.finish()
        tree.finish()
        for flow in flows:
            flow.finish()


GELU_C = math.sqrt(2.0 / math.pi)


def middle(
    o1_ref, x_ref, g_ref, mod_ref, clip_ref, wso_ref, wti_ref, wto_ref, wup_ref, wdn_ref,
    out_ref, act_ref, dz_ref, h3_ref, du_ref, o2_ref, dy2_ref, h2_ref, dqkv_ref, dy1_ref, do1_ref,
    dx1_ref, sum_ref,
    qkv_ref, p_ref, y1_ref, y2_ref, n2_ref, n3_ref, r2_ref, r3_ref, xa_ref, e_ref,
    ua_ref, aa_ref, ub_ref, ab_ref,
):
    count, frames, width = x_ref.shape
    rows = count * frames
    pair = 2 * HEAD_DIM
    hidden = act_ref.shape[1]
    factor = 1.0 / math.sqrt(HEAD_DIM)
    per = frames // ROWS
    steps = rows // ROWS

    @pl.when(pl.program_id(0) == 0)
    def _():
        sum_ref[...] = jnp.zeros_like(sum_ref)

    def at_rows(step):
        return step // per, pl.ds(lax.rem(step, per) * ROWS, ROWS), pl.ds(step * ROWS, ROWS)

    def mod(index, part):
        return mod_ref[index, part, :]

    y1_ref[...] = bdot(o1_ref[...].reshape(rows, width), wso_ref[...])

    def step_one(step, _):
        place, part, flat = at_rows(step)
        x_one = x_ref[place, part, :].astype(f32) + mod(2, part) * y1_ref[flat, :]
        xa_ref[flat, :] = x_one
        normed, inverse = norm_rows(x_one)
        n2_ref[flat, :] = normed
        r2_ref[flat, :] = jnp.broadcast_to(inverse, (ROWS, pair))
        h2_ref[flat, :] = (normed * (1.0 + mod(4, part)) + mod(3, part)).astype(bf16)
        return 0

    lax.fori_loop(0, steps, step_one, 0)
    for third in range(3):
        cols = slice(third * width, (third + 1) * width)
        qkv_ref[:, cols] = bdot(h2_ref[...], wti_ref[:, cols]).astype(bf16)

    masks = pair_masks(1.0)
    masks_q = pair_masks(factor)
    lane_ids = lax.broadcasted_iota(jnp.int32, (1, pair), 1)
    is_low = lane_ids < HEAD_DIM
    allowed = clip_ref[...] > 0.5

    def halves(values, reduce, neutral):
        low_part = reduce(jnp.where(is_low, values, neutral), axis=-1, keepdims=True)
        high_part = reduce(jnp.where(is_low, neutral, values), axis=-1, keepdims=True)
        return jnp.where(is_low, low_part, high_part)

    def stacked(values, pair_of_masks):
        return jnp.concatenate([values * pair_of_masks[0], values * pair_of_masks[1]], axis=0)

    def pair_at(index):
        at = pl.multiple_of(index * pair, pair)
        return (
            pl.ds(at, pair),
            pl.ds(pl.multiple_of(width + at, pair), pair),
            pl.ds(pl.multiple_of(2 * width + at, pair), pair),
        )

    parts = [slice(place * frames, (place + 1) * frames) for place in range(count)]
    same_half = (
        lax.broadcasted_iota(jnp.int32, (pair, pair), 0) // HEAD_DIM
        == lax.broadcasted_iota(jnp.int32, (pair, pair), 1) // HEAD_DIM
    )
    ones = jnp.where(same_half, 1.0, 0.0).astype(bf16)

    def half_sums(values):
        high = values.astype(bf16)
        low = (values - high.astype(f32)).astype(bf16)
        return bdot(high, ones) + bdot(low, ones)

    def time_pair(index, _):
        jobs = [(2 * index + i, part) + pair_at(2 * index + i) for i in range(2) for part in parts]
        keys = [stacked(qkv_ref[part, k_at], masks_q) for _i, part, q_at, k_at, v_at in jobs]
        scores = [bdot_nt(qkv_ref[job[1], job[2]], key) for job, key in zip(jobs, keys)]
        scores = [jnp.where(allowed, score, masked_score) for score in scores]
        tops = [halves(score, jnp.max, -jnp.inf) for score in scores]
        exps = [jnp.exp(score - top) for score, top in zip(scores, tops)]
        sums = [half_sums(exp) for exp in exps]
        probs = [exp / total for exp, total in zip(exps, sums)]
        values = [stacked(qkv_ref[job[1], job[4]], masks) for job in jobs]
        outs = [bdot(prob.astype(bf16), value) for prob, value in zip(probs, values)]
        for (i, part, q_at, _k, _v), prob, out in zip(jobs, probs, outs):
            p_ref[i, part, :] = prob
            o2_ref[part, q_at] = out.astype(bf16)
        return 0

    lax.fori_loop(0, HEADS // 4, time_pair, 0)

    y2_ref[...] = bdot(o2_ref[...], wto_ref[...])

    def step_two(step, _):
        place, part, flat = at_rows(step)
        x_two = xa_ref[flat, :] + mod(5, part) * y2_ref[flat, :]
        xa_ref[flat, :] = x_two
        normed, inverse = norm_rows(x_two)
        n3_ref[flat, :] = normed
        r3_ref[flat, :] = jnp.broadcast_to(inverse, (ROWS, pair))
        h3_ref[flat, :] = (normed * (1.0 + mod(7, part)) + mod(6, part)).astype(bf16)
        dz_ref[flat, :] = (mod(8, part) * g_ref[place, part, :].astype(f32)).astype(bf16)
        return 0

    lax.fori_loop(0, steps, step_two, 0)

    tile = 256

    def products(index, u_ref, a_ref):
        cols = pl.ds(pl.multiple_of(index * tile, tile), tile)
        u_ref[...] = bdot(h3_ref[...], wup_ref[:, cols])
        a_ref[...] = bdot_nt(dz_ref[...], wdn_ref[cols, :])

    def pointwise(index, u_ref, a_ref):
        cols = pl.ds(pl.multiple_of(index * tile, tile), tile)
        u = u_ref[...]
        square = u * u
        half = 0.5 + 0.5 * jnp.tanh(u * (GELU_C + (0.044715 * GELU_C) * square))
        value = u * half
        act_ref[:, cols] = value.astype(bf16)
        slope = half + (value - value * half) * (2.0 * GELU_C + (6.0 * 0.044715 * GELU_C) * square)
        du_ref[:, cols] = (a_ref[...] * slope).astype(bf16)

    tiles = hidden // tile

    def two_tiles(index, _):
        products(2 * index + 1, ub_ref, ab_ref)
        pointwise(2 * index, ua_ref, aa_ref)
        products(jnp.minimum(2 * index + 2, tiles - 1), ua_ref, aa_ref)
        pointwise(2 * index + 1, ub_ref, ab_ref)
        return 0

    products(0, ua_ref, aa_ref)
    lax.fori_loop(0, tiles // 2, two_tiles, 0)
    e_ref[...] = bdot(act_ref[...], wdn_ref[...])

    def step_three(step, _):
        place, part, flat = at_rows(step)
        z = e_ref[flat, :]
        grad = g_ref[place, part, :].astype(f32)
        out_ref[place, part, :] = (xa_ref[flat, :] + mod(8, part) * z).astype(bf16)
        sum_ref[6, part, :] += grad * z
        return 0

    lax.fori_loop(0, steps, step_three, 0)
    e_ref[...] = bdot_nt(du_ref[...], wup_ref[...])

    def step_four(step, _):
        place, part, flat = at_rows(step)
        grad = e_ref[flat, :]
        normed = n3_ref[flat, :]
        sum_ref[4, part, :] += grad
        sum_ref[5, part, :] += grad * normed
        back = norm_rows_back(normed, r3_ref[flat, 0:1], mod(7, part), grad)
        grad_two = g_ref[place, part, :].astype(f32) + back
        xa_ref[flat, :] = grad_two
        sum_ref[3, part, :] += grad_two * y2_ref[flat, :]
        dy2_ref[flat, :] = (mod(5, part) * grad_two).astype(bf16)
        return 0

    lax.fori_loop(0, steps, step_four, 0)
    y2_ref[...] = bdot_nt(dy2_ref[...], wto_ref[...])

    def time_pair_back(index, _):
        q_at, k_at, v_at = pair_at(index)
        gos = [y2_ref[part, q_at].astype(bf16) for part in parts]
        values = [stacked(qkv_ref[part, v_at], masks) for part in parts]
        grads = [bdot_nt(go, value) for go, value in zip(gos, values)]
        probs = [p_ref[index, part, :] for part in parts]
        inner = [half_sums(grad * prob) for grad, prob in zip(grads, probs)]
        scores = [
            (prob * (grad - mean)).astype(bf16) for prob, grad, mean in zip(probs, grads, inner)
        ]
        keys = [stacked(qkv_ref[part, k_at], masks_q) for part in parts]
        qs = [qkv_ref[part, q_at] * factor for part in parts]
        grad_q = [bdot(score, key) for score, key in zip(scores, keys)]
        grad_k = [bdot_tn(score, q) for score, q in zip(scores, qs)]
        grad_v = [bdot_tn(prob.astype(bf16), go) for prob, go in zip(probs, gos)]
        for part, g_q, g_k, g_v in zip(parts, grad_q, grad_k, grad_v):
            dqkv_ref[part, q_at] = g_q.astype(bf16)
            dqkv_ref[part, k_at] = jnp.where(is_low, g_k[:frames], g_k[frames:]).astype(bf16)
            dqkv_ref[part, v_at] = jnp.where(is_low, g_v[:frames], g_v[frames:]).astype(bf16)
        return 0

    lax.fori_loop(0, HEADS // 2, time_pair_back, 0)
    e_ref[...] = bdot_nt(dqkv_ref[...], wti_ref[...])

    def step_five(step, _):
        place, part, flat = at_rows(step)
        grad = e_ref[flat, :]
        normed = n2_ref[flat, :]
        sum_ref[1, part, :] += grad
        sum_ref[2, part, :] += grad * normed
        grad_one = xa_ref[flat, :] + norm_rows_back(normed, r2_ref[flat, 0:1], mod(4, part), grad)
        dx1_ref[place, part, :] = grad_one
        sum_ref[0, part, :] += grad_one * y1_ref[flat, :]
        dy1_ref[flat, :] = (mod(2, part) * grad_one).astype(bf16)
        return 0

    lax.fori_loop(0, steps, step_five, 0)
    do1_ref[...] = bdot_nt(dy1_ref[...], wso_ref[...]).astype(bf16).reshape(count, frames, width)


VMEM_LIMIT = 62 * 1024 * 1024


def resident(shape):
    return pl.BlockSpec(shape, lambda i: (0,) * len(shape), pipeline_mode=pl.Buffered(1))


def call_space_forward(x, mods, weight):
    n_pos, own, places, width = x.shape
    patches = n_pos * places
    pair = 2 * HEAD_DIM
    spread = pl.BlockSpec((n_pos, 1, places, width), lambda i: (0, i, 0, 0))

    def by_frame(*shape):
        return pl.BlockSpec((1,) + shape, lambda i: (i, 0, 0))

    rows = own * patches
    return pl.pallas_call(
        space_forward,
        grid=(own,),
        in_specs=[spread, by_frame(2, width), resident(weight.shape)],
        out_specs=[
            by_frame(patches, width),
            by_frame(patches, 3 * width),
            pl.BlockSpec(memory_space=pl.ANY),
            pl.BlockSpec((1, HEADS // 2, patches, pair), lambda i: (i, 0, 0, 0)),
        ],
        out_shape=[
            jax.ShapeDtypeStruct((own, patches, width), bf16),
            jax.ShapeDtypeStruct((own, patches, 3 * width), bf16),
            jax.ShapeDtypeStruct((n_pos * own, places, width), bf16),
            jax.ShapeDtypeStruct((own, HEADS // 2, patches, pair), f32),
        ],
        scratch_shapes=spread_scratch(own, n_pos, places, width),
        compiler_params=pltpu.CompilerParams(
            vmem_limit_bytes=VMEM_LIMIT, collective_id=0, has_side_effects=True
        ),
        cost_estimate=pl.CostEstimate(
            flops=2 * rows * width * 3 * width + 4 * rows * patches * width,
            bytes_accessed=rows * width * 12 + weight.size * 2,
            transcendentals=rows * patches * HEADS,
        ),
        name="space_forward",
    )(x, mods, weight)


def call_space_backward(go, qkv, lse, x, h, mods, weight, hot, dmod_rest, grads, kinds, n_clip):
    n_pos, own, places, width = x.shape
    patches = n_pos * places
    pair = 2 * HEAD_DIM
    lead = n_pos.bit_length() - 1
    clips = dmod_rest.shape[0]
    spread = pl.BlockSpec((n_pos, 1, places, width), lambda i: (0, i, 0, 0))
    anywhere = pl.BlockSpec(memory_space=pl.ANY)

    def by_frame(*shape):
        return pl.BlockSpec((1,) + shape, lambda i: (i, 0, 0))

    rows = own * patches
    cut = 3 * width // 512 * 256
    late = [jax.ShapeDtypeStruct((width, cols), bf16) for cols in (cut, 3 * width - cut)]
    kinds = kinds + (True, False)
    views, flow_outs, flow_scratch = flow_plan(list(grads) + late, kinds, n_pos, n_clip)
    early = len(grads)
    sizes = sum(grad.size for grad in grads)
    dmod_shape = (n_clip, clips, 9 * width)
    swaps = lead + len(bits_of(n_clip))
    return pl.pallas_call(
        partial(space_backward, n_clip, kinds, early),
        grid=(own,),
        in_specs=[
            spread,
            by_frame(patches, 3 * width),
            pl.BlockSpec((1, HEADS // 2, patches, pair), lambda i: (i, 0, 0, 0)),
            spread,
            by_frame(patches, width),
            by_frame(2, width),
            resident(weight.shape),
            resident(hot.shape),
            resident(dmod_rest.shape),
        ]
        + [anywhere] * early,
        out_specs=[anywhere, resident(dmod_shape)] + [resident(out.shape) for out in flow_outs],
        out_shape=[
            jax.ShapeDtypeStruct((n_pos * own, places, width), bf16),
            jax.ShapeDtypeStruct(dmod_shape, f32),
        ]
        + flow_outs,
        scratch_shapes=[
            pltpu.VMEM((patches, width), f32),
            pltpu.VMEM((patches, 3 * width), bf16),
            pltpu.VMEM((width, 3 * width), f32),
            pltpu.VMEM((clips, 9 * width), f32),
            pltpu.VMEM((lead, clips, 9 * width), f32),
            pltpu.VMEM((lead, clips, 9 * width), f32),
            pltpu.VMEM(dmod_shape, f32),
            pltpu.SemaphoreType.DMA((swaps,)),
            pltpu.SemaphoreType.DMA((swaps,)),
        ]
        + spread_scratch(own, n_pos, places, width)
        + views[early:]
        + flow_scratch,
        compiler_params=pltpu.CompilerParams(
            vmem_limit_bytes=VMEM_LIMIT, collective_id=1, has_side_effects=True
        ),
        cost_estimate=pl.CostEstimate(
            flops=4 * rows * width * 3 * width + 10 * rows * patches * width,
            bytes_accessed=rows * width * 16 + weight.size * 2 + sizes * 4,
            transcendentals=rows * patches * HEADS,
        ),
        name="space_backward",
    )(go, qkv, lse, x, h, mods, weight, hot, dmod_rest, *views[:early])


def call_middle(o_one, x, grad, mods, same_clip, wso, wti, wto, wup, wdn):
    places, frames, width = x.shape
    count = max(1, min(places, 256 // frames))
    rows = count * frames
    hidden = wup.shape[1]
    pair = 2 * HEAD_DIM
    total = places * frames
    chunk = pl.BlockSpec((count, frames, width), lambda i: (i, 0, 0))

    def flat(cols):
        return pl.BlockSpec((rows, cols), lambda i: (i, 0))

    def flat_shape(cols):
        return jax.ShapeDtypeStruct((total, cols), bf16)

    def scratch(cols, dtype=f32):
        return pltpu.VMEM((rows, cols), dtype)

    lanes = jnp.concatenate([same_clip, same_clip], axis=1)
    flops = 2 * total * (2 * (wso.size + wti.size + wto.size + wup.size + wdn.size))
    return pl.pallas_call(
        middle,
        grid=(places // count,),
        in_specs=[chunk, chunk, chunk, resident(mods.shape), resident(lanes.shape)]
        + [resident(w.shape) for w in (wso, wti, wto, wup, wdn)],
        out_specs=[
            chunk,
            flat(hidden),
            flat(width),
            flat(width),
            flat(hidden),
            flat(width),
            flat(width),
            flat(width),
            flat(3 * width),
            flat(width),
            chunk,
            chunk,
            pl.BlockSpec((7, frames, width), lambda i: (0, 0, 0)),
        ],
        out_shape=[
            jax.ShapeDtypeStruct(x.shape, bf16),
            flat_shape(hidden),
            flat_shape(width),
            flat_shape(width),
            flat_shape(hidden),
            flat_shape(width),
            flat_shape(width),
            flat_shape(width),
            flat_shape(3 * width),
            flat_shape(width),
            jax.ShapeDtypeStruct(x.shape, bf16),
            jax.ShapeDtypeStruct(x.shape, f32),
            jax.ShapeDtypeStruct((7, frames, width), f32),
        ],
        scratch_shapes=[
            scratch(3 * width, bf16),
            pltpu.VMEM((HEADS // 2, rows, pair), f32),
            scratch(width),
            scratch(width),
            scratch(width),
            scratch(width),
            scratch(pair),
            scratch(pair),
            scratch(width),
            scratch(width),
        ]
        + [scratch(256)] * 4,
        compiler_params=pltpu.CompilerParams(vmem_limit_bytes=VMEM_LIMIT),
        cost_estimate=pl.CostEstimate(
            flops=flops, bytes_accessed=total * 40000, transcendentals=total * hidden
        ),
        name="middle",
    )(o_one, x, grad, mods, lanes, wso, wti, wto, wup, wdn)


def on_device(
    tokens,
    clip_lengths,
    timesteps,
    embed_first,
    embed_second,
    adaln_weight,
    spatial_in,
    spatial_out,
    temporal_in,
    temporal_out,
    hidden_up,
    hidden_down,
    grad_output,
    n_pos=16,
    n_clip=2,
):
    frames, places, width = tokens.shape
    rows = frames * places
    own = frames // n_pos
    patches = places * n_pos
    me = lax.axis_index("pos")
    clips = clip_lengths.shape[1]

    def exchange(values):
        sent = values.reshape(frames, places, width)
        got = lax.all_to_all(sent, "pos", split_axis=0, concat_axis=0, tiled=True)
        return got.reshape(n_pos, own, places, width)

    x_space = exchange(tokens)

    all_steps = by_distance(timesteps[0], "clip", n_clip)
    freq = frequency(all_steps)
    pre_cond = dot_exact(freq, embed_first)
    hidden_cond = jax.nn.silu(pre_cond)
    cond = dot_exact(hidden_cond, embed_second)
    cond_act = jax.nn.silu(cond)
    modulated = dot_exact(cond_act[:clips], adaln_weight)
    onehot, clip_ids = clip_onehot(clip_lengths[0], frames)
    per_frame = dot_high(onehot, modulated)
    own_frames = lax.dynamic_slice_in_dim(per_frame, me * own, own, 0)

    own_mods = own_frames[:, : 2 * width].reshape(own, 2, width)
    h_one, qkv_one, o_one, lse_one = call_space_forward(x_space, own_mods, spatial_in)

    def turn(values):
        return values.transpose(1, 0, 2)

    o_one = turn(o_one)
    mods = per_frame.reshape(frames, 9, width).transpose(1, 0, 2)
    same_clip = jnp.dot(onehot, onehot.T)
    (block_turned, act, grad_z, h_three, grad_u, o_two, grad_y_two, h_two, grad_qkv_two, grad_y_one, grad_o_one,
     grad_one, sums) = call_middle(
        o_one, turn(tokens), turn(grad_output), mods, same_clip, spatial_out, temporal_in, temporal_out,
        hidden_up, hidden_down,
    )
    block_out = turn(block_turned)
    grad_o_space = exchange(turn(grad_o_one))
    early = (
        weight_grad(h_three, grad_u),
        weight_grad(act, grad_z),
        weight_grad(h_two, grad_qkv_two),
        weight_grad(o_one.reshape(rows, width), grad_y_one),
        weight_grad(o_two, grad_y_two),
    )
    own_hot = lax.dynamic_slice_in_dim(onehot, me * own, own, 0)
    hot = jnp.broadcast_to(own_hot[:, :, None], (own, clips, 128))
    dmod_rest = dot_high(onehot.T, sums.transpose(1, 0, 2).reshape(frames, 7 * width))
    (
        back_places, dmod, g_hidden_up, g_hidden_down, g_temporal_in, g_spatial_out, g_temporal_out,
        in_low, in_high,
    ) = call_space_backward(
        grad_o_space, qkv_one, lse_one, x_space, h_one, own_mods, spatial_in, hot, dmod_rest,
        early, (False, True, True, True, True), n_clip,
    )
    grad_tokens = (turn(grad_one) + back_places.astype(f32)).astype(bf16)
    g_spatial_in = jnp.concatenate([in_low, in_high], axis=1)
    dmod = dmod.reshape(n_clip * clips, 9 * width)

    def own_columns(values):
        block = values.shape[1] // n_pos
        return lax.dynamic_slice_in_dim(values, me * block, block, 1)

    g_adaln = dot_high(own_columns(cond_act).T, dmod)
    grad_cond = dot_exact(dmod, adaln_weight.T) * silu_grad(cond)
    g_second = dot_high(own_columns(hidden_cond).T, grad_cond)
    grad_pre = dot_exact(grad_cond, embed_second.T) * silu_grad(pre_cond)
    g_first = dot_high(own_columns(freq).T, grad_pre)
    return (
        block_out,
        grad_tokens,
        g_first,
        g_second,
        g_adaln,
        g_spatial_in,
        g_spatial_out,
        g_temporal_in,
        g_temporal_out,
        g_hidden_up,
        g_hidden_down,
    )


def solution(mesh):
    in_specs = (
        P("clip", "pos", None),
        P("clip", None),
        P("clip", None),
        P(),
        P(),
        P(),
        P(),
        P(),
        P(),
        P(),
        P(),
        P(),
        P("clip", "pos", None),
    )
    out_specs = (P("clip", "pos", None),) * 2 + (P("pos", None),) * 9
    body = partial(on_device, n_pos=mesh.shape["pos"], n_clip=mesh.shape["clip"])
    return jax.shard_map(body, mesh=mesh, in_specs=in_specs, out_specs=out_specs, check_vma=False)
```

```python
from functools import partial
import math

import jax
import jax.numpy as jnp
from jax import lax
from jax.experimental import pallas as pl
from jax.experimental.pallas import tpu as pltpu
from jax.sharding import PartitionSpec as P

HEADS = 12
HEAD_DIM = 64
FREQ = 256

epsilon = 1e-06
highest = lax.Precision.HIGHEST
masked_score = -1000000000.0
f32 = jnp.float32
bf16 = jnp.bfloat16


def frequency(step_ids):
    half_width = FREQ // 2
    rate_table = jnp.exp(
        -math.log(10000.0) * jnp.arange(half_width, dtype=jnp.float32) / half_width
    )
    angles = step_ids.astype(jnp.float32)[:, None] * rate_table[None, :]
    return jnp.concatenate([jnp.cos(angles), jnp.sin(angles)], axis=1)


def dot_high(left, right):
    return jnp.dot(left, right, precision=highest, preferred_element_type=f32)


def silu_grad(values):
    gate = jax.nn.sigmoid(values)
    return gate * (1.0 + values * (1.0 - gate))


def clip_onehot(lengths, frames):
    clip_ends = jnp.cumsum(lengths)
    frame_ids = jnp.arange(frames, dtype=jnp.int32)
    clip_ids = jnp.sum((frame_ids[:, None] >= clip_ends[None, :]).astype(jnp.int32), axis=1)
    onehot = (clip_ids[:, None] == jnp.arange(lengths.shape[0], dtype=jnp.int32)[None, :]).astype(
        jnp.float32
    )
    return (onehot, clip_ids)


def weight_grad(left, right):
    return jnp.einsum("rd,rk->dk", left, right, preferred_element_type=f32).astype(bf16)


def bdot(left, right):
    return lax.dot_general(left, right, (((1,), (0,)), ((), ())), preferred_element_type=f32)


def bdot_nt(left, right):
    return lax.dot_general(left, right, (((1,), (1,)), ((), ())), preferred_element_type=f32)


def bdot_tn(left, right):
    return lax.dot_general(left, right, (((0,), (0,)), ((), ())), preferred_element_type=f32)


def norm_rows(values):
    width = values.shape[-1]
    centre = values - jnp.sum(values, axis=-1, keepdims=True) * (1.0 / width)
    spread = jnp.sum(centre * centre, axis=-1, keepdims=True) * (1.0 / width)
    inverse = lax.rsqrt(spread + epsilon)
    return centre * inverse, inverse


def norm_rows_back(normed, inverse, scale_vec, grad):
    width = grad.shape[-1]
    inner = grad * (1.0 + scale_vec)
    mean_one = jnp.sum(inner, axis=-1, keepdims=True) * (1.0 / width)
    mean_two = jnp.sum(inner * normed, axis=-1, keepdims=True) * (1.0 / width)
    return inverse * (inner - mean_one - normed * mean_two)


def pair_masks(scale):
    lanes = lax.broadcasted_iota(jnp.int32, (1, 2 * HEAD_DIM), 1)
    low_half = jnp.where(lanes < HEAD_DIM, scale, 0.0).astype(bf16)
    high_half = jnp.where(lanes < HEAD_DIM, 0.0, scale).astype(bf16)
    return low_half, high_half


ROWS = 32


def load_rows(ref, step):
    places, width = ref.shape[2:]
    count = max(1, ROWS // places)
    part = ref[pl.ds(step * count, count), 0].astype(f32)
    return part.reshape(count * places, width)


def swap(values, axis, size, bit):
    return lax.ppermute(values, axis, [(i, i ^ bit) for i in range(size)])


def bits_of(size):
    return [1 << i for i in range(size.bit_length() - 1)]


def by_distance(values, axis, size):
    for bit in bits_of(size):
        values = jnp.concatenate([values, swap(values, axis, size, bit)], axis=0)
    return values


def dot_exact(left, right):
    parts = []
    for _ in range(3):
        part = left.astype(bf16)
        parts.append(part)
        left = left - part.astype(f32)
    count = parts[0].shape[0]
    got = jnp.dot(jnp.concatenate(parts, axis=0), right, preferred_element_type=f32)
    return got[:count] + (got[count : 2 * count] + got[2 * count :])


def flow_stages(n_pos, n_clip, clip_first):
    pos = [("pos", bit, "halve") for bit in bits_of(n_pos)]
    clip = bits_of(n_clip)
    if not clip_first:
        return pos + [("clip", bit, "sum") for bit in clip]
    first = [("clip", clip[0], "columns")]
    last = [("clip", clip[0], "gather")]
    return pos[:1] + first + pos[1:] + [("clip", bit, "sum") for bit in clip[1:]] + last


def flow_shapes(stages, n_pos, block, cols):
    lead = n_pos.bit_length() - 1
    shapes = []
    for _, _, what in stages:
        if what == "halve":
            lead -= 1
        elif what == "columns":
            cols //= 2
        shapes.append((2,) * lead + (block, cols))
    return shapes


class Flow:
    def __init__(self, number, stages, grad, out, keep, gots, sems, place):
        self.number, self.stages = number, stages
        self.grad, self.out, self.keep, self.gots = grad, out, keep, gots
        self.send_sem, self.recv_sem, self.keep_sem = sems
        self.place = place

    def side(self, stage):
        axis, bit, _ = self.stages[stage]
        return lax.rem(self.place[axis] // bit, 2)

    def columns(self, side, width):
        return pl.ds(pl.multiple_of(side * width, width), width)

    def part(self, ref, stage, side):
        what = self.stages[stage][2]
        lead = len(ref.shape) - 2
        if what == "halve":
            return (slice(None),) * (lead - 1) + (side,)
        if what == "columns":
            half = ref.shape[-1] // 2
            return (slice(None),) * (lead + 1) + (self.columns(side, half),)
        return None

    def held(self, stage):
        if stage == 0:
            return self.grad
        return self.keep if stage == 1 else self.gots[stage - 1]

    def copy(self, stage):
        axis, bit, _ = self.stages[stage]
        side = self.side(stage)
        source = self.held(stage)
        at = self.part(source, stage, 1 - side)
        return pltpu.make_async_remote_copy(
            source if at is None else source.at[at],
            self.gots[stage],
            self.send_sem.at[self.number, stage],
            self.recv_sem.at[self.number, stage],
            device_id={axis: self.place[axis] + bit * (1 - 2 * side)},
            device_id_type=pl.DeviceIdType.MESH,
        )

    def own(self):
        at = self.part(self.grad, 0, self.side(0))
        return pltpu.make_async_copy(self.grad.at[at], self.keep, self.keep_sem.at[self.number])

    def start(self):
        self.copy(0).start()
        self.own().start()

    def take(self, stage):
        self.copy(stage).wait_recv()
        if stage == 0:
            self.own().wait()
        what = self.stages[stage][2]
        got = self.gots[stage]
        side = self.side(stage)
        last = stage == len(self.stages) - 1
        lead = len(got.shape) - 2
        if what == "gather":
            half = got.shape[-1]
            self.out[:, self.columns(side, half)] = self.held(stage)[...].astype(f32)
            self.out[:, self.columns(1 - side, half)] = got[...].astype(f32)
            return
        if last:
            self.out[...] = self.held(stage)[...].astype(f32) + got[...].astype(f32)
            return
        target = self.keep if stage == 0 else got

        def one(index, _):
            at = tuple(lax.rem(index // (1 << i), 2) for i in range(lead))
            if stage == 0:
                mine = self.keep[at]
            elif what == "halve":
                mine = self.held(stage)[at + (side,)]
            elif what == "columns":
                mine = self.held(stage)[at + (slice(None), self.columns(side, got.shape[-1]))]
            else:
                mine = self.held(stage)[at]
            target[at] = mine + got[at]
            return 0

        lax.fori_loop(0, 1 << lead, one, 0)
        self.copy(stage + 1).start()

    def finish(self):
        for stage in range(len(self.stages)):
            self.copy(stage).wait_send()


class Butterfly:
    def __init__(self, n_pos, n_clip, values, out, got, acc, sems, place):
        self.pos_bits, self.clip_bits = bits_of(n_pos), bits_of(n_clip)
        self.values, self.out, self.got, self.acc = values, out, got, acc
        self.send_sem, self.recv_sem = sems
        self.place = place
        self.count = len(self.pos_bits) + len(self.clip_bits)

    def copy(self, stage):
        if stage < len(self.pos_bits):
            axis, bit = "pos", self.pos_bits[stage]
            source = self.values if stage == 0 else self.acc.at[stage - 1]
            target = self.got.at[stage]
        else:
            axis, bit = "clip", self.clip_bits[stage - len(self.pos_bits)]
            source, target = self.out.at[pl.ds(0, bit)], self.out.at[pl.ds(bit, bit)]
        side = lax.rem(self.place[axis] // bit, 2)
        return pltpu.make_async_remote_copy(
            source,
            target,
            self.send_sem.at[stage],
            self.recv_sem.at[stage],
            device_id={axis: self.place[axis] + bit * (1 - 2 * side)},
            device_id_type=pl.DeviceIdType.MESH,
        )

    def start(self):
        self.copy(0).start()

    def take(self, stage):
        self.copy(stage).wait_recv()
        last = len(self.pos_bits) - 1
        if stage <= last:
            mine = self.values[...] if stage == 0 else self.acc[stage - 1]
            if stage < last:
                self.acc[stage] = mine + self.got[stage]
            else:
                self.out[0] = mine + self.got[stage]
        if stage + 1 < self.count:
            self.copy(stage + 1).start()

    def finish(self):
        for stage in range(self.count):
            self.copy(stage).wait_send()


def partner_list(n_pos, n_clip):
    return [("pos", bit) for bit in bits_of(n_pos)] + [("clip", bit) for bit in bits_of(n_clip)]


def here():
    return {"pos": lax.axis_index("pos"), "clip": lax.axis_index("clip")}


def signal_swap(barrier, place, axis, bit):
    side = lax.rem(place[axis] // bit, 2)
    pl.semaphore_signal(
        barrier,
        inc=1,
        device_id={axis: place[axis] + bit * (1 - 2 * side)},
        device_id_type=pl.DeviceIdType.MESH,
    )


def make_flows(n_pos, n_clip, kinds, grads, outs, scratch):
    sems, rest = scratch[:3], list(scratch[3:])
    flows = []
    for number, clip_first in enumerate(kinds):
        stages = flow_stages(n_pos, n_clip, clip_first)
        keep, gots = rest[0], rest[1 : 1 + len(stages)]
        rest = rest[1 + len(stages) :]
        flows.append(Flow(number, stages, grads[number], outs[number], keep, gots, sems, here()))
    return flows


def flow_plan(shapes, kinds, n_pos, n_clip):
    lead = n_pos.bit_length() - 1
    most = lead + len(bits_of(n_clip)) + 1
    dma = pltpu.SemaphoreType.DMA
    scratch = [dma((len(shapes), most)), dma((len(shapes), most)), dma((len(shapes),))]
    views, out_shape = [], []
    for (rows, cols), clip_first in zip(shapes, kinds):
        block = rows // n_pos
        views.append((2,) * lead + (block, cols))
        out_shape.append(jax.ShapeDtypeStruct((block, cols), f32))
        stages = flow_stages(n_pos, n_clip, clip_first)
        arrived = flow_shapes(stages, n_pos, block, cols)
        scratch += [pltpu.VMEM(shape, bf16) for shape in [arrived[0]] + arrived]
    return views, out_shape, scratch


class Spread:

    def __init__(self, n_pos, step, steps, hold, out, send_sem, recv_sem, own_sem):
        self.n_pos, self.step, self.steps = n_pos, step, steps
        self.hold, self.out = hold, out
        self.send_sem, self.recv_sem, self.own_sem = send_sem, recv_sem, own_sem
        self.me = lax.axis_index("pos")

    def greet(self, more=0):
        barrier = pltpu.get_barrier_semaphore()

        def signal(shift, _):
            target = lax.rem(self.me + shift, self.n_pos)
            pl.semaphore_signal(
                barrier, inc=1, device_id={"pos": target}, device_id_type=pl.DeviceIdType.MESH
            )
            return 0

        lax.fori_loop(1, self.n_pos, signal, 0)
        pl.semaphore_wait(barrier, self.n_pos - 1 + more)

    def copy(self, step, shift, source):
        target = lax.rem(self.me + shift, self.n_pos)
        return pltpu.make_async_remote_copy(
            self.hold.at[step, target],
            self.out.at[source * self.steps + step],
            self.send_sem.at[step, shift],
            self.recv_sem.at[step, shift],
            device_id={"pos": target},
            device_id_type=pl.DeviceIdType.MESH,
        )

    def stay(self, step):
        return pltpu.make_async_copy(
            self.hold.at[step, self.me],
            self.out.at[self.me * self.steps + step],
            self.own_sem.at[step],
        )

    def send(self):
        def one(shift, _):
            self.copy(self.step, shift, self.me).start()
            return 0

        lax.fori_loop(1, self.n_pos, one, 0)
        self.stay(self.step).start()

    def finish(self):
        def one_step(step, _):
            def one(shift, _):
                self.copy(step, shift, self.me).wait_send()
                source = lax.rem(self.me + self.n_pos - shift, self.n_pos)
                self.copy(step, shift, source).wait_recv()
                return 0

            lax.fori_loop(1, self.n_pos, one, 0)
            self.stay(step).wait()
            return 0

        lax.fori_loop(0, self.steps, one_step, 0)


def spread_scratch(own, n_pos, places, width):
    return [
        pltpu.VMEM((own, n_pos, places, width), bf16),
        pltpu.SemaphoreType.DMA((own, n_pos)),
        pltpu.SemaphoreType.DMA((own, n_pos)),
        pltpu.SemaphoreType.DMA((own,)),
    ]


def space_forward(
    x_ref, mod_ref, w_ref, h_ref, qkv_ref, o_ref, lse_ref, hold, send_sem, recv_sem, own_sem
):
    own, n_pos = hold.shape[:2]
    frame = pl.program_id(0)
    spread = Spread(n_pos, frame, own, hold, o_ref, send_sem, recv_sem, own_sem)
    pl.when(frame == 0)(spread.greet)
    patches, width = h_ref.shape[1:]
    places = x_ref.shape[2]
    pair = 2 * HEAD_DIM
    shift, scale = mod_ref[0, 0:1, :], mod_ref[0, 1:2, :]

    def norm_step(step, _):
        normed, _inverse = norm_rows(load_rows(x_ref, step))
        h_ref[0, pl.ds(step * ROWS, ROWS), :] = (normed * (1.0 + scale) + shift).astype(bf16)
        return 0

    lax.fori_loop(0, patches // ROWS, norm_step, 0)
    for part in range(3):
        cols = slice(part * width, (part + 1) * width)
        qkv_ref[0, :, cols] = bdot(h_ref[0], w_ref[:, cols]).astype(bf16)
    masks = pair_masks(1.0 / math.sqrt(HEAD_DIM))
    is_low = lax.broadcasted_iota(jnp.int32, (1, pair), 1) < HEAD_DIM

    def head_pair(index, _):
        at = pl.multiple_of(index * pair, pair)
        q = qkv_ref[0, :, pl.ds(at, pair)]
        k = qkv_ref[0, :, pl.ds(pl.multiple_of(width + at, pair), pair)]
        v = qkv_ref[0, :, pl.ds(pl.multiple_of(2 * width + at, pair), pair)]
        one = jnp.ones_like(v)
        values = [jnp.where(is_low, v, one), jnp.where(is_low, one, v)]
        scores = [bdot_nt(q * mask, k) for mask in masks]
        tops = [jnp.max(score, axis=-1, keepdims=True) for score in scores]
        exps = [jnp.exp(score - top).astype(bf16) for score, top in zip(scores, tops)]
        outs = [bdot(exp, value) for exp, value in zip(exps, values)]
        total = pltpu.roll(jnp.where(is_low, outs[1], outs[0]), HEAD_DIM, 1)
        both = jnp.where(is_low, outs[0], outs[1]) / total
        lse_ref[0, index] = jnp.where(is_low, tops[0], tops[1]) + jnp.log(total)
        hold[frame, :, :, pl.ds(at, pair)] = both.reshape(n_pos, places, pair).astype(bf16)
        return 0

    lax.fori_loop(0, HEADS // 2, head_pair, 0)
    spread.send()
    pl.when(frame == own - 1)(spread.finish)


def space_backward(n_clip, kinds, sources, *refs):
    go_ref, qkv_ref, lse_ref, x_ref, h_ref, mod_ref, w_ref, hot_ref, rest_ref = refs[:9]
    early = len(sources)
    arrays = 1 + max(source[0] for source in sources)
    whole, refs = refs[9 : 9 + arrays], refs[9 + arrays :]
    grads = []
    for at, first, cols in sources:
        ref = whole[at]
        if cols < ref.shape[-1]:
            ref = ref.at[(slice(None),) * (len(ref.shape) - 1) + (pl.ds(first, cols),)]
        grads.append(ref)
    dv_ref, dmod_ref = refs[:2]
    outs, refs = refs[2 : 2 + len(kinds)], refs[2 + len(kinds) :]
    e_ref, dqkv_ref, total_ref, small_ref, got_ref, acc_ref, every_ref = refs[:7]
    small_send, small_recv, hold, send_sem, recv_sem, own_sem = refs[7:13]
    late_grads, refs = refs[13 : 13 + len(kinds) - early], refs[13 + len(kinds) - early :]
    own, n_pos = hold.shape[:2]
    frame = pl.program_id(0)
    spread = Spread(n_pos, frame, own, hold, dv_ref, send_sem, recv_sem, own_sem)
    flows = make_flows(n_pos, n_clip, kinds, tuple(grads) + tuple(late_grads), outs, refs)
    late = flows[early:]
    tree = Butterfly(
        n_pos, n_clip, small_ref, every_ref, got_ref, acc_ref, (small_send, small_recv), here()
    )
    stages = max(len(flow.stages) for flow in flows)
    points = [
        [(0, 0)],
        [(1, 0)],
        [(i, 0) for i in range(2, early)],
        [],
        [(0, 1)],
        [(1, 1)],
        [(2, 1), (0, 2)],
    ][: 2 * own - 1]
    taken = [step for point in points for step in point]
    order = [(i, stage) for stage in range(stages) for i in range(early)]
    order = [step for step in order if step[1] < len(flows[step[0]].stages) and step not in taken]

    @pl.when(frame == 0)
    def _():
        place = here()
        others = [("clip", bit) for bit in bits_of(n_clip)]
        barrier = pltpu.get_barrier_semaphore()
        for axis, bit in others:
            signal_swap(barrier, place, axis, bit)
        spread.greet(len(others))
        for flow in flows[:early]:
            flow.start()
        total_ref[...] = jnp.zeros_like(total_ref)
        small_ref[:, : 2 * x_ref.shape[3]] = jnp.zeros_like(small_ref[:, : 2 * x_ref.shape[3]])
        small_ref[:, 2 * x_ref.shape[3] :] = rest_ref[...]

    def advance(steps):
        for i, stage in steps:
            flows[i].take(stage)

    def start_late():
        block = late_grads[0].shape[-2]
        lead = len(late_grads[0].shape) - 2

        def one(index, _):
            at = tuple(lax.rem(index // (1 << i), 2) for i in reversed(range(lead)))
            rows = pl.ds(pl.multiple_of(index * block, 8), block)
            first = 0
            for grad in late_grads:
                cols = grad.shape[-1]
                grad[at] = total_ref[rows, first : first + cols].astype(bf16)
                first += cols
            return 0

        lax.fori_loop(0, n_pos, one, 0)
        for flow in late:
            flow.start()

    patches = qkv_ref.shape[1]
    width = x_ref.shape[3]
    places = x_ref.shape[2]
    pair = 2 * HEAD_DIM
    scale = mod_ref[0, 1:2, :]
    factor = 1.0 / math.sqrt(HEAD_DIM)
    masks_q = pair_masks(factor)
    masks = pair_masks(1.0)
    ones = jnp.ones((patches, pair), bf16)

    def key_sums(values):
        high = values.astype(bf16)
        low = (values - high.astype(f32)).astype(bf16)
        total = bdot(high, ones) + bdot(low, ones)
        return jnp.concatenate([total] * (patches // pair), axis=1)

    def head_pair(index, _):
        at = pl.multiple_of(index * pair, pair)
        k_at = pl.multiple_of(width + at, pair)
        v_at = pl.multiple_of(2 * width + at, pair)
        q = qkv_ref[0, :, pl.ds(at, pair)]
        k = qkv_ref[0, :, pl.ds(k_at, pair)]
        v = qkv_ref[0, :, pl.ds(v_at, pair)]
        go = go_ref[:, 0, :, pl.ds(at, pair)].astype(f32).reshape(patches, pair).astype(bf16)
        lse_pair = lse_ref[0, index]
        lses = [lse_pair[:, 0:1], lse_pair[:, HEAD_DIM : HEAD_DIM + 1]]
        q_halves = [q * mask for mask in masks_q]
        go_halves = [go * mask for mask in masks]
        probs = [jnp.exp(bdot_nt(half, k) - lse) for half, lse in zip(q_halves, lses)]
        grads = [bdot_nt(half, v) for half in go_halves]
        inner = [key_sums(grad * prob) for grad, prob in zip(grads, probs)]
        scores = [
            (prob * (grad - mean)).astype(bf16) for prob, grad, mean in zip(probs, grads, inner)
        ]
        gq = sum(bdot(score, k * mask) for score, mask in zip(scores, masks_q))
        gk = sum(bdot_tn(score, half) for score, half in zip(scores, q_halves))
        gv = sum(bdot_tn(prob.astype(bf16), half) for prob, half in zip(probs, go_halves))
        dqkv_ref[:, pl.ds(at, pair)] = gq.astype(bf16)
        dqkv_ref[:, pl.ds(k_at, pair)] = gk.astype(bf16)
        dqkv_ref[:, pl.ds(v_at, pair)] = gv.astype(bf16)
        return 0

    lax.fori_loop(0, HEADS // 2, head_pair, 0)
    for index in range(own):
        pl.when(frame == index)(partial(advance, points[2 * index]))
    e_ref[...] = bdot_nt(dqkv_ref[...], w_ref[...])

    def norm_step(step, sums):
        grad = e_ref[pl.ds(step * ROWS, ROWS), :]
        normed, inverse = norm_rows(load_rows(x_ref, step))
        back = norm_rows_back(normed, inverse, scale, grad)
        count = max(1, ROWS // places)
        back = back.reshape(count, places, width).astype(bf16)
        hold[frame, pl.ds(step * count, count)] = back
        folded = grad.reshape(ROWS // 8, 8, width).sum(axis=0)
        folded_n = (grad * normed).reshape(ROWS // 8, 8, width).sum(axis=0)
        return sums[0] + folded, sums[1] + folded_n

    zero = jnp.zeros((8, width), f32)
    shift_sum, scale_sum = lax.fori_loop(0, patches // ROWS, norm_step, (zero, zero))
    spread.send()
    hot = hot_ref[frame][:, 0:1]
    small_ref[:, :width] += hot * jnp.sum(shift_sum, axis=0, keepdims=True)
    small_ref[:, width : 2 * width] += hot * jnp.sum(scale_sum, axis=0, keepdims=True)
    for third in range(3):
        cols = slice(third * width, (third + 1) * width)
        total_ref[:, cols] += bdot_tn(h_ref[0], dqkv_ref[:, cols])
    for index in range(own - 1):
        pl.when(frame == index)(partial(advance, points[2 * index + 1]))

    @pl.when(frame == own - 1)
    def _():
        tree.start()
        start_late()
        for stage in range(stages + 1):
            mine = [step for step in order if step[1] == stage]
            advance([step for step in mine if step[0] > 1])
            if stage < tree.count:
                tree.take(stage)
            for flow in late:
                if 0 <= stage - 1 < len(flow.stages):
                    flow.take(stage - 1)
            advance([step for step in mine if step[0] <= 1])
        dmod_ref[...] = every_ref[...]
        spread.finish()
        tree.finish()
        for flow in flows:
            flow.finish()


GELU_C = math.sqrt(2.0 / math.pi)


def middle(
    o1_ref, x_ref, g_ref, mod_ref, clip_ref, wso_ref, wti_ref, wto_ref, wup_ref, wdn_ref,
    out_ref, act_ref, dz_ref, h3_ref, du_ref, o2_ref, dy2_ref, h2_ref, dqkv_ref, dy1_ref, do1_ref,
    dx1_ref, sum_ref,
    qkv_ref, p_ref, y1_ref, y2_ref, n2_ref, n3_ref, r2_ref, r3_ref, xa_ref, e_ref,
    ua_ref, aa_ref, ub_ref, ab_ref,
):
    count, frames, width = x_ref.shape
    rows = count * frames
    pair = 2 * HEAD_DIM
    hidden = act_ref.shape[1]
    factor = 1.0 / math.sqrt(HEAD_DIM)
    per = frames // ROWS
    steps = rows // ROWS

    @pl.when(pl.program_id(0) == 0)
    def _():
        sum_ref[...] = jnp.zeros_like(sum_ref)

    def at_rows(step):
        return step // per, pl.ds(lax.rem(step, per) * ROWS, ROWS), pl.ds(step * ROWS, ROWS)

    def mod(index, part):
        return mod_ref[index, part, :]

    y1_ref[...] = bdot(o1_ref[...].reshape(rows, width), wso_ref[...])

    def step_one(step, _):
        place, part, flat = at_rows(step)
        x_one = x_ref[place, part, :].astype(f32) + mod(2, part) * y1_ref[flat, :]
        xa_ref[flat, :] = x_one
        normed, inverse = norm_rows(x_one)
        n2_ref[flat, :] = normed
        r2_ref[flat, :] = jnp.broadcast_to(inverse, (ROWS, pair))
        h2_ref[flat, :] = (normed * (1.0 + mod(4, part)) + mod(3, part)).astype(bf16)
        return 0

    lax.fori_loop(0, steps, step_one, 0)
    for third in range(3):
        cols = slice(third * width, (third + 1) * width)
        qkv_ref[:, cols] = bdot(h2_ref[...], wti_ref[:, cols]).astype(bf16)

    masks = pair_masks(1.0)
    masks_q = pair_masks(factor)
    lane_ids = lax.broadcasted_iota(jnp.int32, (1, pair), 1)
    is_low = lane_ids < HEAD_DIM
    allowed = clip_ref[...] > 0.5

    def halves(values, reduce, neutral):
        low_part = reduce(jnp.where(is_low, values, neutral), axis=-1, keepdims=True)
        high_part = reduce(jnp.where(is_low, neutral, values), axis=-1, keepdims=True)
        return jnp.where(is_low, low_part, high_part)

    def stacked(values, pair_of_masks):
        return jnp.concatenate([values * pair_of_masks[0], values * pair_of_masks[1]], axis=0)

    def pair_at(index):
        at = pl.multiple_of(index * pair, pair)
        return (
            pl.ds(at, pair),
            pl.ds(pl.multiple_of(width + at, pair), pair),
            pl.ds(pl.multiple_of(2 * width + at, pair), pair),
        )

    parts = [slice(place * frames, (place + 1) * frames) for place in range(count)]
    same_half = (
        lax.broadcasted_iota(jnp.int32, (pair, pair), 0) // HEAD_DIM
        == lax.broadcasted_iota(jnp.int32, (pair, pair), 1) // HEAD_DIM
    )
    ones = jnp.where(same_half, 1.0, 0.0).astype(bf16)

    def half_sums(values):
        high = values.astype(bf16)
        low = (values - high.astype(f32)).astype(bf16)
        return bdot(high, ones) + bdot(low, ones)

    def time_pair(index, _):
        jobs = [(2 * index + i, part) + pair_at(2 * index + i) for i in range(2) for part in parts]
        keys = [stacked(qkv_ref[part, k_at], masks_q) for _i, part, q_at, k_at, v_at in jobs]
        scores = [bdot_nt(qkv_ref[job[1], job[2]], key) for job, key in zip(jobs, keys)]
        scores = [jnp.where(allowed, score, masked_score) for score in scores]
        tops = [halves(score, jnp.max, -jnp.inf) for score in scores]
        exps = [jnp.exp(score - top) for score, top in zip(scores, tops)]
        sums = [half_sums(exp) for exp in exps]
        probs = [exp / total for exp, total in zip(exps, sums)]
        values = [stacked(qkv_ref[job[1], job[4]], masks) for job in jobs]
        outs = [bdot(prob.astype(bf16), value) for prob, value in zip(probs, values)]
        for (i, part, q_at, _k, _v), prob, out in zip(jobs, probs, outs):
            p_ref[i, part, :] = prob
            o2_ref[part, q_at] = out.astype(bf16)
        return 0

    lax.fori_loop(0, HEADS // 4, time_pair, 0)

    y2_ref[...] = bdot(o2_ref[...], wto_ref[...])

    def step_two(step, _):
        place, part, flat = at_rows(step)
        x_two = xa_ref[flat, :] + mod(5, part) * y2_ref[flat, :]
        xa_ref[flat, :] = x_two
        normed, inverse = norm_rows(x_two)
        n3_ref[flat, :] = normed
        r3_ref[flat, :] = jnp.broadcast_to(inverse, (ROWS, pair))
        h3_ref[flat, :] = (normed * (1.0 + mod(7, part)) + mod(6, part)).astype(bf16)
        dz_ref[flat, :] = (mod(8, part) * g_ref[place, part, :].astype(f32)).astype(bf16)
        return 0

    lax.fori_loop(0, steps, step_two, 0)

    tile = 256

    def products(index, u_ref, a_ref):
        cols = pl.ds(pl.multiple_of(index * tile, tile), tile)
        u_ref[...] = bdot(h3_ref[...], wup_ref[:, cols])
        a_ref[...] = bdot_nt(dz_ref[...], wdn_ref[cols, :])

    def pointwise(index, u_ref, a_ref):
        cols = pl.ds(pl.multiple_of(index * tile, tile), tile)
        u = u_ref[...]
        square = u * u
        half = 0.5 + 0.5 * jnp.tanh(u * (GELU_C + (0.044715 * GELU_C) * square))
        value = u * half
        act_ref[:, cols] = value.astype(bf16)
        slope = half + (value - value * half) * (2.0 * GELU_C + (6.0 * 0.044715 * GELU_C) * square)
        du_ref[:, cols] = (a_ref[...] * slope).astype(bf16)

    tiles = hidden // tile

    def two_tiles(index, _):
        products(2 * index + 1, ub_ref, ab_ref)
        pointwise(2 * index, ua_ref, aa_ref)
        products(jnp.minimum(2 * index + 2, tiles - 1), ua_ref, aa_ref)
        pointwise(2 * index + 1, ub_ref, ab_ref)
        return 0

    products(0, ua_ref, aa_ref)
    lax.fori_loop(0, tiles // 2, two_tiles, 0)
    e_ref[...] = bdot(act_ref[...], wdn_ref[...])

    def step_three(step, _):
        place, part, flat = at_rows(step)
        z = e_ref[flat, :]
        grad = g_ref[place, part, :].astype(f32)
        out_ref[place, part, :] = (xa_ref[flat, :] + mod(8, part) * z).astype(bf16)
        sum_ref[6, part, :] += grad * z
        return 0

    lax.fori_loop(0, steps, step_three, 0)
    e_ref[...] = bdot_nt(du_ref[...], wup_ref[...])

    def step_four(step, _):
        place, part, flat = at_rows(step)
        grad = e_ref[flat, :]
        normed = n3_ref[flat, :]
        sum_ref[4, part, :] += grad
        sum_ref[5, part, :] += grad * normed
        back = norm_rows_back(normed, r3_ref[flat, 0:1], mod(7, part), grad)
        grad_two = g_ref[place, part, :].astype(f32) + back
        xa_ref[flat, :] = grad_two
        sum_ref[3, part, :] += grad_two * y2_ref[flat, :]
        dy2_ref[flat, :] = (mod(5, part) * grad_two).astype(bf16)
        return 0

    lax.fori_loop(0, steps, step_four, 0)
    y2_ref[...] = bdot_nt(dy2_ref[...], wto_ref[...])

    def time_pair_back(index, _):
        q_at, k_at, v_at = pair_at(index)
        gos = [y2_ref[part, q_at].astype(bf16) for part in parts]
        values = [stacked(qkv_ref[part, v_at], masks) for part in parts]
        grads = [bdot_nt(go, value) for go, value in zip(gos, values)]
        probs = [p_ref[index, part, :] for part in parts]
        inner = [half_sums(grad * prob) for grad, prob in zip(grads, probs)]
        scores = [
            (prob * (grad - mean)).astype(bf16) for prob, grad, mean in zip(probs, grads, inner)
        ]
        keys = [stacked(qkv_ref[part, k_at], masks_q) for part in parts]
        qs = [qkv_ref[part, q_at] * factor for part in parts]
        grad_q = [bdot(score, key) for score, key in zip(scores, keys)]
        grad_k = [bdot_tn(score, q) for score, q in zip(scores, qs)]
        grad_v = [bdot_tn(prob.astype(bf16), go) for prob, go in zip(probs, gos)]
        for part, g_q, g_k, g_v in zip(parts, grad_q, grad_k, grad_v):
            dqkv_ref[part, q_at] = g_q.astype(bf16)
            dqkv_ref[part, k_at] = jnp.where(is_low, g_k[:frames], g_k[frames:]).astype(bf16)
            dqkv_ref[part, v_at] = jnp.where(is_low, g_v[:frames], g_v[frames:]).astype(bf16)
        return 0

    lax.fori_loop(0, HEADS // 2, time_pair_back, 0)
    e_ref[...] = bdot_nt(dqkv_ref[...], wti_ref[...])

    def step_five(step, _):
        place, part, flat = at_rows(step)
        grad = e_ref[flat, :]
        normed = n2_ref[flat, :]
        sum_ref[1, part, :] += grad
        sum_ref[2, part, :] += grad * normed
        grad_one = xa_ref[flat, :] + norm_rows_back(normed, r2_ref[flat, 0:1], mod(4, part), grad)
        dx1_ref[place, part, :] = grad_one
        sum_ref[0, part, :] += grad_one * y1_ref[flat, :]
        dy1_ref[flat, :] = (mod(2, part) * grad_one).astype(bf16)
        return 0

    lax.fori_loop(0, steps, step_five, 0)
    do1_ref[...] = bdot_nt(dy1_ref[...], wso_ref[...]).astype(bf16).reshape(count, frames, width)


VMEM_LIMIT = 62 * 1024 * 1024


def resident(shape):
    return pl.BlockSpec(shape, lambda i: (0,) * len(shape), pipeline_mode=pl.Buffered(1))


def call_space_forward(x, mods, weight):
    n_pos, own, places, width = x.shape
    patches = n_pos * places
    pair = 2 * HEAD_DIM
    spread = pl.BlockSpec((n_pos, 1, places, width), lambda i: (0, i, 0, 0))

    def by_frame(*shape):
        return pl.BlockSpec((1,) + shape, lambda i: (i, 0, 0))

    rows = own * patches
    return pl.pallas_call(
        space_forward,
        grid=(own,),
        in_specs=[spread, by_frame(2, width), resident(weight.shape)],
        out_specs=[
            by_frame(patches, width),
            by_frame(patches, 3 * width),
            pl.BlockSpec(memory_space=pl.ANY),
            pl.BlockSpec((1, HEADS // 2, patches, pair), lambda i: (i, 0, 0, 0)),
        ],
        out_shape=[
            jax.ShapeDtypeStruct((own, patches, width), bf16),
            jax.ShapeDtypeStruct((own, patches, 3 * width), bf16),
            jax.ShapeDtypeStruct((n_pos * own, places, width), bf16),
            jax.ShapeDtypeStruct((own, HEADS // 2, patches, pair), f32),
        ],
        scratch_shapes=spread_scratch(own, n_pos, places, width),
        compiler_params=pltpu.CompilerParams(
            vmem_limit_bytes=VMEM_LIMIT, collective_id=0, has_side_effects=True
        ),
        cost_estimate=pl.CostEstimate(
            flops=2 * rows * width * 3 * width + 4 * rows * patches * width,
            bytes_accessed=rows * width * 12 + weight.size * 2,
            transcendentals=rows * patches * HEADS,
        ),
        name="space_forward",
    )(x, mods, weight)


def call_space_backward(go, qkv, lse, x, h, mods, weight, hot, dmod_rest, grads, early, n_clip):
    n_pos, own, places, width = x.shape
    patches = n_pos * places
    pair = 2 * HEAD_DIM
    lead = n_pos.bit_length() - 1
    clips = dmod_rest.shape[0]
    spread = pl.BlockSpec((n_pos, 1, places, width), lambda i: (0, i, 0, 0))
    anywhere = pl.BlockSpec(memory_space=pl.ANY)

    def by_frame(*shape):
        return pl.BlockSpec((1,) + shape, lambda i: (i, 0, 0))

    rows = own * patches
    cut = 3 * width // 512 * 256
    kinds = tuple(flow[3] for flow in early) + (True, False)
    sources = tuple(flow[:3] for flow in early)
    shapes = [(grads[at].shape[0], cols) for at, _, cols in sources]
    shapes += [(width, cut), (width, 3 * width - cut)]
    views, flow_outs, flow_scratch = flow_plan(shapes, kinds, n_pos, n_clip)
    late = [pltpu.VMEM(view, bf16) for view in views[len(early) :]]
    blocked = [
        grad.reshape((2,) * lead + (grad.shape[0] // n_pos, grad.shape[1])) for grad in grads
    ]
    sizes = sum(grad.size for grad in grads)
    dmod_shape = (n_clip, clips, 9 * width)
    swaps = lead + len(bits_of(n_clip))
    return pl.pallas_call(
        partial(space_backward, n_clip, kinds, sources),
        grid=(own,),
        in_specs=[
            spread,
            by_frame(patches, 3 * width),
            pl.BlockSpec((1, HEADS // 2, patches, pair), lambda i: (i, 0, 0, 0)),
            spread,
            by_frame(patches, width),
            by_frame(2, width),
            resident(weight.shape),
            resident(hot.shape),
            resident(dmod_rest.shape),
        ]
        + [anywhere] * len(blocked),
        out_specs=[anywhere, resident(dmod_shape)] + [resident(out.shape) for out in flow_outs],
        out_shape=[
            jax.ShapeDtypeStruct((n_pos * own, places, width), bf16),
            jax.ShapeDtypeStruct(dmod_shape, f32),
        ]
        + flow_outs,
        scratch_shapes=[
            pltpu.VMEM((patches, width), f32),
            pltpu.VMEM((patches, 3 * width), bf16),
            pltpu.VMEM((width, 3 * width), f32),
            pltpu.VMEM((clips, 9 * width), f32),
            pltpu.VMEM((lead, clips, 9 * width), f32),
            pltpu.VMEM((lead, clips, 9 * width), f32),
            pltpu.VMEM(dmod_shape, f32),
            pltpu.SemaphoreType.DMA((swaps,)),
            pltpu.SemaphoreType.DMA((swaps,)),
        ]
        + spread_scratch(own, n_pos, places, width)
        + late
        + flow_scratch,
        compiler_params=pltpu.CompilerParams(
            vmem_limit_bytes=VMEM_LIMIT, collective_id=1, has_side_effects=True
        ),
        cost_estimate=pl.CostEstimate(
            flops=4 * rows * width * 3 * width + 10 * rows * patches * width,
            bytes_accessed=rows * width * 16 + weight.size * 2 + sizes * 4,
            transcendentals=rows * patches * HEADS,
        ),
        name="space_backward",
    )(go, qkv, lse, x, h, mods, weight, hot, dmod_rest, *blocked)


def call_middle(o_one, x, grad, mods, same_clip, wso, wti, wto, wup, wdn):
    places, frames, width = x.shape
    count = max(1, min(places, 256 // frames))
    rows = count * frames
    hidden = wup.shape[1]
    pair = 2 * HEAD_DIM
    total = places * frames
    chunk = pl.BlockSpec((count, frames, width), lambda i: (i, 0, 0))

    def flat(cols):
        return pl.BlockSpec((rows, cols), lambda i: (i, 0))

    def flat_shape(cols):
        return jax.ShapeDtypeStruct((total, cols), bf16)

    def scratch(cols, dtype=f32):
        return pltpu.VMEM((rows, cols), dtype)

    lanes = jnp.concatenate([same_clip, same_clip], axis=1)
    flops = 2 * total * (2 * (wso.size + wti.size + wto.size + wup.size + wdn.size))
    return pl.pallas_call(
        middle,
        grid=(places // count,),
        in_specs=[chunk, chunk, chunk, resident(mods.shape), resident(lanes.shape)]
        + [resident(w.shape) for w in (wso, wti, wto, wup, wdn)],
        out_specs=[
            chunk,
            flat(hidden),
            flat(width),
            flat(width),
            flat(hidden),
            flat(width),
            flat(width),
            flat(width),
            flat(3 * width),
            flat(width),
            chunk,
            chunk,
            pl.BlockSpec((7, frames, width), lambda i: (0, 0, 0)),
        ],
        out_shape=[
            jax.ShapeDtypeStruct(x.shape, bf16),
            flat_shape(hidden),
            flat_shape(width),
            flat_shape(width),
            flat_shape(hidden),
            flat_shape(width),
            flat_shape(width),
            flat_shape(width),
            flat_shape(3 * width),
            flat_shape(width),
            jax.ShapeDtypeStruct(x.shape, bf16),
            jax.ShapeDtypeStruct(x.shape, f32),
            jax.ShapeDtypeStruct((7, frames, width), f32),
        ],
        scratch_shapes=[
            scratch(3 * width, bf16),
            pltpu.VMEM((HEADS // 2, rows, pair), f32),
            scratch(width),
            scratch(width),
            scratch(width),
            scratch(width),
            scratch(pair),
            scratch(pair),
            scratch(width),
            scratch(width),
        ]
        + [scratch(256)] * 4,
        compiler_params=pltpu.CompilerParams(vmem_limit_bytes=VMEM_LIMIT),
        cost_estimate=pl.CostEstimate(
            flops=flops, bytes_accessed=total * 40000, transcendentals=total * hidden
        ),
        name="middle",
    )(o_one, x, grad, mods, lanes, wso, wti, wto, wup, wdn)


def on_device(
    tokens,
    clip_lengths,
    timesteps,
    embed_first,
    embed_second,
    adaln_weight,
    spatial_in,
    spatial_out,
    temporal_in,
    temporal_out,
    hidden_up,
    hidden_down,
    grad_output,
    n_pos=16,
    n_clip=2,
):
    frames, places, width = tokens.shape
    rows = frames * places
    own = frames // n_pos
    patches = places * n_pos
    me = lax.axis_index("pos")
    clips = clip_lengths.shape[1]

    def exchange(values):
        sent = values.reshape(frames, places, width)
        got = lax.all_to_all(sent, "pos", split_axis=0, concat_axis=0, tiled=True)
        return got.reshape(n_pos, own, places, width)

    x_space = exchange(tokens)

    all_steps = by_distance(timesteps[0], "clip", n_clip)
    freq = frequency(all_steps)
    pre_cond = dot_exact(freq, embed_first)
    hidden_cond = jax.nn.silu(pre_cond)
    cond = dot_exact(hidden_cond, embed_second)
    cond_act = jax.nn.silu(cond)
    modulated = dot_exact(cond_act[:clips], adaln_weight)
    onehot, clip_ids = clip_onehot(clip_lengths[0], frames)
    per_frame = dot_high(onehot, modulated)
    own_frames = lax.dynamic_slice_in_dim(per_frame, me * own, own, 0)

    own_mods = own_frames[:, : 2 * width].reshape(own, 2, width)
    h_one, qkv_one, o_one, lse_one = call_space_forward(x_space, own_mods, spatial_in)

    def turn(values):
        return values.transpose(1, 0, 2)

    o_one = turn(o_one)
    mods = per_frame.reshape(frames, 9, width).transpose(1, 0, 2)
    same_clip = jnp.dot(onehot, onehot.T)
    (block_turned, act, grad_z, h_three, grad_u, o_two, grad_y_two, h_two, grad_qkv_two, grad_y_one, grad_o_one,
     grad_one, sums) = call_middle(
        o_one, turn(tokens), turn(grad_output), mods, same_clip, spatial_out, temporal_in, temporal_out,
        hidden_up, hidden_down,
    )
    block_out = turn(block_turned)
    grad_o_space = exchange(turn(grad_o_one))
    grads = (
        weight_grad(h_three, grad_u),
        weight_grad(act, grad_z),
        weight_grad(h_two, grad_qkv_two),
        weight_grad(o_one.reshape(rows, width), grad_y_one),
        weight_grad(o_two, grad_y_two),
    )
    cut = 3 * width // 512 * 256
    early = (
        (0, 0, grads[0].shape[1], False),
        (1, 0, width, True),
        (2, cut, 3 * width - cut, False),
        (2, 0, cut, True),
        (3, 0, width, True),
        (4, 0, width, True),
    )
    own_hot = lax.dynamic_slice_in_dim(onehot, me * own, own, 0)
    hot = jnp.broadcast_to(own_hot[:, :, None], (own, clips, 128))
    dmod_rest = dot_high(onehot.T, sums.transpose(1, 0, 2).reshape(frames, 7 * width))
    (
        back_places, dmod, g_hidden_up, g_hidden_down, time_high, time_low, g_spatial_out,
        g_temporal_out, in_low, in_high,
    ) = call_space_backward(
        grad_o_space, qkv_one, lse_one, x_space, h_one, own_mods, spatial_in, hot, dmod_rest,
        grads, early, n_clip,
    )
    grad_tokens = (turn(grad_one) + back_places.astype(f32)).astype(bf16)
    g_spatial_in = jnp.concatenate([in_low, in_high], axis=1)
    g_temporal_in = jnp.concatenate([time_low, time_high], axis=1)
    dmod = dmod.reshape(n_clip * clips, 9 * width)

    def own_columns(values):
        block = values.shape[1] // n_pos
        return lax.dynamic_slice_in_dim(values, me * block, block, 1)

    g_adaln = dot_high(own_columns(cond_act).T, dmod)
    grad_cond = dot_exact(dmod, adaln_weight.T) * silu_grad(cond)
    g_second = dot_high(own_columns(hidden_cond).T, grad_cond)
    grad_pre = dot_exact(grad_cond, embed_second.T) * silu_grad(pre_cond)
    g_first = dot_high(own_columns(freq).T, grad_pre)
    return (
        block_out,
        grad_tokens,
        g_first,
        g_second,
        g_adaln,
        g_spatial_in,
        g_spatial_out,
        g_temporal_in,
        g_temporal_out,
        g_hidden_up,
        g_hidden_down,
    )


def solution(mesh):
    in_specs = (
        P("clip", "pos", None),
        P("clip", None),
        P("clip", None),
        P(),
        P(),
        P(),
        P(),
        P(),
        P(),
        P(),
        P(),
        P(),
        P("clip", "pos", None),
    )
    out_specs = (P("clip", "pos", None),) * 2 + (P("pos", None),) * 9
    body = partial(on_device, n_pos=mesh.shape["pos"], n_clip=mesh.shape["clip"])
    return jax.shard_map(body, mesh=mesh, in_specs=in_specs, out_specs=out_specs, check_vma=False)
```

```python
from functools import partial
import math

import jax
import jax.numpy as jnp
from jax import lax
from jax.experimental import pallas as pl
from jax.experimental.pallas import tpu as pltpu
from jax.sharding import PartitionSpec as P

HEADS = 12
HEAD_DIM = 64
FREQ = 256

epsilon = 1e-06
highest = lax.Precision.HIGHEST
masked_score = -1000000000.0
f32 = jnp.float32
bf16 = jnp.bfloat16


def frequency(step_ids):
    half_width = FREQ // 2
    rate_table = jnp.exp(
        -math.log(10000.0) * jnp.arange(half_width, dtype=jnp.float32) / half_width
    )
    angles = step_ids.astype(jnp.float32)[:, None] * rate_table[None, :]
    return jnp.concatenate([jnp.cos(angles), jnp.sin(angles)], axis=1)


def dot_high(left, right):
    return jnp.dot(left, right, precision=highest, preferred_element_type=f32)


def silu_grad(values):
    gate = jax.nn.sigmoid(values)
    return gate * (1.0 + values * (1.0 - gate))


def clip_onehot(lengths, frames):
    clip_ends = jnp.cumsum(lengths)
    frame_ids = jnp.arange(frames, dtype=jnp.int32)
    clip_ids = jnp.sum((frame_ids[:, None] >= clip_ends[None, :]).astype(jnp.int32), axis=1)
    onehot = (clip_ids[:, None] == jnp.arange(lengths.shape[0], dtype=jnp.int32)[None, :]).astype(
        jnp.float32
    )
    return (onehot, clip_ids)


def weight_grad(left, right):
    return jnp.einsum("rd,rk->dk", left, right, preferred_element_type=f32).astype(bf16)


def bdot(left, right):
    return lax.dot_general(left, right, (((1,), (0,)), ((), ())), preferred_element_type=f32)


def bdot_nt(left, right):
    return lax.dot_general(left, right, (((1,), (1,)), ((), ())), preferred_element_type=f32)


def bdot_tn(left, right):
    return lax.dot_general(left, right, (((0,), (0,)), ((), ())), preferred_element_type=f32)


def norm_rows(values):
    width = values.shape[-1]
    centre = values - jnp.sum(values, axis=-1, keepdims=True) * (1.0 / width)
    spread = jnp.sum(centre * centre, axis=-1, keepdims=True) * (1.0 / width)
    inverse = lax.rsqrt(spread + epsilon)
    return centre * inverse, inverse


def norm_rows_back(normed, inverse, scale_vec, grad):
    width = grad.shape[-1]
    inner = grad * (1.0 + scale_vec)
    mean_one = jnp.sum(inner, axis=-1, keepdims=True) * (1.0 / width)
    mean_two = jnp.sum(inner * normed, axis=-1, keepdims=True) * (1.0 / width)
    return inverse * (inner - mean_one - normed * mean_two)


def pair_masks(scale):
    lanes = lax.broadcasted_iota(jnp.int32, (1, 2 * HEAD_DIM), 1)
    low_half = jnp.where(lanes < HEAD_DIM, scale, 0.0).astype(bf16)
    high_half = jnp.where(lanes < HEAD_DIM, 0.0, scale).astype(bf16)
    return low_half, high_half


ROWS = 32


def load_rows(ref, step):
    places, width = ref.shape[2:]
    count = max(1, ROWS // places)
    part = ref[pl.ds(step * count, count), 0].astype(f32)
    return part.reshape(count * places, width)


def swap(values, axis, size, bit):
    return lax.ppermute(values, axis, [(i, i ^ bit) for i in range(size)])


def bits_of(size):
    return [1 << i for i in range(size.bit_length() - 1)]


def by_distance(values, axis, size):
    for bit in bits_of(size):
        values = jnp.concatenate([values, swap(values, axis, size, bit)], axis=0)
    return values


def dot_exact(left, right):
    parts = []
    for _ in range(3):
        part = left.astype(bf16)
        parts.append(part)
        left = left - part.astype(f32)
    count = parts[0].shape[0]
    got = jnp.dot(jnp.concatenate(parts, axis=0), right, preferred_element_type=f32)
    return got[:count] + (got[count : 2 * count] + got[2 * count :])


def flow_stages(n_pos, n_clip, clip_first):
    pos = [("pos", bit, "halve") for bit in bits_of(n_pos)]
    clip = bits_of(n_clip)
    if not clip_first:
        return pos + [("clip", bit, "sum") for bit in clip]
    first = [("clip", clip[0], "columns")]
    last = [("clip", clip[0], "gather")]
    return pos[:1] + first + pos[1:] + [("clip", bit, "sum") for bit in clip[1:]] + last


def flow_shapes(stages, n_pos, block, cols):
    lead = n_pos.bit_length() - 1
    shapes = []
    for _, _, what in stages:
        if what == "halve":
            lead -= 1
        elif what == "columns":
            cols //= 2
        shapes.append((2,) * lead + (block, cols))
    return shapes


class Flow:
    def __init__(self, number, stages, grad, out, keep, gots, sems, place):
        self.number, self.stages = number, stages
        self.grad, self.out, self.keep, self.gots = grad, out, keep, gots
        self.send_sem, self.recv_sem, self.keep_sem = sems
        self.place = place

    def side(self, stage):
        axis, bit, _ = self.stages[stage]
        return lax.rem(self.place[axis] // bit, 2)

    def columns(self, side, width):
        return pl.ds(pl.multiple_of(side * width, width), width)

    def part(self, ref, stage, side):
        what = self.stages[stage][2]
        lead = len(ref.shape) - 2
        if what == "halve":
            return (slice(None),) * (lead - 1) + (side,)
        if what == "columns":
            half = ref.shape[-1] // 2
            return (slice(None),) * (lead + 1) + (self.columns(side, half),)
        return None

    def held(self, stage):
        if stage == 0:
            return self.grad
        return self.keep if stage == 1 else self.gots[stage - 1]

    def copy(self, stage):
        axis, bit, _ = self.stages[stage]
        side = self.side(stage)
        source = self.held(stage)
        at = self.part(source, stage, 1 - side)
        return pltpu.make_async_remote_copy(
            source if at is None else source.at[at],
            self.gots[stage],
            self.send_sem.at[self.number, stage],
            self.recv_sem.at[self.number, stage],
            device_id={axis: self.place[axis] + bit * (1 - 2 * side)},
            device_id_type=pl.DeviceIdType.MESH,
        )

    def own(self):
        at = self.part(self.grad, 0, self.side(0))
        return pltpu.make_async_copy(self.grad.at[at], self.keep, self.keep_sem.at[self.number])

    def start(self):
        self.copy(0).start()
        self.own().start()

    def take(self, stage):
        self.copy(stage).wait_recv()
        if stage == 0:
            self.own().wait()
        what = self.stages[stage][2]
        got = self.gots[stage]
        side = self.side(stage)
        last = stage == len(self.stages) - 1
        lead = len(got.shape) - 2
        if what == "gather":
            half = got.shape[-1]
            self.out[:, self.columns(side, half)] = self.held(stage)[...].astype(f32)
            self.out[:, self.columns(1 - side, half)] = got[...].astype(f32)
            return
        if last:
            self.out[...] = self.held(stage)[...].astype(f32) + got[...].astype(f32)
            return
        target = self.keep if stage == 0 else got

        def one(index, _):
            at = tuple(lax.rem(index // (1 << i), 2) for i in range(lead))
            if stage == 0:
                mine = self.keep[at]
            elif what == "halve":
                mine = self.held(stage)[at + (side,)]
            elif what == "columns":
                mine = self.held(stage)[at + (slice(None), self.columns(side, got.shape[-1]))]
            else:
                mine = self.held(stage)[at]
            target[at] = mine + got[at]
            return 0

        lax.fori_loop(0, 1 << lead, one, 0)
        self.copy(stage + 1).start()

    def finish(self):
        for stage in range(len(self.stages)):
            self.copy(stage).wait_send()


class Butterfly:
    def __init__(self, n_pos, n_clip, values, out, got, acc, sems, place):
        self.pos_bits, self.clip_bits = bits_of(n_pos), bits_of(n_clip)
        self.values, self.out, self.got, self.acc = values, out, got, acc
        self.send_sem, self.recv_sem = sems
        self.place = place
        self.count = len(self.pos_bits) + len(self.clip_bits)

    def copy(self, stage):
        if stage < len(self.pos_bits):
            axis, bit = "pos", self.pos_bits[stage]
            source = self.values if stage == 0 else self.acc.at[stage - 1]
            target = self.got.at[stage]
        else:
            axis, bit = "clip", self.clip_bits[stage - len(self.pos_bits)]
            source, target = self.out.at[pl.ds(0, bit)], self.out.at[pl.ds(bit, bit)]
        side = lax.rem(self.place[axis] // bit, 2)
        return pltpu.make_async_remote_copy(
            source,
            target,
            self.send_sem.at[stage],
            self.recv_sem.at[stage],
            device_id={axis: self.place[axis] + bit * (1 - 2 * side)},
            device_id_type=pl.DeviceIdType.MESH,
        )

    def start(self):
        self.copy(0).start()

    def take(self, stage):
        self.copy(stage).wait_recv()
        last = len(self.pos_bits) - 1
        if stage <= last:
            mine = self.values[...] if stage == 0 else self.acc[stage - 1]
            if stage < last:
                self.acc[stage] = mine + self.got[stage]
            else:
                self.out[0] = mine + self.got[stage]
        if stage + 1 < self.count:
            self.copy(stage + 1).start()

    def finish(self):
        for stage in range(self.count):
            self.copy(stage).wait_send()


def partner_list(n_pos, n_clip):
    return [("pos", bit) for bit in bits_of(n_pos)] + [("clip", bit) for bit in bits_of(n_clip)]


def here():
    return {"pos": lax.axis_index("pos"), "clip": lax.axis_index("clip")}


def signal_swap(barrier, place, axis, bit):
    side = lax.rem(place[axis] // bit, 2)
    pl.semaphore_signal(
        barrier,
        inc=1,
        device_id={axis: place[axis] + bit * (1 - 2 * side)},
        device_id_type=pl.DeviceIdType.MESH,
    )


def make_flows(n_pos, n_clip, kinds, grads, outs, scratch):
    sems, rest = scratch[:3], list(scratch[3:])
    flows = []
    for number, clip_first in enumerate(kinds):
        stages = flow_stages(n_pos, n_clip, clip_first)
        keep, gots = rest[0], rest[1 : 1 + len(stages)]
        rest = rest[1 + len(stages) :]
        flows.append(Flow(number, stages, grads[number], outs[number], keep, gots, sems, here()))
    return flows


def flow_plan(grads, kinds, n_pos, n_clip):
    lead = n_pos.bit_length() - 1
    most = lead + len(bits_of(n_clip)) + 1
    dma = pltpu.SemaphoreType.DMA
    scratch = [dma((len(grads), most)), dma((len(grads), most)), dma((len(grads),))]
    views, out_shape = [], []
    for grad, clip_first in zip(grads, kinds):
        rows, cols = grad.shape
        block = rows // n_pos
        if isinstance(grad, jax.ShapeDtypeStruct):
            views.append(pltpu.VMEM((2,) * lead + (block, cols), bf16))
        else:
            views.append(grad.reshape((2,) * lead + (block, cols)))
        out_shape.append(jax.ShapeDtypeStruct((block, cols), f32))
        shapes = flow_shapes(flow_stages(n_pos, n_clip, clip_first), n_pos, block, cols)
        scratch += [pltpu.VMEM(shape, bf16) for shape in [shapes[0]] + shapes]
    return views, out_shape, scratch


class Spread:

    def __init__(self, n_pos, step, steps, hold, out, send_sem, recv_sem, own_sem):
        self.n_pos, self.step, self.steps = n_pos, step, steps
        self.hold, self.out = hold, out
        self.send_sem, self.recv_sem, self.own_sem = send_sem, recv_sem, own_sem
        self.me = lax.axis_index("pos")

    def greet(self, more=0):
        barrier = pltpu.get_barrier_semaphore()

        def signal(shift, _):
            target = lax.rem(self.me + shift, self.n_pos)
            pl.semaphore_signal(
                barrier, inc=1, device_id={"pos": target}, device_id_type=pl.DeviceIdType.MESH
            )
            return 0

        lax.fori_loop(1, self.n_pos, signal, 0)
        pl.semaphore_wait(barrier, self.n_pos - 1 + more)

    def copy(self, step, shift, source):
        target = lax.rem(self.me + shift, self.n_pos)
        return pltpu.make_async_remote_copy(
            self.hold.at[step, target],
            self.out.at[source * self.steps + step],
            self.send_sem.at[step, shift],
            self.recv_sem.at[step, shift],
            device_id={"pos": target},
            device_id_type=pl.DeviceIdType.MESH,
        )

    def stay(self, step):
        return pltpu.make_async_copy(
            self.hold.at[step, self.me],
            self.out.at[self.me * self.steps + step],
            self.own_sem.at[step],
        )

    def send(self):
        def one(shift, _):
            self.copy(self.step, shift, self.me).start()
            return 0

        lax.fori_loop(1, self.n_pos, one, 0)
        self.stay(self.step).start()

    def finish(self):
        def one_step(step, _):
            def one(shift, _):
                self.copy(step, shift, self.me).wait_send()
                source = lax.rem(self.me + self.n_pos - shift, self.n_pos)
                self.copy(step, shift, source).wait_recv()
                return 0

            lax.fori_loop(1, self.n_pos, one, 0)
            self.stay(step).wait()
            return 0

        lax.fori_loop(0, self.steps, one_step, 0)


def spread_scratch(own, n_pos, places, width):
    return [
        pltpu.VMEM((own, n_pos, places, width), bf16),
        pltpu.SemaphoreType.DMA((own, n_pos)),
        pltpu.SemaphoreType.DMA((own, n_pos)),
        pltpu.SemaphoreType.DMA((own,)),
    ]


def space_forward(
    x_ref, mod_ref, w_ref, h_ref, qkv_ref, o_ref, lse_ref, hold, send_sem, recv_sem, own_sem
):
    own, n_pos = hold.shape[:2]
    frame = pl.program_id(0)
    spread = Spread(n_pos, frame, own, hold, o_ref, send_sem, recv_sem, own_sem)
    pl.when(frame == 0)(spread.greet)
    patches, width = h_ref.shape[1:]
    places = x_ref.shape[2]
    pair = 2 * HEAD_DIM
    shift, scale = mod_ref[0, 0:1, :], mod_ref[0, 1:2, :]

    def norm_step(step, _):
        normed, _inverse = norm_rows(load_rows(x_ref, step))
        h_ref[0, pl.ds(step * ROWS, ROWS), :] = (normed * (1.0 + scale) + shift).astype(bf16)
        return 0

    lax.fori_loop(0, patches // ROWS, norm_step, 0)

    def project(third, _):
        cols = pl.ds(pl.multiple_of(third * width, width), width)
        qkv_ref[0, :, cols] = bdot(h_ref[0], w_ref[:, cols]).astype(bf16)
        return 0

    lax.fori_loop(0, 3, project, 0)
    masks = pair_masks(1.0 / math.sqrt(HEAD_DIM))
    is_low = lax.broadcasted_iota(jnp.int32, (1, pair), 1) < HEAD_DIM

    def head_pair(index, _):
        at = pl.multiple_of(index * pair, pair)
        q = qkv_ref[0, :, pl.ds(at, pair)]
        k = qkv_ref[0, :, pl.ds(pl.multiple_of(width + at, pair), pair)]
        v = qkv_ref[0, :, pl.ds(pl.multiple_of(2 * width + at, pair), pair)]
        one = jnp.ones_like(v)
        values = [jnp.where(is_low, v, one), jnp.where(is_low, one, v)]
        scores = [bdot_nt(q * mask, k) for mask in masks]
        tops = [jnp.max(score, axis=-1, keepdims=True) for score in scores]
        exps = [jnp.exp(score - top).astype(bf16) for score, top in zip(scores, tops)]
        outs = [bdot(exp, value) for exp, value in zip(exps, values)]
        total = pltpu.roll(jnp.where(is_low, outs[1], outs[0]), HEAD_DIM, 1)
        both = jnp.where(is_low, outs[0], outs[1]) / total
        lse_ref[0, index] = jnp.where(is_low, tops[0], tops[1]) + jnp.log(total)
        hold[frame, :, :, pl.ds(at, pair)] = both.reshape(n_pos, places, pair).astype(bf16)
        return 0

    lax.fori_loop(0, HEADS // 2, head_pair, 0)
    spread.send()
    pl.when(frame == own - 1)(spread.finish)


def space_backward(n_clip, kinds, early, *refs):
    go_ref, qkv_ref, lse_ref, x_ref, h_ref, mod_ref, w_ref, hot_ref, rest_ref = refs[:9]
    grads, refs = refs[9 : 9 + early], refs[9 + early :]
    dv_ref, dmod_ref = refs[:2]
    outs, refs = refs[2 : 2 + len(kinds)], refs[2 + len(kinds) :]
    e_ref, dqkv_ref, total_ref, small_ref, got_ref, acc_ref, every_ref = refs[:7]
    small_send, small_recv, hold, send_sem, recv_sem, own_sem = refs[7:13]
    late_grads, refs = refs[13 : 13 + len(kinds) - early], refs[13 + len(kinds) - early :]
    own, n_pos = hold.shape[:2]
    frame = pl.program_id(0)
    spread = Spread(n_pos, frame, own, hold, dv_ref, send_sem, recv_sem, own_sem)
    flows = make_flows(n_pos, n_clip, kinds, tuple(grads) + tuple(late_grads), outs, refs)
    late = flows[early:]
    tree = Butterfly(
        n_pos, n_clip, small_ref, every_ref, got_ref, acc_ref, (small_send, small_recv), here()
    )
    stages = max(len(flow.stages) for flow in flows)
    order = [(i, stage) for stage in range(stages) for i in range(early)]
    order = [(i, stage) for i, stage in order if stage < len(flows[i].stages)]
    cuts = [2, early, early + 2]

    @pl.when(frame == 0)
    def _():
        place = here()
        others = [("clip", bit) for bit in bits_of(n_clip)]
        barrier = pltpu.get_barrier_semaphore()
        for axis, bit in others:
            signal_swap(barrier, place, axis, bit)
        spread.greet(len(others))
        for flow in flows[:early]:
            flow.start()

        def clear(step, _):
            total_ref[pl.ds(step * 8, 8), :] = jnp.zeros((8, total_ref.shape[1]), f32)
            return 0

        lax.fori_loop(0, total_ref.shape[0] // 8, clear, 0)
        small_ref[:, : 2 * x_ref.shape[3]] = jnp.zeros_like(small_ref[:, : 2 * x_ref.shape[3]])
        small_ref[:, 2 * x_ref.shape[3] :] = rest_ref[...]

    def advance(steps):
        for i, stage in steps:
            flows[i].take(stage)

    def start_late():
        block = late_grads[0].shape[-2]
        lead = len(late_grads[0].shape) - 2

        def one(index, _):
            at = tuple(lax.rem(index // (1 << i), 2) for i in reversed(range(lead)))
            rows = pl.ds(pl.multiple_of(index * block, 8), block)
            first = 0
            for grad in late_grads:
                cols = grad.shape[-1]
                grad[at] = total_ref[rows, first : first + cols].astype(bf16)
                first += cols
            return 0

        lax.fori_loop(0, n_pos, one, 0)
        for flow in late:
            flow.start()

    patches = qkv_ref.shape[1]
    width = x_ref.shape[3]
    places = x_ref.shape[2]
    pair = 2 * HEAD_DIM
    scale = mod_ref[0, 1:2, :]
    factor = 1.0 / math.sqrt(HEAD_DIM)
    masks_q = pair_masks(factor)
    masks = pair_masks(1.0)
    ones = jnp.ones((patches, pair), bf16)

    def key_sums(values):
        high = values.astype(bf16)
        low = (values - high.astype(f32)).astype(bf16)
        total = bdot(high, ones) + bdot(low, ones)
        return jnp.concatenate([total] * (patches // pair), axis=1)

    def head_pair(index, _):
        at = pl.multiple_of(index * pair, pair)
        k_at = pl.multiple_of(width + at, pair)
        v_at = pl.multiple_of(2 * width + at, pair)
        q = qkv_ref[0, :, pl.ds(at, pair)]
        k = qkv_ref[0, :, pl.ds(k_at, pair)]
        v = qkv_ref[0, :, pl.ds(v_at, pair)]
        go = go_ref[:, 0, :, pl.ds(at, pair)].astype(f32).reshape(patches, pair).astype(bf16)
        lse_pair = lse_ref[0, index]
        lses = [lse_pair[:, 0:1], lse_pair[:, HEAD_DIM : HEAD_DIM + 1]]
        q_halves = [q * mask for mask in masks_q]
        go_halves = [go * mask for mask in masks]
        probs = [jnp.exp(bdot_nt(half, k) - lse) for half, lse in zip(q_halves, lses)]
        grads = [bdot_nt(half, v) for half in go_halves]
        inner = [key_sums(grad * prob) for grad, prob in zip(grads, probs)]
        scores = [
            (prob * (grad - mean)).astype(bf16) for prob, grad, mean in zip(probs, grads, inner)
        ]
        gq = sum(bdot(score, k * mask) for score, mask in zip(scores, masks_q))
        gk = sum(bdot_tn(score, half) for score, half in zip(scores, q_halves))
        gv = sum(bdot_tn(prob.astype(bf16), half) for prob, half in zip(probs, go_halves))
        dqkv_ref[:, pl.ds(at, pair)] = gq.astype(bf16)
        dqkv_ref[:, pl.ds(k_at, pair)] = gk.astype(bf16)
        dqkv_ref[:, pl.ds(v_at, pair)] = gv.astype(bf16)
        return 0

    lax.fori_loop(0, HEADS // 2, head_pair, 0)
    e_ref[...] = bdot_nt(dqkv_ref[...], w_ref[...])

    def norm_step(step, sums):
        grad = e_ref[pl.ds(step * ROWS, ROWS), :]
        normed, inverse = norm_rows(load_rows(x_ref, step))
        back = norm_rows_back(normed, inverse, scale, grad)
        count = max(1, ROWS // places)
        back = back.reshape(count, places, width).astype(bf16)
        hold[frame, pl.ds(step * count, count)] = back
        folded = grad.reshape(ROWS // 8, 8, width).sum(axis=0)
        folded_n = (grad * normed).reshape(ROWS // 8, 8, width).sum(axis=0)
        return sums[0] + folded, sums[1] + folded_n

    zero = jnp.zeros((8, width), f32)
    shift_sum, scale_sum = lax.fori_loop(0, patches // ROWS, norm_step, (zero, zero))
    spread.send()
    hot = hot_ref[frame][:, 0:1]
    small_ref[:, :width] += hot * jnp.sum(shift_sum, axis=0, keepdims=True)
    small_ref[:, width : 2 * width] += hot * jnp.sum(scale_sum, axis=0, keepdims=True)

    def accumulate(third, _):
        cols = pl.ds(pl.multiple_of(third * width, width), width)
        total_ref[:, cols] += bdot_tn(h_ref[0], dqkv_ref[:, cols])
        return 0

    lax.fori_loop(0, 3, accumulate, 0)
    done = 0
    for index, cut in enumerate(cuts[: own - 1]):
        pl.when(frame == index)(partial(advance, order[done:cut]))
        done = cut

    @pl.when(frame == own - 1)
    def _():
        tree.start()
        start_late()
        left = order[done:]
        for turn in range(stages):
            mine = [step for step in left if step[1] == turn + 1]
            if turn > 0:
                advance([step for step in mine if step[0] < 2])
            if turn < tree.count:
                tree.take(turn)
            for flow in late:
                if turn < len(flow.stages):
                    flow.take(turn)
            advance([step for step in mine if turn == 0 or step[0] >= 2])
        dmod_ref[...] = every_ref[...]
        spread.finish()
        tree.finish()
        for flow in flows:
            flow.finish()


GELU_C = math.sqrt(2.0 / math.pi)


def middle(
    o1_ref, x_ref, g_ref, mod_ref, clip_ref, wso_ref, wti_ref, wto_ref, wup_ref, wdn_ref,
    out_ref, act_ref, dz_ref, h3_ref, du_ref, o2_ref, dy2_ref, h2_ref, dqkv_ref, dy1_ref, do1_ref,
    dx1_ref, sum_ref,
    qkv_ref, p_ref, y1_ref, y2_ref, n2_ref, n3_ref, r2_ref, r3_ref, xa_ref, e_ref,
    ua_ref, aa_ref, ub_ref, ab_ref,
):
    count, frames, width = x_ref.shape
    rows = count * frames
    pair = 2 * HEAD_DIM
    hidden = act_ref.shape[1]
    factor = 1.0 / math.sqrt(HEAD_DIM)
    per = frames // ROWS
    steps = rows // ROWS

    @pl.when(pl.program_id(0) == 0)
    def _():
        sum_ref[...] = jnp.zeros_like(sum_ref)

    def at_rows(step):
        return step // per, pl.ds(lax.rem(step, per) * ROWS, ROWS), pl.ds(step * ROWS, ROWS)

    def mod(index, part):
        return mod_ref[index, part, :]

    y1_ref[...] = bdot(o1_ref[...].reshape(rows, width), wso_ref[...])

    def step_one(step, _):
        place, part, flat = at_rows(step)
        x_one = x_ref[place, part, :].astype(f32) + mod(2, part) * y1_ref[flat, :]
        xa_ref[flat, :] = x_one
        normed, inverse = norm_rows(x_one)
        n2_ref[flat, :] = normed
        r2_ref[flat, :] = jnp.broadcast_to(inverse, (ROWS, pair))
        h2_ref[flat, :] = (normed * (1.0 + mod(4, part)) + mod(3, part)).astype(bf16)
        return 0

    lax.fori_loop(0, steps, step_one, 0)

    def project(third, _):
        cols = pl.ds(pl.multiple_of(third * width, width), width)
        qkv_ref[:, cols] = bdot(h2_ref[...], wti_ref[:, cols]).astype(bf16)
        return 0

    lax.fori_loop(0, 3, project, 0)

    masks = pair_masks(1.0)
    masks_q = pair_masks(factor)
    lane_ids = lax.broadcasted_iota(jnp.int32, (1, pair), 1)
    is_low = lane_ids < HEAD_DIM
    allowed = clip_ref[...] > 0.5

    def halves(values, reduce, neutral):
        low_part = reduce(jnp.where(is_low, values, neutral), axis=-1, keepdims=True)
        high_part = reduce(jnp.where(is_low, neutral, values), axis=-1, keepdims=True)
        return jnp.where(is_low, low_part, high_part)

    def stacked(values, pair_of_masks):
        return jnp.concatenate([values * pair_of_masks[0], values * pair_of_masks[1]], axis=0)

    def pair_at(index):
        at = pl.multiple_of(index * pair, pair)
        return (
            pl.ds(at, pair),
            pl.ds(pl.multiple_of(width + at, pair), pair),
            pl.ds(pl.multiple_of(2 * width + at, pair), pair),
        )

    parts = [slice(place * frames, (place + 1) * frames) for place in range(count)]
    same_half = (
        lax.broadcasted_iota(jnp.int32, (pair, pair), 0) // HEAD_DIM
        == lax.broadcasted_iota(jnp.int32, (pair, pair), 1) // HEAD_DIM
    )
    ones = jnp.where(same_half, 1.0, 0.0).astype(bf16)

    def half_sums(values):
        high = values.astype(bf16)
        low = (values - high.astype(f32)).astype(bf16)
        return bdot(high, ones) + bdot(low, ones)

    def time_pair(index, _):
        jobs = [(2 * index + i, part) + pair_at(2 * index + i) for i in range(2) for part in parts]
        keys = [stacked(qkv_ref[part, k_at], masks_q) for _i, part, q_at, k_at, v_at in jobs]
        scores = [bdot_nt(qkv_ref[job[1], job[2]], key) for job, key in zip(jobs, keys)]
        scores = [jnp.where(allowed, score, masked_score) for score in scores]
        tops = [halves(score, jnp.max, -jnp.inf) for score in scores]
        exps = [jnp.exp(score - top) for score, top in zip(scores, tops)]
        sums = [half_sums(exp) for exp in exps]
        probs = [exp / total for exp, total in zip(exps, sums)]
        values = [stacked(qkv_ref[job[1], job[4]], masks) for job in jobs]
        outs = [bdot(prob.astype(bf16), value) for prob, value in zip(probs, values)]
        for (i, part, q_at, _k, _v), prob, out in zip(jobs, probs, outs):
            p_ref[i, part, :] = prob
            o2_ref[part, q_at] = out.astype(bf16)
        return 0

    lax.fori_loop(0, HEADS // 4, time_pair, 0)

    y2_ref[...] = bdot(o2_ref[...], wto_ref[...])

    def step_two(step, _):
        place, part, flat = at_rows(step)
        x_two = xa_ref[flat, :] + mod(5, part) * y2_ref[flat, :]
        xa_ref[flat, :] = x_two
        normed, inverse = norm_rows(x_two)
        n3_ref[flat, :] = normed
        r3_ref[flat, :] = jnp.broadcast_to(inverse, (ROWS, pair))
        h3_ref[flat, :] = (normed * (1.0 + mod(7, part)) + mod(6, part)).astype(bf16)
        dz_ref[flat, :] = (mod(8, part) * g_ref[place, part, :].astype(f32)).astype(bf16)
        return 0

    lax.fori_loop(0, steps, step_two, 0)

    tile = 256

    def products(index, u_ref, a_ref):
        cols = pl.ds(pl.multiple_of(index * tile, tile), tile)
        u_ref[...] = bdot(h3_ref[...], wup_ref[:, cols])
        a_ref[...] = bdot_nt(dz_ref[...], wdn_ref[cols, :])

    def pointwise(index, u_ref, a_ref):
        cols = pl.ds(pl.multiple_of(index * tile, tile), tile)
        u = u_ref[...]
        square = u * u
        half = 0.5 + 0.5 * jnp.tanh(u * (GELU_C + (0.044715 * GELU_C) * square))
        value = u * half
        act_ref[:, cols] = value.astype(bf16)
        slope = half + (value - value * half) * (2.0 * GELU_C + (6.0 * 0.044715 * GELU_C) * square)
        du_ref[:, cols] = (a_ref[...] * slope).astype(bf16)

    tiles = hidden // tile

    def two_tiles(index, _):
        products(2 * index + 1, ub_ref, ab_ref)
        pointwise(2 * index, ua_ref, aa_ref)
        products(jnp.minimum(2 * index + 2, tiles - 1), ua_ref, aa_ref)
        pointwise(2 * index + 1, ub_ref, ab_ref)
        return 0

    products(0, ua_ref, aa_ref)
    lax.fori_loop(0, tiles // 2, two_tiles, 0)
    e_ref[...] = bdot(act_ref[...], wdn_ref[...])

    def step_three(step, _):
        place, part, flat = at_rows(step)
        z = e_ref[flat, :]
        grad = g_ref[place, part, :].astype(f32)
        out_ref[place, part, :] = (xa_ref[flat, :] + mod(8, part) * z).astype(bf16)
        sum_ref[6, part, :] += grad * z
        return 0

    lax.fori_loop(0, steps, step_three, 0)
    e_ref[...] = bdot_nt(du_ref[...], wup_ref[...])

    def step_four(step, _):
        place, part, flat = at_rows(step)
        grad = e_ref[flat, :]
        normed = n3_ref[flat, :]
        sum_ref[4, part, :] += grad
        sum_ref[5, part, :] += grad * normed
        back = norm_rows_back(normed, r3_ref[flat, 0:1], mod(7, part), grad)
        grad_two = g_ref[place, part, :].astype(f32) + back
        xa_ref[flat, :] = grad_two
        sum_ref[3, part, :] += grad_two * y2_ref[flat, :]
        dy2_ref[flat, :] = (mod(5, part) * grad_two).astype(bf16)
        return 0

    lax.fori_loop(0, steps, step_four, 0)
    y2_ref[...] = bdot_nt(dy2_ref[...], wto_ref[...])

    def time_pair_back(index, _):
        q_at, k_at, v_at = pair_at(index)
        gos = [y2_ref[part, q_at].astype(bf16) for part in parts]
        values = [stacked(qkv_ref[part, v_at], masks) for part in parts]
        grads = [bdot_nt(go, value) for go, value in zip(gos, values)]
        probs = [p_ref[index, part, :] for part in parts]
        inner = [half_sums(grad * prob) for grad, prob in zip(grads, probs)]
        scores = [
            (prob * (grad - mean)).astype(bf16) for prob, grad, mean in zip(probs, grads, inner)
        ]
        keys = [stacked(qkv_ref[part, k_at], masks_q) for part in parts]
        qs = [qkv_ref[part, q_at] * factor for part in parts]
        grad_q = [bdot(score, key) for score, key in zip(scores, keys)]
        grad_k = [bdot_tn(score, q) for score, q in zip(scores, qs)]
        grad_v = [bdot_tn(prob.astype(bf16), go) for prob, go in zip(probs, gos)]
        for part, g_q, g_k, g_v in zip(parts, grad_q, grad_k, grad_v):
            dqkv_ref[part, q_at] = g_q.astype(bf16)
            dqkv_ref[part, k_at] = jnp.where(is_low, g_k[:frames], g_k[frames:]).astype(bf16)
            dqkv_ref[part, v_at] = jnp.where(is_low, g_v[:frames], g_v[frames:]).astype(bf16)
        return 0

    lax.fori_loop(0, HEADS // 2, time_pair_back, 0)
    e_ref[...] = bdot_nt(dqkv_ref[...], wti_ref[...])

    def step_five(step, _):
        place, part, flat = at_rows(step)
        grad = e_ref[flat, :]
        normed = n2_ref[flat, :]
        sum_ref[1, part, :] += grad
        sum_ref[2, part, :] += grad * normed
        grad_one = xa_ref[flat, :] + norm_rows_back(normed, r2_ref[flat, 0:1], mod(4, part), grad)
        dx1_ref[place, part, :] = grad_one
        sum_ref[0, part, :] += grad_one * y1_ref[flat, :]
        dy1_ref[flat, :] = (mod(2, part) * grad_one).astype(bf16)
        return 0

    lax.fori_loop(0, steps, step_five, 0)
    do1_ref[...] = bdot_nt(dy1_ref[...], wso_ref[...]).astype(bf16).reshape(count, frames, width)


VMEM_LIMIT = 62 * 1024 * 1024


def resident(shape):
    return pl.BlockSpec(shape, lambda i: (0,) * len(shape), pipeline_mode=pl.Buffered(1))


def call_space_forward(x, mods, weight):
    n_pos, own, places, width = x.shape
    patches = n_pos * places
    pair = 2 * HEAD_DIM
    spread = pl.BlockSpec((n_pos, 1, places, width), lambda i: (0, i, 0, 0))

    def by_frame(*shape):
        return pl.BlockSpec((1,) + shape, lambda i: (i, 0, 0))

    rows = own * patches
    return pl.pallas_call(
        space_forward,
        grid=(own,),
        in_specs=[spread, by_frame(2, width), resident(weight.shape)],
        out_specs=[
            by_frame(patches, width),
            by_frame(patches, 3 * width),
            pl.BlockSpec(memory_space=pl.ANY),
            pl.BlockSpec((1, HEADS // 2, patches, pair), lambda i: (i, 0, 0, 0)),
        ],
        out_shape=[
            jax.ShapeDtypeStruct((own, patches, width), bf16),
            jax.ShapeDtypeStruct((own, patches, 3 * width), bf16),
            jax.ShapeDtypeStruct((n_pos * own, places, width), bf16),
            jax.ShapeDtypeStruct((own, HEADS // 2, patches, pair), f32),
        ],
        scratch_shapes=spread_scratch(own, n_pos, places, width),
        compiler_params=pltpu.CompilerParams(
            vmem_limit_bytes=VMEM_LIMIT, collective_id=0, has_side_effects=True
        ),
        cost_estimate=pl.CostEstimate(
            flops=2 * rows * width * 3 * width + 4 * rows * patches * width,
            bytes_accessed=rows * width * 12 + weight.size * 2,
            transcendentals=rows * patches * HEADS,
        ),
        name="space_forward",
    )(x, mods, weight)


def call_space_backward(go, qkv, lse, x, h, mods, weight, hot, dmod_rest, grads, kinds, n_clip):
    n_pos, own, places, width = x.shape
    patches = n_pos * places
    pair = 2 * HEAD_DIM
    lead = n_pos.bit_length() - 1
    clips = dmod_rest.shape[0]
    spread = pl.BlockSpec((n_pos, 1, places, width), lambda i: (0, i, 0, 0))
    anywhere = pl.BlockSpec(memory_space=pl.ANY)

    def by_frame(*shape):
        return pl.BlockSpec((1,) + shape, lambda i: (i, 0, 0))

    rows = own * patches
    cut = 3 * width // 512 * 256
    late = [jax.ShapeDtypeStruct((width, cols), bf16) for cols in (cut, 3 * width - cut)]
    kinds = kinds + (True, False)
    views, flow_outs, flow_scratch = flow_plan(list(grads) + late, kinds, n_pos, n_clip)
    early = len(grads)
    sizes = sum(grad.size for grad in grads)
    dmod_shape = (n_clip, clips, 9 * width)
    swaps = lead + len(bits_of(n_clip))
    return pl.pallas_call(
        partial(space_backward, n_clip, kinds, early),
        grid=(own,),
        in_specs=[
            spread,
            by_frame(patches, 3 * width),
            pl.BlockSpec((1, HEADS // 2, patches, pair), lambda i: (i, 0, 0, 0)),
            spread,
            by_frame(patches, width),
            by_frame(2, width),
            resident(weight.shape),
            resident(hot.shape),
            resident(dmod_rest.shape),
        ]
        + [anywhere] * early,
        out_specs=[anywhere, resident(dmod_shape)] + [resident(out.shape) for out in flow_outs],
        out_shape=[
            jax.ShapeDtypeStruct((n_pos * own, places, width), bf16),
            jax.ShapeDtypeStruct(dmod_shape, f32),
        ]
        + flow_outs,
        scratch_shapes=[
            pltpu.VMEM((patches, width), f32),
            pltpu.VMEM((patches, 3 * width), bf16),
            pltpu.VMEM((width, 3 * width), f32),
            pltpu.VMEM((clips, 9 * width), f32),
            pltpu.VMEM((lead, clips, 9 * width), f32),
            pltpu.VMEM((lead, clips, 9 * width), f32),
            pltpu.VMEM(dmod_shape, f32),
            pltpu.SemaphoreType.DMA((swaps,)),
            pltpu.SemaphoreType.DMA((swaps,)),
        ]
        + spread_scratch(own, n_pos, places, width)
        + views[early:]
        + flow_scratch,
        compiler_params=pltpu.CompilerParams(
            vmem_limit_bytes=VMEM_LIMIT, collective_id=1, has_side_effects=True
        ),
        cost_estimate=pl.CostEstimate(
            flops=4 * rows * width * 3 * width + 10 * rows * patches * width,
            bytes_accessed=rows * width * 16 + weight.size * 2 + sizes * 4,
            transcendentals=rows * patches * HEADS,
        ),
        name="space_backward",
    )(go, qkv, lse, x, h, mods, weight, hot, dmod_rest, *views[:early])


def call_middle(o_one, x, grad, mods, same_clip, wso, wti, wto, wup, wdn):
    places, frames, width = x.shape
    count = max(1, min(places, 256 // frames))
    rows = count * frames
    hidden = wup.shape[1]
    pair = 2 * HEAD_DIM
    total = places * frames
    chunk = pl.BlockSpec((count, frames, width), lambda i: (i, 0, 0))

    def flat(cols):
        return pl.BlockSpec((rows, cols), lambda i: (i, 0))

    def flat_shape(cols):
        return jax.ShapeDtypeStruct((total, cols), bf16)

    def scratch(cols, dtype=f32):
        return pltpu.VMEM((rows, cols), dtype)

    lanes = jnp.concatenate([same_clip, same_clip], axis=1)
    flops = 2 * total * (2 * (wso.size + wti.size + wto.size + wup.size + wdn.size))
    return pl.pallas_call(
        middle,
        grid=(places // count,),
        in_specs=[chunk, chunk, chunk, resident(mods.shape), resident(lanes.shape)]
        + [resident(w.shape) for w in (wso, wti, wto, wup, wdn)],
        out_specs=[
            chunk,
            flat(hidden),
            flat(width),
            flat(width),
            flat(hidden),
            flat(width),
            flat(width),
            flat(width),
            flat(3 * width),
            flat(width),
            chunk,
            chunk,
            pl.BlockSpec((7, frames, width), lambda i: (0, 0, 0)),
        ],
        out_shape=[
            jax.ShapeDtypeStruct(x.shape, bf16),
            flat_shape(hidden),
            flat_shape(width),
            flat_shape(width),
            flat_shape(hidden),
            flat_shape(width),
            flat_shape(width),
            flat_shape(width),
            flat_shape(3 * width),
            flat_shape(width),
            jax.ShapeDtypeStruct(x.shape, bf16),
            jax.ShapeDtypeStruct(x.shape, f32),
            jax.ShapeDtypeStruct((7, frames, width), f32),
        ],
        scratch_shapes=[
            scratch(3 * width, bf16),
            pltpu.VMEM((HEADS // 2, rows, pair), f32),
            scratch(width),
            scratch(width),
            scratch(width),
            scratch(width),
            scratch(pair),
            scratch(pair),
            scratch(width),
            scratch(width),
        ]
        + [scratch(256)] * 4,
        compiler_params=pltpu.CompilerParams(vmem_limit_bytes=VMEM_LIMIT),
        cost_estimate=pl.CostEstimate(
            flops=flops, bytes_accessed=total * 40000, transcendentals=total * hidden
        ),
        name="middle",
    )(o_one, x, grad, mods, lanes, wso, wti, wto, wup, wdn)


def on_device(
    tokens,
    clip_lengths,
    timesteps,
    embed_first,
    embed_second,
    adaln_weight,
    spatial_in,
    spatial_out,
    temporal_in,
    temporal_out,
    hidden_up,
    hidden_down,
    grad_output,
    n_pos=16,
    n_clip=2,
):
    frames, places, width = tokens.shape
    rows = frames * places
    own = frames // n_pos
    patches = places * n_pos
    me = lax.axis_index("pos")
    clips = clip_lengths.shape[1]

    def exchange(values):
        sent = values.reshape(frames, places, width)
        got = lax.all_to_all(sent, "pos", split_axis=0, concat_axis=0, tiled=True)
        return got.reshape(n_pos, own, places, width)

    x_space = exchange(tokens)

    all_steps = by_distance(timesteps[0], "clip", n_clip)
    freq = frequency(all_steps)
    pre_cond = dot_exact(freq, embed_first)
    hidden_cond = jax.nn.silu(pre_cond)
    cond = dot_exact(hidden_cond, embed_second)
    cond_act = jax.nn.silu(cond)
    modulated = dot_exact(cond_act[:clips], adaln_weight)
    onehot, clip_ids = clip_onehot(clip_lengths[0], frames)
    per_frame = dot_high(onehot, modulated)
    own_frames = lax.dynamic_slice_in_dim(per_frame, me * own, own, 0)

    own_mods = own_frames[:, : 2 * width].reshape(own, 2, width)
    h_one, qkv_one, o_one, lse_one = call_space_forward(x_space, own_mods, spatial_in)

    def turn(values):
        return values.transpose(1, 0, 2)

    o_one = turn(o_one)
    mods = per_frame.reshape(frames, 9, width).transpose(1, 0, 2)
    same_clip = jnp.dot(onehot, onehot.T)
    (block_turned, act, grad_z, h_three, grad_u, o_two, grad_y_two, h_two, grad_qkv_two, grad_y_one, grad_o_one,
     grad_one, sums) = call_middle(
        o_one, turn(tokens), turn(grad_output), mods, same_clip, spatial_out, temporal_in, temporal_out,
        hidden_up, hidden_down,
    )
    block_out = turn(block_turned)
    grad_o_space = exchange(turn(grad_o_one))
    early = (
        weight_grad(h_three, grad_u),
        weight_grad(act, grad_z),
        weight_grad(h_two, grad_qkv_two),
        weight_grad(o_one.reshape(rows, width), grad_y_one),
        weight_grad(o_two, grad_y_two),
    )
    own_hot = lax.dynamic_slice_in_dim(onehot, me * own, own, 0)
    hot = jnp.broadcast_to(own_hot[:, :, None], (own, clips, 128))
    dmod_rest = dot_high(onehot.T, sums.transpose(1, 0, 2).reshape(frames, 7 * width))
    (
        back_places, dmod, g_hidden_up, g_hidden_down, g_temporal_in, g_spatial_out, g_temporal_out,
        in_low, in_high,
    ) = call_space_backward(
        grad_o_space, qkv_one, lse_one, x_space, h_one, own_mods, spatial_in, hot, dmod_rest,
        early, (False, True, True, True, True), n_clip,
    )
    grad_tokens = (turn(grad_one) + back_places.astype(f32)).astype(bf16)
    g_spatial_in = jnp.concatenate([in_low, in_high], axis=1)
    dmod = dmod.reshape(n_clip * clips, 9 * width)

    def own_columns(values):
        block = values.shape[1] // n_pos
        return lax.dynamic_slice_in_dim(values, me * block, block, 1)

    g_adaln = dot_high(own_columns(cond_act).T, dmod)
    grad_cond = dot_exact(dmod, adaln_weight.T) * silu_grad(cond)
    g_second = dot_high(own_columns(hidden_cond).T, grad_cond)
    grad_pre = dot_exact(grad_cond, embed_second.T) * silu_grad(pre_cond)
    g_first = dot_high(own_columns(freq).T, grad_pre)
    return (
        block_out,
        grad_tokens,
        g_first,
        g_second,
        g_adaln,
        g_spatial_in,
        g_spatial_out,
        g_temporal_in,
        g_temporal_out,
        g_hidden_up,
        g_hidden_down,
    )


def solution(mesh):
    in_specs = (
        P("clip", "pos", None),
        P("clip", None),
        P("clip", None),
        P(),
        P(),
        P(),
        P(),
        P(),
        P(),
        P(),
        P(),
        P(),
        P("clip", "pos", None),
    )
    out_specs = (P("clip", "pos", None),) * 2 + (P("pos", None),) * 9
    body = partial(on_device, n_pos=mesh.shape["pos"], n_clip=mesh.shape["clip"])
    return jax.shard_map(body, mesh=mesh, in_specs=in_specs, out_specs=out_specs, check_vma=False)
```

```python
from functools import partial
import math

import jax
import jax.numpy as jnp
from jax import lax
from jax.experimental import pallas as pl
from jax.experimental.pallas import tpu as pltpu
from jax.sharding import PartitionSpec as P

HEADS = 12
HEAD_DIM = 64
FREQ = 256

epsilon = 1e-06
highest = lax.Precision.HIGHEST
masked_score = -1000000000.0
f32 = jnp.float32
bf16 = jnp.bfloat16


def frequency(step_ids):
    half_width = FREQ // 2
    rate_table = jnp.exp(
        -math.log(10000.0) * jnp.arange(half_width, dtype=jnp.float32) / half_width
    )
    angles = step_ids.astype(jnp.float32)[:, None] * rate_table[None, :]
    return jnp.concatenate([jnp.cos(angles), jnp.sin(angles)], axis=1)


def dot_high(left, right):
    return jnp.dot(left, right, precision=highest, preferred_element_type=f32)


def silu_grad(values):
    gate = jax.nn.sigmoid(values)
    return gate * (1.0 + values * (1.0 - gate))


def clip_onehot(lengths, frames):
    clip_ends = jnp.cumsum(lengths)
    frame_ids = jnp.arange(frames, dtype=jnp.int32)
    clip_ids = jnp.sum((frame_ids[:, None] >= clip_ends[None, :]).astype(jnp.int32), axis=1)
    onehot = (clip_ids[:, None] == jnp.arange(lengths.shape[0], dtype=jnp.int32)[None, :]).astype(
        jnp.float32
    )
    return (onehot, clip_ids)


def weight_grad(left, right):
    return jnp.einsum("rd,rk->dk", left, right, preferred_element_type=f32).astype(bf16)


def bdot(left, right):
    return lax.dot_general(left, right, (((1,), (0,)), ((), ())), preferred_element_type=f32)


def bdot_nt(left, right):
    return lax.dot_general(left, right, (((1,), (1,)), ((), ())), preferred_element_type=f32)


def bdot_tn(left, right):
    return lax.dot_general(left, right, (((0,), (0,)), ((), ())), preferred_element_type=f32)


def norm_rows(values):
    width = values.shape[-1]
    centre = values - jnp.sum(values, axis=-1, keepdims=True) * (1.0 / width)
    spread = jnp.sum(centre * centre, axis=-1, keepdims=True) * (1.0 / width)
    inverse = lax.rsqrt(spread + epsilon)
    return centre * inverse, inverse


def norm_rows_back(normed, inverse, scale_vec, grad):
    width = grad.shape[-1]
    inner = grad * (1.0 + scale_vec)
    mean_one = jnp.sum(inner, axis=-1, keepdims=True) * (1.0 / width)
    mean_two = jnp.sum(inner * normed, axis=-1, keepdims=True) * (1.0 / width)
    return inverse * (inner - mean_one - normed * mean_two)


def pair_masks(scale):
    lanes = lax.broadcasted_iota(jnp.int32, (1, 2 * HEAD_DIM), 1)
    low_half = jnp.where(lanes < HEAD_DIM, scale, 0.0).astype(bf16)
    high_half = jnp.where(lanes < HEAD_DIM, 0.0, scale).astype(bf16)
    return low_half, high_half


ROWS = 32


def load_rows(ref, step):
    places, width = ref.shape[2:]
    count = max(1, ROWS // places)
    part = ref[pl.ds(step * count, count), 0].astype(f32)
    return part.reshape(count * places, width)


def swap(values, axis, size, bit):
    return lax.ppermute(values, axis, [(i, i ^ bit) for i in range(size)])


def bits_of(size):
    return [1 << i for i in range(size.bit_length() - 1)]


def by_distance(values, axis, size):
    for bit in bits_of(size):
        values = jnp.concatenate([values, swap(values, axis, size, bit)], axis=0)
    return values


def first_swap(grad, n_pos):
    rows, cols = grad.shape
    split = grad.reshape(n_pos // 2, 2, rows // n_pos, cols)
    side = lax.rem(lax.axis_index("pos"), 2)
    keep = lax.dynamic_index_in_dim(split, side, 1, keepdims=False)
    send = lax.dynamic_index_in_dim(split, 1 - side, 1, keepdims=False)
    return (keep.astype(f32) + swap(send, "pos", n_pos, 1).astype(f32)).astype(bf16)


def column_swap(values, n_clip):
    half = values.shape[-1] // 2
    low, high = values[..., :half], values[..., half:]
    upper = lax.rem(lax.axis_index("clip"), 2) == 1
    keep, send = jnp.where(upper, high, low), jnp.where(upper, low, high)
    return (keep.astype(f32) + swap(send, "clip", n_clip, 1).astype(f32)).astype(bf16)


def dot_exact(left, right):
    parts = []
    for _ in range(3):
        part = left.astype(bf16)
        parts.append(part)
        left = left - part.astype(f32)
    count = parts[0].shape[0]
    got = jnp.dot(jnp.concatenate(parts, axis=0), right, preferred_element_type=f32)
    return got[:count] + (got[count : 2 * count] + got[2 * count :])


def flow_stages(n_pos, n_clip, clip_first, skip=0):
    pos = [("pos", bit, "halve") for bit in bits_of(n_pos)]
    clip = bits_of(n_clip)
    if not clip_first:
        return (pos + [("clip", bit, "sum") for bit in clip])[skip:]
    first = [("clip", clip[0], "columns")]
    last = [("clip", clip[0], "gather")]
    stages = pos[:1] + first + pos[1:] + [("clip", bit, "sum") for bit in clip[1:]] + last
    return stages[skip:]


def flow_shapes(stages, lead, block, cols):
    shapes = []
    for _, _, what in stages:
        if what == "halve":
            lead -= 1
        elif what == "columns":
            cols //= 2
        shapes.append((2,) * lead + (block, cols))
    return shapes


class Flow:
    def __init__(self, number, stages, grad, out, keep, gots, sems, place):
        self.number, self.stages = number, stages
        self.grad, self.out, self.keep, self.gots = grad, out, keep, gots
        self.send_sem, self.recv_sem, self.keep_sem = sems
        self.place = place

    def side(self, stage):
        axis, bit, _ = self.stages[stage]
        return lax.rem(self.place[axis] // bit, 2)

    def columns(self, side, width):
        return pl.ds(pl.multiple_of(side * width, width), width)

    def part(self, ref, stage, side):
        what = self.stages[stage][2]
        lead = len(ref.shape) - 2
        if what == "halve":
            return (slice(None),) * (lead - 1) + (side,)
        if what == "columns":
            half = ref.shape[-1] // 2
            return (slice(None),) * (lead + 1) + (self.columns(side, half),)
        return None

    def held(self, stage):
        if stage == 0:
            return self.grad
        return self.keep if stage == 1 else self.gots[stage - 1]

    def copy(self, stage):
        axis, bit, _ = self.stages[stage]
        side = self.side(stage)
        source = self.held(stage)
        at = self.part(source, stage, 1 - side)
        return pltpu.make_async_remote_copy(
            source if at is None else source.at[at],
            self.gots[stage],
            self.send_sem.at[self.number, stage],
            self.recv_sem.at[self.number, stage],
            device_id={axis: self.place[axis] + bit * (1 - 2 * side)},
            device_id_type=pl.DeviceIdType.MESH,
        )

    def own(self):
        at = self.part(self.grad, 0, self.side(0))
        return pltpu.make_async_copy(self.grad.at[at], self.keep, self.keep_sem.at[self.number])

    def start(self):
        self.copy(0).start()
        self.own().start()

    def take(self, stage):
        self.copy(stage).wait_recv()
        if stage == 0:
            self.own().wait()
        what = self.stages[stage][2]
        got = self.gots[stage]
        side = self.side(stage)
        last = stage == len(self.stages) - 1
        lead = len(got.shape) - 2
        if what == "gather":
            half = got.shape[-1]
            self.out[:, self.columns(side, half)] = self.held(stage)[...].astype(f32)
            self.out[:, self.columns(1 - side, half)] = got[...].astype(f32)
            return
        if last:
            self.out[...] = self.held(stage)[...].astype(f32) + got[...].astype(f32)
            return
        target = self.keep if stage == 0 else got

        def one(index, _):
            at = tuple(lax.rem(index // (1 << i), 2) for i in range(lead))
            if stage == 0:
                mine = self.keep[at]
            elif what == "halve":
                mine = self.held(stage)[at + (side,)]
            elif what == "columns":
                mine = self.held(stage)[at + (slice(None), self.columns(side, got.shape[-1]))]
            else:
                mine = self.held(stage)[at]
            target[at] = mine + got[at]
            return 0

        lax.fori_loop(0, 1 << lead, one, 0)
        self.copy(stage + 1).start()

    def finish(self):
        for stage in range(len(self.stages)):
            self.copy(stage).wait_send()


class Butterfly:
    def __init__(self, n_pos, n_clip, values, out, got, acc, sems, place):
        self.pos_bits, self.clip_bits = bits_of(n_pos), bits_of(n_clip)
        self.values, self.out, self.got, self.acc = values, out, got, acc
        self.send_sem, self.recv_sem = sems
        self.place = place
        self.count = len(self.pos_bits) + len(self.clip_bits)

    def copy(self, stage):
        if stage < len(self.pos_bits):
            axis, bit = "pos", self.pos_bits[stage]
            source = self.values if stage == 0 else self.acc.at[stage - 1]
            target = self.got.at[stage]
        else:
            axis, bit = "clip", self.clip_bits[stage - len(self.pos_bits)]
            source, target = self.out.at[pl.ds(0, bit)], self.out.at[pl.ds(bit, bit)]
        side = lax.rem(self.place[axis] // bit, 2)
        return pltpu.make_async_remote_copy(
            source,
            target,
            self.send_sem.at[stage],
            self.recv_sem.at[stage],
            device_id={axis: self.place[axis] + bit * (1 - 2 * side)},
            device_id_type=pl.DeviceIdType.MESH,
        )

    def start(self):
        self.copy(0).start()

    def take(self, stage):
        self.copy(stage).wait_recv()
        last = len(self.pos_bits) - 1
        if stage <= last:
            mine = self.values[...] if stage == 0 else self.acc[stage - 1]
            if stage < last:
                self.acc[stage] = mine + self.got[stage]
            else:
                self.out[0] = mine + self.got[stage]
        if stage + 1 < self.count:
            self.copy(stage + 1).start()

    def finish(self):
        for stage in range(self.count):
            self.copy(stage).wait_send()


def partner_list(n_pos, n_clip):
    return [("pos", bit) for bit in bits_of(n_pos)] + [("clip", bit) for bit in bits_of(n_clip)]


def here():
    return {"pos": lax.axis_index("pos"), "clip": lax.axis_index("clip")}


def signal_swap(barrier, place, axis, bit):
    side = lax.rem(place[axis] // bit, 2)
    pl.semaphore_signal(
        barrier,
        inc=1,
        device_id={axis: place[axis] + bit * (1 - 2 * side)},
        device_id_type=pl.DeviceIdType.MESH,
    )


def make_flows(n_pos, n_clip, kinds, grads, outs, scratch):
    sems, rest = scratch[:3], list(scratch[3:])
    flows = []
    for number, (clip_first, skip) in enumerate(kinds):
        stages = flow_stages(n_pos, n_clip, clip_first, skip)
        keep, gots = rest[0], rest[1 : 1 + len(stages)]
        rest = rest[1 + len(stages) :]
        flows.append(Flow(number, stages, grads[number], outs[number], keep, gots, sems, here()))
    return flows


def flow_plan(shapes, kinds, n_pos, n_clip):
    lead = n_pos.bit_length() - 1
    most = lead + len(bits_of(n_clip)) + 1
    dma = pltpu.SemaphoreType.DMA
    scratch = [dma((len(shapes), most)), dma((len(shapes), most)), dma((len(shapes),))]
    views, out_shape = [], []
    for (block, cols), (clip_first, skip) in zip(shapes, kinds):
        out_shape.append(jax.ShapeDtypeStruct((block, cols), f32))
        if clip_first and skip > 1:
            cols //= 2
        left = lead - min(skip, 1)
        views.append((2,) * left + (block, cols))
        stages = flow_stages(n_pos, n_clip, clip_first, skip)
        arrived = flow_shapes(stages, left, block, cols)
        scratch += [pltpu.VMEM(shape, bf16) for shape in [arrived[0]] + arrived]
    return views, out_shape, scratch


class Spread:

    def __init__(self, n_pos, step, steps, hold, out, send_sem, recv_sem, own_sem):
        self.n_pos, self.step, self.steps = n_pos, step, steps
        self.hold, self.out = hold, out
        self.send_sem, self.recv_sem, self.own_sem = send_sem, recv_sem, own_sem
        self.me = lax.axis_index("pos")

    def greet(self, more=0):
        barrier = pltpu.get_barrier_semaphore()

        def signal(shift, _):
            target = lax.rem(self.me + shift, self.n_pos)
            pl.semaphore_signal(
                barrier, inc=1, device_id={"pos": target}, device_id_type=pl.DeviceIdType.MESH
            )
            return 0

        lax.fori_loop(1, self.n_pos, signal, 0)
        pl.semaphore_wait(barrier, self.n_pos - 1 + more)

    def copy(self, step, shift, source):
        target = lax.rem(self.me + shift, self.n_pos)
        return pltpu.make_async_remote_copy(
            self.hold.at[step, target],
            self.out.at[source * self.steps + step],
            self.send_sem.at[step, shift],
            self.recv_sem.at[step, shift],
            device_id={"pos": target},
            device_id_type=pl.DeviceIdType.MESH,
        )

    def stay(self, step):
        return pltpu.make_async_copy(
            self.hold.at[step, self.me],
            self.out.at[self.me * self.steps + step],
            self.own_sem.at[step],
        )

    def send(self):
        def one(shift, _):
            self.copy(self.step, shift, self.me).start()
            return 0

        lax.fori_loop(1, self.n_pos, one, 0)
        self.stay(self.step).start()

    def finish(self):
        def one_step(step, _):
            def one(shift, _):
                self.copy(step, shift, self.me).wait_send()
                source = lax.rem(self.me + self.n_pos - shift, self.n_pos)
                self.copy(step, shift, source).wait_recv()
                return 0

            lax.fori_loop(1, self.n_pos, one, 0)
            self.stay(step).wait()
            return 0

        lax.fori_loop(0, self.steps, one_step, 0)


def spread_scratch(own, n_pos, places, width):
    return [
        pltpu.VMEM((own, n_pos, places, width), bf16),
        pltpu.SemaphoreType.DMA((own, n_pos)),
        pltpu.SemaphoreType.DMA((own, n_pos)),
        pltpu.SemaphoreType.DMA((own,)),
    ]


def space_forward(
    x_ref, mod_ref, w_ref, h_ref, qkv_ref, o_ref, lse_ref, hold, send_sem, recv_sem, own_sem
):
    own, n_pos = hold.shape[:2]
    frame = pl.program_id(0)
    spread = Spread(n_pos, frame, own, hold, o_ref, send_sem, recv_sem, own_sem)
    pl.when(frame == 0)(spread.greet)
    patches, width = h_ref.shape[1:]
    places = x_ref.shape[2]
    pair = 2 * HEAD_DIM
    shift, scale = mod_ref[0, 0:1, :], mod_ref[0, 1:2, :]

    def norm_step(step, _):
        normed, _inverse = norm_rows(load_rows(x_ref, step))
        h_ref[0, pl.ds(step * ROWS, ROWS), :] = (normed * (1.0 + scale) + shift).astype(bf16)
        return 0

    lax.fori_loop(0, patches // ROWS, norm_step, 0)

    def project(third, _):
        cols = pl.ds(pl.multiple_of(third * width, width), width)
        qkv_ref[0, :, cols] = bdot(h_ref[0], w_ref[:, cols]).astype(bf16)
        return 0

    lax.fori_loop(0, 3, project, 0)
    masks = pair_masks(1.0 / math.sqrt(HEAD_DIM))
    is_low = lax.broadcasted_iota(jnp.int32, (1, pair), 1) < HEAD_DIM

    def head_pair(index, _):
        at = pl.multiple_of(index * pair, pair)
        q = qkv_ref[0, :, pl.ds(at, pair)]
        k = qkv_ref[0, :, pl.ds(pl.multiple_of(width + at, pair), pair)]
        v = qkv_ref[0, :, pl.ds(pl.multiple_of(2 * width + at, pair), pair)]
        one = jnp.ones_like(v)
        values = [jnp.where(is_low, v, one), jnp.where(is_low, one, v)]
        scores = [bdot_nt(q * mask, k) for mask in masks]
        tops = [jnp.max(score, axis=-1, keepdims=True) for score in scores]
        exps = [jnp.exp(score - top).astype(bf16) for score, top in zip(scores, tops)]
        outs = [bdot(exp, value) for exp, value in zip(exps, values)]
        total = pltpu.roll(jnp.where(is_low, outs[1], outs[0]), HEAD_DIM, 1)
        both = jnp.where(is_low, outs[0], outs[1]) / total
        lse_ref[0, index] = jnp.where(is_low, tops[0], tops[1]) + jnp.log(total)
        hold[frame, :, :, pl.ds(at, pair)] = both.reshape(n_pos, places, pair).astype(bf16)
        return 0

    lax.fori_loop(0, HEADS // 2, head_pair, 0)
    spread.send()
    pl.when(frame == own - 1)(spread.finish)


def space_backward(n_clip, kinds, early, *refs):
    go_ref, qkv_ref, lse_ref, x_ref, h_ref, mod_ref, w_ref, hot_ref, rest_ref = refs[:9]
    grads, refs = refs[9 : 9 + early], refs[9 + early :]
    dv_ref, dmod_ref = refs[:2]
    outs, refs = refs[2 : 2 + len(kinds)], refs[2 + len(kinds) :]
    e_ref, dqkv_ref, total_ref, small_ref, got_ref, acc_ref, every_ref = refs[:7]
    small_send, small_recv, hold, send_sem, recv_sem, own_sem = refs[7:13]
    late_grads, refs = refs[13 : 13 + len(kinds) - early], refs[13 + len(kinds) - early :]
    own, n_pos = hold.shape[:2]
    frame = pl.program_id(0)
    spread = Spread(n_pos, frame, own, hold, dv_ref, send_sem, recv_sem, own_sem)
    flows = make_flows(n_pos, n_clip, kinds, tuple(grads) + tuple(late_grads), outs, refs)
    late = flows[early:]
    tree = Butterfly(
        n_pos, n_clip, small_ref, every_ref, got_ref, acc_ref, (small_send, small_recv), here()
    )
    stages = max(len(flow.stages) for flow in flows)
    points = [
        [(i, 0) for i in range(2, early)],
        [(1, 0)],
        [(2, 1), (1, 1), (0, 0)],
    ][: own - 1]
    taken = [step for point in points for step in point]
    order = []
    for turn in range(stages):
        for i in range(early):
            step = (i, turn - kinds[i][1])
            if 0 <= step[1] < len(flows[i].stages) and step not in taken:
                order.append((turn, step))

    @pl.when(frame == 0)
    def _():
        place = here()
        others = [("clip", bit) for bit in bits_of(n_clip)]
        barrier = pltpu.get_barrier_semaphore()
        for axis, bit in others:
            signal_swap(barrier, place, axis, bit)
        spread.greet(len(others))
        for i in [1, 0] + list(range(2, early)):
            flows[i].start()

        def clear(step, _):
            total_ref[pl.ds(step * 8, 8), :] = jnp.zeros((8, total_ref.shape[1]), f32)
            return 0

        lax.fori_loop(0, total_ref.shape[0] // 8, clear, 0)
        small_ref[:, : 2 * x_ref.shape[3]] = jnp.zeros_like(small_ref[:, : 2 * x_ref.shape[3]])
        small_ref[:, 2 * x_ref.shape[3] :] = rest_ref[...]

    def advance(steps):
        for i, stage in steps:
            flows[i].take(stage)

    def start_late():
        block = late_grads[0].shape[-2]
        lead = len(late_grads[0].shape) - 2

        def one(index, _):
            at = tuple(lax.rem(index // (1 << i), 2) for i in reversed(range(lead)))
            rows = pl.ds(pl.multiple_of(index * block, 8), block)
            first = 0
            for grad in late_grads:
                cols = grad.shape[-1]
                grad[at] = total_ref[rows, first : first + cols].astype(bf16)
                first += cols
            return 0

        lax.fori_loop(0, n_pos, one, 0)
        for flow in late:
            flow.start()

    patches = qkv_ref.shape[1]
    width = x_ref.shape[3]
    places = x_ref.shape[2]
    pair = 2 * HEAD_DIM
    scale = mod_ref[0, 1:2, :]
    factor = 1.0 / math.sqrt(HEAD_DIM)
    masks_q = pair_masks(factor)
    masks = pair_masks(1.0)
    ones = jnp.ones((patches, pair), bf16)

    def key_sums(values):
        high = values.astype(bf16)
        low = (values - high.astype(f32)).astype(bf16)
        total = bdot(high, ones) + bdot(low, ones)
        return jnp.concatenate([total] * (patches // pair), axis=1)

    def head_pair(index, _):
        at = pl.multiple_of(index * pair, pair)
        k_at = pl.multiple_of(width + at, pair)
        v_at = pl.multiple_of(2 * width + at, pair)
        q = qkv_ref[0, :, pl.ds(at, pair)]
        k = qkv_ref[0, :, pl.ds(k_at, pair)]
        v = qkv_ref[0, :, pl.ds(v_at, pair)]
        go = go_ref[:, 0, :, pl.ds(at, pair)].astype(f32).reshape(patches, pair).astype(bf16)
        lse_pair = lse_ref[0, index]
        lses = [lse_pair[:, 0:1], lse_pair[:, HEAD_DIM : HEAD_DIM + 1]]
        q_halves = [q * mask for mask in masks_q]
        go_halves = [go * mask for mask in masks]
        probs = [jnp.exp(bdot_nt(half, k) - lse) for half, lse in zip(q_halves, lses)]
        grads = [bdot_nt(half, v) for half in go_halves]
        inner = [key_sums(grad * prob) for grad, prob in zip(grads, probs)]
        scores = [
            (prob * (grad - mean)).astype(bf16) for prob, grad, mean in zip(probs, grads, inner)
        ]
        gq = sum(bdot(score, k * mask) for score, mask in zip(scores, masks_q))
        gk = sum(bdot_tn(score, half) for score, half in zip(scores, q_halves))
        gv = sum(bdot_tn(prob.astype(bf16), half) for prob, half in zip(probs, go_halves))
        dqkv_ref[:, pl.ds(at, pair)] = gq.astype(bf16)
        dqkv_ref[:, pl.ds(k_at, pair)] = gk.astype(bf16)
        dqkv_ref[:, pl.ds(v_at, pair)] = gv.astype(bf16)
        return 0

    lax.fori_loop(0, HEADS // 2, head_pair, 0)
    e_ref[...] = bdot_nt(dqkv_ref[...], w_ref[...])

    def norm_step(step, sums):
        grad = e_ref[pl.ds(step * ROWS, ROWS), :]
        normed, inverse = norm_rows(load_rows(x_ref, step))
        back = norm_rows_back(normed, inverse, scale, grad)
        count = max(1, ROWS // places)
        back = back.reshape(count, places, width).astype(bf16)
        hold[frame, pl.ds(step * count, count)] = back
        folded = grad.reshape(ROWS // 8, 8, width).sum(axis=0)
        folded_n = (grad * normed).reshape(ROWS // 8, 8, width).sum(axis=0)
        return sums[0] + folded, sums[1] + folded_n

    zero = jnp.zeros((8, width), f32)
    shift_sum, scale_sum = lax.fori_loop(0, patches // ROWS, norm_step, (zero, zero))
    spread.send()
    hot = hot_ref[frame][:, 0:1]
    small_ref[:, :width] += hot * jnp.sum(shift_sum, axis=0, keepdims=True)
    small_ref[:, width : 2 * width] += hot * jnp.sum(scale_sum, axis=0, keepdims=True)

    def accumulate(third, _):
        cols = pl.ds(pl.multiple_of(third * width, width), width)
        total_ref[:, cols] += bdot_tn(h_ref[0], dqkv_ref[:, cols])
        return 0

    lax.fori_loop(0, 3, accumulate, 0)
    for index in range(own - 1):
        pl.when(frame == index)(partial(advance, points[index]))

    @pl.when(frame == own - 1)
    def _():
        tree.start()
        start_late()
        for turn in range(stages + 1):
            advance([step for at, step in order if at == turn])
            if turn < tree.count:
                tree.take(turn)
            for flow in late:
                if 0 <= turn - 1 < len(flow.stages):
                    flow.take(turn - 1)
        dmod_ref[...] = every_ref[...]
        spread.finish()
        tree.finish()
        for flow in flows:
            flow.finish()


GELU_C = math.sqrt(2.0 / math.pi)


def middle(
    o1_ref, x_ref, g_ref, mod_ref, clip_ref, wso_ref, wti_ref, wto_ref, wup_ref, wdn_ref,
    out_ref, act_ref, dz_ref, h3_ref, du_ref, o2_ref, dy2_ref, h2_ref, dqkv_ref, dy1_ref, do1_ref,
    dx1_ref, sum_ref,
    qkv_ref, p_ref, y1_ref, y2_ref, n2_ref, n3_ref, r2_ref, r3_ref, xa_ref, e_ref,
    ua_ref, aa_ref, ub_ref, ab_ref,
):
    count, frames, width = x_ref.shape
    rows = count * frames
    pair = 2 * HEAD_DIM
    hidden = act_ref.shape[1]
    factor = 1.0 / math.sqrt(HEAD_DIM)
    per = frames // ROWS
    steps = rows // ROWS

    @pl.when(pl.program_id(0) == 0)
    def _():
        sum_ref[...] = jnp.zeros_like(sum_ref)

    def at_rows(step):
        return step // per, pl.ds(lax.rem(step, per) * ROWS, ROWS), pl.ds(step * ROWS, ROWS)

    def mod(index, part):
        return mod_ref[index, part, :]

    def by_columns(product):
        def one(index, _):
            cols = pl.ds(pl.multiple_of(index * 256, 256), 256)
            e_ref[:, cols] = product(cols)
            return 0

        lax.fori_loop(0, width // 256, one, 0)

    y1_ref[...] = bdot(o1_ref[...].reshape(rows, width), wso_ref[...])

    def step_one(step, _):
        place, part, flat = at_rows(step)
        x_one = x_ref[place, part, :].astype(f32) + mod(2, part) * y1_ref[flat, :]
        xa_ref[flat, :] = x_one
        normed, inverse = norm_rows(x_one)
        n2_ref[flat, :] = normed
        r2_ref[flat, :] = jnp.broadcast_to(inverse, (ROWS, pair))
        h2_ref[flat, :] = (normed * (1.0 + mod(4, part)) + mod(3, part)).astype(bf16)
        return 0

    lax.fori_loop(0, steps, step_one, 0)

    def project(third, _):
        cols = pl.ds(pl.multiple_of(third * width, width), width)
        qkv_ref[:, cols] = bdot(h2_ref[...], wti_ref[:, cols]).astype(bf16)
        return 0

    lax.fori_loop(0, 3, project, 0)

    masks = pair_masks(1.0)
    masks_q = pair_masks(factor)
    lane_ids = lax.broadcasted_iota(jnp.int32, (1, pair), 1)
    is_low = lane_ids < HEAD_DIM
    allowed = clip_ref[...] > 0.5

    def halves(values, reduce, neutral):
        low_part = reduce(jnp.where(is_low, values, neutral), axis=-1, keepdims=True)
        high_part = reduce(jnp.where(is_low, neutral, values), axis=-1, keepdims=True)
        return jnp.where(is_low, low_part, high_part)

    def stacked(values, pair_of_masks):
        return jnp.concatenate([values * pair_of_masks[0], values * pair_of_masks[1]], axis=0)

    def pair_at(index):
        at = pl.multiple_of(index * pair, pair)
        return (
            pl.ds(at, pair),
            pl.ds(pl.multiple_of(width + at, pair), pair),
            pl.ds(pl.multiple_of(2 * width + at, pair), pair),
        )

    parts = [slice(place * frames, (place + 1) * frames) for place in range(count)]
    same_half = (
        lax.broadcasted_iota(jnp.int32, (pair, pair), 0) // HEAD_DIM
        == lax.broadcasted_iota(jnp.int32, (pair, pair), 1) // HEAD_DIM
    )
    ones = jnp.where(same_half, 1.0, 0.0).astype(bf16)

    def half_sums(values):
        high = values.astype(bf16)
        low = (values - high.astype(f32)).astype(bf16)
        return bdot(high, ones) + bdot(low, ones)

    def time_pair(index, _):
        jobs = [(2 * index + i, part) + pair_at(2 * index + i) for i in range(2) for part in parts]
        keys = [stacked(qkv_ref[part, k_at], masks_q) for _i, part, q_at, k_at, v_at in jobs]
        scores = [bdot_nt(qkv_ref[job[1], job[2]], key) for job, key in zip(jobs, keys)]
        scores = [jnp.where(allowed, score, masked_score) for score in scores]
        tops = [halves(score, jnp.max, -jnp.inf) for score in scores]
        exps = [jnp.exp(score - top) for score, top in zip(scores, tops)]
        sums = [half_sums(exp) for exp in exps]
        probs = [exp / total for exp, total in zip(exps, sums)]
        values = [stacked(qkv_ref[job[1], job[4]], masks) for job in jobs]
        outs = [bdot(prob.astype(bf16), value) for prob, value in zip(probs, values)]
        for (i, part, q_at, _k, _v), prob, out in zip(jobs, probs, outs):
            p_ref[i, part, :] = prob
            o2_ref[part, q_at] = out.astype(bf16)
        return 0

    lax.fori_loop(0, HEADS // 4, time_pair, 0)

    y2_ref[...] = bdot(o2_ref[...], wto_ref[...])

    def step_two(step, _):
        place, part, flat = at_rows(step)
        x_two = xa_ref[flat, :] + mod(5, part) * y2_ref[flat, :]
        xa_ref[flat, :] = x_two
        normed, inverse = norm_rows(x_two)
        n3_ref[flat, :] = normed
        r3_ref[flat, :] = jnp.broadcast_to(inverse, (ROWS, pair))
        h3_ref[flat, :] = (normed * (1.0 + mod(7, part)) + mod(6, part)).astype(bf16)
        dz_ref[flat, :] = (mod(8, part) * g_ref[place, part, :].astype(f32)).astype(bf16)
        return 0

    lax.fori_loop(0, steps, step_two, 0)

    tile = 256

    def products(index, u_ref, a_ref):
        cols = pl.ds(pl.multiple_of(index * tile, tile), tile)
        u_ref[...] = bdot(h3_ref[...], wup_ref[:, cols])
        a_ref[...] = bdot_nt(dz_ref[...], wdn_ref[cols, :])

    def pointwise(index, u_ref, a_ref):
        cols = pl.ds(pl.multiple_of(index * tile, tile), tile)
        u = u_ref[...]
        square = u * u
        half = 0.5 + 0.5 * jnp.tanh(u * (GELU_C + (0.044715 * GELU_C) * square))
        value = u * half
        act_ref[:, cols] = value.astype(bf16)
        slope = half + (value - value * half) * (2.0 * GELU_C + (6.0 * 0.044715 * GELU_C) * square)
        du_ref[:, cols] = (a_ref[...] * slope).astype(bf16)

    tiles = hidden // tile

    def two_tiles(index, _):
        products(2 * index + 1, ub_ref, ab_ref)
        pointwise(2 * index, ua_ref, aa_ref)
        products(jnp.minimum(2 * index + 2, tiles - 1), ua_ref, aa_ref)
        pointwise(2 * index + 1, ub_ref, ab_ref)
        return 0

    products(0, ua_ref, aa_ref)
    lax.fori_loop(0, tiles // 2, two_tiles, 0)
    by_columns(lambda cols: bdot(act_ref[...], wdn_ref[:, cols]))

    def step_three(step, _):
        place, part, flat = at_rows(step)
        z = e_ref[flat, :]
        grad = g_ref[place, part, :].astype(f32)
        out_ref[place, part, :] = (xa_ref[flat, :] + mod(8, part) * z).astype(bf16)
        sum_ref[6, part, :] += grad * z
        return 0

    lax.fori_loop(0, steps, step_three, 0)
    by_columns(lambda cols: bdot_nt(du_ref[...], wup_ref[cols, :]))

    def step_four(step, _):
        place, part, flat = at_rows(step)
        grad = e_ref[flat, :]
        normed = n3_ref[flat, :]
        sum_ref[4, part, :] += grad
        sum_ref[5, part, :] += grad * normed
        back = norm_rows_back(normed, r3_ref[flat, 0:1], mod(7, part), grad)
        grad_two = g_ref[place, part, :].astype(f32) + back
        xa_ref[flat, :] = grad_two
        sum_ref[3, part, :] += grad_two * y2_ref[flat, :]
        dy2_ref[flat, :] = (mod(5, part) * grad_two).astype(bf16)
        return 0

    lax.fori_loop(0, steps, step_four, 0)
    y2_ref[...] = bdot_nt(dy2_ref[...], wto_ref[...])

    def time_pair_back(index, _):
        q_at, k_at, v_at = pair_at(index)
        gos = [y2_ref[part, q_at].astype(bf16) for part in parts]
        values = [stacked(qkv_ref[part, v_at], masks) for part in parts]
        grads = [bdot_nt(go, value) for go, value in zip(gos, values)]
        probs = [p_ref[index, part, :] for part in parts]
        inner = [half_sums(grad * prob) for grad, prob in zip(grads, probs)]
        scores = [
            (prob * (grad - mean)).astype(bf16) for prob, grad, mean in zip(probs, grads, inner)
        ]
        keys = [stacked(qkv_ref[part, k_at], masks_q) for part in parts]
        qs = [qkv_ref[part, q_at] * factor for part in parts]
        grad_q = [bdot(score, key) for score, key in zip(scores, keys)]
        grad_k = [bdot_tn(score, q) for score, q in zip(scores, qs)]
        grad_v = [bdot_tn(prob.astype(bf16), go) for prob, go in zip(probs, gos)]
        for part, g_q, g_k, g_v in zip(parts, grad_q, grad_k, grad_v):
            dqkv_ref[part, q_at] = g_q.astype(bf16)
            dqkv_ref[part, k_at] = jnp.where(is_low, g_k[:frames], g_k[frames:]).astype(bf16)
            dqkv_ref[part, v_at] = jnp.where(is_low, g_v[:frames], g_v[frames:]).astype(bf16)
        return 0

    lax.fori_loop(0, HEADS // 2, time_pair_back, 0)
    by_columns(lambda cols: bdot_nt(dqkv_ref[...], wti_ref[cols, :]))

    def step_five(step, _):
        place, part, flat = at_rows(step)
        grad = e_ref[flat, :]
        normed = n2_ref[flat, :]
        sum_ref[1, part, :] += grad
        sum_ref[2, part, :] += grad * normed
        grad_one = xa_ref[flat, :] + norm_rows_back(normed, r2_ref[flat, 0:1], mod(4, part), grad)
        dx1_ref[place, part, :] = grad_one
        sum_ref[0, part, :] += grad_one * y1_ref[flat, :]
        dy1_ref[flat, :] = (mod(2, part) * grad_one).astype(bf16)
        return 0

    lax.fori_loop(0, steps, step_five, 0)
    do1_ref[...] = bdot_nt(dy1_ref[...], wso_ref[...]).astype(bf16).reshape(count, frames, width)


VMEM_LIMIT = 62 * 1024 * 1024


def resident(shape):
    return pl.BlockSpec(shape, lambda i: (0,) * len(shape), pipeline_mode=pl.Buffered(1))


def call_space_forward(x, mods, weight):
    n_pos, own, places, width = x.shape
    patches = n_pos * places
    pair = 2 * HEAD_DIM
    spread = pl.BlockSpec((n_pos, 1, places, width), lambda i: (0, i, 0, 0))

    def by_frame(*shape):
        return pl.BlockSpec((1,) + shape, lambda i: (i, 0, 0))

    rows = own * patches
    return pl.pallas_call(
        space_forward,
        grid=(own,),
        in_specs=[spread, by_frame(2, width), resident(weight.shape)],
        out_specs=[
            by_frame(patches, width),
            by_frame(patches, 3 * width),
            pl.BlockSpec(memory_space=pl.ANY),
            pl.BlockSpec((1, HEADS // 2, patches, pair), lambda i: (i, 0, 0, 0)),
        ],
        out_shape=[
            jax.ShapeDtypeStruct((own, patches, width), bf16),
            jax.ShapeDtypeStruct((own, patches, 3 * width), bf16),
            jax.ShapeDtypeStruct((n_pos * own, places, width), bf16),
            jax.ShapeDtypeStruct((own, HEADS // 2, patches, pair), f32),
        ],
        scratch_shapes=spread_scratch(own, n_pos, places, width),
        compiler_params=pltpu.CompilerParams(
            vmem_limit_bytes=VMEM_LIMIT, collective_id=0, has_side_effects=True
        ),
        cost_estimate=pl.CostEstimate(
            flops=2 * rows * width * 3 * width + 4 * rows * patches * width,
            bytes_accessed=rows * width * 12 + weight.size * 2,
            transcendentals=rows * patches * HEADS,
        ),
        name="space_forward",
    )(x, mods, weight)


def call_space_backward(
    go, qkv, lse, x, h, mods, weight, hot, dmod_rest, grads, shapes, kinds, n_clip
):
    n_pos, own, places, width = x.shape
    patches = n_pos * places
    pair = 2 * HEAD_DIM
    lead = n_pos.bit_length() - 1
    clips = dmod_rest.shape[0]
    spread = pl.BlockSpec((n_pos, 1, places, width), lambda i: (0, i, 0, 0))
    anywhere = pl.BlockSpec(memory_space=pl.ANY)

    def by_frame(*shape):
        return pl.BlockSpec((1,) + shape, lambda i: (i, 0, 0))

    rows = own * patches
    cut = 3 * width // 512 * 256
    kinds = kinds + ((True, 0), (False, 0))
    block = width // n_pos
    flow_rows = shapes + [(block, cut), (block, 3 * width - cut)]
    views, flow_outs, flow_scratch = flow_plan(flow_rows, kinds, n_pos, n_clip)
    early = len(grads)
    late = [pltpu.VMEM(view, bf16) for view in views[early:]]
    blocked = [grad.reshape(view) for grad, view in zip(grads, views)]
    sizes = sum(grad.size for grad in grads)
    dmod_shape = (n_clip, clips, 9 * width)
    swaps = lead + len(bits_of(n_clip))
    return pl.pallas_call(
        partial(space_backward, n_clip, kinds, early),
        grid=(own,),
        in_specs=[
            spread,
            by_frame(patches, 3 * width),
            pl.BlockSpec((1, HEADS // 2, patches, pair), lambda i: (i, 0, 0, 0)),
            spread,
            by_frame(patches, width),
            by_frame(2, width),
            resident(weight.shape),
            resident(hot.shape),
            resident(dmod_rest.shape),
        ]
        + [anywhere] * len(blocked),
        out_specs=[anywhere, resident(dmod_shape)] + [resident(out.shape) for out in flow_outs],
        out_shape=[
            jax.ShapeDtypeStruct((n_pos * own, places, width), bf16),
            jax.ShapeDtypeStruct(dmod_shape, f32),
        ]
        + flow_outs,
        scratch_shapes=[
            pltpu.VMEM((patches, width), f32),
            pltpu.VMEM((patches, 3 * width), bf16),
            pltpu.VMEM((width, 3 * width), f32),
            pltpu.VMEM((clips, 9 * width), f32),
            pltpu.VMEM((lead, clips, 9 * width), f32),
            pltpu.VMEM((lead, clips, 9 * width), f32),
            pltpu.VMEM(dmod_shape, f32),
            pltpu.SemaphoreType.DMA((swaps,)),
            pltpu.SemaphoreType.DMA((swaps,)),
        ]
        + spread_scratch(own, n_pos, places, width)
        + late
        + flow_scratch,
        compiler_params=pltpu.CompilerParams(
            vmem_limit_bytes=VMEM_LIMIT, collective_id=1, has_side_effects=True
        ),
        cost_estimate=pl.CostEstimate(
            flops=4 * rows * width * 3 * width + 10 * rows * patches * width,
            bytes_accessed=rows * width * 16 + weight.size * 2 + sizes * 4,
            transcendentals=rows * patches * HEADS,
        ),
        name="space_backward",
    )(go, qkv, lse, x, h, mods, weight, hot, dmod_rest, *blocked)


def call_middle(o_one, x, grad, mods, same_clip, wso, wti, wto, wup, wdn):
    places, frames, width = x.shape
    count = max(1, min(places, 256 // frames))
    rows = count * frames
    hidden = wup.shape[1]
    pair = 2 * HEAD_DIM
    total = places * frames
    chunk = pl.BlockSpec((count, frames, width), lambda i: (i, 0, 0))

    def flat(cols):
        return pl.BlockSpec((rows, cols), lambda i: (i, 0))

    def flat_shape(cols):
        return jax.ShapeDtypeStruct((total, cols), bf16)

    def scratch(cols, dtype=f32):
        return pltpu.VMEM((rows, cols), dtype)

    lanes = jnp.concatenate([same_clip, same_clip], axis=1)
    flops = 2 * total * (2 * (wso.size + wti.size + wto.size + wup.size + wdn.size))
    return pl.pallas_call(
        middle,
        grid=(places // count,),
        in_specs=[chunk, chunk, chunk, resident(mods.shape), resident(lanes.shape)]
        + [resident(w.shape) for w in (wso, wti, wto, wup, wdn)],
        out_specs=[
            chunk,
            flat(hidden),
            flat(width),
            flat(width),
            flat(hidden),
            flat(width),
            flat(width),
            flat(width),
            flat(3 * width),
            flat(width),
            chunk,
            chunk,
            pl.BlockSpec((7, frames, width), lambda i: (0, 0, 0)),
        ],
        out_shape=[
            jax.ShapeDtypeStruct(x.shape, bf16),
            flat_shape(hidden),
            flat_shape(width),
            flat_shape(width),
            flat_shape(hidden),
            flat_shape(width),
            flat_shape(width),
            flat_shape(width),
            flat_shape(3 * width),
            flat_shape(width),
            jax.ShapeDtypeStruct(x.shape, bf16),
            jax.ShapeDtypeStruct(x.shape, f32),
            jax.ShapeDtypeStruct((7, frames, width), f32),
        ],
        scratch_shapes=[
            scratch(3 * width, bf16),
            pltpu.VMEM((HEADS // 2, rows, pair), f32),
            scratch(width),
            scratch(width),
            scratch(width),
            scratch(width),
            scratch(pair),
            scratch(pair),
            scratch(width),
            scratch(width),
        ]
        + [scratch(256)] * 4,
        compiler_params=pltpu.CompilerParams(vmem_limit_bytes=VMEM_LIMIT),
        cost_estimate=pl.CostEstimate(
            flops=flops, bytes_accessed=total * 40000, transcendentals=total * hidden
        ),
        name="middle",
    )(o_one, x, grad, mods, lanes, wso, wti, wto, wup, wdn)


def on_device(
    tokens,
    clip_lengths,
    timesteps,
    embed_first,
    embed_second,
    adaln_weight,
    spatial_in,
    spatial_out,
    temporal_in,
    temporal_out,
    hidden_up,
    hidden_down,
    grad_output,
    n_pos=16,
    n_clip=2,
):
    frames, places, width = tokens.shape
    rows = frames * places
    own = frames // n_pos
    patches = places * n_pos
    me = lax.axis_index("pos")
    clips = clip_lengths.shape[1]

    def exchange(values):
        sent = values.reshape(frames, places, width)
        got = lax.all_to_all(sent, "pos", split_axis=0, concat_axis=0, tiled=True)
        return got.reshape(n_pos, own, places, width)

    x_space = exchange(tokens)

    all_steps = by_distance(timesteps[0], "clip", n_clip)
    freq = frequency(all_steps)
    pre_cond = dot_exact(freq, embed_first)
    hidden_cond = jax.nn.silu(pre_cond)
    cond = dot_exact(hidden_cond, embed_second)
    cond_act = jax.nn.silu(cond)
    modulated = dot_exact(cond_act[:clips], adaln_weight)
    onehot, clip_ids = clip_onehot(clip_lengths[0], frames)
    per_frame = dot_high(onehot, modulated)
    own_frames = lax.dynamic_slice_in_dim(per_frame, me * own, own, 0)

    own_mods = own_frames[:, : 2 * width].reshape(own, 2, width)
    h_one, qkv_one, o_one, lse_one = call_space_forward(x_space, own_mods, spatial_in)

    def turn(values):
        return values.transpose(1, 0, 2)

    o_one = turn(o_one)
    mods = per_frame.reshape(frames, 9, width).transpose(1, 0, 2)
    same_clip = jnp.dot(onehot, onehot.T)
    (block_turned, act, grad_z, h_three, grad_u, o_two, grad_y_two, h_two, grad_qkv_two, grad_y_one, grad_o_one,
     grad_one, sums) = call_middle(
        o_one, turn(tokens), turn(grad_output), mods, same_clip, spatial_out, temporal_in, temporal_out,
        hidden_up, hidden_down,
    )
    block_out = turn(block_turned)
    grad_o_space = exchange(turn(grad_o_one))
    down = weight_grad(act, grad_z)
    down, h_three, grad_u = lax.optimization_barrier((down, h_three, grad_u))
    down_block, up_block = down.shape[0] // n_pos, width // n_pos
    up = weight_grad(h_three, grad_u)
    up, h_two, grad_qkv_two, o_one, grad_y_one, o_two, grad_y_two = lax.optimization_barrier(
        (up, h_two, grad_qkv_two, o_one, grad_y_one, o_two, grad_y_two)
    )
    grads = (
        first_swap(up, n_pos),
        column_swap(first_swap(down, n_pos), n_clip),
        weight_grad(h_two, grad_qkv_two),
        weight_grad(o_one.reshape(rows, width), grad_y_one),
        weight_grad(o_two, grad_y_two),
    )
    shapes = [
        (up_block, up.shape[1]),
        (down_block, width),
        (up_block, 3 * width),
        (up_block, width),
        (up_block, width),
    ]
    kinds = ((False, 1), (True, 2), (True, 0), (True, 0), (True, 0))
    own_hot = lax.dynamic_slice_in_dim(onehot, me * own, own, 0)
    hot = jnp.broadcast_to(own_hot[:, :, None], (own, clips, 128))
    dmod_rest = dot_high(onehot.T, sums.transpose(1, 0, 2).reshape(frames, 7 * width))
    (
        back_places, dmod, g_hidden_up, g_hidden_down, g_temporal_in, g_spatial_out, g_temporal_out,
        in_low, in_high,
    ) = call_space_backward(
        grad_o_space, qkv_one, lse_one, x_space, h_one, own_mods, spatial_in, hot, dmod_rest,
        grads, shapes, kinds, n_clip,
    )
    grad_tokens = (turn(grad_one) + back_places.astype(f32)).astype(bf16)
    g_spatial_in = jnp.concatenate([in_low, in_high], axis=1)
    dmod = dmod.reshape(n_clip * clips, 9 * width)

    def own_columns(values):
        block = values.shape[1] // n_pos
        return lax.dynamic_slice_in_dim(values, me * block, block, 1)

    g_adaln = dot_high(own_columns(cond_act).T, dmod)
    grad_cond = dot_exact(dmod, adaln_weight.T) * silu_grad(cond)
    g_second = dot_high(own_columns(hidden_cond).T, grad_cond)
    grad_pre = dot_exact(grad_cond, embed_second.T) * silu_grad(pre_cond)
    g_first = dot_high(own_columns(freq).T, grad_pre)
    return (
        block_out,
        grad_tokens,
        g_first,
        g_second,
        g_adaln,
        g_spatial_in,
        g_spatial_out,
        g_temporal_in,
        g_temporal_out,
        g_hidden_up,
        g_hidden_down,
    )


def solution(mesh):
    in_specs = (
        P("clip", "pos", None),
        P("clip", None),
        P("clip", None),
        P(),
        P(),
        P(),
        P(),
        P(),
        P(),
        P(),
        P(),
        P(),
        P("clip", "pos", None),
    )
    out_specs = (P("clip", "pos", None),) * 2 + (P("pos", None),) * 9
    body = partial(on_device, n_pos=mesh.shape["pos"], n_clip=mesh.shape["clip"])
    return jax.shard_map(body, mesh=mesh, in_specs=in_specs, out_specs=out_specs, check_vma=False)
```

```python
from functools import partial
import math

import jax
import jax.numpy as jnp
from jax import lax
from jax.experimental import pallas as pl
from jax.experimental.pallas import tpu as pltpu
from jax.sharding import PartitionSpec as P

HEADS = 12
HEAD_DIM = 64
FREQ = 256

epsilon = 1e-06
highest = lax.Precision.HIGHEST
masked_score = -1000000000.0
f32 = jnp.float32
bf16 = jnp.bfloat16


def frequency(step_ids):
    half_width = FREQ // 2
    rate_table = jnp.exp(
        -math.log(10000.0) * jnp.arange(half_width, dtype=jnp.float32) / half_width
    )
    angles = step_ids.astype(jnp.float32)[:, None] * rate_table[None, :]
    return jnp.concatenate([jnp.cos(angles), jnp.sin(angles)], axis=1)


def dot_high(left, right):
    return jnp.dot(left, right, precision=highest, preferred_element_type=f32)


def silu_grad(values):
    gate = jax.nn.sigmoid(values)
    return gate * (1.0 + values * (1.0 - gate))


def clip_onehot(lengths, frames):
    clip_ends = jnp.cumsum(lengths)
    frame_ids = jnp.arange(frames, dtype=jnp.int32)
    clip_ids = jnp.sum((frame_ids[:, None] >= clip_ends[None, :]).astype(jnp.int32), axis=1)
    onehot = (clip_ids[:, None] == jnp.arange(lengths.shape[0], dtype=jnp.int32)[None, :]).astype(
        jnp.float32
    )
    return (onehot, clip_ids)


def weight_grad(left, right):
    return jnp.einsum("rd,rk->dk", left, right, preferred_element_type=f32).astype(bf16)


def bdot(left, right):
    return lax.dot_general(left, right, (((1,), (0,)), ((), ())), preferred_element_type=f32)


def bdot_nt(left, right):
    return lax.dot_general(left, right, (((1,), (1,)), ((), ())), preferred_element_type=f32)


def bdot_tn(left, right):
    return lax.dot_general(left, right, (((0,), (0,)), ((), ())), preferred_element_type=f32)


def norm_rows(values):
    width = values.shape[-1]
    centre = values - jnp.sum(values, axis=-1, keepdims=True) * (1.0 / width)
    spread = jnp.sum(centre * centre, axis=-1, keepdims=True) * (1.0 / width)
    inverse = lax.rsqrt(spread + epsilon)
    return centre * inverse, inverse


def norm_rows_back(normed, inverse, scale_vec, grad):
    width = grad.shape[-1]
    inner = grad * (1.0 + scale_vec)
    mean_one = jnp.sum(inner, axis=-1, keepdims=True) * (1.0 / width)
    mean_two = jnp.sum(inner * normed, axis=-1, keepdims=True) * (1.0 / width)
    return inverse * (inner - mean_one - normed * mean_two)


def pair_masks(scale):
    lanes = lax.broadcasted_iota(jnp.int32, (1, 2 * HEAD_DIM), 1)
    low_half = jnp.where(lanes < HEAD_DIM, scale, 0.0).astype(bf16)
    high_half = jnp.where(lanes < HEAD_DIM, 0.0, scale).astype(bf16)
    return low_half, high_half


ROWS = 32


def load_rows(ref, step):
    places, width = ref.shape[2:]
    count = max(1, ROWS // places)
    part = ref[pl.ds(step * count, count), 0].astype(f32)
    return part.reshape(count * places, width)


def swap(values, axis, size, bit):
    return lax.ppermute(values, axis, [(i, i ^ bit) for i in range(size)])


def bits_of(size):
    return [1 << i for i in range(size.bit_length() - 1)]


def by_distance(values, axis, size):
    for bit in bits_of(size):
        values = jnp.concatenate([values, swap(values, axis, size, bit)], axis=0)
    return values


def dot_exact(left, right):
    parts = []
    for _ in range(3):
        part = left.astype(bf16)
        parts.append(part)
        left = left - part.astype(f32)
    count = parts[0].shape[0]
    got = jnp.dot(jnp.concatenate(parts, axis=0), right, preferred_element_type=f32)
    return got[:count] + (got[count : 2 * count] + got[2 * count :])


def flow_stages(n_pos, n_clip, clip_first):
    pos = [("pos", bit, "halve") for bit in bits_of(n_pos)]
    clip = bits_of(n_clip)
    if not clip_first:
        return pos + [("clip", bit, "sum") for bit in clip]
    first = [("clip", clip[0], "columns")]
    last = [("clip", clip[0], "gather")]
    return pos[:1] + first + pos[1:] + [("clip", bit, "sum") for bit in clip[1:]] + last


def flow_shapes(stages, n_pos, block, cols):
    lead = n_pos.bit_length() - 1
    shapes = []
    for _, _, what in stages:
        if what == "halve":
            lead -= 1
        elif what == "columns":
            cols //= 2
        shapes.append((2,) * lead + (block, cols))
    return shapes


class Flow:
    def __init__(self, number, stages, grad, out, keep, gots, sems, place):
        self.number, self.stages = number, stages
        self.grad, self.out, self.keep, self.gots = grad, out, keep, gots
        self.send_sem, self.recv_sem, self.keep_sem = sems
        self.place = place

    def side(self, stage):
        axis, bit, _ = self.stages[stage]
        return lax.rem(self.place[axis] // bit, 2)

    def columns(self, side, width):
        return pl.ds(pl.multiple_of(side * width, width), width)

    def part(self, ref, stage, side):
        what = self.stages[stage][2]
        lead = len(ref.shape) - 2
        if what == "halve":
            return (slice(None),) * (lead - 1) + (side,)
        if what == "columns":
            half = ref.shape[-1] // 2
            return (slice(None),) * (lead + 1) + (self.columns(side, half),)
        return None

    def held(self, stage):
        if stage == 0:
            return self.grad
        return self.keep if stage == 1 else self.gots[stage - 1]

    def copy(self, stage):
        axis, bit, _ = self.stages[stage]
        side = self.side(stage)
        source = self.held(stage)
        at = self.part(source, stage, 1 - side)
        return pltpu.make_async_remote_copy(
            source if at is None else source.at[at],
            self.gots[stage],
            self.send_sem.at[self.number, stage],
            self.recv_sem.at[self.number, stage],
            device_id={axis: self.place[axis] + bit * (1 - 2 * side)},
            device_id_type=pl.DeviceIdType.MESH,
        )

    def own(self):
        at = self.part(self.grad, 0, self.side(0))
        return pltpu.make_async_copy(self.grad.at[at], self.keep, self.keep_sem.at[self.number])

    def start(self):
        self.copy(0).start()
        self.own().start()

    def take(self, stage):
        self.copy(stage).wait_recv()
        if stage == 0:
            self.own().wait()
        what = self.stages[stage][2]
        got = self.gots[stage]
        side = self.side(stage)
        last = stage == len(self.stages) - 1
        lead = len(got.shape) - 2
        if what == "gather":
            half = got.shape[-1]
            self.out[:, self.columns(side, half)] = self.held(stage)[...].astype(f32)
            self.out[:, self.columns(1 - side, half)] = got[...].astype(f32)
            return
        if last:
            self.out[...] = self.held(stage)[...].astype(f32) + got[...].astype(f32)
            return
        target = self.keep if stage == 0 else got

        def one(index, _):
            at = tuple(lax.rem(index // (1 << i), 2) for i in range(lead))
            if stage == 0:
                mine = self.keep[at]
            elif what == "halve":
                mine = self.held(stage)[at + (side,)]
            elif what == "columns":
                mine = self.held(stage)[at + (slice(None), self.columns(side, got.shape[-1]))]
            else:
                mine = self.held(stage)[at]
            target[at] = mine + got[at]
            return 0

        lax.fori_loop(0, 1 << lead, one, 0)
        self.copy(stage + 1).start()

    def finish(self):
        for stage in range(len(self.stages)):
            self.copy(stage).wait_send()


class Butterfly:
    def __init__(self, n_pos, n_clip, values, out, got, acc, sems, place):
        self.pos_bits, self.clip_bits = bits_of(n_pos), bits_of(n_clip)
        self.values, self.out, self.got, self.acc = values, out, got, acc
        self.send_sem, self.recv_sem = sems
        self.place = place
        self.count = len(self.pos_bits) + len(self.clip_bits)

    def copy(self, stage):
        if stage < len(self.pos_bits):
            axis, bit = "pos", self.pos_bits[stage]
            source = self.values if stage == 0 else self.acc.at[stage - 1]
            target = self.got.at[stage]
        else:
            axis, bit = "clip", self.clip_bits[stage - len(self.pos_bits)]
            source, target = self.out.at[pl.ds(0, bit)], self.out.at[pl.ds(bit, bit)]
        side = lax.rem(self.place[axis] // bit, 2)
        return pltpu.make_async_remote_copy(
            source,
            target,
            self.send_sem.at[stage],
            self.recv_sem.at[stage],
            device_id={axis: self.place[axis] + bit * (1 - 2 * side)},
            device_id_type=pl.DeviceIdType.MESH,
        )

    def start(self):
        self.copy(0).start()

    def take(self, stage):
        self.copy(stage).wait_recv()
        last = len(self.pos_bits) - 1
        if stage <= last:
            mine = self.values[...] if stage == 0 else self.acc[stage - 1]
            if stage < last:
                self.acc[stage] = mine + self.got[stage]
            else:
                self.out[0] = mine + self.got[stage]
        if stage + 1 < self.count:
            self.copy(stage + 1).start()

    def finish(self):
        for stage in range(self.count):
            self.copy(stage).wait_send()


def partner_list(n_pos, n_clip):
    return [("pos", bit) for bit in bits_of(n_pos)] + [("clip", bit) for bit in bits_of(n_clip)]


def here():
    return {"pos": lax.axis_index("pos"), "clip": lax.axis_index("clip")}


def signal_swap(barrier, place, axis, bit):
    side = lax.rem(place[axis] // bit, 2)
    pl.semaphore_signal(
        barrier,
        inc=1,
        device_id={axis: place[axis] + bit * (1 - 2 * side)},
        device_id_type=pl.DeviceIdType.MESH,
    )


def make_flows(n_pos, n_clip, kinds, grads, outs, scratch):
    sems, rest = scratch[:3], list(scratch[3:])
    flows = []
    for number, clip_first in enumerate(kinds):
        stages = flow_stages(n_pos, n_clip, clip_first)
        keep, gots = rest[0], rest[1 : 1 + len(stages)]
        rest = rest[1 + len(stages) :]
        flows.append(Flow(number, stages, grads[number], outs[number], keep, gots, sems, here()))
    return flows


def flow_plan(grads, kinds, n_pos, n_clip):
    lead = n_pos.bit_length() - 1
    most = lead + len(bits_of(n_clip)) + 1
    dma = pltpu.SemaphoreType.DMA
    scratch = [dma((len(grads), most)), dma((len(grads), most)), dma((len(grads),))]
    views, out_shape = [], []
    for grad, clip_first in zip(grads, kinds):
        rows, cols = grad.shape
        block = rows // n_pos
        if isinstance(grad, jax.ShapeDtypeStruct):
            views.append(pltpu.VMEM((2,) * lead + (block, cols), bf16))
        else:
            views.append(grad.reshape((2,) * lead + (block, cols)))
        out_shape.append(jax.ShapeDtypeStruct((block, cols), f32))
        shapes = flow_shapes(flow_stages(n_pos, n_clip, clip_first), n_pos, block, cols)
        scratch += [pltpu.VMEM(shape, bf16) for shape in [shapes[0]] + shapes]
    return views, out_shape, scratch


class Spread:

    def __init__(self, n_pos, step, steps, hold, out, send_sem, recv_sem, own_sem):
        self.n_pos, self.step, self.steps = n_pos, step, steps
        self.hold, self.out = hold, out
        self.send_sem, self.recv_sem, self.own_sem = send_sem, recv_sem, own_sem
        self.me = lax.axis_index("pos")

    def greet(self, more=0):
        barrier = pltpu.get_barrier_semaphore()

        def signal(shift, _):
            target = lax.rem(self.me + shift, self.n_pos)
            pl.semaphore_signal(
                barrier, inc=1, device_id={"pos": target}, device_id_type=pl.DeviceIdType.MESH
            )
            return 0

        lax.fori_loop(1, self.n_pos, signal, 0)
        pl.semaphore_wait(barrier, self.n_pos - 1 + more)

    def copy(self, step, shift, source):
        target = lax.rem(self.me + shift, self.n_pos)
        return pltpu.make_async_remote_copy(
            self.hold.at[step, target],
            self.out.at[source * self.steps + step],
            self.send_sem.at[step, shift],
            self.recv_sem.at[step, shift],
            device_id={"pos": target},
            device_id_type=pl.DeviceIdType.MESH,
        )

    def stay(self, step):
        return pltpu.make_async_copy(
            self.hold.at[step, self.me],
            self.out.at[self.me * self.steps + step],
            self.own_sem.at[step],
        )

    def send(self):
        def one(shift, _):
            self.copy(self.step, shift, self.me).start()
            return 0

        lax.fori_loop(1, self.n_pos, one, 0)
        self.stay(self.step).start()

    def finish(self):
        def one_step(step, _):
            def one(shift, _):
                self.copy(step, shift, self.me).wait_send()
                source = lax.rem(self.me + self.n_pos - shift, self.n_pos)
                self.copy(step, shift, source).wait_recv()
                return 0

            lax.fori_loop(1, self.n_pos, one, 0)
            self.stay(step).wait()
            return 0

        lax.fori_loop(0, self.steps, one_step, 0)


def spread_scratch(own, n_pos, places, width):
    return [
        pltpu.VMEM((own, n_pos, places, width), bf16),
        pltpu.SemaphoreType.DMA((own, n_pos)),
        pltpu.SemaphoreType.DMA((own, n_pos)),
        pltpu.SemaphoreType.DMA((own,)),
    ]


def space_forward(
    x_ref, mod_ref, w_ref, h_ref, qkv_ref, o_ref, lse_ref, hold, send_sem, recv_sem, own_sem
):
    own, n_pos = hold.shape[:2]
    frame = pl.program_id(0)
    spread = Spread(n_pos, frame, own, hold, o_ref, send_sem, recv_sem, own_sem)
    pl.when(frame == 0)(spread.greet)
    patches, width = h_ref.shape[1:]
    places = x_ref.shape[2]
    pair = 2 * HEAD_DIM
    shift, scale = mod_ref[0, 0:1, :], mod_ref[0, 1:2, :]

    def norm_step(step, _):
        normed, _inverse = norm_rows(load_rows(x_ref, step))
        h_ref[0, pl.ds(step * ROWS, ROWS), :] = (normed * (1.0 + scale) + shift).astype(bf16)
        return 0

    lax.fori_loop(0, patches // ROWS, norm_step, 0)

    def project(third, _):
        cols = pl.ds(pl.multiple_of(third * width, width), width)
        qkv_ref[0, :, cols] = bdot(h_ref[0], w_ref[:, cols]).astype(bf16)
        return 0

    lax.fori_loop(0, 3, project, 0)
    masks = pair_masks(1.0 / math.sqrt(HEAD_DIM))
    is_low = lax.broadcasted_iota(jnp.int32, (1, pair), 1) < HEAD_DIM

    def head_pair(index, _):
        at = pl.multiple_of(index * pair, pair)
        q = qkv_ref[0, :, pl.ds(at, pair)]
        k = qkv_ref[0, :, pl.ds(pl.multiple_of(width + at, pair), pair)]
        v = qkv_ref[0, :, pl.ds(pl.multiple_of(2 * width + at, pair), pair)]
        one = jnp.ones_like(v)
        values = [jnp.where(is_low, v, one), jnp.where(is_low, one, v)]
        scores = [bdot_nt(q * mask, k) for mask in masks]
        tops = [jnp.max(score, axis=-1, keepdims=True) for score in scores]
        exps = [jnp.exp(score - top).astype(bf16) for score, top in zip(scores, tops)]
        outs = [bdot(exp, value) for exp, value in zip(exps, values)]
        total = pltpu.roll(jnp.where(is_low, outs[1], outs[0]), HEAD_DIM, 1)
        both = jnp.where(is_low, outs[0], outs[1]) / total
        lse_ref[0, index] = jnp.where(is_low, tops[0], tops[1]) + jnp.log(total)
        hold[frame, :, :, pl.ds(at, pair)] = both.reshape(n_pos, places, pair).astype(bf16)
        return 0

    lax.fori_loop(0, HEADS // 2, head_pair, 0)
    spread.send()
    pl.when(frame == own - 1)(spread.finish)


def space_backward(n_clip, kinds, early, *refs):
    go_ref, qkv_ref, lse_ref, x_ref, h_ref, mod_ref, w_ref, hot_ref, rest_ref = refs[:9]
    grads, refs = refs[9 : 9 + early], refs[9 + early :]
    dv_ref, dmod_ref = refs[:2]
    outs, refs = refs[2 : 2 + len(kinds)], refs[2 + len(kinds) :]
    e_ref, dqkv_ref, total_ref, small_ref, got_ref, acc_ref, every_ref = refs[:7]
    small_send, small_recv, hold, send_sem, recv_sem, own_sem = refs[7:13]
    late_grads, refs = refs[13 : 13 + len(kinds) - early], refs[13 + len(kinds) - early :]
    own, n_pos = hold.shape[:2]
    frame = pl.program_id(0)
    spread = Spread(n_pos, frame, own, hold, dv_ref, send_sem, recv_sem, own_sem)
    flows = make_flows(n_pos, n_clip, kinds, tuple(grads) + tuple(late_grads), outs, refs)
    late = flows[early:]
    tree = Butterfly(
        n_pos, n_clip, small_ref, every_ref, got_ref, acc_ref, (small_send, small_recv), here()
    )
    stages = max(len(flow.stages) for flow in flows)
    order = [(i, stage) for stage in range(stages) for i in range(early)]
    order = [(i, stage) for i, stage in order if stage < len(flows[i].stages)]
    cuts = [2, early, early + 2]

    @pl.when(frame == 0)
    def _():
        place = here()
        others = [("clip", bit) for bit in bits_of(n_clip)]
        barrier = pltpu.get_barrier_semaphore()
        for axis, bit in others:
            signal_swap(barrier, place, axis, bit)
        spread.greet(len(others))
        for flow in flows[:early]:
            flow.start()

        def clear(step, _):
            total_ref[pl.ds(step * 8, 8), :] = jnp.zeros((8, total_ref.shape[1]), f32)
            return 0

        lax.fori_loop(0, total_ref.shape[0] // 8, clear, 0)
        small_ref[:, : 2 * x_ref.shape[3]] = jnp.zeros_like(small_ref[:, : 2 * x_ref.shape[3]])
        small_ref[:, 2 * x_ref.shape[3] :] = rest_ref[...]

    def advance(steps):
        for i, stage in steps:
            flows[i].take(stage)

    def start_late():
        block = late_grads[0].shape[-2]
        lead = len(late_grads[0].shape) - 2

        def one(index, _):
            at = tuple(lax.rem(index // (1 << i), 2) for i in reversed(range(lead)))
            rows = pl.ds(pl.multiple_of(index * block, 8), block)
            first = 0
            for grad in late_grads:
                cols = grad.shape[-1]
                grad[at] = total_ref[rows, first : first + cols].astype(bf16)
                first += cols
            return 0

        lax.fori_loop(0, n_pos, one, 0)
        for flow in late:
            flow.start()

    patches = qkv_ref.shape[1]
    width = x_ref.shape[3]
    places = x_ref.shape[2]
    pair = 2 * HEAD_DIM
    scale = mod_ref[0, 1:2, :]
    factor = 1.0 / math.sqrt(HEAD_DIM)
    masks_q = pair_masks(factor)
    masks = pair_masks(1.0)
    ones = jnp.ones((patches, pair), bf16)

    def key_sums(values):
        high = values.astype(bf16)
        low = (values - high.astype(f32)).astype(bf16)
        total = bdot(high, ones) + bdot(low, ones)
        return jnp.concatenate([total] * (patches // pair), axis=1)

    def head_pair(index, _):
        at = pl.multiple_of(index * pair, pair)
        k_at = pl.multiple_of(width + at, pair)
        v_at = pl.multiple_of(2 * width + at, pair)
        q = qkv_ref[0, :, pl.ds(at, pair)]
        k = qkv_ref[0, :, pl.ds(k_at, pair)]
        v = qkv_ref[0, :, pl.ds(v_at, pair)]
        go = go_ref[:, 0, :, pl.ds(at, pair)].astype(f32).reshape(patches, pair).astype(bf16)
        lse_pair = lse_ref[0, index]
        lses = [lse_pair[:, 0:1], lse_pair[:, HEAD_DIM : HEAD_DIM + 1]]
        q_halves = [q * mask for mask in masks_q]
        go_halves = [go * mask for mask in masks]
        probs = [jnp.exp(bdot_nt(half, k) - lse) for half, lse in zip(q_halves, lses)]
        grads = [bdot_nt(half, v) for half in go_halves]
        inner = [key_sums(grad * prob) for grad, prob in zip(grads, probs)]
        scores = [
            (prob * (grad - mean)).astype(bf16) for prob, grad, mean in zip(probs, grads, inner)
        ]
        gq = sum(bdot(score, k * mask) for score, mask in zip(scores, masks_q))
        gk = sum(bdot_tn(score, half) for score, half in zip(scores, q_halves))
        gv = sum(bdot_tn(prob.astype(bf16), half) for prob, half in zip(probs, go_halves))
        dqkv_ref[:, pl.ds(at, pair)] = gq.astype(bf16)
        dqkv_ref[:, pl.ds(k_at, pair)] = gk.astype(bf16)
        dqkv_ref[:, pl.ds(v_at, pair)] = gv.astype(bf16)
        return 0

    lax.fori_loop(0, HEADS // 2, head_pair, 0)
    e_ref[...] = bdot_nt(dqkv_ref[...], w_ref[...])

    def norm_step(step, sums):
        grad = e_ref[pl.ds(step * ROWS, ROWS), :]
        normed, inverse = norm_rows(load_rows(x_ref, step))
        back = norm_rows_back(normed, inverse, scale, grad)
        count = max(1, ROWS // places)
        back = back.reshape(count, places, width).astype(bf16)
        hold[frame, pl.ds(step * count, count)] = back
        folded = grad.reshape(ROWS // 8, 8, width).sum(axis=0)
        folded_n = (grad * normed).reshape(ROWS // 8, 8, width).sum(axis=0)
        return sums[0] + folded, sums[1] + folded_n

    zero = jnp.zeros((8, width), f32)
    shift_sum, scale_sum = lax.fori_loop(0, patches // ROWS, norm_step, (zero, zero))
    spread.send()
    hot = hot_ref[frame][:, 0:1]
    small_ref[:, :width] += hot * jnp.sum(shift_sum, axis=0, keepdims=True)
    small_ref[:, width : 2 * width] += hot * jnp.sum(scale_sum, axis=0, keepdims=True)

    def accumulate(third, _):
        cols = pl.ds(pl.multiple_of(third * width, width), width)
        total_ref[:, cols] += bdot_tn(h_ref[0], dqkv_ref[:, cols])
        return 0

    lax.fori_loop(0, 3, accumulate, 0)
    done = 0
    for index, cut in enumerate(cuts[: own - 1]):
        pl.when(frame == index)(partial(advance, order[done:cut]))
        done = cut

    @pl.when(frame == own - 1)
    def _():
        tree.start()
        start_late()
        left = order[done:]
        for turn in range(stages + 1):
            advance([step for step in left if step[1] == turn])
            if turn < tree.count:
                tree.take(turn)
            for flow in late:
                if 0 <= turn - 1 < len(flow.stages):
                    flow.take(turn - 1)
        dmod_ref[...] = every_ref[...]
        spread.finish()
        tree.finish()
        for flow in flows:
            flow.finish()


GELU_C = math.sqrt(2.0 / math.pi)


def middle(
    o1_ref, x_ref, g_ref, mod_ref, clip_ref, wso_ref, wti_ref, wto_ref, wup_ref, wdn_ref,
    out_ref, act_ref, dz_ref, h3_ref, du_ref, o2_ref, dy2_ref, h2_ref, dqkv_ref, dy1_ref, do1_ref,
    dx1_ref, sum_ref,
    qkv_ref, p_ref, y1_ref, y2_ref, n2_ref, n3_ref, r2_ref, r3_ref, xa_ref, e_ref,
    ua_ref, aa_ref, ub_ref, ab_ref,
):
    count, frames, width = x_ref.shape
    rows = count * frames
    pair = 2 * HEAD_DIM
    hidden = act_ref.shape[1]
    factor = 1.0 / math.sqrt(HEAD_DIM)
    per = frames // ROWS
    steps = rows // ROWS

    @pl.when(pl.program_id(0) == 0)
    def _():
        sum_ref[...] = jnp.zeros_like(sum_ref)

    def at_rows(step):
        return step // per, pl.ds(lax.rem(step, per) * ROWS, ROWS), pl.ds(step * ROWS, ROWS)

    def mod(index, part):
        return mod_ref[index, part, :]

    y1_ref[...] = bdot(o1_ref[...].reshape(rows, width), wso_ref[...])

    def step_one(step, _):
        place, part, flat = at_rows(step)
        x_one = x_ref[place, part, :].astype(f32) + mod(2, part) * y1_ref[flat, :]
        xa_ref[flat, :] = x_one
        normed, inverse = norm_rows(x_one)
        n2_ref[flat, :] = normed
        r2_ref[flat, :] = jnp.broadcast_to(inverse, (ROWS, pair))
        h2_ref[flat, :] = (normed * (1.0 + mod(4, part)) + mod(3, part)).astype(bf16)
        return 0

    lax.fori_loop(0, steps, step_one, 0)

    def project(third, _):
        cols = pl.ds(pl.multiple_of(third * width, width), width)
        qkv_ref[:, cols] = bdot(h2_ref[...], wti_ref[:, cols]).astype(bf16)
        return 0

    lax.fori_loop(0, 3, project, 0)

    masks = pair_masks(1.0)
    masks_q = pair_masks(factor)
    lane_ids = lax.broadcasted_iota(jnp.int32, (1, pair), 1)
    is_low = lane_ids < HEAD_DIM
    allowed = clip_ref[...] > 0.5

    def halves(values, reduce, neutral):
        low_part = reduce(jnp.where(is_low, values, neutral), axis=-1, keepdims=True)
        high_part = reduce(jnp.where(is_low, neutral, values), axis=-1, keepdims=True)
        return jnp.where(is_low, low_part, high_part)

    def stacked(values, pair_of_masks):
        return jnp.concatenate([values * pair_of_masks[0], values * pair_of_masks[1]], axis=0)

    def pair_at(index):
        at = pl.multiple_of(index * pair, pair)
        return (
            pl.ds(at, pair),
            pl.ds(pl.multiple_of(width + at, pair), pair),
            pl.ds(pl.multiple_of(2 * width + at, pair), pair),
        )

    parts = [slice(place * frames, (place + 1) * frames) for place in range(count)]
    same_half = (
        lax.broadcasted_iota(jnp.int32, (pair, pair), 0) // HEAD_DIM
        == lax.broadcasted_iota(jnp.int32, (pair, pair), 1) // HEAD_DIM
    )
    ones = jnp.where(same_half, 1.0, 0.0).astype(bf16)

    def half_sums(values):
        high = values.astype(bf16)
        low = (values - high.astype(f32)).astype(bf16)
        return bdot(high, ones) + bdot(low, ones)

    def time_pair(index, _):
        jobs = [(2 * index + i, part) + pair_at(2 * index + i) for i in range(2) for part in parts]
        keys = [stacked(qkv_ref[part, k_at], masks_q) for _i, part, q_at, k_at, v_at in jobs]
        scores = [bdot_nt(qkv_ref[job[1], job[2]], key) for job, key in zip(jobs, keys)]
        scores = [jnp.where(allowed, score, masked_score) for score in scores]
        tops = [halves(score, jnp.max, -jnp.inf) for score in scores]
        exps = [jnp.exp(score - top) for score, top in zip(scores, tops)]
        sums = [half_sums(exp) for exp in exps]
        probs = [exp / total for exp, total in zip(exps, sums)]
        values = [stacked(qkv_ref[job[1], job[4]], masks) for job in jobs]
        outs = [bdot(prob.astype(bf16), value) for prob, value in zip(probs, values)]
        for (i, part, q_at, _k, _v), prob, out in zip(jobs, probs, outs):
            p_ref[i, part, :] = prob
            o2_ref[part, q_at] = out.astype(bf16)
        return 0

    lax.fori_loop(0, HEADS // 4, time_pair, 0)

    y2_ref[...] = bdot(o2_ref[...], wto_ref[...])

    def step_two(step, _):
        place, part, flat = at_rows(step)
        x_two = xa_ref[flat, :] + mod(5, part) * y2_ref[flat, :]
        xa_ref[flat, :] = x_two
        normed, inverse = norm_rows(x_two)
        n3_ref[flat, :] = normed
        r3_ref[flat, :] = jnp.broadcast_to(inverse, (ROWS, pair))
        h3_ref[flat, :] = (normed * (1.0 + mod(7, part)) + mod(6, part)).astype(bf16)
        dz_ref[flat, :] = (mod(8, part) * g_ref[place, part, :].astype(f32)).astype(bf16)
        return 0

    lax.fori_loop(0, steps, step_two, 0)

    tile = 256

    def products(index, u_ref, a_ref):
        cols = pl.ds(pl.multiple_of(index * tile, tile), tile)
        u_ref[...] = bdot(h3_ref[...], wup_ref[:, cols])
        a_ref[...] = bdot_nt(dz_ref[...], wdn_ref[cols, :])

    def pointwise(index, u_ref, a_ref):
        cols = pl.ds(pl.multiple_of(index * tile, tile), tile)
        u = u_ref[...]
        square = u * u
        half = 0.5 + 0.5 * jnp.tanh(u * (GELU_C + (0.044715 * GELU_C) * square))
        value = u * half
        act_ref[:, cols] = value.astype(bf16)
        slope = half + (value - value * half) * (2.0 * GELU_C + (6.0 * 0.044715 * GELU_C) * square)
        du_ref[:, cols] = (a_ref[...] * slope).astype(bf16)

    tiles = hidden // tile

    def two_tiles(index, _):
        products(2 * index + 1, ub_ref, ab_ref)
        pointwise(2 * index, ua_ref, aa_ref)
        products(jnp.minimum(2 * index + 2, tiles - 1), ua_ref, aa_ref)
        pointwise(2 * index + 1, ub_ref, ab_ref)
        return 0

    products(0, ua_ref, aa_ref)
    lax.fori_loop(0, tiles // 2, two_tiles, 0)
    e_ref[...] = bdot(act_ref[...], wdn_ref[...])

    def step_three(step, _):
        place, part, flat = at_rows(step)
        z = e_ref[flat, :]
        grad = g_ref[place, part, :].astype(f32)
        out_ref[place, part, :] = (xa_ref[flat, :] + mod(8, part) * z).astype(bf16)
        sum_ref[6, part, :] += grad * z
        return 0

    lax.fori_loop(0, steps, step_three, 0)

    def back_up(index, _):
        cols = pl.ds(pl.multiple_of(index * tile, tile), tile)
        e_ref[:, cols] = bdot_nt(du_ref[...], wup_ref[cols, :])
        return 0

    lax.fori_loop(0, width // tile, back_up, 0)

    def step_four(step, _):
        place, part, flat = at_rows(step)
        grad = e_ref[flat, :]
        normed = n3_ref[flat, :]
        sum_ref[4, part, :] += grad
        sum_ref[5, part, :] += grad * normed
        back = norm_rows_back(normed, r3_ref[flat, 0:1], mod(7, part), grad)
        grad_two = g_ref[place, part, :].astype(f32) + back
        xa_ref[flat, :] = grad_two
        sum_ref[3, part, :] += grad_two * y2_ref[flat, :]
        dy2_ref[flat, :] = (mod(5, part) * grad_two).astype(bf16)
        return 0

    lax.fori_loop(0, steps, step_four, 0)
    y2_ref[...] = bdot_nt(dy2_ref[...], wto_ref[...])

    def time_pair_back(index, _):
        q_at, k_at, v_at = pair_at(index)
        gos = [y2_ref[part, q_at].astype(bf16) for part in parts]
        values = [stacked(qkv_ref[part, v_at], masks) for part in parts]
        grads = [bdot_nt(go, value) for go, value in zip(gos, values)]
        probs = [p_ref[index, part, :] for part in parts]
        inner = [half_sums(grad * prob) for grad, prob in zip(grads, probs)]
        scores = [
            (prob * (grad - mean)).astype(bf16) for prob, grad, mean in zip(probs, grads, inner)
        ]
        keys = [stacked(qkv_ref[part, k_at], masks_q) for part in parts]
        qs = [qkv_ref[part, q_at] * factor for part in parts]
        grad_q = [bdot(score, key) for score, key in zip(scores, keys)]
        grad_k = [bdot_tn(score, q) for score, q in zip(scores, qs)]
        grad_v = [bdot_tn(prob.astype(bf16), go) for prob, go in zip(probs, gos)]
        for part, g_q, g_k, g_v in zip(parts, grad_q, grad_k, grad_v):
            dqkv_ref[part, q_at] = g_q.astype(bf16)
            dqkv_ref[part, k_at] = jnp.where(is_low, g_k[:frames], g_k[frames:]).astype(bf16)
            dqkv_ref[part, v_at] = jnp.where(is_low, g_v[:frames], g_v[frames:]).astype(bf16)
        return 0

    lax.fori_loop(0, HEADS // 2, time_pair_back, 0)
    e_ref[...] = bdot_nt(dqkv_ref[...], wti_ref[...])

    def step_five(step, _):
        place, part, flat = at_rows(step)
        grad = e_ref[flat, :]
        normed = n2_ref[flat, :]
        sum_ref[1, part, :] += grad
        sum_ref[2, part, :] += grad * normed
        grad_one = xa_ref[flat, :] + norm_rows_back(normed, r2_ref[flat, 0:1], mod(4, part), grad)
        dx1_ref[place, part, :] = grad_one
        sum_ref[0, part, :] += grad_one * y1_ref[flat, :]
        dy1_ref[flat, :] = (mod(2, part) * grad_one).astype(bf16)
        return 0

    lax.fori_loop(0, steps, step_five, 0)
    do1_ref[...] = bdot_nt(dy1_ref[...], wso_ref[...]).astype(bf16).reshape(count, frames, width)


VMEM_LIMIT = 62 * 1024 * 1024


def resident(shape):
    return pl.BlockSpec(shape, lambda i: (0,) * len(shape), pipeline_mode=pl.Buffered(1))


def call_space_forward(x, mods, weight):
    n_pos, own, places, width = x.shape
    patches = n_pos * places
    pair = 2 * HEAD_DIM
    spread = pl.BlockSpec((n_pos, 1, places, width), lambda i: (0, i, 0, 0))

    def by_frame(*shape):
        return pl.BlockSpec((1,) + shape, lambda i: (i, 0, 0))

    rows = own * patches
    return pl.pallas_call(
        space_forward,
        grid=(own,),
        in_specs=[spread, by_frame(2, width), resident(weight.shape)],
        out_specs=[
            by_frame(patches, width),
            by_frame(patches, 3 * width),
            pl.BlockSpec(memory_space=pl.ANY),
            pl.BlockSpec((1, HEADS // 2, patches, pair), lambda i: (i, 0, 0, 0)),
        ],
        out_shape=[
            jax.ShapeDtypeStruct((own, patches, width), bf16),
            jax.ShapeDtypeStruct((own, patches, 3 * width), bf16),
            jax.ShapeDtypeStruct((n_pos * own, places, width), bf16),
            jax.ShapeDtypeStruct((own, HEADS // 2, patches, pair), f32),
        ],
        scratch_shapes=spread_scratch(own, n_pos, places, width),
        compiler_params=pltpu.CompilerParams(
            vmem_limit_bytes=VMEM_LIMIT, collective_id=0, has_side_effects=True
        ),
        cost_estimate=pl.CostEstimate(
            flops=2 * rows * width * 3 * width + 4 * rows * patches * width,
            bytes_accessed=rows * width * 12 + weight.size * 2,
            transcendentals=rows * patches * HEADS,
        ),
        name="space_forward",
    )(x, mods, weight)


def call_space_backward(go, qkv, lse, x, h, mods, weight, hot, dmod_rest, grads, kinds, n_clip):
    n_pos, own, places, width = x.shape
    patches = n_pos * places
    pair = 2 * HEAD_DIM
    lead = n_pos.bit_length() - 1
    clips = dmod_rest.shape[0]
    spread = pl.BlockSpec((n_pos, 1, places, width), lambda i: (0, i, 0, 0))
    anywhere = pl.BlockSpec(memory_space=pl.ANY)

    def by_frame(*shape):
        return pl.BlockSpec((1,) + shape, lambda i: (i, 0, 0))

    rows = own * patches
    cut = 3 * width // 512 * 256
    late = [jax.ShapeDtypeStruct((width, cols), bf16) for cols in (cut, 3 * width - cut)]
    kinds = kinds + (True, False)
    views, flow_outs, flow_scratch = flow_plan(list(grads) + late, kinds, n_pos, n_clip)
    early = len(grads)
    sizes = sum(grad.size for grad in grads)
    dmod_shape = (n_clip, clips, 9 * width)
    swaps = lead + len(bits_of(n_clip))
    return pl.pallas_call(
        partial(space_backward, n_clip, kinds, early),
        grid=(own,),
        in_specs=[
            spread,
            by_frame(patches, 3 * width),
            pl.BlockSpec((1, HEADS // 2, patches, pair), lambda i: (i, 0, 0, 0)),
            spread,
            by_frame(patches, width),
            by_frame(2, width),
            resident(weight.shape),
            resident(hot.shape),
            resident(dmod_rest.shape),
        ]
        + [anywhere] * early,
        out_specs=[anywhere, resident(dmod_shape)] + [resident(out.shape) for out in flow_outs],
        out_shape=[
            jax.ShapeDtypeStruct((n_pos * own, places, width), bf16),
            jax.ShapeDtypeStruct(dmod_shape, f32),
        ]
        + flow_outs,
        scratch_shapes=[
            pltpu.VMEM((patches, width), f32),
            pltpu.VMEM((patches, 3 * width), bf16),
            pltpu.VMEM((width, 3 * width), f32),
            pltpu.VMEM((clips, 9 * width), f32),
            pltpu.VMEM((lead, clips, 9 * width), f32),
            pltpu.VMEM((lead, clips, 9 * width), f32),
            pltpu.VMEM(dmod_shape, f32),
            pltpu.SemaphoreType.DMA((swaps,)),
            pltpu.SemaphoreType.DMA((swaps,)),
        ]
        + spread_scratch(own, n_pos, places, width)
        + views[early:]
        + flow_scratch,
        compiler_params=pltpu.CompilerParams(
            vmem_limit_bytes=VMEM_LIMIT, collective_id=1, has_side_effects=True
        ),
        cost_estimate=pl.CostEstimate(
            flops=4 * rows * width * 3 * width + 10 * rows * patches * width,
            bytes_accessed=rows * width * 16 + weight.size * 2 + sizes * 4,
            transcendentals=rows * patches * HEADS,
        ),
        name="space_backward",
    )(go, qkv, lse, x, h, mods, weight, hot, dmod_rest, *views[:early])


def call_middle(o_one, x, grad, mods, same_clip, wso, wti, wto, wup, wdn):
    places, frames, width = x.shape
    count = max(1, min(places, 256 // frames))
    rows = count * frames
    hidden = wup.shape[1]
    pair = 2 * HEAD_DIM
    total = places * frames
    chunk = pl.BlockSpec((count, frames, width), lambda i: (i, 0, 0))

    def flat(cols):
        return pl.BlockSpec((rows, cols), lambda i: (i, 0))

    def flat_shape(cols):
        return jax.ShapeDtypeStruct((total, cols), bf16)

    def scratch(cols, dtype=f32):
        return pltpu.VMEM((rows, cols), dtype)

    lanes = jnp.concatenate([same_clip, same_clip], axis=1)
    flops = 2 * total * (2 * (wso.size + wti.size + wto.size + wup.size + wdn.size))
    return pl.pallas_call(
        middle,
        grid=(places // count,),
        in_specs=[chunk, chunk, chunk, resident(mods.shape), resident(lanes.shape)]
        + [resident(w.shape) for w in (wso, wti, wto, wup, wdn)],
        out_specs=[
            chunk,
            flat(hidden),
            flat(width),
            flat(width),
            flat(hidden),
            flat(width),
            flat(width),
            flat(width),
            flat(3 * width),
            flat(width),
            chunk,
            chunk,
            pl.BlockSpec((7, frames, width), lambda i: (0, 0, 0)),
        ],
        out_shape=[
            jax.ShapeDtypeStruct(x.shape, bf16),
            flat_shape(hidden),
            flat_shape(width),
            flat_shape(width),
            flat_shape(hidden),
            flat_shape(width),
            flat_shape(width),
            flat_shape(width),
            flat_shape(3 * width),
            flat_shape(width),
            jax.ShapeDtypeStruct(x.shape, bf16),
            jax.ShapeDtypeStruct(x.shape, f32),
            jax.ShapeDtypeStruct((7, frames, width), f32),
        ],
        scratch_shapes=[
            scratch(3 * width, bf16),
            pltpu.VMEM((HEADS // 2, rows, pair), f32),
            scratch(width),
            scratch(width),
            scratch(width),
            scratch(width),
            scratch(pair),
            scratch(pair),
            scratch(width),
            scratch(width),
        ]
        + [scratch(256)] * 4,
        compiler_params=pltpu.CompilerParams(vmem_limit_bytes=VMEM_LIMIT),
        cost_estimate=pl.CostEstimate(
            flops=flops, bytes_accessed=total * 40000, transcendentals=total * hidden
        ),
        name="middle",
    )(o_one, x, grad, mods, lanes, wso, wti, wto, wup, wdn)


def on_device(
    tokens,
    clip_lengths,
    timesteps,
    embed_first,
    embed_second,
    adaln_weight,
    spatial_in,
    spatial_out,
    temporal_in,
    temporal_out,
    hidden_up,
    hidden_down,
    grad_output,
    n_pos=16,
    n_clip=2,
):
    frames, places, width = tokens.shape
    rows = frames * places
    own = frames // n_pos
    patches = places * n_pos
    me = lax.axis_index("pos")
    clips = clip_lengths.shape[1]

    def exchange(values):
        sent = values.reshape(frames, places, width)
        got = lax.all_to_all(sent, "pos", split_axis=0, concat_axis=0, tiled=True)
        return got.reshape(n_pos, own, places, width)

    x_space = exchange(tokens)

    all_steps = by_distance(timesteps[0], "clip", n_clip)
    freq = frequency(all_steps)
    pre_cond = dot_exact(freq, embed_first)
    hidden_cond = jax.nn.silu(pre_cond)
    cond = dot_exact(hidden_cond, embed_second)
    cond_act = jax.nn.silu(cond)
    modulated = dot_exact(cond_act[:clips], adaln_weight)
    onehot, clip_ids = clip_onehot(clip_lengths[0], frames)
    per_frame = dot_high(onehot, modulated)
    own_frames = lax.dynamic_slice_in_dim(per_frame, me * own, own, 0)

    own_mods = own_frames[:, : 2 * width].reshape(own, 2, width)
    h_one, qkv_one, o_one, lse_one = call_space_forward(x_space, own_mods, spatial_in)

    def turn(values):
        return values.transpose(1, 0, 2)

    o_one = turn(o_one)
    mods = per_frame.reshape(frames, 9, width).transpose(1, 0, 2)
    same_clip = jnp.dot(onehot, onehot.T)
    (block_turned, act, grad_z, h_three, grad_u, o_two, grad_y_two, h_two, grad_qkv_two, grad_y_one, grad_o_one,
     grad_one, sums) = call_middle(
        o_one, turn(tokens), turn(grad_output), mods, same_clip, spatial_out, temporal_in, temporal_out,
        hidden_up, hidden_down,
    )
    block_out = turn(block_turned)
    grad_o_space = exchange(turn(grad_o_one))
    early = (
        weight_grad(h_three, grad_u),
        weight_grad(act, grad_z),
        weight_grad(h_two, grad_qkv_two),
        weight_grad(o_one.reshape(rows, width), grad_y_one),
        weight_grad(o_two, grad_y_two),
    )
    own_hot = lax.dynamic_slice_in_dim(onehot, me * own, own, 0)
    hot = jnp.broadcast_to(own_hot[:, :, None], (own, clips, 128))
    dmod_rest = dot_high(onehot.T, sums.transpose(1, 0, 2).reshape(frames, 7 * width))
    (
        back_places, dmod, g_hidden_up, g_hidden_down, g_temporal_in, g_spatial_out, g_temporal_out,
        in_low, in_high,
    ) = call_space_backward(
        grad_o_space, qkv_one, lse_one, x_space, h_one, own_mods, spatial_in, hot, dmod_rest,
        early, (False, True, True, True, True), n_clip,
    )
    grad_tokens = (turn(grad_one) + back_places.astype(f32)).astype(bf16)
    g_spatial_in = jnp.concatenate([in_low, in_high], axis=1)
    dmod = dmod.reshape(n_clip * clips, 9 * width)

    def own_columns(values):
        block = values.shape[1] // n_pos
        return lax.dynamic_slice_in_dim(values, me * block, block, 1)

    g_adaln = dot_high(own_columns(cond_act).T, dmod)
    grad_cond = dot_exact(dmod, adaln_weight.T) * silu_grad(cond)
    g_second = dot_high(own_columns(hidden_cond).T, grad_cond)
    grad_pre = dot_exact(grad_cond, embed_second.T) * silu_grad(pre_cond)
    g_first = dot_high(own_columns(freq).T, grad_pre)
    return (
        block_out,
        grad_tokens,
        g_first,
        g_second,
        g_adaln,
        g_spatial_in,
        g_spatial_out,
        g_temporal_in,
        g_temporal_out,
        g_hidden_up,
        g_hidden_down,
    )


def solution(mesh):
    in_specs = (
        P("clip", "pos", None),
        P("clip", None),
        P("clip", None),
        P(),
        P(),
        P(),
        P(),
        P(),
        P(),
        P(),
        P(),
        P(),
        P("clip", "pos", None),
    )
    out_specs = (P("clip", "pos", None),) * 2 + (P("pos", None),) * 9
    body = partial(on_device, n_pos=mesh.shape["pos"], n_clip=mesh.shape["clip"])
    return jax.shard_map(body, mesh=mesh, in_specs=in_specs, out_specs=out_specs, check_vma=False)
```

```python
from functools import partial
import math

import jax
import jax.numpy as jnp
from jax import lax
from jax.experimental import pallas as pl
from jax.experimental.pallas import tpu as pltpu
from jax.sharding import PartitionSpec as P

HEADS = 12
HEAD_DIM = 64
FREQ = 256

epsilon = 1e-06
highest = lax.Precision.HIGHEST
masked_score = -1000000000.0
f32 = jnp.float32
bf16 = jnp.bfloat16


def frequency(step_ids):
    half_width = FREQ // 2
    rate_table = jnp.exp(
        -math.log(10000.0) * jnp.arange(half_width, dtype=jnp.float32) / half_width
    )
    angles = step_ids.astype(jnp.float32)[:, None] * rate_table[None, :]
    return jnp.concatenate([jnp.cos(angles), jnp.sin(angles)], axis=1)


def dot_high(left, right):
    return jnp.dot(left, right, precision=highest, preferred_element_type=f32)


def silu_grad(values):
    gate = jax.nn.sigmoid(values)
    return gate * (1.0 + values * (1.0 - gate))


def clip_onehot(lengths, frames):
    clip_ends = jnp.cumsum(lengths)
    frame_ids = jnp.arange(frames, dtype=jnp.int32)
    clip_ids = jnp.sum((frame_ids[:, None] >= clip_ends[None, :]).astype(jnp.int32), axis=1)
    onehot = (clip_ids[:, None] == jnp.arange(lengths.shape[0], dtype=jnp.int32)[None, :]).astype(
        jnp.float32
    )
    return (onehot, clip_ids)


def weight_grad(left, right):
    return jnp.einsum("rd,rk->dk", left, right, preferred_element_type=f32).astype(bf16)


def bdot(left, right):
    return lax.dot_general(left, right, (((1,), (0,)), ((), ())), preferred_element_type=f32)


def bdot_nt(left, right):
    return lax.dot_general(left, right, (((1,), (1,)), ((), ())), preferred_element_type=f32)


def bdot_tn(left, right):
    return lax.dot_general(left, right, (((0,), (0,)), ((), ())), preferred_element_type=f32)


def norm_rows(values):
    width = values.shape[-1]
    centre = values - jnp.sum(values, axis=-1, keepdims=True) * (1.0 / width)
    spread = jnp.sum(centre * centre, axis=-1, keepdims=True) * (1.0 / width)
    inverse = lax.rsqrt(spread + epsilon)
    return centre * inverse, inverse


def norm_rows_back(normed, inverse, scale_vec, grad):
    width = grad.shape[-1]
    inner = grad * (1.0 + scale_vec)
    mean_one = jnp.sum(inner, axis=-1, keepdims=True) * (1.0 / width)
    mean_two = jnp.sum(inner * normed, axis=-1, keepdims=True) * (1.0 / width)
    return inverse * (inner - mean_one - normed * mean_two)


def pair_masks(scale):
    lanes = lax.broadcasted_iota(jnp.int32, (1, 2 * HEAD_DIM), 1)
    low_half = jnp.where(lanes < HEAD_DIM, scale, 0.0).astype(bf16)
    high_half = jnp.where(lanes < HEAD_DIM, 0.0, scale).astype(bf16)
    return low_half, high_half


ROWS = 32


def load_rows(ref, step):
    places, width = ref.shape[2:]
    count = max(1, ROWS // places)
    part = ref[pl.ds(step * count, count), 0].astype(f32)
    return part.reshape(count * places, width)


def swap(values, axis, size, bit):
    return lax.ppermute(values, axis, [(i, i ^ bit) for i in range(size)])


def bits_of(size):
    return [1 << i for i in range(size.bit_length() - 1)]


def by_distance(values, axis, size):
    for bit in bits_of(size):
        values = jnp.concatenate([values, swap(values, axis, size, bit)], axis=0)
    return values


def dot_exact(left, right):
    parts = []
    for _ in range(3):
        part = left.astype(bf16)
        parts.append(part)
        left = left - part.astype(f32)
    count = parts[0].shape[0]
    got = jnp.dot(jnp.concatenate(parts, axis=0), right, preferred_element_type=f32)
    return got[:count] + (got[count : 2 * count] + got[2 * count :])


def flow_stages(n_pos, n_clip, clip_first):
    pos = [("pos", bit, "halve") for bit in bits_of(n_pos)]
    clip = bits_of(n_clip)
    if not clip_first:
        return pos + [("clip", bit, "sum") for bit in clip]
    first = [("clip", clip[0], "columns")]
    last = [("clip", clip[0], "gather")]
    return pos[:1] + first + pos[1:] + [("clip", bit, "sum") for bit in clip[1:]] + last


def flow_shapes(stages, n_pos, block, cols):
    lead = n_pos.bit_length() - 1
    shapes = []
    for _, _, what in stages:
        if what == "halve":
            lead -= 1
        elif what == "columns":
            cols //= 2
        shapes.append((2,) * lead + (block, cols))
    return shapes


class Flow:
    def __init__(self, number, stages, grad, out, keep, gots, sems, place):
        self.number, self.stages = number, stages
        self.grad, self.out, self.keep, self.gots = grad, out, keep, gots
        self.send_sem, self.recv_sem, self.keep_sem = sems
        self.place = place

    def side(self, stage):
        axis, bit, _ = self.stages[stage]
        return lax.rem(self.place[axis] // bit, 2)

    def columns(self, side, width):
        return pl.ds(pl.multiple_of(side * width, width), width)

    def part(self, ref, stage, side):
        what = self.stages[stage][2]
        lead = len(ref.shape) - 2
        if what == "halve":
            return (slice(None),) * (lead - 1) + (side,)
        if what == "columns":
            half = ref.shape[-1] // 2
            return (slice(None),) * (lead + 1) + (self.columns(side, half),)
        return None

    def held(self, stage):
        if stage == 0:
            return self.grad
        return self.keep if stage == 1 else self.gots[stage - 1]

    def copy(self, stage):
        axis, bit, _ = self.stages[stage]
        side = self.side(stage)
        source = self.held(stage)
        at = self.part(source, stage, 1 - side)
        return pltpu.make_async_remote_copy(
            source if at is None else source.at[at],
            self.gots[stage],
            self.send_sem.at[self.number, stage],
            self.recv_sem.at[self.number, stage],
            device_id={axis: self.place[axis] + bit * (1 - 2 * side)},
            device_id_type=pl.DeviceIdType.MESH,
        )

    def own(self):
        at = self.part(self.grad, 0, self.side(0))
        return pltpu.make_async_copy(self.grad.at[at], self.keep, self.keep_sem.at[self.number])

    def start(self):
        self.copy(0).start()
        self.own().start()

    def take(self, stage):
        self.copy(stage).wait_recv()
        if stage == 0:
            self.own().wait()
        what = self.stages[stage][2]
        got = self.gots[stage]
        side = self.side(stage)
        last = stage == len(self.stages) - 1
        lead = len(got.shape) - 2
        if what == "gather":
            half = got.shape[-1]
            self.out[:, self.columns(side, half)] = self.held(stage)[...].astype(f32)
            self.out[:, self.columns(1 - side, half)] = got[...].astype(f32)
            return
        if last:
            self.out[...] = self.held(stage)[...].astype(f32) + got[...].astype(f32)
            return
        target = self.keep if stage == 0 else got

        def one(index, _):
            at = tuple(lax.rem(index // (1 << i), 2) for i in range(lead))
            if stage == 0:
                mine = self.keep[at]
            elif what == "halve":
                mine = self.held(stage)[at + (side,)]
            elif what == "columns":
                mine = self.held(stage)[at + (slice(None), self.columns(side, got.shape[-1]))]
            else:
                mine = self.held(stage)[at]
            target[at] = mine + got[at]
            return 0

        lax.fori_loop(0, 1 << lead, one, 0)
        self.copy(stage + 1).start()

    def finish(self):
        for stage in range(len(self.stages)):
            self.copy(stage).wait_send()


class Butterfly:
    def __init__(self, n_pos, n_clip, values, out, got, acc, sems, place):
        self.pos_bits, self.clip_bits = bits_of(n_pos), bits_of(n_clip)
        self.values, self.out, self.got, self.acc = values, out, got, acc
        self.send_sem, self.recv_sem = sems
        self.place = place
        self.count = len(self.pos_bits) + len(self.clip_bits)

    def copy(self, stage):
        if stage < len(self.pos_bits):
            axis, bit = "pos", self.pos_bits[stage]
            source = self.values if stage == 0 else self.acc.at[stage - 1]
            target = self.got.at[stage]
        else:
            axis, bit = "clip", self.clip_bits[stage - len(self.pos_bits)]
            source, target = self.out.at[pl.ds(0, bit)], self.out.at[pl.ds(bit, bit)]
        side = lax.rem(self.place[axis] // bit, 2)
        return pltpu.make_async_remote_copy(
            source,
            target,
            self.send_sem.at[stage],
            self.recv_sem.at[stage],
            device_id={axis: self.place[axis] + bit * (1 - 2 * side)},
            device_id_type=pl.DeviceIdType.MESH,
        )

    def start(self):
        self.copy(0).start()

    def take(self, stage):
        self.copy(stage).wait_recv()
        last = len(self.pos_bits) - 1
        if stage <= last:
            mine = self.values[...] if stage == 0 else self.acc[stage - 1]
            if stage < last:
                self.acc[stage] = mine + self.got[stage]
            else:
                self.out[0] = mine + self.got[stage]
        if stage + 1 < self.count:
            self.copy(stage + 1).start()

    def finish(self):
        for stage in range(self.count):
            self.copy(stage).wait_send()


def partner_list(n_pos, n_clip):
    return [("pos", bit) for bit in bits_of(n_pos)] + [("clip", bit) for bit in bits_of(n_clip)]


def here():
    return {"pos": lax.axis_index("pos"), "clip": lax.axis_index("clip")}


def signal_swap(barrier, place, axis, bit):
    side = lax.rem(place[axis] // bit, 2)
    pl.semaphore_signal(
        barrier,
        inc=1,
        device_id={axis: place[axis] + bit * (1 - 2 * side)},
        device_id_type=pl.DeviceIdType.MESH,
    )


def make_flows(n_pos, n_clip, kinds, grads, outs, scratch):
    sems, rest = scratch[:3], list(scratch[3:])
    flows = []
    for number, clip_first in enumerate(kinds):
        stages = flow_stages(n_pos, n_clip, clip_first)
        keep, gots = rest[0], rest[1 : 1 + len(stages)]
        rest = rest[1 + len(stages) :]
        flows.append(Flow(number, stages, grads[number], outs[number], keep, gots, sems, here()))
    return flows


def flow_plan(grads, kinds, n_pos, n_clip):
    lead = n_pos.bit_length() - 1
    most = lead + len(bits_of(n_clip)) + 1
    dma = pltpu.SemaphoreType.DMA
    scratch = [dma((len(grads), most)), dma((len(grads), most)), dma((len(grads),))]
    views, out_shape = [], []
    for grad, clip_first in zip(grads, kinds):
        rows, cols = grad.shape
        block = rows // n_pos
        if isinstance(grad, jax.ShapeDtypeStruct):
            views.append(pltpu.VMEM((2,) * lead + (block, cols), bf16))
        else:
            views.append(grad.reshape((2,) * lead + (block, cols)))
        out_shape.append(jax.ShapeDtypeStruct((block, cols), f32))
        shapes = flow_shapes(flow_stages(n_pos, n_clip, clip_first), n_pos, block, cols)
        scratch += [pltpu.VMEM(shape, bf16) for shape in [shapes[0]] + shapes]
    return views, out_shape, scratch


class Spread:

    def __init__(self, n_pos, step, steps, hold, out, send_sem, recv_sem, own_sem):
        self.n_pos, self.step, self.steps = n_pos, step, steps
        self.hold, self.out = hold, out
        self.send_sem, self.recv_sem, self.own_sem = send_sem, recv_sem, own_sem
        self.me = lax.axis_index("pos")

    def greet(self, more=0):
        barrier = pltpu.get_barrier_semaphore()

        def signal(shift, _):
            target = lax.rem(self.me + shift, self.n_pos)
            pl.semaphore_signal(
                barrier, inc=1, device_id={"pos": target}, device_id_type=pl.DeviceIdType.MESH
            )
            return 0

        lax.fori_loop(1, self.n_pos, signal, 0)
        pl.semaphore_wait(barrier, self.n_pos - 1 + more)

    def copy(self, step, shift, source):
        target = lax.rem(self.me + shift, self.n_pos)
        return pltpu.make_async_remote_copy(
            self.hold.at[step, target],
            self.out.at[source * self.steps + step],
            self.send_sem.at[step, shift],
            self.recv_sem.at[step, shift],
            device_id={"pos": target},
            device_id_type=pl.DeviceIdType.MESH,
        )

    def stay(self, step):
        return pltpu.make_async_copy(
            self.hold.at[step, self.me],
            self.out.at[self.me * self.steps + step],
            self.own_sem.at[step],
        )

    def send(self):
        def one(shift, _):
            self.copy(self.step, shift, self.me).start()
            return 0

        lax.fori_loop(1, self.n_pos, one, 0)
        self.stay(self.step).start()

    def finish(self):
        def one_step(step, _):
            def one(shift, _):
                self.copy(step, shift, self.me).wait_send()
                source = lax.rem(self.me + self.n_pos - shift, self.n_pos)
                self.copy(step, shift, source).wait_recv()
                return 0

            lax.fori_loop(1, self.n_pos, one, 0)
            self.stay(step).wait()
            return 0

        lax.fori_loop(0, self.steps, one_step, 0)


def spread_scratch(own, n_pos, places, width):
    return [
        pltpu.VMEM((own, n_pos, places, width), bf16),
        pltpu.SemaphoreType.DMA((own, n_pos)),
        pltpu.SemaphoreType.DMA((own, n_pos)),
        pltpu.SemaphoreType.DMA((own,)),
    ]


def space_forward(
    x_ref, mod_ref, w_ref, h_ref, qkv_ref, o_ref, lse_ref, hold, send_sem, recv_sem, own_sem
):
    own, n_pos = hold.shape[:2]
    frame = pl.program_id(0)
    spread = Spread(n_pos, frame, own, hold, o_ref, send_sem, recv_sem, own_sem)
    pl.when(frame == 0)(spread.greet)
    patches, width = h_ref.shape[1:]
    places = x_ref.shape[2]
    pair = 2 * HEAD_DIM
    shift, scale = mod_ref[0, 0:1, :], mod_ref[0, 1:2, :]

    def norm_step(step, _):
        normed, _inverse = norm_rows(load_rows(x_ref, step))
        h_ref[0, pl.ds(step * ROWS, ROWS), :] = (normed * (1.0 + scale) + shift).astype(bf16)
        return 0

    lax.fori_loop(0, patches // ROWS, norm_step, 0)

    def project(third, _):
        cols = pl.ds(pl.multiple_of(third * width, width), width)
        qkv_ref[0, :, cols] = bdot(h_ref[0], w_ref[:, cols]).astype(bf16)
        return 0

    lax.fori_loop(0, 3, project, 0)
    masks = pair_masks(1.0 / math.sqrt(HEAD_DIM))
    is_low = lax.broadcasted_iota(jnp.int32, (1, pair), 1) < HEAD_DIM

    def head_pair(index, _):
        at = pl.multiple_of(index * pair, pair)
        q = qkv_ref[0, :, pl.ds(at, pair)]
        k = qkv_ref[0, :, pl.ds(pl.multiple_of(width + at, pair), pair)]
        v = qkv_ref[0, :, pl.ds(pl.multiple_of(2 * width + at, pair), pair)]
        one = jnp.ones_like(v)
        values = [jnp.where(is_low, v, one), jnp.where(is_low, one, v)]
        scores = [bdot_nt(q * mask, k) for mask in masks]
        tops = [jnp.max(score, axis=-1, keepdims=True) for score in scores]
        exps = [jnp.exp(score - top).astype(bf16) for score, top in zip(scores, tops)]
        outs = [bdot(exp, value) for exp, value in zip(exps, values)]
        total = pltpu.roll(jnp.where(is_low, outs[1], outs[0]), HEAD_DIM, 1)
        both = jnp.where(is_low, outs[0], outs[1]) / total
        lse_ref[0, index] = jnp.where(is_low, tops[0], tops[1]) + jnp.log(total)
        hold[frame, :, :, pl.ds(at, pair)] = both.reshape(n_pos, places, pair).astype(bf16)
        return 0

    lax.fori_loop(0, HEADS // 2, head_pair, 0)
    spread.send()
    pl.when(frame == own - 1)(spread.finish)


def space_backward(n_clip, kinds, early, *refs):
    go_ref, qkv_ref, lse_ref, x_ref, h_ref, mod_ref, w_ref, hot_ref, rest_ref = refs[:9]
    grads, refs = refs[9 : 9 + early], refs[9 + early :]
    dv_ref, dmod_ref = refs[:2]
    outs, refs = refs[2 : 2 + len(kinds)], refs[2 + len(kinds) :]
    e_ref, dqkv_ref, total_ref, small_ref, got_ref, acc_ref, every_ref = refs[:7]
    small_send, small_recv, hold, send_sem, recv_sem, own_sem = refs[7:13]
    late_grads, refs = refs[13 : 13 + len(kinds) - early], refs[13 + len(kinds) - early :]
    own, n_pos = hold.shape[:2]
    frame = pl.program_id(0)
    spread = Spread(n_pos, frame, own, hold, dv_ref, send_sem, recv_sem, own_sem)
    flows = make_flows(n_pos, n_clip, kinds, tuple(grads) + tuple(late_grads), outs, refs)
    late = flows[early:]
    tree = Butterfly(
        n_pos, n_clip, small_ref, every_ref, got_ref, acc_ref, (small_send, small_recv), here()
    )
    stages = max(len(flow.stages) for flow in flows)
    order = [(i, stage) for stage in range(stages) for i in range(early)]
    order = [(i, stage) for i, stage in order if stage < len(flows[i].stages)]
    cuts = [2, early, early]

    @pl.when(frame == 0)
    def _():
        place = here()
        others = [("clip", bit) for bit in bits_of(n_clip)]
        barrier = pltpu.get_barrier_semaphore()
        for axis, bit in others:
            signal_swap(barrier, place, axis, bit)
        spread.greet(len(others))
        for flow in flows[:early]:
            flow.start()

        def clear(step, _):
            total_ref[pl.ds(step * 8, 8), :] = jnp.zeros((8, total_ref.shape[1]), f32)
            return 0

        lax.fori_loop(0, total_ref.shape[0] // 8, clear, 0)
        small_ref[:, : 2 * x_ref.shape[3]] = jnp.zeros_like(small_ref[:, : 2 * x_ref.shape[3]])
        small_ref[:, 2 * x_ref.shape[3] :] = rest_ref[...]

    def advance(steps):
        for i, stage in steps:
            flows[i].take(stage)

    def start_late():
        block = late_grads[0].shape[-2]
        lead = len(late_grads[0].shape) - 2

        def one(index, _):
            at = tuple(lax.rem(index // (1 << i), 2) for i in reversed(range(lead)))
            rows = pl.ds(pl.multiple_of(index * block, 8), block)
            first = 0
            for grad in late_grads:
                cols = grad.shape[-1]
                grad[at] = total_ref[rows, first : first + cols].astype(bf16)
                first += cols
            return 0

        lax.fori_loop(0, n_pos, one, 0)
        for flow in late:
            flow.start()

    patches = qkv_ref.shape[1]
    width = x_ref.shape[3]
    places = x_ref.shape[2]
    pair = 2 * HEAD_DIM
    scale = mod_ref[0, 1:2, :]
    factor = 1.0 / math.sqrt(HEAD_DIM)
    masks_q = pair_masks(factor)
    masks = pair_masks(1.0)
    ones = jnp.ones((patches, pair), bf16)

    def key_sums(values):
        high = values.astype(bf16)
        low = (values - high.astype(f32)).astype(bf16)
        total = bdot(high, ones) + bdot(low, ones)
        return jnp.concatenate([total] * (patches // pair), axis=1)

    def head_pair(index, _):
        at = pl.multiple_of(index * pair, pair)
        k_at = pl.multiple_of(width + at, pair)
        v_at = pl.multiple_of(2 * width + at, pair)
        q = qkv_ref[0, :, pl.ds(at, pair)]
        k = qkv_ref[0, :, pl.ds(k_at, pair)]
        v = qkv_ref[0, :, pl.ds(v_at, pair)]
        go = go_ref[:, 0, :, pl.ds(at, pair)].astype(f32).reshape(patches, pair).astype(bf16)
        lse_pair = lse_ref[0, index]
        lses = [lse_pair[:, 0:1], lse_pair[:, HEAD_DIM : HEAD_DIM + 1]]
        q_halves = [q * mask for mask in masks_q]
        go_halves = [go * mask for mask in masks]
        probs = [jnp.exp(bdot_nt(half, k) - lse) for half, lse in zip(q_halves, lses)]
        grads = [bdot_nt(half, v) for half in go_halves]
        inner = [key_sums(grad * prob) for grad, prob in zip(grads, probs)]
        scores = [
            (prob * (grad - mean)).astype(bf16) for prob, grad, mean in zip(probs, grads, inner)
        ]
        gq = sum(bdot(score, k * mask) for score, mask in zip(scores, masks_q))
        gk = sum(bdot_tn(score, half) for score, half in zip(scores, q_halves))
        gv = sum(bdot_tn(prob.astype(bf16), half) for prob, half in zip(probs, go_halves))
        dqkv_ref[:, pl.ds(at, pair)] = gq.astype(bf16)
        dqkv_ref[:, pl.ds(k_at, pair)] = gk.astype(bf16)
        dqkv_ref[:, pl.ds(v_at, pair)] = gv.astype(bf16)
        return 0

    lax.fori_loop(0, HEADS // 2, head_pair, 0)
    e_ref[...] = bdot_nt(dqkv_ref[...], w_ref[...])

    def norm_step(step, sums):
        grad = e_ref[pl.ds(step * ROWS, ROWS), :]
        normed, inverse = norm_rows(load_rows(x_ref, step))
        back = norm_rows_back(normed, inverse, scale, grad)
        count = max(1, ROWS // places)
        back = back.reshape(count, places, width).astype(bf16)
        hold[frame, pl.ds(step * count, count)] = back
        folded = grad.reshape(ROWS // 8, 8, width).sum(axis=0)
        folded_n = (grad * normed).reshape(ROWS // 8, 8, width).sum(axis=0)
        return sums[0] + folded, sums[1] + folded_n

    zero = jnp.zeros((8, width), f32)
    shift_sum, scale_sum = lax.fori_loop(0, patches // ROWS, norm_step, (zero, zero))
    spread.send()
    hot = hot_ref[frame][:, 0:1]
    small_ref[:, :width] += hot * jnp.sum(shift_sum, axis=0, keepdims=True)
    small_ref[:, width : 2 * width] += hot * jnp.sum(scale_sum, axis=0, keepdims=True)

    def accumulate(third, _):
        cols = pl.ds(pl.multiple_of(third * width, width), width)
        total_ref[:, cols] += bdot_tn(h_ref[0], dqkv_ref[:, cols])
        return 0

    lax.fori_loop(0, 3, accumulate, 0)
    done = 0
    for index, cut in enumerate(cuts[: own - 1]):
        pl.when(frame == index)(partial(advance, order[done:cut]))
        done = cut

    @pl.when(frame == own - 1)
    def _():
        tree.start()
        start_late()
        left = order[done:]
        for turn in range(stages + 1):
            advance([step for step in left if step[1] == turn])
            if turn < tree.count:
                tree.take(turn)
            for flow in late:
                if 0 <= turn - 1 < len(flow.stages):
                    flow.take(turn - 1)
        dmod_ref[...] = every_ref[...]
        spread.finish()
        tree.finish()
        for flow in flows:
            flow.finish()


GELU_C = math.sqrt(2.0 / math.pi)


def middle(
    o1_ref, x_ref, g_ref, mod_ref, clip_ref, wso_ref, wti_ref, wto_ref, wup_ref, wdn_ref,
    out_ref, act_ref, dz_ref, h3_ref, du_ref, o2_ref, dy2_ref, h2_ref, dqkv_ref, dy1_ref, do1_ref,
    dx1_ref, sum_ref,
    qkv_ref, p_ref, y1_ref, y2_ref, n2_ref, n3_ref, r2_ref, r3_ref, xa_ref, e_ref,
    ua_ref, aa_ref, ub_ref, ab_ref,
):
    count, frames, width = x_ref.shape
    rows = count * frames
    pair = 2 * HEAD_DIM
    hidden = act_ref.shape[1]
    factor = 1.0 / math.sqrt(HEAD_DIM)
    per = frames // ROWS
    steps = rows // ROWS

    @pl.when(pl.program_id(0) == 0)
    def _():
        sum_ref[...] = jnp.zeros_like(sum_ref)

    def at_rows(step):
        return step // per, pl.ds(lax.rem(step, per) * ROWS, ROWS), pl.ds(step * ROWS, ROWS)

    def mod(index, part):
        return mod_ref[index, part, :]

    y1_ref[...] = bdot(o1_ref[...].reshape(rows, width), wso_ref[...])

    def step_one(step, _):
        place, part, flat = at_rows(step)
        x_one = x_ref[place, part, :].astype(f32) + mod(2, part) * y1_ref[flat, :]
        xa_ref[flat, :] = x_one
        normed, inverse = norm_rows(x_one)
        n2_ref[flat, :] = normed
        r2_ref[flat, :] = jnp.broadcast_to(inverse, (ROWS, pair))
        h2_ref[flat, :] = (normed * (1.0 + mod(4, part)) + mod(3, part)).astype(bf16)
        return 0

    lax.fori_loop(0, steps, step_one, 0)

    def project(third, _):
        cols = pl.ds(pl.multiple_of(third * width, width), width)
        qkv_ref[:, cols] = bdot(h2_ref[...], wti_ref[:, cols]).astype(bf16)
        return 0

    lax.fori_loop(0, 3, project, 0)

    masks = pair_masks(1.0)
    masks_q = pair_masks(factor)
    lane_ids = lax.broadcasted_iota(jnp.int32, (1, pair), 1)
    is_low = lane_ids < HEAD_DIM
    allowed = clip_ref[...] > 0.5

    def halves(values, reduce, neutral):
        low_part = reduce(jnp.where(is_low, values, neutral), axis=-1, keepdims=True)
        high_part = reduce(jnp.where(is_low, neutral, values), axis=-1, keepdims=True)
        return jnp.where(is_low, low_part, high_part)

    def stacked(values, pair_of_masks):
        return jnp.concatenate([values * pair_of_masks[0], values * pair_of_masks[1]], axis=0)

    def pair_at(index):
        at = pl.multiple_of(index * pair, pair)
        return (
            pl.ds(at, pair),
            pl.ds(pl.multiple_of(width + at, pair), pair),
            pl.ds(pl.multiple_of(2 * width + at, pair), pair),
        )

    parts = [slice(place * frames, (place + 1) * frames) for place in range(count)]
    same_half = (
        lax.broadcasted_iota(jnp.int32, (pair, pair), 0) // HEAD_DIM
        == lax.broadcasted_iota(jnp.int32, (pair, pair), 1) // HEAD_DIM
    )
    ones = jnp.where(same_half, 1.0, 0.0).astype(bf16)

    def half_sums(values):
        high = values.astype(bf16)
        low = (values - high.astype(f32)).astype(bf16)
        return bdot(high, ones) + bdot(low, ones)

    def time_pair(index, _):
        jobs = [(2 * index + i, part) + pair_at(2 * index + i) for i in range(2) for part in parts]
        keys = [stacked(qkv_ref[part, k_at], masks_q) for _i, part, q_at, k_at, v_at in jobs]
        scores = [bdot_nt(qkv_ref[job[1], job[2]], key) for job, key in zip(jobs, keys)]
        scores = [jnp.where(allowed, score, masked_score) for score in scores]
        tops = [halves(score, jnp.max, -jnp.inf) for score in scores]
        exps = [jnp.exp(score - top) for score, top in zip(scores, tops)]
        sums = [half_sums(exp) for exp in exps]
        probs = [exp / total for exp, total in zip(exps, sums)]
        values = [stacked(qkv_ref[job[1], job[4]], masks) for job in jobs]
        outs = [bdot(prob.astype(bf16), value) for prob, value in zip(probs, values)]
        for (i, part, q_at, _k, _v), prob, out in zip(jobs, probs, outs):
            p_ref[i, part, :] = prob
            o2_ref[part, q_at] = out.astype(bf16)
        return 0

    lax.fori_loop(0, HEADS // 4, time_pair, 0)

    y2_ref[...] = bdot(o2_ref[...], wto_ref[...])

    def step_two(step, _):
        place, part, flat = at_rows(step)
        x_two = xa_ref[flat, :] + mod(5, part) * y2_ref[flat, :]
        xa_ref[flat, :] = x_two
        normed, inverse = norm_rows(x_two)
        n3_ref[flat, :] = normed
        r3_ref[flat, :] = jnp.broadcast_to(inverse, (ROWS, pair))
        h3_ref[flat, :] = (normed * (1.0 + mod(7, part)) + mod(6, part)).astype(bf16)
        dz_ref[flat, :] = (mod(8, part) * g_ref[place, part, :].astype(f32)).astype(bf16)
        return 0

    lax.fori_loop(0, steps, step_two, 0)

    tile = 256

    def products(index, u_ref, a_ref):
        cols = pl.ds(pl.multiple_of(index * tile, tile), tile)
        u_ref[...] = bdot(h3_ref[...], wup_ref[:, cols])
        a_ref[...] = bdot_nt(dz_ref[...], wdn_ref[cols, :])

    def pointwise(index, u_ref, a_ref):
        cols = pl.ds(pl.multiple_of(index * tile, tile), tile)
        u = u_ref[...]
        square = u * u
        half = 0.5 + 0.5 * jnp.tanh(u * (GELU_C + (0.044715 * GELU_C) * square))
        value = u * half
        act_ref[:, cols] = value.astype(bf16)
        slope = half + (value - value * half) * (2.0 * GELU_C + (6.0 * 0.044715 * GELU_C) * square)
        du_ref[:, cols] = (a_ref[...] * slope).astype(bf16)

    tiles = hidden // tile

    def two_tiles(index, _):
        products(2 * index + 1, ub_ref, ab_ref)
        pointwise(2 * index, ua_ref, aa_ref)
        products(jnp.minimum(2 * index + 2, tiles - 1), ua_ref, aa_ref)
        pointwise(2 * index + 1, ub_ref, ab_ref)
        return 0

    products(0, ua_ref, aa_ref)
    lax.fori_loop(0, tiles // 2, two_tiles, 0)
    e_ref[...] = bdot(act_ref[...], wdn_ref[...])

    def step_three(step, _):
        place, part, flat = at_rows(step)
        z = e_ref[flat, :]
        grad = g_ref[place, part, :].astype(f32)
        out_ref[place, part, :] = (xa_ref[flat, :] + mod(8, part) * z).astype(bf16)
        sum_ref[6, part, :] += grad * z
        return 0

    lax.fori_loop(0, steps, step_three, 0)

    def back_up(index, _):
        cols = pl.ds(pl.multiple_of(index * tile, tile), tile)
        e_ref[:, cols] = bdot_nt(du_ref[...], wup_ref[cols, :])
        return 0

    lax.fori_loop(0, width // tile, back_up, 0)

    def step_four(step, _):
        place, part, flat = at_rows(step)
        grad = e_ref[flat, :]
        normed = n3_ref[flat, :]
        sum_ref[4, part, :] += grad
        sum_ref[5, part, :] += grad * normed
        back = norm_rows_back(normed, r3_ref[flat, 0:1], mod(7, part), grad)
        grad_two = g_ref[place, part, :].astype(f32) + back
        xa_ref[flat, :] = grad_two
        sum_ref[3, part, :] += grad_two * y2_ref[flat, :]
        dy2_ref[flat, :] = (mod(5, part) * grad_two).astype(bf16)
        return 0

    lax.fori_loop(0, steps, step_four, 0)
    y2_ref[...] = bdot_nt(dy2_ref[...], wto_ref[...])

    def time_pair_back(index, _):
        q_at, k_at, v_at = pair_at(index)
        gos = [y2_ref[part, q_at].astype(bf16) for part in parts]
        values = [stacked(qkv_ref[part, v_at], masks) for part in parts]
        grads = [bdot_nt(go, value) for go, value in zip(gos, values)]
        probs = [p_ref[index, part, :] for part in parts]
        inner = [half_sums(grad * prob) for grad, prob in zip(grads, probs)]
        scores = [
            (prob * (grad - mean)).astype(bf16) for prob, grad, mean in zip(probs, grads, inner)
        ]
        keys = [stacked(qkv_ref[part, k_at], masks_q) for part in parts]
        qs = [qkv_ref[part, q_at] * factor for part in parts]
        grad_q = [bdot(score, key) for score, key in zip(scores, keys)]
        grad_k = [bdot_tn(score, q) for score, q in zip(scores, qs)]
        grad_v = [bdot_tn(prob.astype(bf16), go) for prob, go in zip(probs, gos)]
        for part, g_q, g_k, g_v in zip(parts, grad_q, grad_k, grad_v):
            dqkv_ref[part, q_at] = g_q.astype(bf16)
            dqkv_ref[part, k_at] = jnp.where(is_low, g_k[:frames], g_k[frames:]).astype(bf16)
            dqkv_ref[part, v_at] = jnp.where(is_low, g_v[:frames], g_v[frames:]).astype(bf16)
        return 0

    lax.fori_loop(0, HEADS // 2, time_pair_back, 0)
    e_ref[...] = bdot_nt(dqkv_ref[...], wti_ref[...])

    def step_five(step, _):
        place, part, flat = at_rows(step)
        grad = e_ref[flat, :]
        normed = n2_ref[flat, :]
        sum_ref[1, part, :] += grad
        sum_ref[2, part, :] += grad * normed
        grad_one = xa_ref[flat, :] + norm_rows_back(normed, r2_ref[flat, 0:1], mod(4, part), grad)
        dx1_ref[place, part, :] = grad_one
        sum_ref[0, part, :] += grad_one * y1_ref[flat, :]
        dy1_ref[flat, :] = (mod(2, part) * grad_one).astype(bf16)
        return 0

    lax.fori_loop(0, steps, step_five, 0)
    do1_ref[...] = bdot_nt(dy1_ref[...], wso_ref[...]).astype(bf16).reshape(count, frames, width)


VMEM_LIMIT = 62 * 1024 * 1024


def resident(shape):
    return pl.BlockSpec(shape, lambda i: (0,) * len(shape), pipeline_mode=pl.Buffered(1))


def call_space_forward(x, mods, weight):
    n_pos, own, places, width = x.shape
    patches = n_pos * places
    pair = 2 * HEAD_DIM
    spread = pl.BlockSpec((n_pos, 1, places, width), lambda i: (0, i, 0, 0))

    def by_frame(*shape):
        return pl.BlockSpec((1,) + shape, lambda i: (i, 0, 0))

    rows = own * patches
    return pl.pallas_call(
        space_forward,
        grid=(own,),
        in_specs=[spread, by_frame(2, width), resident(weight.shape)],
        out_specs=[
            by_frame(patches, width),
            by_frame(patches, 3 * width),
            pl.BlockSpec(memory_space=pl.ANY),
            pl.BlockSpec((1, HEADS // 2, patches, pair), lambda i: (i, 0, 0, 0)),
        ],
        out_shape=[
            jax.ShapeDtypeStruct((own, patches, width), bf16),
            jax.ShapeDtypeStruct((own, patches, 3 * width), bf16),
            jax.ShapeDtypeStruct((n_pos * own, places, width), bf16),
            jax.ShapeDtypeStruct((own, HEADS // 2, patches, pair), f32),
        ],
        scratch_shapes=spread_scratch(own, n_pos, places, width),
        compiler_params=pltpu.CompilerParams(
            vmem_limit_bytes=VMEM_LIMIT, collective_id=0, has_side_effects=True
        ),
        cost_estimate=pl.CostEstimate(
            flops=2 * rows * width * 3 * width + 4 * rows * patches * width,
            bytes_accessed=rows * width * 12 + weight.size * 2,
            transcendentals=rows * patches * HEADS,
        ),
        name="space_forward",
    )(x, mods, weight)


def call_space_backward(go, qkv, lse, x, h, mods, weight, hot, dmod_rest, grads, kinds, n_clip):
    n_pos, own, places, width = x.shape
    patches = n_pos * places
    pair = 2 * HEAD_DIM
    lead = n_pos.bit_length() - 1
    clips = dmod_rest.shape[0]
    spread = pl.BlockSpec((n_pos, 1, places, width), lambda i: (0, i, 0, 0))
    anywhere = pl.BlockSpec(memory_space=pl.ANY)

    def by_frame(*shape):
        return pl.BlockSpec((1,) + shape, lambda i: (i, 0, 0))

    rows = own * patches
    cut = 3 * width // 512 * 256
    late = [jax.ShapeDtypeStruct((width, cols), bf16) for cols in (cut, 3 * width - cut)]
    kinds = kinds + (True, False)
    views, flow_outs, flow_scratch = flow_plan(list(grads) + late, kinds, n_pos, n_clip)
    early = len(grads)
    sizes = sum(grad.size for grad in grads)
    dmod_shape = (n_clip, clips, 9 * width)
    swaps = lead + len(bits_of(n_clip))
    return pl.pallas_call(
        partial(space_backward, n_clip, kinds, early),
        grid=(own,),
        in_specs=[
            spread,
            by_frame(patches, 3 * width),
            pl.BlockSpec((1, HEADS // 2, patches, pair), lambda i: (i, 0, 0, 0)),
            spread,
            by_frame(patches, width),
            by_frame(2, width),
            resident(weight.shape),
            resident(hot.shape),
            resident(dmod_rest.shape),
        ]
        + [anywhere] * early,
        out_specs=[anywhere, resident(dmod_shape)] + [resident(out.shape) for out in flow_outs],
        out_shape=[
            jax.ShapeDtypeStruct((n_pos * own, places, width), bf16),
            jax.ShapeDtypeStruct(dmod_shape, f32),
        ]
        + flow_outs,
        scratch_shapes=[
            pltpu.VMEM((patches, width), f32),
            pltpu.VMEM((patches, 3 * width), bf16),
            pltpu.VMEM((width, 3 * width), f32),
            pltpu.VMEM((clips, 9 * width), f32),
            pltpu.VMEM((lead, clips, 9 * width), f32),
            pltpu.VMEM((lead, clips, 9 * width), f32),
            pltpu.VMEM(dmod_shape, f32),
            pltpu.SemaphoreType.DMA((swaps,)),
            pltpu.SemaphoreType.DMA((swaps,)),
        ]
        + spread_scratch(own, n_pos, places, width)
        + views[early:]
        + flow_scratch,
        compiler_params=pltpu.CompilerParams(
            vmem_limit_bytes=VMEM_LIMIT, collective_id=1, has_side_effects=True
        ),
        cost_estimate=pl.CostEstimate(
            flops=4 * rows * width * 3 * width + 10 * rows * patches * width,
            bytes_accessed=rows * width * 16 + weight.size * 2 + sizes * 4,
            transcendentals=rows * patches * HEADS,
        ),
        name="space_backward",
    )(go, qkv, lse, x, h, mods, weight, hot, dmod_rest, *views[:early])


def call_middle(o_one, x, grad, mods, same_clip, wso, wti, wto, wup, wdn):
    places, frames, width = x.shape
    count = max(1, min(places, 256 // frames))
    rows = count * frames
    hidden = wup.shape[1]
    pair = 2 * HEAD_DIM
    total = places * frames
    chunk = pl.BlockSpec((count, frames, width), lambda i: (i, 0, 0))

    def flat(cols):
        return pl.BlockSpec((rows, cols), lambda i: (i, 0))

    def flat_shape(cols):
        return jax.ShapeDtypeStruct((total, cols), bf16)

    def scratch(cols, dtype=f32):
        return pltpu.VMEM((rows, cols), dtype)

    lanes = jnp.concatenate([same_clip, same_clip], axis=1)
    flops = 2 * total * (2 * (wso.size + wti.size + wto.size + wup.size + wdn.size))
    return pl.pallas_call(
        middle,
        grid=(places // count,),
        in_specs=[chunk, chunk, chunk, resident(mods.shape), resident(lanes.shape)]
        + [resident(w.shape) for w in (wso, wti, wto, wup, wdn)],
        out_specs=[
            chunk,
            flat(hidden),
            flat(width),
            flat(width),
            flat(hidden),
            flat(width),
            flat(width),
            flat(width),
            flat(3 * width),
            flat(width),
            chunk,
            chunk,
            pl.BlockSpec((7, frames, width), lambda i: (0, 0, 0)),
        ],
        out_shape=[
            jax.ShapeDtypeStruct(x.shape, bf16),
            flat_shape(hidden),
            flat_shape(width),
            flat_shape(width),
            flat_shape(hidden),
            flat_shape(width),
            flat_shape(width),
            flat_shape(width),
            flat_shape(3 * width),
            flat_shape(width),
            jax.ShapeDtypeStruct(x.shape, bf16),
            jax.ShapeDtypeStruct(x.shape, f32),
            jax.ShapeDtypeStruct((7, frames, width), f32),
        ],
        scratch_shapes=[
            scratch(3 * width, bf16),
            pltpu.VMEM((HEADS // 2, rows, pair), f32),
            scratch(width),
            scratch(width),
            scratch(width),
            scratch(width),
            scratch(pair),
            scratch(pair),
            scratch(width),
            scratch(width),
        ]
        + [scratch(256)] * 4,
        compiler_params=pltpu.CompilerParams(vmem_limit_bytes=VMEM_LIMIT),
        cost_estimate=pl.CostEstimate(
            flops=flops, bytes_accessed=total * 40000, transcendentals=total * hidden
        ),
        name="middle",
    )(o_one, x, grad, mods, lanes, wso, wti, wto, wup, wdn)


def on_device(
    tokens,
    clip_lengths,
    timesteps,
    embed_first,
    embed_second,
    adaln_weight,
    spatial_in,
    spatial_out,
    temporal_in,
    temporal_out,
    hidden_up,
    hidden_down,
    grad_output,
    n_pos=16,
    n_clip=2,
):
    frames, places, width = tokens.shape
    rows = frames * places
    own = frames // n_pos
    patches = places * n_pos
    me = lax.axis_index("pos")
    clips = clip_lengths.shape[1]

    def exchange(values):
        sent = values.reshape(frames, places, width)
        got = lax.all_to_all(sent, "pos", split_axis=0, concat_axis=0, tiled=True)
        return got.reshape(n_pos, own, places, width)

    x_space = exchange(tokens)

    all_steps = by_distance(timesteps[0], "clip", n_clip)
    freq = frequency(all_steps)
    pre_cond = dot_exact(freq, embed_first)
    hidden_cond = jax.nn.silu(pre_cond)
    cond = dot_exact(hidden_cond, embed_second)
    cond_act = jax.nn.silu(cond)
    modulated = dot_exact(cond_act[:clips], adaln_weight)
    onehot, clip_ids = clip_onehot(clip_lengths[0], frames)
    per_frame = dot_high(onehot, modulated)
    own_frames = lax.dynamic_slice_in_dim(per_frame, me * own, own, 0)

    own_mods = own_frames[:, : 2 * width].reshape(own, 2, width)
    h_one, qkv_one, o_one, lse_one = call_space_forward(x_space, own_mods, spatial_in)

    def turn(values):
        return values.transpose(1, 0, 2)

    o_one = turn(o_one)
    mods = per_frame.reshape(frames, 9, width).transpose(1, 0, 2)
    same_clip = jnp.dot(onehot, onehot.T)
    (block_turned, act, grad_z, h_three, grad_u, o_two, grad_y_two, h_two, grad_qkv_two, grad_y_one, grad_o_one,
     grad_one, sums) = call_middle(
        o_one, turn(tokens), turn(grad_output), mods, same_clip, spatial_out, temporal_in, temporal_out,
        hidden_up, hidden_down,
    )
    block_out = turn(block_turned)
    grad_o_space = exchange(turn(grad_o_one))
    early = (
        weight_grad(h_three, grad_u),
        weight_grad(act, grad_z),
        weight_grad(h_two, grad_qkv_two),
        weight_grad(o_one.reshape(rows, width), grad_y_one),
        weight_grad(o_two, grad_y_two),
    )
    own_hot = lax.dynamic_slice_in_dim(onehot, me * own, own, 0)
    hot = jnp.broadcast_to(own_hot[:, :, None], (own, clips, 128))
    dmod_rest = dot_high(onehot.T, sums.transpose(1, 0, 2).reshape(frames, 7 * width))
    (
        back_places, dmod, g_hidden_up, g_hidden_down, g_temporal_in, g_spatial_out, g_temporal_out,
        in_low, in_high,
    ) = call_space_backward(
        grad_o_space, qkv_one, lse_one, x_space, h_one, own_mods, spatial_in, hot, dmod_rest,
        early, (False, True, True, True, True), n_clip,
    )
    grad_tokens = (turn(grad_one) + back_places.astype(f32)).astype(bf16)
    g_spatial_in = jnp.concatenate([in_low, in_high], axis=1)
    dmod = dmod.reshape(n_clip * clips, 9 * width)

    def own_columns(values):
        block = values.shape[1] // n_pos
        return lax.dynamic_slice_in_dim(values, me * block, block, 1)

    g_adaln = dot_high(own_columns(cond_act).T, dmod)
    grad_cond = dot_exact(dmod, adaln_weight.T) * silu_grad(cond)
    g_second = dot_high(own_columns(hidden_cond).T, grad_cond)
    grad_pre = dot_exact(grad_cond, embed_second.T) * silu_grad(pre_cond)
    g_first = dot_high(own_columns(freq).T, grad_pre)
    return (
        block_out,
        grad_tokens,
        g_first,
        g_second,
        g_adaln,
        g_spatial_in,
        g_spatial_out,
        g_temporal_in,
        g_temporal_out,
        g_hidden_up,
        g_hidden_down,
    )


def solution(mesh):
    in_specs = (
        P("clip", "pos", None),
        P("clip", None),
        P("clip", None),
        P(),
        P(),
        P(),
        P(),
        P(),
        P(),
        P(),
        P(),
        P(),
        P("clip", "pos", None),
    )
    out_specs = (P("clip", "pos", None),) * 2 + (P("pos", None),) * 9
    body = partial(on_device, n_pos=mesh.shape["pos"], n_clip=mesh.shape["clip"])
    return jax.shard_map(body, mesh=mesh, in_specs=in_specs, out_specs=out_specs, check_vma=False)
```
